32 devices in a mesh: groups: 2 (over y), tok: 4 (over z), mod: 2 (over x), fsdp: 2 (over core).
Axes of the slice: x: 2, y: 2, z: 4, core: 2. Of those that a mesh axis runs over, the one named last changes fastest.
Arguments:
- residual: bfloat16 [1024, 4096], P(('groups', 'tok'), ('fsdp', 'mod')), parts along dimension 0, may hold values from -30 to 30
- context: bfloat16 [1024, 4096], P(('groups', 'tok'), ('mod', 'fsdp')), parts along dimension 0, may hold values from -6 to 6
- out_proj: bfloat16 [4096, 4096], P('tok', ('fsdp', 'mod')), may hold values from -0.09375 to 0.09375
- norm_gain: bfloat16 [2, 4096], P(None, ('fsdp', 'mod')), may hold values from 0.099609375 to 1.8984375
- router_weight: bfloat16 [4096, 4], P(('fsdp', 'mod')), may hold values from -0.25 to 0.25
- block_modality: int32 [8], P(('groups', 'tok')), parts along dimension 0, may hold values from 0 to 1, as said below
- expert_rows: int32 [4, 128], P(None, ('groups', 'tok')), parts along dimension 1, may hold values from -1 to 127, as said below
- gate_weight: bfloat16 [4, 4096, 11008], P('mod', 'fsdp', 'tok'), may hold values from -0.09375 to 0.09375
- up_weight: bfloat16 [4, 4096, 11008], P('mod', 'fsdp', 'tok'), may hold values from -0.09375 to 0.09375
- down_weight: bfloat16 [4, 11008, 4096], P('mod', 'tok', 'fsdp'), may hold values from -0.0546875 to 0.0546875
Outputs:
- expert_out: bfloat16 [1024, 4096], P(('groups', 'tok'), ('fsdp', 'mod')), parts along dimension 0
The draws below stay inside these ranges and needn't reach their ends.
There are 2 independent parts, one for each index of `groups`. The reference program is written for one: setup_inputs(seed, part) draws one part's arguments, and reference() takes and returns one part's arrays. A program takes and returns all parts, laid end to end along the dimension named above; an argument that names none is the same for every part. Nothing has to cross between parts.
Inputs may be any that keep to these rules, and one draw needn't show every extreme that they name: `block_modality`: both modalities occur in every window. `expert_rows`: slot s = t * 16 + j of expert e names a row among tokens t * 128 to (t + 1) * 128 - 1, or is -1 if unused. Experts below 2 take only text tokens, the others only image tokens; no expert takes a token twice; in each aligned block of 16 slots the used ones come first; every expert fills all 16 slots of at least one index of tok whose tokens have the expert's modality.
All inputs are finite; a program needn't handle non-finite values.
Results may differ from the reference program's by a relative error of at most 0.02.
Values may be sent and summed in bfloat16 or wider, within the bound.
No kernel may reach another device: no remote copies, remote signals or barrier semaphores. Data moves between devices by JAX's collectives and lax.ppermute only.
A program may use at most 192 MiB of HBM per device.

```python
import jax
import jax.numpy as jnp
from jax import lax

D = 4096
FF = 11008
EXPERTS = 4
BLOCK = 128
TOK_DEV = 128
CAPACITY = 16
TOKENS = 512
BLOCKS = 4
SLOTS = 64
UNITS_DEV = 2752
N_TOK = 4


def modality_layout(key):
    base_key = jax.random.fold_in(key, 5)
    flags = jax.random.randint(jax.random.fold_in(base_key, 1), (BLOCKS,), 0, 2)
    ordering = jax.random.permutation(jax.random.fold_in(base_key, 2), BLOCKS)
    flags = flags.at[ordering[0]].set(0)
    flags = flags.at[ordering[1]].set(1)
    return flags.astype(jnp.int32)


def draw_block_modality(key, part):
    return modality_layout(key)


def draw_expert_rows(key, part):
    flags = modality_layout(key)
    devices = TOKENS // TOK_DEV
    token_flags = jnp.repeat(flags, BLOCK).reshape(devices, TOK_DEV)
    expert_flag = (jnp.arange(EXPERTS) // (EXPERTS // 2)).astype(jnp.int32)
    eligible = (token_flags[None, :, :] == expert_flag[:, None, None]).astype(jnp.int32)
    random_key = jax.random.fold_in(key, 9)
    row_noise = jax.random.randint(jax.random.fold_in(random_key, 1), (EXPERTS, devices, TOK_DEV), 0, 65536)
    row_score = row_noise * TOK_DEV + jnp.arange(TOK_DEV, dtype=jnp.int32)[None, None, :] + eligible * 2 ** 27
    chosen_rows = lax.top_k(row_score, CAPACITY)[1]
    has_rows = jnp.max(eligible, axis=2)
    counts = jax.random.randint(jax.random.fold_in(random_key, 2), (EXPERTS, devices), (3 * CAPACITY + 3) // 4, CAPACITY + 1)
    device_noise = jax.random.randint(jax.random.fold_in(random_key, 3), (EXPERTS, devices), 0, 65536)
    device_score = device_noise * devices + jnp.arange(devices, dtype=jnp.int32)[None, :] + has_rows * 2 ** 27
    favored = lax.top_k(device_score, 1)[1]
    is_favored = jnp.arange(devices, dtype=jnp.int32)[None, :] == favored
    counts = jnp.where(is_favored, CAPACITY, counts) * has_rows
    slot_index = jnp.arange(CAPACITY, dtype=jnp.int32)[None, None, :]
    rows = jnp.where(slot_index < counts[:, :, None], chosen_rows, -1)
    return rows.reshape(EXPERTS, devices * CAPACITY).astype(jnp.int32)


def draw_residual(key, part):
    position = jnp.arange(D, dtype=jnp.float32) / D
    rough = jax.random.uniform(jax.random.fold_in(key, 1), (D,), jnp.float32, 0.7, 1.4)
    column_scale = 0.6 * jnp.exp(position * jnp.log(3.0)) * rough
    row_scale = jnp.exp(jax.random.uniform(jax.random.fold_in(key, 2), (TOKENS, 1), jnp.float32, jnp.log(0.3), jnp.log(3.0)))
    values = jnp.clip(jax.random.normal(jax.random.fold_in(key, 4), (TOKENS, D), jnp.float32), -5.0, 5.0)
    result = jnp.clip(values * row_scale * column_scale[None, :], -30.0, 30.0)
    return result.astype(jnp.bfloat16)


def shard_levels(stream_key, shape, shards, smallest, top_value):
    loudness, own = 1.0, jax.random.fold_in(stream_key, 6)
    for axis_at, shards_of in shards:
        draws = jnp.exp(jax.random.uniform(jax.random.fold_in(own, axis_at), (shards_of,), jnp.float32, smallest / len(shards), top_value / len(shards)))
        loudness = loudness * jnp.repeat(draws, shape[axis_at] // shards_of).reshape([-1 if axis == axis_at else 1 for axis in range(len(shape))])
    return loudness


def noise(key, extent, deviation, bound, cuts=(), kind=jnp.bfloat16):
    loudness = shard_levels(key, extent, cuts, -0.22, 0.18) if cuts else 1.0
    drawn = jax.random.normal(key, extent, jnp.float32) * deviation * loudness
    return jnp.minimum(jnp.maximum(drawn, -bound), bound).astype(kind)


def setup_inputs(seed: int = 0, part: int = 0) -> dict:
    key_list = jax.random.split(jax.random.key(seed), 11)
    part_splits = jax.random.split(jax.random.fold_in(key_list[10], part), 11)
    residual = draw_residual(jax.random.fold_in(jax.random.fold_in(key_list[10], part), 71), part)
    context = noise(part_splits[1], (TOKENS, D), 1.0, 6.0, ((0, 4), (1, 4)))
    out_proj = noise(key_list[2], (D, D), D ** -0.5, 0.09375, ((0, 4), (1, 4)))
    norm_gain = jnp.clip(1.0 + 0.18 * jax.random.normal(key_list[3], (2, D), jnp.float32), 0.099609375, 1.8984375).astype(jnp.bfloat16)
    router_weight = noise(key_list[4], (D, EXPERTS), (D // 8) ** -0.5, 0.25, ((0, 4),))
    block_modality = draw_block_modality(jax.random.fold_in(jax.random.fold_in(key_list[10], part), 71), part)
    expert_rows = draw_expert_rows(jax.random.fold_in(jax.random.fold_in(key_list[10], part), 71), part)
    gate_weight = noise(key_list[7], (EXPERTS, D, FF), D ** -0.5, 0.09375, ((0, 2), (1, 2), (2, 4)))
    up_weight = noise(key_list[8], (EXPERTS, D, FF), D ** -0.5, 0.09375, ((0, 2), (1, 2), (2, 4)))
    down_weight = noise(key_list[9], (EXPERTS, FF, D), FF ** -0.5, 0.0546875, ((0, 2), (1, 4), (2, 2)))
    return dict(residual=residual, context=context, out_proj=out_proj, norm_gain=norm_gain, router_weight=router_weight, block_modality=block_modality, expert_rows=expert_rows, gate_weight=gate_weight, up_weight=up_weight, down_weight=down_weight)


def reference(residual, context, out_proj, norm_gain, router_weight, block_modality, expert_rows, gate_weight, up_weight, down_weight):
    projected = jnp.dot(context, out_proj, preferred_element_type=jnp.float32)
    hidden = residual.astype(jnp.float32) + projected
    inverse = lax.rsqrt(lax.optimization_barrier(jnp.mean(hidden * hidden, axis=1)) + 1e-05)
    token_mod = jnp.repeat(block_modality, BLOCK)
    gain_table = norm_gain.astype(jnp.float32)
    token_gain = jnp.where(token_mod[:, None] == 0, gain_table[0][None, :], gain_table[1][None, :])
    normed = hidden * inverse[:, None] * token_gain
    normed_rows = normed.astype(jnp.bfloat16)
    logits = jnp.dot(normed, router_weight.astype(jnp.float32), precision=lax.Precision.HIGHEST)
    score = jax.nn.sigmoid(logits)
    slot_owner = jnp.arange(SLOTS, dtype=jnp.int32) // CAPACITY

    def one_expert(running, inputs):
        rows, expert_index, gate_w, up_w, down_w = inputs
        valid = rows >= 0
        token = (slot_owner * TOK_DEV + jnp.maximum(rows, 0)).astype(jnp.int32)
        picked = jnp.where(valid[:, None], normed_rows[token], jnp.zeros((), jnp.bfloat16))
        gate_pre = jnp.dot(picked, gate_w, preferred_element_type=jnp.float32)
        up_pre = jnp.dot(picked, up_w, preferred_element_type=jnp.float32)
        activation = (jax.nn.silu(gate_pre) * up_pre).astype(jnp.bfloat16)

        def add_block(accum, block_index):
            offset = (block_index * UNITS_DEV).astype(jnp.int32)
            act_rows = lax.dynamic_slice_in_dim(activation, offset, UNITS_DEV, 1)
            down_rows = lax.dynamic_slice_in_dim(down_w, offset, UNITS_DEV, 0)
            product = jnp.dot(act_rows, down_rows, preferred_element_type=jnp.float32)
            product = lax.optimization_barrier(product.astype(jnp.bfloat16)).astype(jnp.float32)
            return (accum + product, None)
        expert_value = lax.scan(add_block, jnp.zeros((SLOTS, D), jnp.float32), jnp.arange(N_TOK, dtype=jnp.int32))[0]
        weight = jnp.where(valid, score[token, expert_index], jnp.zeros((), jnp.float32))
        running = running.at[token].add(expert_value * weight[:, None])
        return (running, None)
    expert_ids = jnp.arange(EXPERTS, dtype=jnp.int32)
    total = lax.scan(one_expert, jnp.zeros((TOKENS, D), jnp.float32), (expert_rows, expert_ids, gate_weight, up_weight, down_weight))[0]
    return total.astype(jnp.bfloat16)
```

```python
import functools

import jax
import jax.numpy as jnp
from jax import lax
from jax.sharding import PartitionSpec as P

D = 4096
STAT_COLS = 128
FEW = 4


def ring(size, step):
    return [(i, (i + step) % size) for i in range(size)]


def reduce_tok(blocks, n_tok):
    if n_tok > FEW:
        return lax.psum_scatter(blocks, "tok", scatter_dimension=0, tiled=False).astype(jnp.float32)
    own = lax.axis_index("tok")
    total = lax.dynamic_index_in_dim(blocks, own, 0, False).astype(jnp.float32)
    for step in range(1, n_tok):
        sent = lax.dynamic_index_in_dim(blocks, (own + step) % n_tok, 0, False)
        total = total + lax.ppermute(sent, "tok", ring(n_tok, step)).astype(jnp.float32)
    return total


def gather_tok(rows, n_tok):
    if n_tok > FEW:
        return lax.all_gather(rows, "tok", axis=0, tiled=False)
    own = lax.axis_index("tok")
    result = jnp.zeros((n_tok,) + rows.shape, rows.dtype)
    result = lax.dynamic_update_index_in_dim(result, rows, own, 0)
    for step in range(1, n_tok):
        got = lax.ppermute(rows, "tok", ring(n_tok, step))
        result = lax.dynamic_update_index_in_dim(result, got, (own - step) % n_tok, 0)
    return result


def spread_context(rows, n_tok, n_mod, n_fsdp):
    if n_tok > FEW or n_tok != n_mod * n_fsdp:
        full = lax.all_gather(rows, ("mod", "fsdp"), axis=1, tiled=True)
        split = full.reshape(full.shape[0], n_tok, full.shape[1] // n_tok).transpose(1, 0, 2)
        return lax.all_to_all(split, "tok", 0, 0, tiled=True)
    pairs = [(t * n_tok + q, q * n_tok + t) for t in range(n_tok) for q in range(n_tok)]
    swapped = lax.ppermute(rows, ("tok", "mod", "fsdp"), pairs)
    return lax.all_gather(swapped, ("mod", "fsdp"), axis=0, tiled=False)


def local(
    residual,
    context,
    out_proj,
    norm_gain,
    router_weight,
    block_modality,
    expert_rows,
    gate_weight,
    up_weight,
    down_weight,
    *,
    n_tok,
    n_mod,
    n_fsdp,
):
    token_count = residual.shape[0]
    experts, capacity = expert_rows.shape
    kind_experts = experts // 2
    slots = kind_experts * capacity
    local_experts = gate_weight.shape[0]
    columns = residual.shape[1]
    assert block_modality.shape == (1,) and n_mod * local_experts == experts
    modality = block_modality[0]
    first = modality * kind_experts
    mod_index = lax.axis_index("mod")

    own_rows = lax.dynamic_slice_in_dim(expert_rows, first, kind_experts, 0).reshape(slots)
    pick = own_rows[:, None] == lax.iota(jnp.int32, token_count)[None, :]
    pick_half = pick.astype(jnp.bfloat16)
    picked_context = jnp.dot(pick_half, context, preferred_element_type=jnp.float32).astype(jnp.bfloat16)
    picked_residual = jnp.dot(pick_half, residual, preferred_element_type=jnp.float32)

    spread = spread_context(picked_context, n_tok, n_mod, n_fsdp)
    partial = jnp.einsum("tsk,kc->tsc", spread, out_proj, preferred_element_type=jnp.float32)
    hidden = picked_residual + reduce_tok(partial.astype(jnp.bfloat16), n_tok)

    gain_table = norm_gain.astype(jnp.float32)
    gained = hidden * jnp.where(modality == 0, gain_table[0], gain_table[1])[None, :]
    router = lax.dynamic_slice_in_dim(router_weight.astype(jnp.float32), first, kind_experts, 1)
    slot_router = jnp.repeat(router.T, capacity, axis=0)
    squares = jnp.sum(hidden * hidden, axis=1, keepdims=True)
    logits = jnp.sum(gained * slot_router, axis=1, keepdims=True)
    flag = jnp.broadcast_to(modality.astype(jnp.bfloat16), (slots, 1))
    stat_list = []
    for stat in (squares, logits):
        high = lax.reduce_precision(stat, 8, 7)
        stat_list += [high.astype(jnp.bfloat16), (stat - high).astype(jnp.bfloat16)]
    packed = jnp.concatenate(
        [gained.astype(jnp.bfloat16)] + stat_list
        + [flag, jnp.zeros((slots, STAT_COLS - 5), jnp.bfloat16)],
        axis=1,
    )

    everyone = gather_tok(packed, n_tok)
    both = lax.all_gather(everyone, "mod", axis=0, tiled=False)
    kind_first = (mod_index * local_experts) % kind_experts
    both = both.reshape(n_mod, n_tok, kind_experts, capacity, columns + STAT_COLS)
    mine = lax.dynamic_slice_in_dim(both, kind_first, local_experts, 2)
    piece = mine[..., :columns].transpose(2, 1, 3, 0, 4).reshape(
        local_experts, n_tok * capacity, n_mod * columns
    )
    tail = mine[..., columns : columns + 5].astype(jnp.float32)
    half_stats = jnp.sum(
        jnp.stack([tail[..., 0] + tail[..., 1], tail[..., 2] + tail[..., 3]], axis=-1), axis=0
    )
    stats = lax.psum(half_stats, "fsdp")
    flags = tail[0, :, :, :, 4]
    by_expert = stats.transpose(1, 0, 2, 3).reshape(local_experts, n_tok * capacity, 2)
    inverse = lax.rsqrt(by_expert[..., 0:1] / D + 1e-05)
    score = jax.nn.sigmoid(by_expert[..., 1:2] * inverse)

    gate_part = jnp.einsum("esd,edf->esf", piece, gate_weight, preferred_element_type=jnp.float32)
    up_part = jnp.einsum("esd,edf->esf", piece, up_weight, preferred_element_type=jnp.float32)
    gate_half = gate_part.astype(jnp.bfloat16)
    up_half = up_part.astype(jnp.bfloat16)
    if n_fsdp == 2:
        swap = [(0, 1), (1, 0)]
        gate_sum = gate_half.astype(jnp.float32) + lax.ppermute(gate_half, "fsdp", swap).astype(jnp.float32)
        up_sum = up_half.astype(jnp.float32) + lax.ppermute(up_half, "fsdp", swap).astype(jnp.float32)
    else:
        gate_sum = lax.psum(gate_half, "fsdp").astype(jnp.float32)
        up_sum = lax.psum(up_half, "fsdp").astype(jnp.float32)
    activation = (jax.nn.silu(gate_sum * inverse) * (up_sum * inverse)).astype(jnp.bfloat16)
    value = jnp.einsum("esf,efd->esd", activation, down_weight, preferred_element_type=jnp.float32)
    value = (value * score).astype(jnp.bfloat16)
    value = value.reshape(local_experts, n_tok, capacity, n_mod * columns).transpose(1, 0, 2, 3)

    own_kind = (mod_index * local_experts) // kind_experts
    valid = (flags == own_kind.astype(jnp.float32))[..., None]
    if n_mod == 2:
        value = value.reshape(n_tok, local_experts, capacity, n_mod, columns)
        kept = lax.dynamic_index_in_dim(value, mod_index, 3, False)
        sent = lax.dynamic_index_in_dim(value, 1 - mod_index, 3, False)
        got = lax.ppermute(sent, "mod", [(0, 1), (1, 0)])
        merged = jnp.where(valid, kept, got).reshape(n_tok, slots, columns)
    else:
        value = jnp.where(valid, value, jnp.zeros((), jnp.bfloat16))
        wide = jnp.zeros((n_tok, kind_experts, capacity, n_mod * columns), jnp.bfloat16)
        wide = lax.dynamic_update_slice_in_dim(wide, value, kind_first, 1)
        wide = wide.reshape(n_tok, slots, n_mod * columns)
        merged = lax.psum_scatter(wide, "mod", scatter_dimension=2, tiled=True)
    summed = reduce_tok(merged, n_tok)
    return jnp.dot(
        pick.astype(jnp.float32).T, summed, precision=lax.Precision.HIGHEST
    ).astype(jnp.bfloat16)


def solution(mesh):
    placed = (
        P(("groups", "tok"), ("fsdp", "mod")),
        P(("groups", "tok"), ("mod", "fsdp")),
        P("tok", ("fsdp", "mod")),
        P(None, ("fsdp", "mod")),
        P(("fsdp", "mod"), None),
        P(("groups", "tok")),
        P(None, ("groups", "tok")),
        P("mod", "fsdp", "tok"),
        P("mod", "fsdp", "tok"),
        P("mod", "tok", "fsdp"),
    )
    sizes = dict(n_tok=mesh.shape["tok"], n_mod=mesh.shape["mod"], n_fsdp=mesh.shape["fsdp"])
    return jax.shard_map(
        functools.partial(local, **sizes),
        mesh=mesh,
        in_specs=placed,
        out_specs=P(("groups", "tok"), ("fsdp", "mod")),
        check_vma=False,
    )
```

```python
import functools

import jax
import jax.numpy as jnp
from jax import lax
from jax.experimental import pallas as pl
from jax.experimental.pallas import tpu as pltpu
from jax.sharding import PartitionSpec as P

D = 4096
STAT_COLS = 128
FEW = 4


def ring(size, step):
    return [(i, (i + step) % size) for i in range(size)]


def reduce_tok(blocks, n_tok):
    if n_tok > FEW:
        return lax.psum_scatter(blocks, "tok", scatter_dimension=0, tiled=False).astype(jnp.float32)
    own = lax.axis_index("tok")
    total = lax.dynamic_index_in_dim(blocks, own, 0, False).astype(jnp.float32)
    for step in range(1, n_tok):
        sent = lax.dynamic_index_in_dim(blocks, (own + step) % n_tok, 0, False)
        total = total + lax.ppermute(sent, "tok", ring(n_tok, step)).astype(jnp.float32)
    return total


def gather_tok(rows, n_tok):
    if n_tok > FEW:
        return lax.all_gather(rows, "tok", axis=0, tiled=False)
    own = lax.axis_index("tok")
    result = jnp.zeros((n_tok,) + rows.shape, rows.dtype)
    result = lax.dynamic_update_index_in_dim(result, rows, own, 0)
    for step in range(1, n_tok):
        got = lax.ppermute(rows, "tok", ring(n_tok, step))
        result = lax.dynamic_update_index_in_dim(result, got, (own - step) % n_tok, 0)
    return result


def spread_context(rows, n_tok, n_mod, n_fsdp):
    if n_tok > FEW or n_tok != n_mod * n_fsdp:
        full = lax.all_gather(rows, ("mod", "fsdp"), axis=1, tiled=True)
        split = full.reshape(full.shape[0], n_tok, full.shape[1] // n_tok).transpose(1, 0, 2)
        return lax.all_to_all(split, "tok", 0, 0, tiled=True)
    pairs = [(t * n_tok + q, q * n_tok + t) for t in range(n_tok) for q in range(n_tok)]
    swapped = lax.ppermute(rows, ("tok", "mod", "fsdp"), pairs)
    return lax.all_gather(swapped, ("mod", "fsdp"), axis=0, tiled=False)


def local(
    residual,
    context,
    out_proj,
    norm_gain,
    router_weight,
    block_modality,
    expert_rows,
    gate_weight,
    up_weight,
    down_weight,
    *,
    n_tok,
    n_mod,
    n_fsdp,
):
    token_count = residual.shape[0]
    experts, capacity = expert_rows.shape
    kind_experts = experts // 2
    slots = kind_experts * capacity
    local_experts = gate_weight.shape[0]
    columns = residual.shape[1]
    assert block_modality.shape == (1,) and n_mod * local_experts == experts
    modality = block_modality[0]
    first = modality * kind_experts
    mod_index = lax.axis_index("mod")

    own_rows = lax.dynamic_slice_in_dim(expert_rows, first, kind_experts, 0).reshape(slots)
    pick = own_rows[:, None] == lax.iota(jnp.int32, token_count)[None, :]
    pick_half = pick.astype(jnp.bfloat16)
    picked_context = jnp.dot(pick_half, context, preferred_element_type=jnp.float32).astype(jnp.bfloat16)
    picked_residual = jnp.dot(pick_half, residual, preferred_element_type=jnp.float32)

    spread = spread_context(picked_context, n_tok, n_mod, n_fsdp)
    partial = jnp.einsum("tsk,kc->tsc", spread, out_proj, preferred_element_type=jnp.float32)
    hidden = picked_residual + reduce_tok(partial.astype(jnp.bfloat16), n_tok)

    gain_table = norm_gain.astype(jnp.float32)
    gained = hidden * jnp.where(modality == 0, gain_table[0], gain_table[1])[None, :]
    router = lax.dynamic_slice_in_dim(router_weight.astype(jnp.float32), first, kind_experts, 1)
    slot_router = jnp.repeat(router.T, capacity, axis=0)
    squares = jnp.sum(hidden * hidden, axis=1, keepdims=True)
    logits = jnp.sum(gained * slot_router, axis=1, keepdims=True)
    flag = jnp.broadcast_to(modality.astype(jnp.bfloat16), (slots, 1))
    stat_list = []
    for stat in (squares, logits):
        high = lax.reduce_precision(stat, 8, 7)
        stat_list += [high.astype(jnp.bfloat16), (stat - high).astype(jnp.bfloat16)]
    packed = jnp.concatenate(
        [gained.astype(jnp.bfloat16)] + stat_list
        + [flag, jnp.zeros((slots, STAT_COLS - 5), jnp.bfloat16)],
        axis=1,
    )

    everyone = gather_tok(packed, n_tok)
    both = lax.all_gather(everyone, "mod", axis=0, tiled=False)
    kind_first = (mod_index * local_experts) % kind_experts
    both = both.reshape(n_mod, n_tok, kind_experts, capacity, columns + STAT_COLS)
    mine = lax.dynamic_slice_in_dim(both, kind_first, local_experts, 2)
    piece = mine[..., :columns].transpose(2, 1, 3, 0, 4).reshape(
        local_experts, n_tok * capacity, n_mod * columns
    )
    tail = mine[..., columns : columns + 5].astype(jnp.float32)
    half_stats = jnp.sum(
        jnp.stack([tail[..., 0] + tail[..., 1], tail[..., 2] + tail[..., 3]], axis=-1), axis=0
    )
    stats = lax.psum(half_stats, "fsdp")
    flags = tail[0, :, :, :, 4]
    by_expert = stats.transpose(1, 0, 2, 3).reshape(local_experts, n_tok * capacity, 2)
    inverse = lax.rsqrt(by_expert[..., 0:1] / D + 1e-05)
    score = jax.nn.sigmoid(by_expert[..., 1:2] * inverse)

    gate_part = jnp.einsum("esd,edf->esf", piece, gate_weight, preferred_element_type=jnp.float32)
    up_part = jnp.einsum("esd,edf->esf", piece, up_weight, preferred_element_type=jnp.float32)
    gate_half = gate_part.astype(jnp.bfloat16)
    up_half = up_part.astype(jnp.bfloat16)
    if n_fsdp == 2:
        swap = [(0, 1), (1, 0)]
        gate_sum = gate_half.astype(jnp.float32) + lax.ppermute(gate_half, "fsdp", swap).astype(jnp.float32)
        up_sum = up_half.astype(jnp.float32) + lax.ppermute(up_half, "fsdp", swap).astype(jnp.float32)
    else:
        gate_sum = lax.psum(gate_half, "fsdp").astype(jnp.float32)
        up_sum = lax.psum(up_half, "fsdp").astype(jnp.float32)
    activation = (jax.nn.silu(gate_sum * inverse) * (up_sum * inverse)).astype(jnp.bfloat16)
    value = jnp.einsum("esf,efd->esd", activation, down_weight, preferred_element_type=jnp.float32)
    value = (value * score).astype(jnp.bfloat16)
    value = value.reshape(local_experts, n_tok, capacity, n_mod * columns).transpose(1, 0, 2, 3)

    own_kind = (mod_index * local_experts) // kind_experts
    valid = (flags == own_kind.astype(jnp.float32))[..., None]
    if n_mod == 2:
        value = value.reshape(n_tok, local_experts, capacity, n_mod, columns)
        kept = lax.dynamic_index_in_dim(value, mod_index, 3, False)
        sent = lax.dynamic_index_in_dim(value, 1 - mod_index, 3, False)
        got = lax.ppermute(sent, "mod", [(0, 1), (1, 0)])
        merged = jnp.where(valid, kept, got).reshape(n_tok, slots, columns)
    else:
        value = jnp.where(valid, value, jnp.zeros((), jnp.bfloat16))
        wide = jnp.zeros((n_tok, kind_experts, capacity, n_mod * columns), jnp.bfloat16)
        wide = lax.dynamic_update_slice_in_dim(wide, value, kind_first, 1)
        wide = wide.reshape(n_tok, slots, n_mod * columns)
        merged = lax.psum_scatter(wide, "mod", scatter_dimension=2, tiled=True)
    summed = reduce_tok(merged, n_tok)
    return jnp.dot(
        pick.astype(jnp.float32).T, summed, precision=lax.Precision.HIGHEST
    ).astype(jnp.bfloat16)


SWAP = [(0, 1), (1, 0)]
CHUNK = 512


def crossed(axis_sizes_bits, flip):
    return [(i, i ^ flip) for i in range(1 << axis_sizes_bits)]


def keep_kernel(index_ref, weight_ref, held_ref, semaphore):
    copy = pltpu.make_async_copy(weight_ref.at[index_ref[0]], held_ref, semaphore)
    copy.start()
    copy.wait()


def keep_on_chip(index, weight, name):
    weight = pltpu.with_memory_space_constraint(weight, pltpu.HBM)
    size = weight.shape[1] * weight.shape[2] * 2
    return pl.pallas_call(
        keep_kernel,
        out_shape=pltpu.VMEM(weight.shape[1:], weight.dtype),
        in_specs=[pl.BlockSpec(memory_space=pltpu.SMEM), pl.BlockSpec(memory_space=pltpu.HBM)],
        out_specs=pl.BlockSpec(memory_space=pltpu.VMEM),
        scratch_shapes=[pltpu.SemaphoreType.DMA(())],
        compiler_params=pltpu.CompilerParams(vmem_limit_bytes=1 << 20),
        cost_estimate=pl.CostEstimate(flops=0, transcendentals=0, bytes_accessed=size),
        name=name,
    )(index, weight)


def project_kernel(flip_ref, *refs):
    block_refs, weight_ref, out_ref, rows_ref = refs[:4], refs[4], refs[5], refs[6]
    slots = block_refs[0].shape[0]
    for u, block_ref in enumerate(block_refs):
        rows_ref[u * slots : (u + 1) * slots, :] = block_ref[...]
    product = jnp.dot(rows_ref[...], weight_ref[...], preferred_element_type=jnp.float32)
    product = product.astype(jnp.bfloat16)
    for u in range(len(block_refs)):
        out_ref[flip_ref[0] ^ u] = product[u * slots : (u + 1) * slots, :]


def project(flip, blocks, weight):
    slots, depth = blocks[0].shape
    return pl.pallas_call(
        project_kernel,
        out_shape=jax.ShapeDtypeStruct((len(blocks), slots, weight.shape[1]), jnp.bfloat16),
        in_specs=[pl.BlockSpec(memory_space=pltpu.SMEM)]
        + [pl.BlockSpec(memory_space=pltpu.VMEM)] * (len(blocks) + 1),
        out_specs=pl.BlockSpec(memory_space=pltpu.VMEM),
        scratch_shapes=[pltpu.VMEM((len(blocks) * slots, depth), jnp.bfloat16)],
        compiler_params=pltpu.CompilerParams(vmem_limit_bytes=8 << 20),
        name="project",
    )(flip, *blocks, weight)


def gate_up_kernel(side_ref, own_ref, far_ref, side_own_ref, side_far_ref, gate_ref, up_ref, out_ref, rows_ref):
    half = own_ref.shape[0]
    columns = rows_ref.shape[1] // 2
    units = gate_ref.shape[0]
    for side in range(2):

        @pl.when(side_ref[0] == side)
        def _():
            here, there = side * columns, (1 - side) * columns
            rows_ref[:half, here : here + columns] = own_ref[:, :columns]
            rows_ref[half:, here : here + columns] = far_ref[:, :columns]
            rows_ref[:half, there : there + columns] = side_own_ref[:, :columns]
            rows_ref[half:, there : there + columns] = side_far_ref[:, :columns]

    rows = rows_ref[...]
    for which, weight_ref in enumerate((gate_ref, up_ref)):
        for start in range(0, units, CHUNK):
            stop = min(start + CHUNK, units)
            product = lax.dot_general(
                rows, weight_ref[start:stop, :], (((1,), (1,)), ((), ())),
                preferred_element_type=jnp.float32,
            )
            out_ref[which, :, start:stop] = product.astype(jnp.bfloat16)


def gate_up(side, blocks, gate, up):
    half = blocks[0].shape[0]
    units, depth = gate.shape
    return pl.pallas_call(
        gate_up_kernel,
        out_shape=jax.ShapeDtypeStruct((2, 2 * half, units), jnp.bfloat16),
        in_specs=[pl.BlockSpec(memory_space=pltpu.SMEM)] + [pl.BlockSpec(memory_space=pltpu.VMEM)] * 6,
        out_specs=pl.BlockSpec(memory_space=pltpu.VMEM),
        scratch_shapes=[pltpu.VMEM((2 * half, depth), jnp.bfloat16)],
        compiler_params=pltpu.CompilerParams(vmem_limit_bytes=8 << 20),
        cost_estimate=pl.CostEstimate(
            flops=8 * half * units * depth, transcendentals=0, bytes_accessed=4 * half * units * 2
        ),
        name="gate_up",
    )(side, *blocks, gate, up)


def down_kernel(side_ref, mine_ref, other_ref, stat_ref, weight_ref, out_ref, act_ref):
    units, width = weight_ref.shape
    stat = stat_ref[...]
    squares = stat[:, 0:1] + stat[:, 1:2]
    inverse = lax.rsqrt(squares / D + 1e-05)
    logits = (stat[:, 2:3] + stat[:, 3:4]) * inverse
    score = 1.0 / (1.0 + jnp.exp(-logits))
    for start in range(0, units, CHUNK):
        stop = min(start + CHUNK, units)
        gate, up = [
            (
                mine_ref[which, :, start:stop].astype(jnp.float32)
                + other_ref[which, :, start:stop].astype(jnp.float32)
            )
            * inverse
            for which in range(2)
        ]
        act_ref[:, start:stop] = (gate / (1.0 + jnp.exp(-gate)) * up).astype(jnp.bfloat16)
    columns = width // 2
    for start in range(0, width, CHUNK):
        value = jnp.dot(
            act_ref[...], weight_ref[:, start : start + CHUNK], preferred_element_type=jnp.float32
        )
        quarter = start // columns
        at = start - quarter * columns
        out_ref[side_ref[0] ^ quarter, :, at : at + CHUNK] = (value * score).astype(jnp.bfloat16)


def down(side, mine, other, stat, weight):
    rows = stat.shape[0]
    units, width = weight.shape
    return pl.pallas_call(
        down_kernel,
        out_shape=jax.ShapeDtypeStruct((2, rows, width // 2), jnp.bfloat16),
        in_specs=[pl.BlockSpec(memory_space=pltpu.SMEM)] + [pl.BlockSpec(memory_space=pltpu.VMEM)] * 4,
        out_specs=pl.BlockSpec(memory_space=pltpu.VMEM),
        scratch_shapes=[pltpu.VMEM((rows, units), jnp.bfloat16)],
        compiler_params=pltpu.CompilerParams(vmem_limit_bytes=8 << 20),
        cost_estimate=pl.CostEstimate(
            flops=2 * rows * units * width, transcendentals=2 * rows * units, bytes_accessed=rows * width * 2
        ),
        name="down",
    )(side, mine, other, stat, weight)


def paired_local(
    residual,
    context,
    out_proj,
    norm_gain,
    router_weight,
    block_modality,
    expert_rows,
    gate_weight,
    up_weight,
    down_weight,
):
    token_count, columns = residual.shape
    experts, capacity = expert_rows.shape
    kind_experts = experts // 2
    slots = kind_experts * capacity
    assert block_modality.shape == (1,) and kind_experts == 2 and gate_weight.shape[0] == 2
    modality = block_modality[0]
    first = modality * kind_experts
    group = lax.axis_index("groups")
    tok = lax.axis_index("tok")
    side = lax.axis_index("mod")
    group_list, side_list = group.reshape(1), side.reshape(1)

    gate_held = keep_on_chip(group_list, gate_weight.swapaxes(1, 2), "keep_gate")
    up_held = keep_on_chip(group_list, up_weight.swapaxes(1, 2), "keep_up")
    down_held = keep_on_chip(group_list, down_weight, "keep_down")

    kind_rows = lax.dynamic_slice_in_dim(expert_rows, first, kind_experts, 0)
    own_rows = jnp.where(group == 0, kind_rows, kind_rows[::-1]).reshape(slots)
    pick = own_rows[:, None] == lax.iota(jnp.int32, token_count)[None, :]
    pick_half = pick.astype(jnp.bfloat16)
    picked_context = jnp.dot(pick_half, context, preferred_element_type=jnp.float32).astype(jnp.bfloat16)
    picked_residual = jnp.dot(pick_half, residual, preferred_element_type=jnp.float32)

    plane = ("tok", "mod", "fsdp")
    to_first = [(t * 4 + q, q * 4 + t) for t in range(4) for q in range(4)]
    to_second = [(t * 4 + q, q * 4 + (t ^ 2)) for t in range(4) for q in range(4)]
    near = lax.ppermute(picked_context, plane, to_first)
    across = lax.ppermute(picked_context, plane, to_second)
    near_core = lax.ppermute(near, "fsdp", SWAP)
    across_core = lax.ppermute(across, "fsdp", SWAP)
    corner = 2 * side + lax.axis_index("fsdp")
    partial = project((tok ^ corner).reshape(1), [near, near_core, across, across_core], out_proj)
    hidden = picked_residual + partial[0].astype(jnp.float32)
    for v in (3, 2, 1):
        hidden = hidden + lax.ppermute(partial[v], "tok", crossed(2, v)).astype(jnp.float32)

    gain_table = norm_gain.astype(jnp.float32)
    gained = hidden * jnp.where(modality == 0, gain_table[0], gain_table[1])[None, :]
    router = lax.dynamic_slice_in_dim(router_weight.astype(jnp.float32), first, kind_experts, 1).T
    router = jnp.where(group == 0, router, router[::-1])
    slot_router = jnp.repeat(router, capacity, axis=0)
    squares = jnp.sum(hidden * hidden, axis=1, keepdims=True)
    logits = jnp.sum(gained * slot_router, axis=1, keepdims=True)
    lane = lax.broadcasted_iota(jnp.int32, (slots, STAT_COLS), 1)
    squares_high = lax.reduce_precision(squares, 8, 7)
    logits_high = lax.reduce_precision(logits, 8, 7)
    extra = jnp.where(lane == 0, squares_high, 0.0)
    extra = jnp.where(lane == 1, squares - squares_high, extra)
    extra = jnp.where(lane == 2, logits_high, extra)
    extra = jnp.where(lane == 3, logits - logits_high, extra)
    extra = jnp.where(lane == 4, modality.astype(jnp.float32), extra)
    packed = jnp.concatenate([gained, extra], axis=1).astype(jnp.bfloat16)

    everyone = jnp.stack([packed] + [lax.ppermute(packed, "tok", crossed(2, v)) for v in (1, 2, 3)])
    packed_columns = columns + STAT_COLS
    own = everyone[:, :capacity].reshape(4 * capacity, packed_columns)
    given = everyone[:, capacity:].reshape(4 * capacity, packed_columns)
    both_axes = ("groups", "mod")
    side_far = lax.ppermute(given, both_axes, crossed(2, 3))
    far = lax.ppermute(given, "groups", SWAP)
    side_own = lax.ppermute(own, "mod", SWAP)
    flags = own[:, columns + 4].astype(jnp.float32)
    half_stat = jnp.concatenate(
        [
            own[:, columns:].astype(jnp.float32) + side_own[:, columns:].astype(jnp.float32),
            far[:, columns:].astype(jnp.float32) + side_far[:, columns:].astype(jnp.float32),
        ]
    )
    stat = half_stat + lax.ppermute(half_stat, "fsdp", SWAP)

    mine = gate_up(side_list, [own, far, side_own, side_far], gate_held, up_held)
    other = lax.ppermute(mine, "fsdp", SWAP)
    value = down(side_list, mine, other, stat, down_held)

    half = 4 * capacity
    from_side_far = lax.ppermute(value[1, half:], both_axes, crossed(2, 3))
    from_far = lax.ppermute(value[0, half:], "groups", SWAP)
    from_side = lax.ppermute(value[1, :half], "mod", SWAP)
    valid = (flags == side.astype(jnp.float32))[:, None]
    first_expert = jnp.where(valid, value[0, :half], from_side).reshape(4, capacity, columns)
    second_expert = jnp.where(valid, from_far, from_side_far).reshape(4, capacity, columns)
    merged = jnp.concatenate([first_expert, second_expert], axis=1)
    summed = merged[0].astype(jnp.float32)
    for v in (3, 2, 1):
        summed = summed + lax.ppermute(merged[v], "tok", crossed(2, v)).astype(jnp.float32)
    return jnp.dot(
        pick.astype(jnp.float32).T, summed, precision=lax.Precision.HIGHEST
    ).astype(jnp.bfloat16)


def solution(mesh):
    placed = (
        P(("groups", "tok"), ("fsdp", "mod")),
        P(("groups", "tok"), ("mod", "fsdp")),
        P("tok", ("fsdp", "mod")),
        P(None, ("fsdp", "mod")),
        P(("fsdp", "mod"), None),
        P(("groups", "tok")),
        P(None, ("groups", "tok")),
        P("mod", "fsdp", "tok"),
        P("mod", "fsdp", "tok"),
        P("mod", "tok", "fsdp"),
    )
    sizes = dict(n_tok=mesh.shape["tok"], n_mod=mesh.shape["mod"], n_fsdp=mesh.shape["fsdp"])
    paired = (
        mesh.shape["groups"] == 2
        and sizes == dict(n_tok=4, n_mod=2, n_fsdp=2)
    )
    body = paired_local if paired else functools.partial(local, **sizes)
    return jax.shard_map(
        body,
        mesh=mesh,
        in_specs=placed,
        out_specs=P(("groups", "tok"), ("fsdp", "mod")),
        check_vma=False,
    )
```

```python
import functools

import jax
import jax.numpy as jnp
from jax import lax
from jax.experimental import pallas as pl
from jax.experimental.pallas import tpu as pltpu
from jax.sharding import PartitionSpec as P

D = 4096
STAT_COLS = 128
FEW = 4


def ring(size, step):
    return [(i, (i + step) % size) for i in range(size)]


def reduce_tok(blocks, n_tok):
    if n_tok > FEW:
        return lax.psum_scatter(blocks, "tok", scatter_dimension=0, tiled=False).astype(jnp.float32)
    own = lax.axis_index("tok")
    total = lax.dynamic_index_in_dim(blocks, own, 0, False).astype(jnp.float32)
    for step in range(1, n_tok):
        sent = lax.dynamic_index_in_dim(blocks, (own + step) % n_tok, 0, False)
        total = total + lax.ppermute(sent, "tok", ring(n_tok, step)).astype(jnp.float32)
    return total


def gather_tok(rows, n_tok):
    if n_tok > FEW:
        return lax.all_gather(rows, "tok", axis=0, tiled=False)
    own = lax.axis_index("tok")
    result = jnp.zeros((n_tok,) + rows.shape, rows.dtype)
    result = lax.dynamic_update_index_in_dim(result, rows, own, 0)
    for step in range(1, n_tok):
        got = lax.ppermute(rows, "tok", ring(n_tok, step))
        result = lax.dynamic_update_index_in_dim(result, got, (own - step) % n_tok, 0)
    return result


def spread_context(rows, n_tok, n_mod, n_fsdp):
    if n_tok > FEW or n_tok != n_mod * n_fsdp:
        full = lax.all_gather(rows, ("mod", "fsdp"), axis=1, tiled=True)
        split = full.reshape(full.shape[0], n_tok, full.shape[1] // n_tok).transpose(1, 0, 2)
        return lax.all_to_all(split, "tok", 0, 0, tiled=True)
    pairs = [(t * n_tok + q, q * n_tok + t) for t in range(n_tok) for q in range(n_tok)]
    swapped = lax.ppermute(rows, ("tok", "mod", "fsdp"), pairs)
    return lax.all_gather(swapped, ("mod", "fsdp"), axis=0, tiled=False)


def local(
    residual,
    context,
    out_proj,
    norm_gain,
    router_weight,
    block_modality,
    expert_rows,
    gate_weight,
    up_weight,
    down_weight,
    *,
    n_tok,
    n_mod,
    n_fsdp,
):
    token_count = residual.shape[0]
    experts, capacity = expert_rows.shape
    kind_experts = experts // 2
    slots = kind_experts * capacity
    local_experts = gate_weight.shape[0]
    columns = residual.shape[1]
    assert block_modality.shape == (1,) and n_mod * local_experts == experts
    modality = block_modality[0]
    first = modality * kind_experts
    mod_index = lax.axis_index("mod")

    own_rows = lax.dynamic_slice_in_dim(expert_rows, first, kind_experts, 0).reshape(slots)
    pick = own_rows[:, None] == lax.iota(jnp.int32, token_count)[None, :]
    pick_half = pick.astype(jnp.bfloat16)
    picked_context = jnp.dot(pick_half, context, preferred_element_type=jnp.float32).astype(jnp.bfloat16)
    picked_residual = jnp.dot(pick_half, residual, preferred_element_type=jnp.float32)

    spread = spread_context(picked_context, n_tok, n_mod, n_fsdp)
    partial = jnp.einsum("tsk,kc->tsc", spread, out_proj, preferred_element_type=jnp.float32)
    hidden = picked_residual + reduce_tok(partial.astype(jnp.bfloat16), n_tok)

    gain_table = norm_gain.astype(jnp.float32)
    gained = hidden * jnp.where(modality == 0, gain_table[0], gain_table[1])[None, :]
    router = lax.dynamic_slice_in_dim(router_weight.astype(jnp.float32), first, kind_experts, 1)
    slot_router = jnp.repeat(router.T, capacity, axis=0)
    squares = jnp.sum(hidden * hidden, axis=1, keepdims=True)
    logits = jnp.sum(gained * slot_router, axis=1, keepdims=True)
    flag = jnp.broadcast_to(modality.astype(jnp.bfloat16), (slots, 1))
    stat_list = []
    for stat in (squares, logits):
        high = lax.reduce_precision(stat, 8, 7)
        stat_list += [high.astype(jnp.bfloat16), (stat - high).astype(jnp.bfloat16)]
    packed = jnp.concatenate(
        [gained.astype(jnp.bfloat16)] + stat_list
        + [flag, jnp.zeros((slots, STAT_COLS - 5), jnp.bfloat16)],
        axis=1,
    )

    everyone = gather_tok(packed, n_tok)
    both = lax.all_gather(everyone, "mod", axis=0, tiled=False)
    kind_first = (mod_index * local_experts) % kind_experts
    both = both.reshape(n_mod, n_tok, kind_experts, capacity, columns + STAT_COLS)
    mine = lax.dynamic_slice_in_dim(both, kind_first, local_experts, 2)
    piece = mine[..., :columns].transpose(2, 1, 3, 0, 4).reshape(
        local_experts, n_tok * capacity, n_mod * columns
    )
    tail = mine[..., columns : columns + 5].astype(jnp.float32)
    half_stats = jnp.sum(
        jnp.stack([tail[..., 0] + tail[..., 1], tail[..., 2] + tail[..., 3]], axis=-1), axis=0
    )
    stats = lax.psum(half_stats, "fsdp")
    flags = tail[0, :, :, :, 4]
    by_expert = stats.transpose(1, 0, 2, 3).reshape(local_experts, n_tok * capacity, 2)
    inverse = lax.rsqrt(by_expert[..., 0:1] / D + 1e-05)
    score = jax.nn.sigmoid(by_expert[..., 1:2] * inverse)

    gate_part = jnp.einsum("esd,edf->esf", piece, gate_weight, preferred_element_type=jnp.float32)
    up_part = jnp.einsum("esd,edf->esf", piece, up_weight, preferred_element_type=jnp.float32)
    gate_half = gate_part.astype(jnp.bfloat16)
    up_half = up_part.astype(jnp.bfloat16)
    if n_fsdp == 2:
        swap = [(0, 1), (1, 0)]
        gate_sum = gate_half.astype(jnp.float32) + lax.ppermute(gate_half, "fsdp", swap).astype(jnp.float32)
        up_sum = up_half.astype(jnp.float32) + lax.ppermute(up_half, "fsdp", swap).astype(jnp.float32)
    else:
        gate_sum = lax.psum(gate_half, "fsdp").astype(jnp.float32)
        up_sum = lax.psum(up_half, "fsdp").astype(jnp.float32)
    activation = (jax.nn.silu(gate_sum * inverse) * (up_sum * inverse)).astype(jnp.bfloat16)
    value = jnp.einsum("esf,efd->esd", activation, down_weight, preferred_element_type=jnp.float32)
    value = (value * score).astype(jnp.bfloat16)
    value = value.reshape(local_experts, n_tok, capacity, n_mod * columns).transpose(1, 0, 2, 3)

    own_kind = (mod_index * local_experts) // kind_experts
    valid = (flags == own_kind.astype(jnp.float32))[..., None]
    if n_mod == 2:
        value = value.reshape(n_tok, local_experts, capacity, n_mod, columns)
        kept = lax.dynamic_index_in_dim(value, mod_index, 3, False)
        sent = lax.dynamic_index_in_dim(value, 1 - mod_index, 3, False)
        got = lax.ppermute(sent, "mod", [(0, 1), (1, 0)])
        merged = jnp.where(valid, kept, got).reshape(n_tok, slots, columns)
    else:
        value = jnp.where(valid, value, jnp.zeros((), jnp.bfloat16))
        wide = jnp.zeros((n_tok, kind_experts, capacity, n_mod * columns), jnp.bfloat16)
        wide = lax.dynamic_update_slice_in_dim(wide, value, kind_first, 1)
        wide = wide.reshape(n_tok, slots, n_mod * columns)
        merged = lax.psum_scatter(wide, "mod", scatter_dimension=2, tiled=True)
    summed = reduce_tok(merged, n_tok)
    return jnp.dot(
        pick.astype(jnp.float32).T, summed, precision=lax.Precision.HIGHEST
    ).astype(jnp.bfloat16)


SWAP = [(0, 1), (1, 0)]
CHUNK = 512
STRIP = 688
TILE = 16
ON_CHIP = pl.BlockSpec(memory_space=pltpu.VMEM)
SCALARS = pl.BlockSpec(memory_space=pltpu.SMEM)
IN_HBM = pl.BlockSpec(memory_space=pltpu.HBM)
ANYWHERE = pl.BlockSpec(memory_space=pl.ANY)
GROUP, FLIP, SIDE, KIND = range(4)


def crossed(bits, flip):
    return [(i, i ^ flip) for i in range(1 << bits)]


def call(kernel, name, outs, specs, args, scratch=(), flops=0, moved=0, limit=8 << 20):
    return pl.pallas_call(
        kernel,
        out_shape=outs,
        in_specs=specs,
        out_specs=jax.tree.map(lambda _: ON_CHIP, outs),
        scratch_shapes=list(scratch),
        compiler_params=pltpu.CompilerParams(vmem_limit_bytes=limit),
        cost_estimate=pl.CostEstimate(flops=flops, transcendentals=0, bytes_accessed=moved),
        name=name,
    )(*args)


def array(*shape, dtype=jnp.bfloat16):
    return jax.ShapeDtypeStruct(shape, dtype)


def keep_kernel(ids_ref, after_ref, *refs):
    count = (len(refs) - 1) // 2
    weights, held, semaphores = refs[:count], refs[count : 2 * count], refs[-1]
    copies = []
    for n in reversed(range(count)):
        source = weights[n].at[ids_ref[GROUP]] if n == 0 else weights[n]
        copies.append(pltpu.make_async_copy(source, held[n], semaphores.at[n]))
        copies[-1].start()
    for copy in copies:
        copy.wait()


def keep_on_chip(ids, after, weights, name):
    weights = [pltpu.with_memory_space_constraint(weight, pltpu.HBM) for weight in weights]
    shapes = [weight.shape[1:] if n == 0 else weight.shape for n, weight in enumerate(weights)]
    return call(
        keep_kernel,
        name,
        [pltpu.VMEM(shape, jnp.bfloat16) for shape in shapes],
        [SCALARS, ANYWHERE] + [IN_HBM] * len(weights),
        [ids, after] + weights,
        scratch=[pltpu.SemaphoreType.DMA((len(weights),))],
        moved=sum(2 * a * b for a, b in shapes),
        limit=1 << 20,
    )


def select_kernel(ids_ref, rows_ref, context_ref, residual_ref, picked_ref, rest_ref, pick_ref):
    capacity = rows_ref.shape[1]
    slots, tokens = pick_ref.shape
    row = lax.broadcasted_iota(jnp.int32, (slots, tokens), 0)
    token = lax.broadcasted_iota(jnp.int32, (slots, tokens), 1)
    wanted = jnp.full((slots, tokens), -1, jnp.int32)
    for e in range(2):
        expert = 2 * ids_ref[KIND] + (ids_ref[GROUP] ^ e)
        for s in range(capacity):
            wanted = jnp.where(row == e * capacity + s, rows_ref[expert, s], wanted)
    pick = jnp.where(wanted == token, 1.0, 0.0).astype(jnp.bfloat16)
    pick_ref[...] = pick
    picked_ref[...] = jnp.dot(pick, context_ref[...], preferred_element_type=jnp.float32).astype(jnp.bfloat16)
    rest_ref[...] = jnp.dot(pick, residual_ref[...], preferred_element_type=jnp.float32)


def project_kernel(ids_ref, *refs):
    block_refs, weight_ref, out_ref, rows_ref = refs[:4], refs[4], refs[6], refs[7]
    slots = block_refs[0].shape[0]
    for u, block_ref in enumerate(block_refs):
        rows_ref[u * slots : (u + 1) * slots, :] = block_ref[...]
    product = jnp.dot(rows_ref[...], weight_ref[...], preferred_element_type=jnp.float32)
    product = product.astype(jnp.bfloat16)
    for u in range(len(block_refs)):
        out_ref[ids_ref[FLIP] ^ u] = product[u * slots : (u + 1) * slots, :]


def split_high_low(value):
    high = value.astype(jnp.bfloat16).astype(jnp.float32)
    return high, value - high


def norm_kernel(ids_ref, rest_ref, partial_ref, one_ref, two_ref, three_ref, gain_ref, router_ref, _, out_ref):
    slots, columns = rest_ref.shape
    hidden = rest_ref[...] + partial_ref[0].astype(jnp.float32)
    for got_ref in (three_ref, two_ref, one_ref):
        hidden = hidden + got_ref[...].astype(jnp.float32)
    gains = gain_ref[...].astype(jnp.float32)
    gained = hidden * jnp.where(ids_ref[KIND] == 0, gains[0:1], gains[1:2])
    out_ref[:, :columns] = gained.astype(jnp.bfloat16)
    table = router_ref[...].astype(jnp.float32)
    pieces = []
    for e in range(2):
        expert = 2 * ids_ref[KIND] + (ids_ref[GROUP] ^ e)
        weights = table[0:1]
        for k in range(1, table.shape[0]):
            weights = jnp.where(expert == k, table[k : k + 1], weights)
        half = slots // 2
        pieces.append(jnp.sum(gained[e * half : (e + 1) * half] * weights, axis=1, keepdims=True))
    logits = jnp.concatenate(pieces, axis=0)
    squares = jnp.sum(hidden * hidden, axis=1, keepdims=True)
    lane = lax.broadcasted_iota(jnp.int32, (slots, STAT_COLS), 1)
    extra = jnp.where(lane == 4, ids_ref[KIND].astype(jnp.float32), 0.0)
    for at, stat in enumerate(split_high_low(squares) + split_high_low(logits)):
        extra = jnp.where(lane == at, stat, extra)
    out_ref[:, columns:] = extra.astype(jnp.bfloat16)


def arrange_kernel(zero_ref, one_ref, two_ref, three_ref, _, own_ref, given_ref):
    half = zero_ref.shape[0] // 2
    for v, ref in enumerate((zero_ref, one_ref, two_ref, three_ref)):
        own_ref[v * half : (v + 1) * half, :] = ref[:half, :]
        given_ref[v * half : (v + 1) * half, :] = ref[half:, :]


def weight_times_rows(weight_ref, rows, out_ref):
    units = weight_ref.shape[0]
    for start in range(0, units, STRIP):
        stop = min(start + STRIP, units)
        out_ref[start:stop, :] = lax.dot_general(
            weight_ref[start:stop, :], rows, (((1,), (1,)), ((), ())), preferred_element_type=jnp.float32
        ).astype(jnp.bfloat16)


def gate_kernel(ids_ref, own_ref, far_ref, side_own_ref, side_far_ref, weight_ref, out_ref, rows_ref):
    half = own_ref.shape[0]
    units, width = weight_ref.shape
    columns = width // 2
    for side in range(2):

        @pl.when(ids_ref[SIDE] == side)
        def _():
            here, there = side * columns, (1 - side) * columns
            rows_ref[:half, here : here + columns] = own_ref[:, :columns]
            rows_ref[half:, here : here + columns] = far_ref[:, :columns]
            rows_ref[:half, there : there + columns] = side_own_ref[:, :columns]
            rows_ref[half:, there : there + columns] = side_far_ref[:, :columns]

    weight_times_rows(weight_ref, rows_ref[...], out_ref)
    tails = [ref[:, columns:].astype(jnp.float32) for ref in (own_ref, side_own_ref, far_ref, side_far_ref)]
    stat = jnp.concatenate([tails[0] + tails[1], tails[2] + tails[3]], axis=0).T
    squares = stat[0:1] + stat[1:2]
    logits = stat[2:3] + stat[3:4]
    at_row = lax.broadcasted_iota(jnp.int32, (TILE, 2 * half), 0)
    extra = jnp.zeros((TILE, 2 * half), jnp.float32)
    for at, piece in enumerate(split_high_low(squares) + split_high_low(logits)):
        extra = jnp.where(at_row == at, piece, extra)
    out_ref[units:, :] = extra.astype(jnp.bfloat16)


def up_kernel(rows_ref, weight_ref, out_ref):
    weight_times_rows(weight_ref, rows_ref[...], out_ref)


def down_kernel(ids_ref, gate_ref, gate_other_ref, up_ref, up_other_ref, weight_ref, *refs):
    out_refs, act_ref = refs[:4], refs[4]
    units, width = weight_ref.shape
    rows = act_ref.shape[1]
    stat = gate_ref[units:, :].astype(jnp.float32) + gate_other_ref[units:, :].astype(jnp.float32)
    inverse = lax.rsqrt((stat[0:1] + stat[1:2]) / D + 1e-05)
    logits = (stat[2:3] + stat[3:4]) * inverse
    score = 1.0 / (1.0 + jnp.exp(-logits))
    score = jnp.broadcast_to(score, (rows, rows)).T[:, 0:1]
    for start in range(0, units, STRIP):
        stop = min(start + STRIP, units)
        gate = gate_ref[start:stop, :].astype(jnp.float32) + gate_other_ref[start:stop, :].astype(jnp.float32)
        up = up_ref[start:stop, :].astype(jnp.float32) + up_other_ref[start:stop, :].astype(jnp.float32)
        gate, up = gate * inverse, up * inverse
        act_ref[start:stop, :] = (gate / (1.0 + jnp.exp(-gate)) * up).astype(jnp.bfloat16)
    columns = width // 2
    half = rows // 2
    for start in range(0, width, CHUNK):
        value = lax.dot_general(
            act_ref[...], weight_ref[:, start : start + CHUNK], (((0,), (0,)), ((), ())),
            preferred_element_type=jnp.float32,
        )
        value = (value * score).astype(jnp.bfloat16)
        quarter, at = divmod(start, columns)
        for across in range(2):

            @pl.when((ids_ref[SIDE] ^ quarter) == across)
            def _():
                out_refs[2 * across][:, at : at + CHUNK] = value[:half]
                out_refs[2 * across + 1][:, at : at + CHUNK] = value[half:]


def merge_kernel(ids_ref, own_ref, kept_ref, side_ref, far_ref, side_far_ref, *out_refs):
    half, columns = kept_ref.shape
    capacity = half // len(out_refs)
    side = ids_ref[SIDE].astype(jnp.float32)
    for v, out_ref in enumerate(out_refs):
        span = slice(v * capacity, (v + 1) * capacity)
        valid = own_ref[span, columns : columns + STAT_COLS].astype(jnp.float32)[:, 4:5] == side
        for e, (mine, other) in enumerate(((kept_ref, side_ref), (far_ref, side_far_ref))):
            chosen = jnp.where(valid, mine[span, :].astype(jnp.float32), other[span, :].astype(jnp.float32))
            out_ref[e * capacity : (e + 1) * capacity, :] = chosen.astype(jnp.bfloat16)


def scatter_kernel(pick_ref, zero_ref, one_ref, two_ref, three_ref, out_ref):
    total = zero_ref[...].astype(jnp.float32)
    for got_ref in (three_ref, two_ref, one_ref):
        total = total + got_ref[...].astype(jnp.float32)
    high, rest = split_high_low(total)
    middle, low = split_high_low(rest)
    result = 0.0
    for piece in (low, middle, high):
        result = result + lax.dot_general(
            pick_ref[...], piece.astype(jnp.bfloat16), (((0,), (0,)), ((), ())),
            preferred_element_type=jnp.float32,
        )
    out_ref[...] = result.astype(jnp.bfloat16)


def paired_local(
    residual,
    context,
    out_proj,
    norm_gain,
    router_weight,
    block_modality,
    expert_rows,
    gate_weight,
    up_weight,
    down_weight,
):
    tokens, columns = residual.shape
    experts, capacity = expert_rows.shape
    slots = 2 * capacity
    half = 4 * capacity
    rows = 2 * half
    units, width = down_weight.shape[1:]
    assert block_modality.shape == (1,) and experts == 4 and gate_weight.shape[0] == 2
    tok, side = lax.axis_index("tok"), lax.axis_index("mod")
    corner = 2 * side + lax.axis_index("fsdp")
    ids = jnp.stack([lax.axis_index("groups"), tok ^ corner, side, block_modality[0]])

    picked, rest, pick = call(
        select_kernel,
        "select",
        [array(slots, columns), array(slots, columns, dtype=jnp.float32), array(slots, tokens)],
        [SCALARS, SCALARS, ON_CHIP, ON_CHIP],
        [ids, expert_rows, context, residual],
    )
    plane = ("tok", "mod", "fsdp")
    to_first = [(t * 4 + q, q * 4 + t) for t in range(4) for q in range(4)]
    to_second = [(t * 4 + q, q * 4 + (t ^ 2)) for t in range(4) for q in range(4)]
    near = lax.ppermute(picked, plane, to_first)
    across = lax.ppermute(picked, plane, to_second)
    near_core = lax.ppermute(near, "fsdp", SWAP)
    across_core = lax.ppermute(across, "fsdp", SWAP)
    gate_held, proj_held = keep_on_chip(ids, picked, [gate_weight.swapaxes(1, 2), out_proj], "keep_gate")
    partial = call(
        project_kernel,
        "project",
        array(4, slots, columns),
        [SCALARS] + [ON_CHIP] * 6,
        [ids, near, near_core, across, across_core, proj_held, gate_held],
        scratch=[pltpu.VMEM((rows, columns), jnp.bfloat16)],
    )
    sums = [lax.ppermute(partial[v], "tok", crossed(2, v)) for v in (1, 2, 3)]
    (up_held,) = keep_on_chip(ids, partial, [up_weight.swapaxes(1, 2)], "keep_up")
    packed_columns = columns + STAT_COLS
    packed = call(
        norm_kernel,
        "norm",
        array(slots, packed_columns),
        [SCALARS] + [ON_CHIP] * 8,
        [ids, rest, partial, *sums, norm_gain, router_weight.T, up_held],
    )
    others = [lax.ppermute(packed, "tok", crossed(2, v)) for v in (1, 2, 3)]
    (down_held,) = keep_on_chip(ids, packed, [down_weight], "keep_down")
    own, given = call(
        arrange_kernel,
        "arrange",
        [array(half, packed_columns)] * 2,
        [ON_CHIP] * 5,
        [packed, *others, down_held],
    )
    both_axes = ("groups", "mod")
    side_far = lax.ppermute(given, both_axes, crossed(2, 3))
    far = lax.ppermute(given, "groups", SWAP)
    side_own = lax.ppermute(own, "mod", SWAP)

    flops = 2 * rows * units * width
    gate, gathered = call(
        gate_kernel,
        "gate",
        [array(units + TILE, rows), array(rows, width)],
        [SCALARS] + [ON_CHIP] * 5,
        [ids, own, far, side_own, side_far, gate_held],
        flops=flops,
    )
    up = call(
        up_kernel, "up", array(units, rows), [ON_CHIP] * 2, [gathered, up_held], flops=flops
    )
    gate_other = lax.ppermute(gate, "fsdp", SWAP)
    up_other = lax.ppermute(up, "fsdp", SWAP)
    kept, to_far, to_side, to_side_far = call(
        down_kernel,
        "down",
        [array(half, columns)] * 4,
        [SCALARS] + [ON_CHIP] * 5,
        [ids, gate, gate_other, up, up_other, down_held],
        scratch=[pltpu.VMEM((units, rows), jnp.bfloat16)],
        flops=flops,
    )
    from_side_far = lax.ppermute(to_side_far, both_axes, crossed(2, 3))
    from_far = lax.ppermute(to_far, "groups", SWAP)
    from_side = lax.ppermute(to_side, "mod", SWAP)
    merged = call(
        merge_kernel,
        "merge",
        [array(slots, columns)] * 4,
        [SCALARS] + [ON_CHIP] * 5,
        [ids, own, kept, from_side, from_far, from_side_far],
    )
    values = [merged[0]] + [lax.ppermute(merged[v], "tok", crossed(2, v)) for v in (1, 2, 3)]
    return call(
        scatter_kernel, "scatter", array(tokens, columns), [ON_CHIP] * 5, [pick, *values]
    )


def solution(mesh):
    placed = (
        P(("groups", "tok"), ("fsdp", "mod")),
        P(("groups", "tok"), ("mod", "fsdp")),
        P("tok", ("fsdp", "mod")),
        P(None, ("fsdp", "mod")),
        P(("fsdp", "mod"), None),
        P(("groups", "tok")),
        P(None, ("groups", "tok")),
        P("mod", "fsdp", "tok"),
        P("mod", "fsdp", "tok"),
        P("mod", "tok", "fsdp"),
    )
    sizes = dict(n_tok=mesh.shape["tok"], n_mod=mesh.shape["mod"], n_fsdp=mesh.shape["fsdp"])
    paired = (
        mesh.shape["groups"] == 2
        and sizes == dict(n_tok=4, n_mod=2, n_fsdp=2)
    )
    body = paired_local if paired else functools.partial(local, **sizes)
    return jax.shard_map(
        body,
        mesh=mesh,
        in_specs=placed,
        out_specs=P(("groups", "tok"), ("fsdp", "mod")),
        check_vma=False,
    )
```

```python
import functools

import jax
import jax.numpy as jnp
from jax import lax
from jax.experimental import pallas as pl
from jax.experimental.pallas import tpu as pltpu
from jax.sharding import PartitionSpec as P

D = 4096
STAT_COLS = 128
FEW = 4


def ring(size, step):
    return [(i, (i + step) % size) for i in range(size)]


def reduce_tok(blocks, n_tok):
    if n_tok > FEW:
        return lax.psum_scatter(blocks, "tok", scatter_dimension=0, tiled=False).astype(jnp.float32)
    own = lax.axis_index("tok")
    total = lax.dynamic_index_in_dim(blocks, own, 0, False).astype(jnp.float32)
    for step in range(1, n_tok):
        sent = lax.dynamic_index_in_dim(blocks, (own + step) % n_tok, 0, False)
        total = total + lax.ppermute(sent, "tok", ring(n_tok, step)).astype(jnp.float32)
    return total


def gather_tok(rows, n_tok):
    if n_tok > FEW:
        return lax.all_gather(rows, "tok", axis=0, tiled=False)
    own = lax.axis_index("tok")
    result = jnp.zeros((n_tok,) + rows.shape, rows.dtype)
    result = lax.dynamic_update_index_in_dim(result, rows, own, 0)
    for step in range(1, n_tok):
        got = lax.ppermute(rows, "tok", ring(n_tok, step))
        result = lax.dynamic_update_index_in_dim(result, got, (own - step) % n_tok, 0)
    return result


def spread_context(rows, n_tok, n_mod, n_fsdp):
    if n_tok > FEW or n_tok != n_mod * n_fsdp:
        full = lax.all_gather(rows, ("mod", "fsdp"), axis=1, tiled=True)
        split = full.reshape(full.shape[0], n_tok, full.shape[1] // n_tok).transpose(1, 0, 2)
        return lax.all_to_all(split, "tok", 0, 0, tiled=True)
    pairs = [(t * n_tok + q, q * n_tok + t) for t in range(n_tok) for q in range(n_tok)]
    swapped = lax.ppermute(rows, ("tok", "mod", "fsdp"), pairs)
    return lax.all_gather(swapped, ("mod", "fsdp"), axis=0, tiled=False)


def local(
    residual,
    context,
    out_proj,
    norm_gain,
    router_weight,
    block_modality,
    expert_rows,
    gate_weight,
    up_weight,
    down_weight,
    *,
    n_tok,
    n_mod,
    n_fsdp,
):
    token_count = residual.shape[0]
    experts, capacity = expert_rows.shape
    kind_experts = experts // 2
    slots = kind_experts * capacity
    local_experts = gate_weight.shape[0]
    columns = residual.shape[1]
    assert block_modality.shape == (1,) and n_mod * local_experts == experts
    modality = block_modality[0]
    first = modality * kind_experts
    mod_index = lax.axis_index("mod")

    own_rows = lax.dynamic_slice_in_dim(expert_rows, first, kind_experts, 0).reshape(slots)
    pick = own_rows[:, None] == lax.iota(jnp.int32, token_count)[None, :]
    pick_half = pick.astype(jnp.bfloat16)
    picked_context = jnp.dot(pick_half, context, preferred_element_type=jnp.float32).astype(jnp.bfloat16)
    picked_residual = jnp.dot(pick_half, residual, preferred_element_type=jnp.float32)

    spread = spread_context(picked_context, n_tok, n_mod, n_fsdp)
    partial = jnp.einsum("tsk,kc->tsc", spread, out_proj, preferred_element_type=jnp.float32)
    hidden = picked_residual + reduce_tok(partial.astype(jnp.bfloat16), n_tok)

    gain_table = norm_gain.astype(jnp.float32)
    gained = hidden * jnp.where(modality == 0, gain_table[0], gain_table[1])[None, :]
    router = lax.dynamic_slice_in_dim(router_weight.astype(jnp.float32), first, kind_experts, 1)
    slot_router = jnp.repeat(router.T, capacity, axis=0)
    squares = jnp.sum(hidden * hidden, axis=1, keepdims=True)
    logits = jnp.sum(gained * slot_router, axis=1, keepdims=True)
    flag = jnp.broadcast_to(modality.astype(jnp.bfloat16), (slots, 1))
    stat_list = []
    for stat in (squares, logits):
        high = lax.reduce_precision(stat, 8, 7)
        stat_list += [high.astype(jnp.bfloat16), (stat - high).astype(jnp.bfloat16)]
    packed = jnp.concatenate(
        [gained.astype(jnp.bfloat16)] + stat_list
        + [flag, jnp.zeros((slots, STAT_COLS - 5), jnp.bfloat16)],
        axis=1,
    )

    everyone = gather_tok(packed, n_tok)
    both = lax.all_gather(everyone, "mod", axis=0, tiled=False)
    kind_first = (mod_index * local_experts) % kind_experts
    both = both.reshape(n_mod, n_tok, kind_experts, capacity, columns + STAT_COLS)
    mine = lax.dynamic_slice_in_dim(both, kind_first, local_experts, 2)
    piece = mine[..., :columns].transpose(2, 1, 3, 0, 4).reshape(
        local_experts, n_tok * capacity, n_mod * columns
    )
    tail = mine[..., columns : columns + 5].astype(jnp.float32)
    half_stats = jnp.sum(
        jnp.stack([tail[..., 0] + tail[..., 1], tail[..., 2] + tail[..., 3]], axis=-1), axis=0
    )
    stats = lax.psum(half_stats, "fsdp")
    flags = tail[0, :, :, :, 4]
    by_expert = stats.transpose(1, 0, 2, 3).reshape(local_experts, n_tok * capacity, 2)
    inverse = lax.rsqrt(by_expert[..., 0:1] / D + 1e-05)
    score = jax.nn.sigmoid(by_expert[..., 1:2] * inverse)

    gate_part = jnp.einsum("esd,edf->esf", piece, gate_weight, preferred_element_type=jnp.float32)
    up_part = jnp.einsum("esd,edf->esf", piece, up_weight, preferred_element_type=jnp.float32)
    gate_half = gate_part.astype(jnp.bfloat16)
    up_half = up_part.astype(jnp.bfloat16)
    if n_fsdp == 2:
        swap = [(0, 1), (1, 0)]
        gate_sum = gate_half.astype(jnp.float32) + lax.ppermute(gate_half, "fsdp", swap).astype(jnp.float32)
        up_sum = up_half.astype(jnp.float32) + lax.ppermute(up_half, "fsdp", swap).astype(jnp.float32)
    else:
        gate_sum = lax.psum(gate_half, "fsdp").astype(jnp.float32)
        up_sum = lax.psum(up_half, "fsdp").astype(jnp.float32)
    activation = (jax.nn.silu(gate_sum * inverse) * (up_sum * inverse)).astype(jnp.bfloat16)
    value = jnp.einsum("esf,efd->esd", activation, down_weight, preferred_element_type=jnp.float32)
    value = (value * score).astype(jnp.bfloat16)
    value = value.reshape(local_experts, n_tok, capacity, n_mod * columns).transpose(1, 0, 2, 3)

    own_kind = (mod_index * local_experts) // kind_experts
    valid = (flags == own_kind.astype(jnp.float32))[..., None]
    if n_mod == 2:
        value = value.reshape(n_tok, local_experts, capacity, n_mod, columns)
        kept = lax.dynamic_index_in_dim(value, mod_index, 3, False)
        sent = lax.dynamic_index_in_dim(value, 1 - mod_index, 3, False)
        got = lax.ppermute(sent, "mod", [(0, 1), (1, 0)])
        merged = jnp.where(valid, kept, got).reshape(n_tok, slots, columns)
    else:
        value = jnp.where(valid, value, jnp.zeros((), jnp.bfloat16))
        wide = jnp.zeros((n_tok, kind_experts, capacity, n_mod * columns), jnp.bfloat16)
        wide = lax.dynamic_update_slice_in_dim(wide, value, kind_first, 1)
        wide = wide.reshape(n_tok, slots, n_mod * columns)
        merged = lax.psum_scatter(wide, "mod", scatter_dimension=2, tiled=True)
    summed = reduce_tok(merged, n_tok)
    return jnp.dot(
        pick.astype(jnp.float32).T, summed, precision=lax.Precision.HIGHEST
    ).astype(jnp.bfloat16)


SWAP = [(0, 1), (1, 0)]
CHUNK = 512
STRIP = 688
TILE = 16
ON_CHIP = pl.BlockSpec(memory_space=pltpu.VMEM)
SCALARS = pl.BlockSpec(memory_space=pltpu.SMEM)
IN_HBM = pl.BlockSpec(memory_space=pltpu.HBM)
ANYWHERE = pl.BlockSpec(memory_space=pl.ANY)
GROUP, FLIP, SIDE = range(3)


def crossed(bits, flip):
    return [(i, i ^ flip) for i in range(1 << bits)]


def call(kernel, name, outs, specs, args, scratch=(), flops=0, moved=0, limit=8 << 20):
    return pl.pallas_call(
        kernel,
        out_shape=outs,
        in_specs=specs,
        out_specs=jax.tree.map(lambda _: ON_CHIP, outs),
        scratch_shapes=list(scratch),
        compiler_params=pltpu.CompilerParams(vmem_limit_bytes=limit),
        cost_estimate=pl.CostEstimate(flops=flops, transcendentals=0, bytes_accessed=moved),
        name=name,
    )(*args)


def array(*shape, dtype=jnp.bfloat16):
    return jax.ShapeDtypeStruct(shape, dtype)


def keep_kernel(ids_ref, after_ref, weight_ref, held_ref, semaphore):
    copy = pltpu.make_async_copy(weight_ref.at[ids_ref[GROUP]], held_ref, semaphore)
    copy.start()
    copy.wait()


def in_hbm(value):
    return pltpu.with_memory_space_constraint(value, pltpu.HBM)


def keep_on_chip(ids, after, weight, name):
    shape = weight.shape[1:]
    return call(
        keep_kernel,
        name,
        pltpu.VMEM(shape, jnp.bfloat16),
        [SCALARS, ANYWHERE, IN_HBM],
        [ids, after, in_hbm(weight)],
        scratch=[pltpu.SemaphoreType.DMA(())],
        moved=2 * shape[0] * shape[1],
        limit=1 << 20,
    )


def select_kernel(ids_ref, kind_ref, rows_hbm, context_hbm, picked_ref, pick_ref, rows_ref, context_ref, semaphores):
    rows_copy = pltpu.make_async_copy(rows_hbm, rows_ref, semaphores.at[0])
    context_copy = pltpu.make_async_copy(context_hbm, context_ref, semaphores.at[1])
    rows_copy.start()
    context_copy.start()
    rows_copy.wait()
    capacity = rows_ref.shape[1]
    slots, tokens = pick_ref.shape
    row = lax.broadcasted_iota(jnp.int32, (slots, tokens), 0)
    token = lax.broadcasted_iota(jnp.int32, (slots, tokens), 1)
    wanted = jnp.full((slots, tokens), -1, jnp.int32)
    for e in range(2):
        expert = 2 * kind_ref[0] + (ids_ref[GROUP] ^ e)
        for s in range(capacity):
            wanted = jnp.where(row == e * capacity + s, rows_ref[expert, s], wanted)
    pick = jnp.where(wanted == token, 1.0, 0.0).astype(jnp.bfloat16)
    pick_ref[...] = pick
    context_copy.wait()
    picked_ref[...] = jnp.dot(pick, context_ref[...], preferred_element_type=jnp.float32).astype(jnp.bfloat16)


def keep_gate_kernel(
    ids_ref, pick_ref, residual_hbm, gate_ref, proj_ref, gate_held, proj_held, rest_ref, residual_ref, semaphores
):
    copies = [
        pltpu.make_async_copy(residual_hbm, residual_ref, semaphores.at[0]),
        pltpu.make_async_copy(proj_ref, proj_held, semaphores.at[1]),
        pltpu.make_async_copy(gate_ref.at[ids_ref[GROUP]], gate_held, semaphores.at[2]),
    ]
    for copy in copies:
        copy.start()
    copies[0].wait()
    rest_ref[...] = jnp.dot(pick_ref[...], residual_ref[...], preferred_element_type=jnp.float32)
    for copy in copies[1:]:
        copy.wait()


def join_kernel(near_ref, across_ref, _, out_ref):
    slots = near_ref.shape[0]
    out_ref[:slots, :] = near_ref[...]
    out_ref[slots:, :] = across_ref[...]


def project_kernel(ids_ref, joined_ref, other_ref, weight_ref, out_ref, rows_ref):
    pair = joined_ref.shape[0]
    slots = pair // 2
    rows_ref[:pair, :] = joined_ref[...]
    rows_ref[pair:, :] = other_ref[...]
    product = jnp.dot(rows_ref[...], weight_ref[...], preferred_element_type=jnp.float32)
    product = product.astype(jnp.bfloat16)
    for n, u in enumerate((0, 2, 1, 3)):
        out_ref[ids_ref[FLIP] ^ u] = product[n * slots : (n + 1) * slots, :]


def split_high_low(value):
    high = value.astype(jnp.bfloat16).astype(jnp.float32)
    return high, value - high


def norm_kernel(ids_ref, kind_ref, rest_ref, partial_ref, one_ref, two_ref, three_ref, gain_ref, router_ref, _, out_ref):
    slots, columns = rest_ref.shape
    hidden = rest_ref[...] + partial_ref[0].astype(jnp.float32)
    for got_ref in (three_ref, two_ref, one_ref):
        hidden = hidden + got_ref[...].astype(jnp.float32)
    gains = gain_ref[...].astype(jnp.float32)
    gained = hidden * jnp.where(kind_ref[0] == 0, gains[0:1], gains[1:2])
    out_ref[:, :columns] = gained.astype(jnp.bfloat16)
    table = router_ref[...].astype(jnp.float32)
    pieces = []
    for e in range(2):
        expert = 2 * kind_ref[0] + (ids_ref[GROUP] ^ e)
        weights = table[0:1]
        for k in range(1, table.shape[0]):
            weights = jnp.where(expert == k, table[k : k + 1], weights)
        half = slots // 2
        pieces.append(jnp.sum(gained[e * half : (e + 1) * half] * weights, axis=1, keepdims=True))
    logits = jnp.concatenate(pieces, axis=0)
    squares = jnp.sum(hidden * hidden, axis=1, keepdims=True)
    lane = lax.broadcasted_iota(jnp.int32, (slots, STAT_COLS), 1)
    extra = jnp.where(lane == 4, kind_ref[0].astype(jnp.float32), 0.0)
    for at, stat in enumerate(split_high_low(squares) + split_high_low(logits)):
        extra = jnp.where(lane == at, stat, extra)
    out_ref[:, columns:] = extra.astype(jnp.bfloat16)


def arrange_kernel(zero_ref, one_ref, two_ref, three_ref, _, own_ref, given_ref):
    half = zero_ref.shape[0] // 2
    for v, ref in enumerate((zero_ref, one_ref, two_ref, three_ref)):
        own_ref[v * half : (v + 1) * half, :] = ref[:half, :]
        given_ref[v * half : (v + 1) * half, :] = ref[half:, :]


def weight_times_rows(weight_ref, rows, out_ref):
    units = weight_ref.shape[0]
    for start in range(0, units, STRIP):
        stop = min(start + STRIP, units)
        out_ref[start:stop, :] = lax.dot_general(
            weight_ref[start:stop, :], rows, (((1,), (1,)), ((), ())), preferred_element_type=jnp.float32
        ).astype(jnp.bfloat16)


def gate_kernel(ids_ref, own_ref, far_ref, side_own_ref, side_far_ref, weight_ref, out_ref, rows_ref):
    half = own_ref.shape[0]
    units, width = weight_ref.shape
    columns = width // 2
    for side in range(2):

        @pl.when(ids_ref[SIDE] == side)
        def _():
            here, there = side * columns, (1 - side) * columns
            rows_ref[:half, here : here + columns] = own_ref[:, :columns]
            rows_ref[half:, here : here + columns] = far_ref[:, :columns]
            rows_ref[:half, there : there + columns] = side_own_ref[:, :columns]
            rows_ref[half:, there : there + columns] = side_far_ref[:, :columns]

    weight_times_rows(weight_ref, rows_ref[...], out_ref)
    tails = [ref[:, columns:].astype(jnp.float32) for ref in (own_ref, side_own_ref, far_ref, side_far_ref)]
    stat = jnp.concatenate([tails[0] + tails[1], tails[2] + tails[3]], axis=0).T
    squares = stat[0:1] + stat[1:2]
    logits = stat[2:3] + stat[3:4]
    at_row = lax.broadcasted_iota(jnp.int32, (TILE, 2 * half), 0)
    extra = jnp.zeros((TILE, 2 * half), jnp.float32)
    for at, piece in enumerate(split_high_low(squares) + split_high_low(logits)):
        extra = jnp.where(at_row == at, piece, extra)
    out_ref[units:, :] = extra.astype(jnp.bfloat16)


def up_kernel(rows_ref, weight_ref, out_ref):
    weight_times_rows(weight_ref, rows_ref[...], out_ref)


def silu_kernel(gate_ref, gate_other_ref, out_ref, stat_ref):
    units = out_ref.shape[0]
    stat = gate_ref[units:, :].astype(jnp.float32) + gate_other_ref[units:, :].astype(jnp.float32)
    inverse = lax.rsqrt((stat[0:1] + stat[1:2]) / D + 1e-05)
    logits = (stat[2:3] + stat[3:4]) * inverse
    score = 1.0 / (1.0 + jnp.exp(-logits))
    at_row = lax.broadcasted_iota(jnp.int32, stat_ref.shape, 0)
    stat_ref[...] = jnp.where(at_row == 0, inverse, score)
    for start in range(0, units, STRIP):
        stop = min(start + STRIP, units)
        gate = gate_ref[start:stop, :].astype(jnp.float32) + gate_other_ref[start:stop, :].astype(jnp.float32)
        gate = gate * inverse
        out_ref[start:stop, :] = gate / (1.0 + jnp.exp(-gate)) * inverse


def scored_product(act_ref, weight_ref, stat_ref, quarter, span, out_refs):
    rows = act_ref.shape[1]
    columns = out_refs[0].shape[1]
    score = jnp.broadcast_to(stat_ref[1:2, :], (rows, rows)).T[span, 0:1]
    for start in range(0, columns, CHUNK):
        at = pl.multiple_of(quarter * columns + start, CHUNK)
        value = lax.dot_general(
            act_ref[:, span], weight_ref[:, pl.ds(at, CHUNK)], (((0,), (0,)), ((), ())),
            preferred_element_type=jnp.float32,
        )
        value = (value * score).astype(jnp.bfloat16)
        done = 0
        for out_ref in out_refs:
            out_ref[:, start : start + CHUNK] = value[done : done + out_ref.shape[0]]
            done += out_ref.shape[0]


def down_sent_kernel(
    ids_ref, silu_ref, stat_ref, up_ref, up_other_ref, weight_ref, side_ref, side_far_ref, far_ref, act_ref
):
    units, rows = act_ref.shape
    for start in range(0, units, STRIP):
        stop = min(start + STRIP, units)
        up = up_ref[start:stop, :].astype(jnp.float32) + up_other_ref[start:stop, :].astype(jnp.float32)
        act_ref[start:stop, :] = (silu_ref[start:stop, :] * up).astype(jnp.bfloat16)
    side = ids_ref[SIDE]
    scored_product(act_ref, weight_ref, stat_ref, 1 - side, slice(0, rows), (side_ref, side_far_ref))
    scored_product(act_ref, weight_ref, stat_ref, side, slice(rows // 2, rows), (far_ref,))


def down_kept_kernel(ids_ref, act_ref, stat_ref, weight_ref, kept_ref):
    rows = act_ref.shape[1]
    scored_product(act_ref, weight_ref, stat_ref, ids_ref[SIDE], slice(0, rows // 2), (kept_ref,))


def merge_kernel(ids_ref, own_ref, kept_ref, side_ref, far_ref, side_far_ref, *out_refs):
    half, columns = kept_ref.shape
    capacity = half // len(out_refs)
    side = ids_ref[SIDE].astype(jnp.float32)
    for v, out_ref in enumerate(out_refs):
        span = slice(v * capacity, (v + 1) * capacity)
        valid = own_ref[span, columns : columns + STAT_COLS].astype(jnp.float32)[:, 4:5] == side
        for e, (mine, other) in enumerate(((kept_ref, side_ref), (far_ref, side_far_ref))):
            chosen = jnp.where(valid, mine[span, :].astype(jnp.float32), other[span, :].astype(jnp.float32))
            out_ref[e * capacity : (e + 1) * capacity, :] = chosen.astype(jnp.bfloat16)


def scatter_kernel(pick_ref, zero_ref, one_ref, two_ref, three_ref, out_ref):
    total = zero_ref[...].astype(jnp.float32)
    for got_ref in (three_ref, two_ref, one_ref):
        total = total + got_ref[...].astype(jnp.float32)
    high, rest = split_high_low(total)
    middle, low = split_high_low(rest)
    result = 0.0
    for piece in (low, middle, high):
        result = result + lax.dot_general(
            pick_ref[...], piece.astype(jnp.bfloat16), (((0,), (0,)), ((), ())),
            preferred_element_type=jnp.float32,
        )
    out_ref[...] = result.astype(jnp.bfloat16)


def paired_local(
    residual,
    context,
    out_proj,
    norm_gain,
    router_weight,
    block_modality,
    expert_rows,
    gate_weight,
    up_weight,
    down_weight,
):
    tokens, columns = residual.shape
    experts, capacity = expert_rows.shape
    slots = 2 * capacity
    half = 4 * capacity
    rows = 2 * half
    units, width = down_weight.shape[1:]
    assert block_modality.shape == (1,) and experts == 4 and gate_weight.shape[0] == 2
    tok, side = lax.axis_index("tok"), lax.axis_index("mod")
    corner = 2 * side + lax.axis_index("fsdp")
    ids = jnp.stack([lax.axis_index("groups"), tok ^ corner, side])

    picked, pick = call(
        select_kernel,
        "select",
        [array(slots, columns), array(slots, tokens)],
        [SCALARS] * 2 + [IN_HBM] * 2,
        [ids, block_modality, in_hbm(expert_rows), in_hbm(context)],
        scratch=[
            pltpu.SMEM((experts, capacity), jnp.int32),
            pltpu.VMEM((tokens, columns), jnp.bfloat16),
            pltpu.SemaphoreType.DMA((2,)),
        ],
    )
    plane = ("tok", "mod", "fsdp")
    to_first = [(t * 4 + q, q * 4 + t) for t in range(4) for q in range(4)]
    to_second = [(t * 4 + q, q * 4 + (t ^ 2)) for t in range(4) for q in range(4)]
    near = lax.ppermute(picked, plane, to_first)
    across = lax.ppermute(picked, plane, to_second)
    gate_held, proj_held, rest = call(
        keep_gate_kernel,
        "keep_gate",
        [
            pltpu.VMEM((units, width), jnp.bfloat16),
            pltpu.VMEM(out_proj.shape, jnp.bfloat16),
            array(slots, columns, dtype=jnp.float32),
        ],
        [SCALARS, ON_CHIP, IN_HBM, IN_HBM, IN_HBM],
        [ids, pick, in_hbm(residual), in_hbm(gate_weight.swapaxes(1, 2)), in_hbm(out_proj)],
        scratch=[pltpu.VMEM((tokens, columns), jnp.bfloat16), pltpu.SemaphoreType.DMA((3,))],
        moved=2 * units * width,
        limit=2 << 20,
    )
    joined = call(join_kernel, "join", array(half, columns), [ON_CHIP] * 3, [near, across, gate_held])
    other = lax.ppermute(joined, "fsdp", SWAP)
    partial = call(
        project_kernel,
        "project",
        array(4, slots, columns),
        [SCALARS] + [ON_CHIP] * 3,
        [ids, joined, other, proj_held],
        scratch=[pltpu.VMEM((rows, columns), jnp.bfloat16)],
    )
    sums = [lax.ppermute(partial[v], "tok", crossed(2, v)) for v in (1, 2, 3)]
    up_held = keep_on_chip(ids, partial, up_weight.swapaxes(1, 2), "keep_up")
    packed_columns = columns + STAT_COLS
    packed = call(
        norm_kernel,
        "norm",
        array(slots, packed_columns),
        [SCALARS, SCALARS] + [ON_CHIP] * 8,
        [ids, block_modality, rest, partial, *sums, norm_gain, router_weight.T, up_held],
    )
    others = [lax.ppermute(packed, "tok", crossed(2, v)) for v in (1, 2, 3)]
    down_held = keep_on_chip(ids, packed, down_weight, "keep_down")
    own, given = call(
        arrange_kernel,
        "arrange",
        [array(half, packed_columns)] * 2,
        [ON_CHIP] * 5,
        [packed, *others, down_held],
    )
    both_axes = ("groups", "mod")
    side_far = lax.ppermute(given, both_axes, crossed(2, 3))
    far = lax.ppermute(given, "groups", SWAP)
    side_own = lax.ppermute(own, "mod", SWAP)

    flops = 2 * rows * units * width
    gate, gathered = call(
        gate_kernel,
        "gate",
        [array(units + TILE, rows), array(rows, width)],
        [SCALARS] + [ON_CHIP] * 5,
        [ids, own, far, side_own, side_far, gate_held],
        flops=flops,
    )
    up = call(
        up_kernel, "up", array(units, rows), [ON_CHIP] * 2, [gathered, up_held], flops=flops
    )
    gate_other = lax.ppermute(gate, "fsdp", SWAP)
    up_other = lax.ppermute(up, "fsdp", SWAP)
    silu, stat = call(
        silu_kernel,
        "silu",
        [array(units, rows, dtype=jnp.float32), array(8, rows, dtype=jnp.float32)],
        [ON_CHIP] * 2,
        [gate, gate_other],
        moved=8 * units * rows,
    )
    to_side, to_side_far, to_far, act = call(
        down_sent_kernel,
        "down_sent",
        [array(half, columns)] * 3 + [array(units, rows)],
        [SCALARS] + [ON_CHIP] * 5,
        [ids, silu, stat, up, up_other, down_held],
        flops=flops // 4 * 3,
    )
    kept = call(
        down_kept_kernel,
        "down_kept",
        array(half, columns),
        [SCALARS] + [ON_CHIP] * 3,
        [ids, act, stat, down_held],
        flops=flops // 4,
    )
    from_side_far = lax.ppermute(to_side_far, both_axes, crossed(2, 3))
    from_far = lax.ppermute(to_far, "groups", SWAP)
    from_side = lax.ppermute(to_side, "mod", SWAP)
    merged = call(
        merge_kernel,
        "merge",
        [array(slots, columns)] * 4,
        [SCALARS] + [ON_CHIP] * 5,
        [ids, own, kept, from_side, from_far, from_side_far],
    )
    values = [merged[0]] + [lax.ppermute(merged[v], "tok", crossed(2, v)) for v in (1, 2, 3)]
    return call(
        scatter_kernel, "scatter", array(tokens, columns), [ON_CHIP] * 5, [pick, *values]
    )


def solution(mesh):
    placed = (
        P(("groups", "tok"), ("fsdp", "mod")),
        P(("groups", "tok"), ("mod", "fsdp")),
        P("tok", ("fsdp", "mod")),
        P(None, ("fsdp", "mod")),
        P(("fsdp", "mod"), None),
        P(("groups", "tok")),
        P(None, ("groups", "tok")),
        P("mod", "fsdp", "tok"),
        P("mod", "fsdp", "tok"),
        P("mod", "tok", "fsdp"),
    )
    sizes = dict(n_tok=mesh.shape["tok"], n_mod=mesh.shape["mod"], n_fsdp=mesh.shape["fsdp"])
    paired = (
        mesh.shape["groups"] == 2
        and sizes == dict(n_tok=4, n_mod=2, n_fsdp=2)
    )
    body = paired_local if paired else functools.partial(local, **sizes)
    return jax.shard_map(
        body,
        mesh=mesh,
        in_specs=placed,
        out_specs=P(("groups", "tok"), ("fsdp", "mod")),
        check_vma=False,
    )
```

```python
import functools

import jax
import jax.numpy as jnp
from jax import lax
from jax.experimental import pallas as pl
from jax.experimental.pallas import tpu as pltpu
from jax.sharding import PartitionSpec as P

D = 4096
STAT_COLS = 128
FEW = 4


def ring(size, step):
    return [(i, (i + step) % size) for i in range(size)]


def reduce_tok(blocks, n_tok):
    if n_tok > FEW:
        return lax.psum_scatter(blocks, "tok", scatter_dimension=0, tiled=False).astype(jnp.float32)
    own = lax.axis_index("tok")
    total = lax.dynamic_index_in_dim(blocks, own, 0, False).astype(jnp.float32)
    for step in range(1, n_tok):
        sent = lax.dynamic_index_in_dim(blocks, (own + step) % n_tok, 0, False)
        total = total + lax.ppermute(sent, "tok", ring(n_tok, step)).astype(jnp.float32)
    return total


def gather_tok(rows, n_tok):
    if n_tok > FEW:
        return lax.all_gather(rows, "tok", axis=0, tiled=False)
    own = lax.axis_index("tok")
    result = jnp.zeros((n_tok,) + rows.shape, rows.dtype)
    result = lax.dynamic_update_index_in_dim(result, rows, own, 0)
    for step in range(1, n_tok):
        got = lax.ppermute(rows, "tok", ring(n_tok, step))
        result = lax.dynamic_update_index_in_dim(result, got, (own - step) % n_tok, 0)
    return result


def spread_context(rows, n_tok, n_mod, n_fsdp):
    if n_tok > FEW or n_tok != n_mod * n_fsdp:
        full = lax.all_gather(rows, ("mod", "fsdp"), axis=1, tiled=True)
        split = full.reshape(full.shape[0], n_tok, full.shape[1] // n_tok).transpose(1, 0, 2)
        return lax.all_to_all(split, "tok", 0, 0, tiled=True)
    pairs = [(t * n_tok + q, q * n_tok + t) for t in range(n_tok) for q in range(n_tok)]
    swapped = lax.ppermute(rows, ("tok", "mod", "fsdp"), pairs)
    return lax.all_gather(swapped, ("mod", "fsdp"), axis=0, tiled=False)


def local(
    residual,
    context,
    out_proj,
    norm_gain,
    router_weight,
    block_modality,
    expert_rows,
    gate_weight,
    up_weight,
    down_weight,
    *,
    n_tok,
    n_mod,
    n_fsdp,
):
    token_count = residual.shape[0]
    experts, capacity = expert_rows.shape
    kind_experts = experts // 2
    slots = kind_experts * capacity
    local_experts = gate_weight.shape[0]
    columns = residual.shape[1]
    assert block_modality.shape == (1,) and n_mod * local_experts == experts
    modality = block_modality[0]
    first = modality * kind_experts
    mod_index = lax.axis_index("mod")

    own_rows = lax.dynamic_slice_in_dim(expert_rows, first, kind_experts, 0).reshape(slots)
    pick = own_rows[:, None] == lax.iota(jnp.int32, token_count)[None, :]
    pick_half = pick.astype(jnp.bfloat16)
    picked_context = jnp.dot(pick_half, context, preferred_element_type=jnp.float32).astype(jnp.bfloat16)
    picked_residual = jnp.dot(pick_half, residual, preferred_element_type=jnp.float32)

    spread = spread_context(picked_context, n_tok, n_mod, n_fsdp)
    partial = jnp.einsum("tsk,kc->tsc", spread, out_proj, preferred_element_type=jnp.float32)
    hidden = picked_residual + reduce_tok(partial.astype(jnp.bfloat16), n_tok)

    gain_table = norm_gain.astype(jnp.float32)
    gained = hidden * jnp.where(modality == 0, gain_table[0], gain_table[1])[None, :]
    router = lax.dynamic_slice_in_dim(router_weight.astype(jnp.float32), first, kind_experts, 1)
    slot_router = jnp.repeat(router.T, capacity, axis=0)
    squares = jnp.sum(hidden * hidden, axis=1, keepdims=True)
    logits = jnp.sum(gained * slot_router, axis=1, keepdims=True)
    flag = jnp.broadcast_to(modality.astype(jnp.bfloat16), (slots, 1))
    stat_list = []
    for stat in (squares, logits):
        high = lax.reduce_precision(stat, 8, 7)
        stat_list += [high.astype(jnp.bfloat16), (stat - high).astype(jnp.bfloat16)]
    packed = jnp.concatenate(
        [gained.astype(jnp.bfloat16)] + stat_list
        + [flag, jnp.zeros((slots, STAT_COLS - 5), jnp.bfloat16)],
        axis=1,
    )

    everyone = gather_tok(packed, n_tok)
    both = lax.all_gather(everyone, "mod", axis=0, tiled=False)
    kind_first = (mod_index * local_experts) % kind_experts
    both = both.reshape(n_mod, n_tok, kind_experts, capacity, columns + STAT_COLS)
    mine = lax.dynamic_slice_in_dim(both, kind_first, local_experts, 2)
    piece = mine[..., :columns].transpose(2, 1, 3, 0, 4).reshape(
        local_experts, n_tok * capacity, n_mod * columns
    )
    tail = mine[..., columns : columns + 5].astype(jnp.float32)
    half_stats = jnp.sum(
        jnp.stack([tail[..., 0] + tail[..., 1], tail[..., 2] + tail[..., 3]], axis=-1), axis=0
    )
    stats = lax.psum(half_stats, "fsdp")
    flags = tail[0, :, :, :, 4]
    by_expert = stats.transpose(1, 0, 2, 3).reshape(local_experts, n_tok * capacity, 2)
    inverse = lax.rsqrt(by_expert[..., 0:1] / D + 1e-05)
    score = jax.nn.sigmoid(by_expert[..., 1:2] * inverse)

    gate_part = jnp.einsum("esd,edf->esf", piece, gate_weight, preferred_element_type=jnp.float32)
    up_part = jnp.einsum("esd,edf->esf", piece, up_weight, preferred_element_type=jnp.float32)
    gate_half = gate_part.astype(jnp.bfloat16)
    up_half = up_part.astype(jnp.bfloat16)
    if n_fsdp == 2:
        swap = [(0, 1), (1, 0)]
        gate_sum = gate_half.astype(jnp.float32) + lax.ppermute(gate_half, "fsdp", swap).astype(jnp.float32)
        up_sum = up_half.astype(jnp.float32) + lax.ppermute(up_half, "fsdp", swap).astype(jnp.float32)
    else:
        gate_sum = lax.psum(gate_half, "fsdp").astype(jnp.float32)
        up_sum = lax.psum(up_half, "fsdp").astype(jnp.float32)
    activation = (jax.nn.silu(gate_sum * inverse) * (up_sum * inverse)).astype(jnp.bfloat16)
    value = jnp.einsum("esf,efd->esd", activation, down_weight, preferred_element_type=jnp.float32)
    value = (value * score).astype(jnp.bfloat16)
    value = value.reshape(local_experts, n_tok, capacity, n_mod * columns).transpose(1, 0, 2, 3)

    own_kind = (mod_index * local_experts) // kind_experts
    valid = (flags == own_kind.astype(jnp.float32))[..., None]
    if n_mod == 2:
        value = value.reshape(n_tok, local_experts, capacity, n_mod, columns)
        kept = lax.dynamic_index_in_dim(value, mod_index, 3, False)
        sent = lax.dynamic_index_in_dim(value, 1 - mod_index, 3, False)
        got = lax.ppermute(sent, "mod", [(0, 1), (1, 0)])
        merged = jnp.where(valid, kept, got).reshape(n_tok, slots, columns)
    else:
        value = jnp.where(valid, value, jnp.zeros((), jnp.bfloat16))
        wide = jnp.zeros((n_tok, kind_experts, capacity, n_mod * columns), jnp.bfloat16)
        wide = lax.dynamic_update_slice_in_dim(wide, value, kind_first, 1)
        wide = wide.reshape(n_tok, slots, n_mod * columns)
        merged = lax.psum_scatter(wide, "mod", scatter_dimension=2, tiled=True)
    summed = reduce_tok(merged, n_tok)
    return jnp.dot(
        pick.astype(jnp.float32).T, summed, precision=lax.Precision.HIGHEST
    ).astype(jnp.bfloat16)


SWAP = [(0, 1), (1, 0)]
CHUNK = 1024
STRIP = 688
TILE = 16
ON_CHIP = pl.BlockSpec(memory_space=pltpu.VMEM)
SCALARS = pl.BlockSpec(memory_space=pltpu.SMEM)
IN_HBM = pl.BlockSpec(memory_space=pltpu.HBM)
ANYWHERE = pl.BlockSpec(memory_space=pl.ANY)
GROUP, FLIP, SIDE = range(3)


def crossed(bits, flip):
    return [(i, i ^ flip) for i in range(1 << bits)]


def call(kernel, name, outs, specs, args, scratch=(), flops=0, moved=0, limit=8 << 20):
    return pl.pallas_call(
        kernel,
        out_shape=outs,
        in_specs=specs,
        out_specs=jax.tree.map(lambda _: ON_CHIP, outs),
        scratch_shapes=list(scratch),
        compiler_params=pltpu.CompilerParams(vmem_limit_bytes=limit),
        cost_estimate=pl.CostEstimate(flops=flops, transcendentals=0, bytes_accessed=moved),
        name=name,
    )(*args)


def array(*shape, dtype=jnp.bfloat16):
    return jax.ShapeDtypeStruct(shape, dtype)


def keep_kernel(spans, ids_ref, after_ref, *refs):
    count = len(spans)
    weights, held, semaphores = refs[:count], refs[count : 2 * count], refs[-1]
    copies = [
        pltpu.make_async_copy(weight.at[ids_ref[GROUP], a:b], to, semaphores.at[n])
        for n, (weight, to, (a, b)) in enumerate(zip(weights, held, spans))
    ]
    for copy in copies:
        copy.start()
    for copy in copies:
        copy.wait()


def in_hbm(value):
    return pltpu.with_memory_space_constraint(value, pltpu.HBM)


def keep_on_chip(ids, after, weights, spans, name):
    width = weights[0].shape[2]
    return call(
        functools.partial(keep_kernel, spans),
        name,
        [pltpu.VMEM((b - a, width), jnp.bfloat16) for a, b in spans],
        [SCALARS, ANYWHERE] + [IN_HBM] * len(spans),
        [ids, after] + [in_hbm(weight) for weight in weights],
        scratch=[pltpu.SemaphoreType.DMA((len(spans),))],
        moved=2 * width * sum(b - a for a, b in spans),
        limit=1 << 20,
    )


def select_kernel(ids_ref, kind_ref, rows_hbm, context_hbm, picked_ref, pick_ref, rows_ref, context_ref, semaphores):
    rows_copy = pltpu.make_async_copy(rows_hbm, rows_ref, semaphores.at[0])
    context_copy = pltpu.make_async_copy(context_hbm, context_ref, semaphores.at[1])
    rows_copy.start()
    context_copy.start()
    rows_copy.wait()
    capacity = rows_ref.shape[1]
    slots, tokens = pick_ref.shape
    row = lax.broadcasted_iota(jnp.int32, (slots, tokens), 0)
    token = lax.broadcasted_iota(jnp.int32, (slots, tokens), 1)
    wanted = jnp.full((slots, tokens), -1, jnp.int32)
    for e in range(2):
        expert = 2 * kind_ref[0] + (ids_ref[GROUP] ^ e)
        for s in range(capacity):
            wanted = jnp.where(row == e * capacity + s, rows_ref[expert, s], wanted)
    pick = jnp.where(wanted == token, 1.0, 0.0).astype(jnp.bfloat16)
    pick_ref[...] = pick
    context_copy.wait()
    picked_ref[...] = jnp.dot(pick, context_ref[...], preferred_element_type=jnp.float32).astype(jnp.bfloat16)


def keep_gate_kernel(
    ids_ref, pick_ref, residual_hbm, gate_ref, proj_ref, gate_held, proj_held, rest_ref, residual_ref, semaphores
):
    copies = [
        pltpu.make_async_copy(residual_hbm, residual_ref, semaphores.at[0]),
        pltpu.make_async_copy(proj_ref, proj_held, semaphores.at[1]),
        pltpu.make_async_copy(gate_ref.at[ids_ref[GROUP], : gate_held.shape[0]], gate_held, semaphores.at[2]),
    ]
    for copy in copies:
        copy.start()
    copies[0].wait()
    rest_ref[...] = jnp.dot(pick_ref[...], residual_ref[...], preferred_element_type=jnp.float32)
    for copy in copies[1:]:
        copy.wait()


def join_kernel(near_ref, across_ref, _, out_ref):
    slots = near_ref.shape[0]
    out_ref[:slots, :] = near_ref[...]
    out_ref[slots:, :] = across_ref[...]


def project_kernel(ids_ref, joined_ref, other_ref, weight_ref, out_ref, rows_ref):
    pair = joined_ref.shape[0]
    slots = pair // 2
    rows_ref[:pair, :] = joined_ref[...]
    rows_ref[pair:, :] = other_ref[...]
    product = jnp.dot(rows_ref[...], weight_ref[...], preferred_element_type=jnp.float32)
    product = product.astype(jnp.bfloat16)
    for n, u in enumerate((0, 2, 1, 3)):
        out_ref[ids_ref[FLIP] ^ u] = product[n * slots : (n + 1) * slots, :]


def split_high_low(value):
    high = value.astype(jnp.bfloat16).astype(jnp.float32)
    return high, value - high


def norm_kernel(ids_ref, kind_ref, rest_ref, partial_ref, one_ref, two_ref, three_ref, gain_ref, router_ref, _, out_ref):
    slots, columns = rest_ref.shape
    hidden = rest_ref[...] + partial_ref[0].astype(jnp.float32)
    for got_ref in (three_ref, two_ref, one_ref):
        hidden = hidden + got_ref[...].astype(jnp.float32)
    gains = gain_ref[...].astype(jnp.float32)
    gained = hidden * jnp.where(kind_ref[0] == 0, gains[0:1], gains[1:2])
    out_ref[:, :columns] = gained.astype(jnp.bfloat16)
    table = router_ref[...].astype(jnp.float32)
    pieces = []
    for e in range(2):
        expert = 2 * kind_ref[0] + (ids_ref[GROUP] ^ e)
        weights = table[0:1]
        for k in range(1, table.shape[0]):
            weights = jnp.where(expert == k, table[k : k + 1], weights)
        half = slots // 2
        pieces.append(jnp.sum(gained[e * half : (e + 1) * half] * weights, axis=1, keepdims=True))
    logits = jnp.concatenate(pieces, axis=0)
    squares = jnp.sum(hidden * hidden, axis=1, keepdims=True)
    lane = lax.broadcasted_iota(jnp.int32, (slots, STAT_COLS), 1)
    extra = jnp.where(lane == 4, kind_ref[0].astype(jnp.float32), 0.0)
    for at, stat in enumerate(split_high_low(squares) + split_high_low(logits)):
        extra = jnp.where(lane == at, stat, extra)
    out_ref[:, columns:] = extra.astype(jnp.bfloat16)


def arrange_kernel(zero_ref, one_ref, two_ref, three_ref, _, own_ref, given_ref):
    half = zero_ref.shape[0] // 2
    for v, ref in enumerate((zero_ref, one_ref, two_ref, three_ref)):
        own_ref[v * half : (v + 1) * half, :] = ref[:half, :]
        given_ref[v * half : (v + 1) * half, :] = ref[half:, :]


def weights_times_rows(weight_refs, rows, out_ref):
    at = 0
    for weight_ref in weight_refs:
        for start in range(0, weight_ref.shape[0], STRIP):
            stop = min(start + STRIP, weight_ref.shape[0])
            out_ref[at : at + stop - start, :] = lax.dot_general(
                weight_ref[start:stop, :], rows, (((1,), (1,)), ((), ())), preferred_element_type=jnp.float32
            ).astype(jnp.bfloat16)
            at += stop - start


def gate_kernel(ids_ref, own_ref, far_ref, side_own_ref, side_far_ref, *refs):
    weight_refs, out_ref, rows_ref = refs[:2], refs[-2], refs[-1]
    half = own_ref.shape[0]
    units = out_ref.shape[0] - TILE
    columns = rows_ref.shape[1] // 2
    for side in range(2):

        @pl.when(ids_ref[SIDE] == side)
        def _():
            here, there = side * columns, (1 - side) * columns
            rows_ref[:half, here : here + columns] = own_ref[:, :columns]
            rows_ref[half:, here : here + columns] = far_ref[:, :columns]
            rows_ref[:half, there : there + columns] = side_own_ref[:, :columns]
            rows_ref[half:, there : there + columns] = side_far_ref[:, :columns]

    weights_times_rows(weight_refs, rows_ref[...], out_ref)
    tails = [ref[:, columns:].astype(jnp.float32) for ref in (own_ref, side_own_ref, far_ref, side_far_ref)]
    stat = jnp.concatenate([tails[0] + tails[1], tails[2] + tails[3]], axis=0).T
    squares = stat[0:1] + stat[1:2]
    logits = stat[2:3] + stat[3:4]
    at_row = lax.broadcasted_iota(jnp.int32, (TILE, 2 * half), 0)
    extra = jnp.zeros((TILE, 2 * half), jnp.float32)
    for at, piece in enumerate(split_high_low(squares) + split_high_low(logits)):
        extra = jnp.where(at_row == at, piece, extra)
    out_ref[units:, :] = extra.astype(jnp.bfloat16)


def up_kernel(rows_ref, *refs):
    weight_refs, out_ref = refs[:-1], refs[-1]
    weights_times_rows(weight_refs, rows_ref[...], out_ref)


def silu_kernel(gate_ref, gate_other_ref, out_ref, stat_ref):
    units = out_ref.shape[0]
    stat = gate_ref[units:, :].astype(jnp.float32) + gate_other_ref[units:, :].astype(jnp.float32)
    inverse = lax.rsqrt((stat[0:1] + stat[1:2]) / D + 1e-05)
    logits = (stat[2:3] + stat[3:4]) * inverse
    score = 1.0 / (1.0 + jnp.exp(-logits))
    at_row = lax.broadcasted_iota(jnp.int32, stat_ref.shape, 0)
    stat_ref[...] = jnp.where(at_row == 0, inverse, score)
    for start in range(0, units, STRIP):
        stop = min(start + STRIP, units)
        gate = gate_ref[start:stop, :].astype(jnp.float32) + gate_other_ref[start:stop, :].astype(jnp.float32)
        gate = gate * inverse
        out_ref[start:stop, :] = gate / (1.0 + jnp.exp(-gate)) * inverse


def down_kernel(
    ids_ref, silu_ref, stat_ref, up_ref, up_other_ref, weight_ref, kept_ref, far_ref, side_ref, side_far_ref, act_ref
):
    units, rows = act_ref.shape
    for start in range(0, units, STRIP):
        stop = min(start + STRIP, units)
        up = up_ref[start:stop, :].astype(jnp.float32) + up_other_ref[start:stop, :].astype(jnp.float32)
        act_ref[start:stop, :] = (silu_ref[start:stop, :] * up).astype(jnp.bfloat16)
    half, columns = kept_ref.shape
    score = jnp.broadcast_to(stat_ref[1:2, :], (rows, rows)).T[:, 0:1]
    for start in range(0, 2 * columns, CHUNK):
        value = lax.dot_general(
            act_ref[...], weight_ref[:, start : start + CHUNK], (((0,), (0,)), ((), ())),
            preferred_element_type=jnp.float32,
        )
        value = (value * score).astype(jnp.bfloat16)
        quarter, at = divmod(start, columns)
        for across, (own_out, far_out) in enumerate(((kept_ref, far_ref), (side_ref, side_far_ref))):

            @pl.when((ids_ref[SIDE] ^ quarter) == across)
            def _():
                own_out[:, at : at + CHUNK] = value[:half]
                far_out[:, at : at + CHUNK] = value[half:]


def merge_kernel(ids_ref, own_ref, kept_ref, side_ref, far_ref, side_far_ref, *out_refs):
    half, columns = kept_ref.shape
    capacity = half // len(out_refs)
    side = ids_ref[SIDE].astype(jnp.float32)
    for v, out_ref in enumerate(out_refs):
        span = slice(v * capacity, (v + 1) * capacity)
        valid = own_ref[span, columns : columns + STAT_COLS].astype(jnp.float32)[:, 4:5] == side
        for e, (mine, other) in enumerate(((kept_ref, side_ref), (far_ref, side_far_ref))):
            chosen = jnp.where(valid, mine[span, :].astype(jnp.float32), other[span, :].astype(jnp.float32))
            out_ref[e * capacity : (e + 1) * capacity, :] = chosen.astype(jnp.bfloat16)


def scatter_kernel(pick_ref, zero_ref, one_ref, two_ref, three_ref, out_ref):
    total = zero_ref[...].astype(jnp.float32)
    for got_ref in (three_ref, two_ref, one_ref):
        total = total + got_ref[...].astype(jnp.float32)
    high, rest = split_high_low(total)
    middle, low = split_high_low(rest)
    result = 0.0
    for piece in (low, middle, high):
        result = result + lax.dot_general(
            pick_ref[...], piece.astype(jnp.bfloat16), (((0,), (0,)), ((), ())),
            preferred_element_type=jnp.float32,
        )
    out_ref[...] = result.astype(jnp.bfloat16)


def paired_local(
    residual,
    context,
    out_proj,
    norm_gain,
    router_weight,
    block_modality,
    expert_rows,
    gate_weight,
    up_weight,
    down_weight,
):
    tokens, columns = residual.shape
    experts, capacity = expert_rows.shape
    slots = 2 * capacity
    half = 4 * capacity
    rows = 2 * half
    units, width = down_weight.shape[1:]
    assert block_modality.shape == (1,) and experts == 4 and gate_weight.shape[0] == 2
    tok, side = lax.axis_index("tok"), lax.axis_index("mod")
    corner = 2 * side + lax.axis_index("fsdp")
    ids = jnp.stack([lax.axis_index("groups"), tok ^ corner, side])

    picked, pick = call(
        select_kernel,
        "select",
        [array(slots, columns), array(slots, tokens)],
        [SCALARS] * 2 + [IN_HBM] * 2,
        [ids, block_modality, in_hbm(expert_rows), in_hbm(context)],
        scratch=[
            pltpu.SMEM((experts, capacity), jnp.int32),
            pltpu.VMEM((tokens, columns), jnp.bfloat16),
            pltpu.SemaphoreType.DMA((2,)),
        ],
    )
    plane = ("tok", "mod", "fsdp")
    to_first = [(t * 4 + q, q * 4 + t) for t in range(4) for q in range(4)]
    to_second = [(t * 4 + q, q * 4 + (t ^ 2)) for t in range(4) for q in range(4)]
    near = lax.ppermute(picked, plane, to_first)
    across = lax.ppermute(picked, plane, to_second)
    units_first = units // 2
    gate_first, proj_held, rest = call(
        keep_gate_kernel,
        "keep_gate",
        [
            pltpu.VMEM((units_first, width), jnp.bfloat16),
            pltpu.VMEM(out_proj.shape, jnp.bfloat16),
            array(slots, columns, dtype=jnp.float32),
        ],
        [SCALARS, ON_CHIP, IN_HBM, IN_HBM, IN_HBM],
        [ids, pick, in_hbm(residual), in_hbm(gate_weight.swapaxes(1, 2)), in_hbm(out_proj)],
        scratch=[pltpu.VMEM((tokens, columns), jnp.bfloat16), pltpu.SemaphoreType.DMA((3,))],
        moved=units * width,
        limit=2 << 20,
    )
    joined = call(join_kernel, "join", array(half, columns), [ON_CHIP] * 3, [near, across, gate_first])
    other = lax.ppermute(joined, "fsdp", SWAP)
    partial = call(
        project_kernel,
        "project",
        array(4, slots, columns),
        [SCALARS] + [ON_CHIP] * 3,
        [ids, joined, other, proj_held],
        scratch=[pltpu.VMEM((rows, columns), jnp.bfloat16)],
    )
    sums = [lax.ppermute(partial[v], "tok", crossed(2, v)) for v in (1, 2, 3)]
    gate_second, up_first = keep_on_chip(
        ids,
        partial,
        [gate_weight.swapaxes(1, 2), up_weight.swapaxes(1, 2)],
        [(units_first, units), (0, units // 4)],
        "keep_more",
    )
    packed_columns = columns + STAT_COLS
    packed = call(
        norm_kernel,
        "norm",
        array(slots, packed_columns),
        [SCALARS, SCALARS] + [ON_CHIP] * 8,
        [ids, block_modality, rest, partial, *sums, norm_gain, router_weight.T, up_first],
    )
    others = [lax.ppermute(packed, "tok", crossed(2, v)) for v in (1, 2, 3)]
    (up_second,) = keep_on_chip(ids, packed, [up_weight.swapaxes(1, 2)], [(units // 4, units)], "keep_up")
    own, given = call(
        arrange_kernel,
        "arrange",
        [array(half, packed_columns)] * 2,
        [ON_CHIP] * 5,
        [packed, *others, up_second],
    )
    both_axes = ("groups", "mod")
    side_far = lax.ppermute(given, both_axes, crossed(2, 3))
    far = lax.ppermute(given, "groups", SWAP)
    side_own = lax.ppermute(own, "mod", SWAP)

    (down_held,) = keep_on_chip(ids, own, [down_weight], [(0, units)], "keep_down")

    flops = 2 * rows * units * width
    gate, gathered = call(
        gate_kernel,
        "gate",
        [array(units + TILE, rows), array(rows, width)],
        [SCALARS] + [ON_CHIP] * 7,
        [ids, own, far, side_own, side_far, gate_first, gate_second, down_held],
        flops=flops,
    )
    up = call(
        up_kernel, "up", array(units, rows), [ON_CHIP] * 3, [gathered, up_first, up_second], flops=flops
    )
    gate_other = lax.ppermute(gate, "fsdp", SWAP)
    up_other = lax.ppermute(up, "fsdp", SWAP)
    silu, stat = call(
        silu_kernel,
        "silu",
        [array(units, rows, dtype=jnp.float32), array(8, rows, dtype=jnp.float32)],
        [ON_CHIP] * 2,
        [gate, gate_other],
        moved=8 * units * rows,
    )
    kept, to_far, to_side, to_side_far = call(
        down_kernel,
        "down",
        [array(half, columns)] * 4,
        [SCALARS] + [ON_CHIP] * 5,
        [ids, silu, stat, up, up_other, down_held],
        scratch=[pltpu.VMEM((units, rows), jnp.bfloat16)],
        flops=flops,
    )
    from_side_far = lax.ppermute(to_side_far, both_axes, crossed(2, 3))
    from_far = lax.ppermute(to_far, "groups", SWAP)
    from_side = lax.ppermute(to_side, "mod", SWAP)
    merged = call(
        merge_kernel,
        "merge",
        [array(slots, columns)] * 4,
        [SCALARS] + [ON_CHIP] * 5,
        [ids, own, kept, from_side, from_far, from_side_far],
    )
    values = [merged[0]] + [lax.ppermute(merged[v], "tok", crossed(2, v)) for v in (1, 2, 3)]
    return call(
        scatter_kernel, "scatter", array(tokens, columns), [ON_CHIP] * 5, [pick, *values]
    )


def solution(mesh):
    placed = (
        P(("groups", "tok"), ("fsdp", "mod")),
        P(("groups", "tok"), ("mod", "fsdp")),
        P("tok", ("fsdp", "mod")),
        P(None, ("fsdp", "mod")),
        P(("fsdp", "mod"), None),
        P(("groups", "tok")),
        P(None, ("groups", "tok")),
        P("mod", "fsdp", "tok"),
        P("mod", "fsdp", "tok"),
        P("mod", "tok", "fsdp"),
    )
    sizes = dict(n_tok=mesh.shape["tok"], n_mod=mesh.shape["mod"], n_fsdp=mesh.shape["fsdp"])
    paired = (
        mesh.shape["groups"] == 2
        and sizes == dict(n_tok=4, n_mod=2, n_fsdp=2)
    )
    body = paired_local if paired else functools.partial(local, **sizes)
    return jax.shard_map(
        body,
        mesh=mesh,
        in_specs=placed,
        out_specs=P(("groups", "tok"), ("fsdp", "mod")),
        check_vma=False,
    )
```

```python
import functools

import jax
import jax.numpy as jnp
from jax import lax
from jax.experimental import pallas as pl
from jax.experimental.pallas import tpu as pltpu
from jax.sharding import PartitionSpec as P

D = 4096
STAT_COLS = 128
FEW = 4


def ring(size, step):
    return [(i, (i + step) % size) for i in range(size)]


def reduce_tok(blocks, n_tok):
    if n_tok > FEW:
        return lax.psum_scatter(blocks, "tok", scatter_dimension=0, tiled=False).astype(jnp.float32)
    own = lax.axis_index("tok")
    total = lax.dynamic_index_in_dim(blocks, own, 0, False).astype(jnp.float32)
    for step in range(1, n_tok):
        sent = lax.dynamic_index_in_dim(blocks, (own + step) % n_tok, 0, False)
        total = total + lax.ppermute(sent, "tok", ring(n_tok, step)).astype(jnp.float32)
    return total


def gather_tok(rows, n_tok):
    if n_tok > FEW:
        return lax.all_gather(rows, "tok", axis=0, tiled=False)
    own = lax.axis_index("tok")
    result = jnp.zeros((n_tok,) + rows.shape, rows.dtype)
    result = lax.dynamic_update_index_in_dim(result, rows, own, 0)
    for step in range(1, n_tok):
        got = lax.ppermute(rows, "tok", ring(n_tok, step))
        result = lax.dynamic_update_index_in_dim(result, got, (own - step) % n_tok, 0)
    return result


def spread_context(rows, n_tok, n_mod, n_fsdp):
    if n_tok > FEW or n_tok != n_mod * n_fsdp:
        full = lax.all_gather(rows, ("mod", "fsdp"), axis=1, tiled=True)
        split = full.reshape(full.shape[0], n_tok, full.shape[1] // n_tok).transpose(1, 0, 2)
        return lax.all_to_all(split, "tok", 0, 0, tiled=True)
    pairs = [(t * n_tok + q, q * n_tok + t) for t in range(n_tok) for q in range(n_tok)]
    swapped = lax.ppermute(rows, ("tok", "mod", "fsdp"), pairs)
    return lax.all_gather(swapped, ("mod", "fsdp"), axis=0, tiled=False)


def local(
    residual,
    context,
    out_proj,
    norm_gain,
    router_weight,
    block_modality,
    expert_rows,
    gate_weight,
    up_weight,
    down_weight,
    *,
    n_tok,
    n_mod,
    n_fsdp,
):
    token_count = residual.shape[0]
    experts, capacity = expert_rows.shape
    kind_experts = experts // 2
    slots = kind_experts * capacity
    local_experts = gate_weight.shape[0]
    columns = residual.shape[1]
    assert block_modality.shape == (1,) and n_mod * local_experts == experts
    modality = block_modality[0]
    first = modality * kind_experts
    mod_index = lax.axis_index("mod")

    own_rows = lax.dynamic_slice_in_dim(expert_rows, first, kind_experts, 0).reshape(slots)
    pick = own_rows[:, None] == lax.iota(jnp.int32, token_count)[None, :]
    pick_half = pick.astype(jnp.bfloat16)
    picked_context = jnp.dot(pick_half, context, preferred_element_type=jnp.float32).astype(jnp.bfloat16)
    picked_residual = jnp.dot(pick_half, residual, preferred_element_type=jnp.float32)

    spread = spread_context(picked_context, n_tok, n_mod, n_fsdp)
    partial = jnp.einsum("tsk,kc->tsc", spread, out_proj, preferred_element_type=jnp.float32)
    hidden = picked_residual + reduce_tok(partial.astype(jnp.bfloat16), n_tok)

    gain_table = norm_gain.astype(jnp.float32)
    gained = hidden * jnp.where(modality == 0, gain_table[0], gain_table[1])[None, :]
    router = lax.dynamic_slice_in_dim(router_weight.astype(jnp.float32), first, kind_experts, 1)
    slot_router = jnp.repeat(router.T, capacity, axis=0)
    squares = jnp.sum(hidden * hidden, axis=1, keepdims=True)
    logits = jnp.sum(gained * slot_router, axis=1, keepdims=True)
    flag = jnp.broadcast_to(modality.astype(jnp.bfloat16), (slots, 1))
    stat_list = []
    for stat in (squares, logits):
        high = lax.reduce_precision(stat, 8, 7)
        stat_list += [high.astype(jnp.bfloat16), (stat - high).astype(jnp.bfloat16)]
    packed = jnp.concatenate(
        [gained.astype(jnp.bfloat16)] + stat_list
        + [flag, jnp.zeros((slots, STAT_COLS - 5), jnp.bfloat16)],
        axis=1,
    )

    everyone = gather_tok(packed, n_tok)
    both = lax.all_gather(everyone, "mod", axis=0, tiled=False)
    kind_first = (mod_index * local_experts) % kind_experts
    both = both.reshape(n_mod, n_tok, kind_experts, capacity, columns + STAT_COLS)
    mine = lax.dynamic_slice_in_dim(both, kind_first, local_experts, 2)
    piece = mine[..., :columns].transpose(2, 1, 3, 0, 4).reshape(
        local_experts, n_tok * capacity, n_mod * columns
    )
    tail = mine[..., columns : columns + 5].astype(jnp.float32)
    half_stats = jnp.sum(
        jnp.stack([tail[..., 0] + tail[..., 1], tail[..., 2] + tail[..., 3]], axis=-1), axis=0
    )
    stats = lax.psum(half_stats, "fsdp")
    flags = tail[0, :, :, :, 4]
    by_expert = stats.transpose(1, 0, 2, 3).reshape(local_experts, n_tok * capacity, 2)
    inverse = lax.rsqrt(by_expert[..., 0:1] / D + 1e-05)
    score = jax.nn.sigmoid(by_expert[..., 1:2] * inverse)

    gate_part = jnp.einsum("esd,edf->esf", piece, gate_weight, preferred_element_type=jnp.float32)
    up_part = jnp.einsum("esd,edf->esf", piece, up_weight, preferred_element_type=jnp.float32)
    gate_half = gate_part.astype(jnp.bfloat16)
    up_half = up_part.astype(jnp.bfloat16)
    if n_fsdp == 2:
        swap = [(0, 1), (1, 0)]
        gate_sum = gate_half.astype(jnp.float32) + lax.ppermute(gate_half, "fsdp", swap).astype(jnp.float32)
        up_sum = up_half.astype(jnp.float32) + lax.ppermute(up_half, "fsdp", swap).astype(jnp.float32)
    else:
        gate_sum = lax.psum(gate_half, "fsdp").astype(jnp.float32)
        up_sum = lax.psum(up_half, "fsdp").astype(jnp.float32)
    activation = (jax.nn.silu(gate_sum * inverse) * (up_sum * inverse)).astype(jnp.bfloat16)
    value = jnp.einsum("esf,efd->esd", activation, down_weight, preferred_element_type=jnp.float32)
    value = (value * score).astype(jnp.bfloat16)
    value = value.reshape(local_experts, n_tok, capacity, n_mod * columns).transpose(1, 0, 2, 3)

    own_kind = (mod_index * local_experts) // kind_experts
    valid = (flags == own_kind.astype(jnp.float32))[..., None]
    if n_mod == 2:
        value = value.reshape(n_tok, local_experts, capacity, n_mod, columns)
        kept = lax.dynamic_index_in_dim(value, mod_index, 3, False)
        sent = lax.dynamic_index_in_dim(value, 1 - mod_index, 3, False)
        got = lax.ppermute(sent, "mod", [(0, 1), (1, 0)])
        merged = jnp.where(valid, kept, got).reshape(n_tok, slots, columns)
    else:
        value = jnp.where(valid, value, jnp.zeros((), jnp.bfloat16))
        wide = jnp.zeros((n_tok, kind_experts, capacity, n_mod * columns), jnp.bfloat16)
        wide = lax.dynamic_update_slice_in_dim(wide, value, kind_first, 1)
        wide = wide.reshape(n_tok, slots, n_mod * columns)
        merged = lax.psum_scatter(wide, "mod", scatter_dimension=2, tiled=True)
    summed = reduce_tok(merged, n_tok)
    return jnp.dot(
        pick.astype(jnp.float32).T, summed, precision=lax.Precision.HIGHEST
    ).astype(jnp.bfloat16)


SWAP = [(0, 1), (1, 0)]
STRIP = 688
TILE = 16
ON_CHIP = pl.BlockSpec(memory_space=pltpu.VMEM)
SCALARS = pl.BlockSpec(memory_space=pltpu.SMEM)
IN_HBM = pl.BlockSpec(memory_space=pltpu.HBM)
ANYWHERE = pl.BlockSpec(memory_space=pl.ANY)
GROUP, FLIP, SIDE = range(3)


def crossed(bits, flip):
    return [(i, i ^ flip) for i in range(1 << bits)]


def call(kernel, name, outs, specs, args, scratch=(), flops=0, moved=0, limit=8 << 20):
    return pl.pallas_call(
        kernel,
        out_shape=outs,
        in_specs=specs,
        out_specs=jax.tree.map(lambda _: ON_CHIP, outs),
        scratch_shapes=list(scratch),
        compiler_params=pltpu.CompilerParams(vmem_limit_bytes=limit),
        cost_estimate=pl.CostEstimate(flops=flops, transcendentals=0, bytes_accessed=moved),
        name=name,
    )(*args)


def array(*shape, dtype=jnp.bfloat16):
    return jax.ShapeDtypeStruct(shape, dtype)


def keep_kernel(spans, ids_ref, after_ref, *refs):
    count = len(spans)
    weights, held, semaphores = refs[:count], refs[count : 2 * count], refs[-1]
    copies = [
        pltpu.make_async_copy(weight.at[ids_ref[GROUP], a:b, c:d], to, semaphores.at[n])
        for n, (weight, to, (a, b, c, d)) in enumerate(zip(weights, held, spans))
    ]
    for copy in copies:
        copy.start()
    for copy in copies:
        copy.wait()


def in_hbm(value):
    return pltpu.with_memory_space_constraint(value, pltpu.HBM)


def keep_on_chip(ids, after, weights, spans, name):
    return call(
        functools.partial(keep_kernel, spans),
        name,
        [pltpu.VMEM((b - a, d - c), jnp.bfloat16) for a, b, c, d in spans],
        [SCALARS, ANYWHERE] + [IN_HBM] * len(spans),
        [ids, after] + [in_hbm(weight) for weight in weights],
        scratch=[pltpu.SemaphoreType.DMA((len(spans),))],
        moved=sum(2 * (b - a) * (d - c) for a, b, c, d in spans),
        limit=1 << 20,
    )


def select_kernel(ids_ref, kind_ref, rows_hbm, context_hbm, picked_ref, pick_ref, rows_ref, context_ref, semaphores):
    rows_copy = pltpu.make_async_copy(rows_hbm, rows_ref, semaphores.at[0])
    context_copy = pltpu.make_async_copy(context_hbm, context_ref, semaphores.at[1])
    rows_copy.start()
    context_copy.start()
    rows_copy.wait()
    capacity = rows_ref.shape[1]
    slots, tokens = pick_ref.shape
    row = lax.broadcasted_iota(jnp.int32, (slots, tokens), 0)
    token = lax.broadcasted_iota(jnp.int32, (slots, tokens), 1)
    wanted = jnp.full((slots, tokens), -1, jnp.int32)
    for e in range(2):
        expert = 2 * kind_ref[0] + (ids_ref[GROUP] ^ e)
        for s in range(capacity):
            wanted = jnp.where(row == e * capacity + s, rows_ref[expert, s], wanted)
    pick = jnp.where(wanted == token, 1.0, 0.0).astype(jnp.bfloat16)
    pick_ref[...] = pick
    context_copy.wait()
    picked_ref[...] = jnp.dot(pick, context_ref[...], preferred_element_type=jnp.float32).astype(jnp.bfloat16)


def keep_gate_kernel(
    ids_ref, pick_ref, residual_hbm, gate_ref, proj_ref, gate_held, proj_held, rest_ref, residual_ref, semaphores
):
    copies = [
        pltpu.make_async_copy(residual_hbm, residual_ref, semaphores.at[0]),
        pltpu.make_async_copy(proj_ref, proj_held, semaphores.at[1]),
        pltpu.make_async_copy(gate_ref.at[ids_ref[GROUP], : gate_held.shape[0]], gate_held, semaphores.at[2]),
    ]
    for copy in copies:
        copy.start()
    copies[0].wait()
    rest_ref[...] = jnp.dot(pick_ref[...], residual_ref[...], preferred_element_type=jnp.float32)
    for copy in copies[1:]:
        copy.wait()


def join_kernel(near_ref, across_ref, _, out_ref):
    slots = near_ref.shape[0]
    out_ref[:slots, :] = near_ref[...]
    out_ref[slots:, :] = across_ref[...]


def project_kernel(ids_ref, joined_ref, other_ref, weight_ref, out_ref, rows_ref):
    pair = joined_ref.shape[0]
    slots = pair // 2
    rows_ref[:pair, :] = joined_ref[...]
    rows_ref[pair:, :] = other_ref[...]
    product = jnp.dot(rows_ref[...], weight_ref[...], preferred_element_type=jnp.float32)
    product = product.astype(jnp.bfloat16)
    for n, u in enumerate((0, 2, 1, 3)):
        out_ref[ids_ref[FLIP] ^ u] = product[n * slots : (n + 1) * slots, :]


def split_high_low(value):
    high = value.astype(jnp.bfloat16).astype(jnp.float32)
    return high, value - high


def norm_kernel(ids_ref, kind_ref, rest_ref, partial_ref, one_ref, two_ref, three_ref, gain_ref, router_ref, _, out_ref):
    slots, columns = rest_ref.shape
    hidden = rest_ref[...] + partial_ref[0].astype(jnp.float32)
    for got_ref in (three_ref, two_ref, one_ref):
        hidden = hidden + got_ref[...].astype(jnp.float32)
    gains = gain_ref[...].astype(jnp.float32)
    gained = hidden * jnp.where(kind_ref[0] == 0, gains[0:1], gains[1:2])
    out_ref[:, :columns] = gained.astype(jnp.bfloat16)
    table = router_ref[...].astype(jnp.float32)
    pieces = []
    for e in range(2):
        expert = 2 * kind_ref[0] + (ids_ref[GROUP] ^ e)
        weights = table[0:1]
        for k in range(1, table.shape[0]):
            weights = jnp.where(expert == k, table[k : k + 1], weights)
        half = slots // 2
        pieces.append(jnp.sum(gained[e * half : (e + 1) * half] * weights, axis=1, keepdims=True))
    logits = jnp.concatenate(pieces, axis=0)
    squares = jnp.sum(hidden * hidden, axis=1, keepdims=True)
    lane = lax.broadcasted_iota(jnp.int32, (slots, STAT_COLS), 1)
    extra = jnp.where(lane == 4, kind_ref[0].astype(jnp.float32), 0.0)
    for at, stat in enumerate(split_high_low(squares) + split_high_low(logits)):
        extra = jnp.where(lane == at, stat, extra)
    out_ref[:, columns:] = extra.astype(jnp.bfloat16)


def places(ids_ref, packed_refs, columns):
    side = ids_ref[SIDE]
    matches, found, before = [], [], 0
    for v, ref in enumerate(packed_refs):
        tail = ref[:, columns:].astype(jnp.float32)
        lane = lax.broadcasted_iota(jnp.int32, tail.shape, 1)
        kind = jnp.where(jnp.max(jnp.where(lane == 4, tail, 0.0)) > 0.5, 1, 0)
        match = kind == side
        place = jnp.minimum(jnp.where(match, before, v - before), len(packed_refs) - 2)
        matches.append(match)
        found.append(place)
        before = before + jnp.where(match, 1, 0)
    return matches, found


def arrange_kernel(ids_ref, zero_ref, one_ref, two_ref, three_ref, _, *out_refs):
    packed_refs = (zero_ref, one_ref, two_ref, three_ref)
    capacity = zero_ref.shape[0] // 2
    for out_ref in out_refs:
        out_ref[...] = jnp.zeros(out_ref.shape, out_ref.dtype)
    matches, found = places(ids_ref, packed_refs, zero_ref.shape[1] - STAT_COLS)
    for ref, match, place in zip(packed_refs, matches, found):
        span = pl.ds(pl.multiple_of(place * capacity, capacity), capacity)
        for wanted, (own_ref, given_ref) in ((True, out_refs[:2]), (False, out_refs[2:])):

            @pl.when(match == wanted)
            def _():
                own_ref[span, :] = ref[:capacity, :]
                given_ref[span, :] = ref[capacity:, :]


def weights_times_rows(weight_refs, rows, out_ref):
    at = 0
    for weight_ref in weight_refs:
        for start in range(0, weight_ref.shape[0], STRIP):
            stop = min(start + STRIP, weight_ref.shape[0])
            out_ref[at : at + stop - start, :] = lax.dot_general(
                weight_ref[start:stop, :], rows, (((1,), (1,)), ((), ())), preferred_element_type=jnp.float32
            ).astype(jnp.bfloat16)
            at += stop - start


def gate_kernel(ids_ref, own_ref, far_ref, side_own_ref, side_far_ref, *refs):
    weight_refs, out_ref, rows_ref = refs[:2], refs[-2], refs[-1]
    half = own_ref.shape[0]
    rows = rows_ref.shape[0]
    units = out_ref.shape[0] - TILE
    columns = rows_ref.shape[1] // 2
    rows_ref[2 * half :, :] = jnp.zeros((rows - 2 * half, 2 * columns), rows_ref.dtype)
    for side in range(2):

        @pl.when(ids_ref[SIDE] == side)
        def _():
            here, there = side * columns, (1 - side) * columns
            rows_ref[:half, here : here + columns] = own_ref[:, :columns]
            rows_ref[half : 2 * half, here : here + columns] = far_ref[:, :columns]
            rows_ref[:half, there : there + columns] = side_own_ref[:, :columns]
            rows_ref[half : 2 * half, there : there + columns] = side_far_ref[:, :columns]

    weights_times_rows(weight_refs, rows_ref[...], out_ref)
    tails = [ref[:, columns:].astype(jnp.float32) for ref in (own_ref, side_own_ref, far_ref, side_far_ref)]
    unused = jnp.zeros((rows - 2 * half, STAT_COLS), jnp.float32)
    stat = jnp.concatenate([tails[0] + tails[1], tails[2] + tails[3], unused], axis=0).T
    squares = stat[0:1] + stat[1:2]
    logits = stat[2:3] + stat[3:4]
    at_row = lax.broadcasted_iota(jnp.int32, (TILE, rows), 0)
    extra = jnp.zeros((TILE, rows), jnp.float32)
    for at, piece in enumerate(split_high_low(squares) + split_high_low(logits)):
        extra = jnp.where(at_row == at, piece, extra)
    out_ref[units:, :] = extra.astype(jnp.bfloat16)


def up_kernel(rows_ref, *refs):
    weight_refs, out_ref = refs[:-1], refs[-1]
    weights_times_rows(weight_refs, rows_ref[...], out_ref)


def silu_kernel(gate_ref, gate_other_ref, out_ref, stat_ref):
    units = out_ref.shape[0]
    stat = gate_ref[units:, :].astype(jnp.float32) + gate_other_ref[units:, :].astype(jnp.float32)
    inverse = lax.rsqrt((stat[0:1] + stat[1:2]) / D + 1e-05)
    logits = (stat[2:3] + stat[3:4]) * inverse
    score = 1.0 / (1.0 + jnp.exp(-logits))
    at_row = lax.broadcasted_iota(jnp.int32, stat_ref.shape, 0)
    stat_ref[...] = jnp.where(at_row == 0, inverse, score)
    for start in range(0, units, STRIP):
        stop = min(start + STRIP, units)
        gate = gate_ref[start:stop, :].astype(jnp.float32) + gate_other_ref[start:stop, :].astype(jnp.float32)
        gate = gate * inverse
        out_ref[start:stop, :] = gate / (1.0 + jnp.exp(-gate)) * inverse


def down_kernel(
    ids_ref, silu_ref, stat_ref, up_ref, up_other_ref, first_ref, second_ref,
    kept_ref, far_ref, side_ref, side_far_ref, act_ref,
):
    units, rows = act_ref.shape
    for start in range(0, units, STRIP):
        stop = min(start + STRIP, units)
        up = up_ref[start:stop, :].astype(jnp.float32) + up_other_ref[start:stop, :].astype(jnp.float32)
        act_ref[start:stop, :] = (silu_ref[start:stop, :] * up).astype(jnp.bfloat16)
    half, columns = kept_ref.shape
    score = jnp.broadcast_to(stat_ref[1:2, :], (rows, rows)).T[:, 0:1]
    width_first = first_ref.shape[1]
    for start, weight_ref, a, b in (
        (0, first_ref, 0, columns),
        (columns, first_ref, columns, width_first),
        (width_first, second_ref, 0, 2 * columns - width_first),
    ):
        value = lax.dot_general(
            act_ref[...], weight_ref[:, a:b], (((0,), (0,)), ((), ())), preferred_element_type=jnp.float32
        )
        value = (value * score).astype(jnp.bfloat16)
        quarter, at = divmod(start, columns)
        for across, (own_out, far_out) in enumerate(((kept_ref, far_ref), (side_ref, side_far_ref))):

            @pl.when((ids_ref[SIDE] ^ quarter) == across)
            def _():
                own_out[:, at : at + b - a] = value[:half]
                far_out[:, at : at + b - a] = value[half : 2 * half]


def merge_kernel(ids_ref, zero_ref, one_ref, two_ref, three_ref, kept_ref, side_ref, far_ref, side_far_ref, *out_refs):
    columns = kept_ref.shape[1]
    capacity = zero_ref.shape[0] // 2
    matches, found = places(ids_ref, (zero_ref, one_ref, two_ref, three_ref), columns)
    for out_ref, match, place in zip(out_refs, matches, found):
        span = pl.ds(pl.multiple_of(place * capacity, capacity), capacity)
        for wanted, (first_ref, second_ref) in ((True, (kept_ref, far_ref)), (False, (side_ref, side_far_ref))):

            @pl.when(match == wanted)
            def _():
                out_ref[:capacity, :] = first_ref[span, :]
                out_ref[capacity:, :] = second_ref[span, :]


def scatter_kernel(pick_ref, zero_ref, one_ref, two_ref, three_ref, out_ref):
    total = zero_ref[...].astype(jnp.float32)
    for got_ref in (three_ref, two_ref, one_ref):
        total = total + got_ref[...].astype(jnp.float32)
    high, rest = split_high_low(total)
    middle, low = split_high_low(rest)
    result = 0.0
    for piece in (low, middle, high):
        result = result + lax.dot_general(
            pick_ref[...], piece.astype(jnp.bfloat16), (((0,), (0,)), ((), ())),
            preferred_element_type=jnp.float32,
        )
    out_ref[...] = result.astype(jnp.bfloat16)


def paired_local(
    residual,
    context,
    out_proj,
    norm_gain,
    router_weight,
    block_modality,
    expert_rows,
    gate_weight,
    up_weight,
    down_weight,
):
    tokens, columns = residual.shape
    experts, capacity = expert_rows.shape
    slots = 2 * capacity
    half = 4 * capacity
    rows = 2 * half
    units, width = down_weight.shape[1:]
    assert block_modality.shape == (1,) and experts == 4 and gate_weight.shape[0] == 2
    tok, side = lax.axis_index("tok"), lax.axis_index("mod")
    corner = 2 * side + lax.axis_index("fsdp")
    ids = jnp.stack([lax.axis_index("groups"), tok ^ corner, side])

    picked, pick = call(
        select_kernel,
        "select",
        [array(slots, columns), array(slots, tokens)],
        [SCALARS] * 2 + [IN_HBM] * 2,
        [ids, block_modality, in_hbm(expert_rows), in_hbm(context)],
        scratch=[
            pltpu.SMEM((experts, capacity), jnp.int32),
            pltpu.VMEM((tokens, columns), jnp.bfloat16),
            pltpu.SemaphoreType.DMA((2,)),
        ],
    )
    plane = ("tok", "mod", "fsdp")
    to_first = [(t * 4 + q, q * 4 + t) for t in range(4) for q in range(4)]
    to_second = [(t * 4 + q, q * 4 + (t ^ 2)) for t in range(4) for q in range(4)]
    near = lax.ppermute(picked, plane, to_first)
    across = lax.ppermute(picked, plane, to_second)
    units_first = units // 2
    gate_first, proj_held, rest = call(
        keep_gate_kernel,
        "keep_gate",
        [
            pltpu.VMEM((units_first, width), jnp.bfloat16),
            pltpu.VMEM(out_proj.shape, jnp.bfloat16),
            array(slots, columns, dtype=jnp.float32),
        ],
        [SCALARS, ON_CHIP, IN_HBM, IN_HBM, IN_HBM],
        [ids, pick, in_hbm(residual), in_hbm(gate_weight.swapaxes(1, 2)), in_hbm(out_proj)],
        scratch=[pltpu.VMEM((tokens, columns), jnp.bfloat16), pltpu.SemaphoreType.DMA((3,))],
        moved=units * width,
        limit=2 << 20,
    )
    joined = call(join_kernel, "join", array(half, columns), [ON_CHIP] * 3, [near, across, gate_first])
    other = lax.ppermute(joined, "fsdp", SWAP)
    partial = call(
        project_kernel,
        "project",
        array(4, slots, columns),
        [SCALARS] + [ON_CHIP] * 3,
        [ids, joined, other, proj_held],
        scratch=[pltpu.VMEM((rows, columns), jnp.bfloat16)],
    )
    sums = [lax.ppermute(partial[v], "tok", crossed(2, v)) for v in (1, 2, 3)]
    gate_second, up_first = keep_on_chip(
        ids,
        partial,
        [gate_weight.swapaxes(1, 2), up_weight.swapaxes(1, 2)],
        [(units_first, units, 0, width), (0, units // 4, 0, width)],
        "keep_more",
    )
    packed_columns = columns + STAT_COLS
    packed = call(
        norm_kernel,
        "norm",
        array(slots, packed_columns),
        [SCALARS, SCALARS] + [ON_CHIP] * 8,
        [ids, block_modality, rest, partial, *sums, norm_gain, router_weight.T, up_first],
    )
    others = [lax.ppermute(packed, "tok", crossed(2, v)) for v in (1, 2, 3)]
    (up_second,) = keep_on_chip(ids, packed, [up_weight.swapaxes(1, 2)], [(units // 4, units, 0, width)], "keep_up")
    kept_slots = 3 * capacity
    own, to_far_rows, to_side_rows, to_corner_rows = call(
        arrange_kernel,
        "arrange",
        [array(kept_slots, packed_columns)] * 4,
        [SCALARS] + [ON_CHIP] * 5,
        [ids, packed, *others, up_second],
    )
    both_axes = ("groups", "mod")
    side_far = lax.ppermute(to_corner_rows, both_axes, crossed(2, 3))
    far = lax.ppermute(to_far_rows, "groups", SWAP)
    side_own = lax.ppermute(to_side_rows, "mod", SWAP)

    width_first = width // 4 * 3
    (down_first,) = keep_on_chip(ids, own, [down_weight], [(0, units, 0, width_first)], "keep_down")

    flops = 2 * rows * units * width
    gate, gathered = call(
        gate_kernel,
        "gate",
        [array(units + TILE, rows), array(rows, width)],
        [SCALARS] + [ON_CHIP] * 7,
        [ids, own, far, side_own, side_far, gate_first, gate_second, down_first],
        flops=flops,
    )
    up = call(
        up_kernel, "up", array(units, rows), [ON_CHIP] * 3, [gathered, up_first, up_second], flops=flops
    )
    gate_other = lax.ppermute(gate, "fsdp", SWAP)
    up_other = lax.ppermute(up, "fsdp", SWAP)
    (down_second,) = keep_on_chip(ids, up, [down_weight], [(0, units, width_first, width)], "keep_last")
    silu, stat = call(
        silu_kernel,
        "silu",
        [array(units, rows, dtype=jnp.float32), array(8, rows, dtype=jnp.float32)],
        [ON_CHIP] * 2,
        [gate, gate_other],
        moved=8 * units * rows,
    )
    kept, to_far, to_side, to_side_far = call(
        down_kernel,
        "down",
        [array(kept_slots, columns)] * 4,
        [SCALARS] + [ON_CHIP] * 6,
        [ids, silu, stat, up, up_other, down_first, down_second],
        scratch=[pltpu.VMEM((units, rows), jnp.bfloat16)],
        flops=flops,
    )
    from_side_far = lax.ppermute(to_side_far, both_axes, crossed(2, 3))
    from_far = lax.ppermute(to_far, "groups", SWAP)
    from_side = lax.ppermute(to_side, "mod", SWAP)
    merged = call(
        merge_kernel,
        "merge",
        [array(slots, columns)] * 4,
        [SCALARS] + [ON_CHIP] * 8,
        [ids, packed, *others, kept, from_side, from_far, from_side_far],
    )
    values = [merged[0]] + [lax.ppermute(merged[v], "tok", crossed(2, v)) for v in (1, 2, 3)]
    return call(
        scatter_kernel, "scatter", array(tokens, columns), [ON_CHIP] * 5, [pick, *values]
    )


def solution(mesh):
    placed = (
        P(("groups", "tok"), ("fsdp", "mod")),
        P(("groups", "tok"), ("mod", "fsdp")),
        P("tok", ("fsdp", "mod")),
        P(None, ("fsdp", "mod")),
        P(("fsdp", "mod"), None),
        P(("groups", "tok")),
        P(None, ("groups", "tok")),
        P("mod", "fsdp", "tok"),
        P("mod", "fsdp", "tok"),
        P("mod", "tok", "fsdp"),
    )
    sizes = dict(n_tok=mesh.shape["tok"], n_mod=mesh.shape["mod"], n_fsdp=mesh.shape["fsdp"])
    paired = (
        mesh.shape["groups"] == 2
        and sizes == dict(n_tok=4, n_mod=2, n_fsdp=2)
    )
    body = paired_local if paired else functools.partial(local, **sizes)
    return jax.shard_map(
        body,
        mesh=mesh,
        in_specs=placed,
        out_specs=P(("groups", "tok"), ("fsdp", "mod")),
        check_vma=False,
    )
```

```python
import functools

import jax
import jax.numpy as jnp
from jax import lax
from jax.experimental import pallas as pl
from jax.experimental.pallas import tpu as pltpu
from jax.sharding import PartitionSpec as P

D = 4096
STAT_COLS = 128
FEW = 4


def ring(size, step):
    return [(i, (i + step) % size) for i in range(size)]


def reduce_tok(blocks, n_tok):
    if n_tok > FEW:
        return lax.psum_scatter(blocks, "tok", scatter_dimension=0, tiled=False).astype(jnp.float32)
    own = lax.axis_index("tok")
    total = lax.dynamic_index_in_dim(blocks, own, 0, False).astype(jnp.float32)
    for step in range(1, n_tok):
        sent = lax.dynamic_index_in_dim(blocks, (own + step) % n_tok, 0, False)
        total = total + lax.ppermute(sent, "tok", ring(n_tok, step)).astype(jnp.float32)
    return total


def gather_tok(rows, n_tok):
    if n_tok > FEW:
        return lax.all_gather(rows, "tok", axis=0, tiled=False)
    own = lax.axis_index("tok")
    result = jnp.zeros((n_tok,) + rows.shape, rows.dtype)
    result = lax.dynamic_update_index_in_dim(result, rows, own, 0)
    for step in range(1, n_tok):
        got = lax.ppermute(rows, "tok", ring(n_tok, step))
        result = lax.dynamic_update_index_in_dim(result, got, (own - step) % n_tok, 0)
    return result


def spread_context(rows, n_tok, n_mod, n_fsdp):
    if n_tok > FEW or n_tok != n_mod * n_fsdp:
        full = lax.all_gather(rows, ("mod", "fsdp"), axis=1, tiled=True)
        split = full.reshape(full.shape[0], n_tok, full.shape[1] // n_tok).transpose(1, 0, 2)
        return lax.all_to_all(split, "tok", 0, 0, tiled=True)
    pairs = [(t * n_tok + q, q * n_tok + t) for t in range(n_tok) for q in range(n_tok)]
    swapped = lax.ppermute(rows, ("tok", "mod", "fsdp"), pairs)
    return lax.all_gather(swapped, ("mod", "fsdp"), axis=0, tiled=False)


def local(
    residual,
    context,
    out_proj,
    norm_gain,
    router_weight,
    block_modality,
    expert_rows,
    gate_weight,
    up_weight,
    down_weight,
    *,
    n_tok,
    n_mod,
    n_fsdp,
):
    token_count = residual.shape[0]
    experts, capacity = expert_rows.shape
    kind_experts = experts // 2
    slots = kind_experts * capacity
    local_experts = gate_weight.shape[0]
    columns = residual.shape[1]
    assert block_modality.shape == (1,) and n_mod * local_experts == experts
    modality = block_modality[0]
    first = modality * kind_experts
    mod_index = lax.axis_index("mod")

    own_rows = lax.dynamic_slice_in_dim(expert_rows, first, kind_experts, 0).reshape(slots)
    pick = own_rows[:, None] == lax.iota(jnp.int32, token_count)[None, :]
    pick_half = pick.astype(jnp.bfloat16)
    picked_context = jnp.dot(pick_half, context, preferred_element_type=jnp.float32).astype(jnp.bfloat16)
    picked_residual = jnp.dot(pick_half, residual, preferred_element_type=jnp.float32)

    spread = spread_context(picked_context, n_tok, n_mod, n_fsdp)
    partial = jnp.einsum("tsk,kc->tsc", spread, out_proj, preferred_element_type=jnp.float32)
    hidden = picked_residual + reduce_tok(partial.astype(jnp.bfloat16), n_tok)

    gain_table = norm_gain.astype(jnp.float32)
    gained = hidden * jnp.where(modality == 0, gain_table[0], gain_table[1])[None, :]
    router = lax.dynamic_slice_in_dim(router_weight.astype(jnp.float32), first, kind_experts, 1)
    slot_router = jnp.repeat(router.T, capacity, axis=0)
    squares = jnp.sum(hidden * hidden, axis=1, keepdims=True)
    logits = jnp.sum(gained * slot_router, axis=1, keepdims=True)
    flag = jnp.broadcast_to(modality.astype(jnp.bfloat16), (slots, 1))
    stat_list = []
    for stat in (squares, logits):
        high = lax.reduce_precision(stat, 8, 7)
        stat_list += [high.astype(jnp.bfloat16), (stat - high).astype(jnp.bfloat16)]
    packed = jnp.concatenate(
        [gained.astype(jnp.bfloat16)] + stat_list
        + [flag, jnp.zeros((slots, STAT_COLS - 5), jnp.bfloat16)],
        axis=1,
    )

    everyone = gather_tok(packed, n_tok)
    both = lax.all_gather(everyone, "mod", axis=0, tiled=False)
    kind_first = (mod_index * local_experts) % kind_experts
    both = both.reshape(n_mod, n_tok, kind_experts, capacity, columns + STAT_COLS)
    mine = lax.dynamic_slice_in_dim(both, kind_first, local_experts, 2)
    piece = mine[..., :columns].transpose(2, 1, 3, 0, 4).reshape(
        local_experts, n_tok * capacity, n_mod * columns
    )
    tail = mine[..., columns : columns + 5].astype(jnp.float32)
    half_stats = jnp.sum(
        jnp.stack([tail[..., 0] + tail[..., 1], tail[..., 2] + tail[..., 3]], axis=-1), axis=0
    )
    stats = lax.psum(half_stats, "fsdp")
    flags = tail[0, :, :, :, 4]
    by_expert = stats.transpose(1, 0, 2, 3).reshape(local_experts, n_tok * capacity, 2)
    inverse = lax.rsqrt(by_expert[..., 0:1] / D + 1e-05)
    score = jax.nn.sigmoid(by_expert[..., 1:2] * inverse)

    gate_part = jnp.einsum("esd,edf->esf", piece, gate_weight, preferred_element_type=jnp.float32)
    up_part = jnp.einsum("esd,edf->esf", piece, up_weight, preferred_element_type=jnp.float32)
    gate_half = gate_part.astype(jnp.bfloat16)
    up_half = up_part.astype(jnp.bfloat16)
    if n_fsdp == 2:
        swap = [(0, 1), (1, 0)]
        gate_sum = gate_half.astype(jnp.float32) + lax.ppermute(gate_half, "fsdp", swap).astype(jnp.float32)
        up_sum = up_half.astype(jnp.float32) + lax.ppermute(up_half, "fsdp", swap).astype(jnp.float32)
    else:
        gate_sum = lax.psum(gate_half, "fsdp").astype(jnp.float32)
        up_sum = lax.psum(up_half, "fsdp").astype(jnp.float32)
    activation = (jax.nn.silu(gate_sum * inverse) * (up_sum * inverse)).astype(jnp.bfloat16)
    value = jnp.einsum("esf,efd->esd", activation, down_weight, preferred_element_type=jnp.float32)
    value = (value * score).astype(jnp.bfloat16)
    value = value.reshape(local_experts, n_tok, capacity, n_mod * columns).transpose(1, 0, 2, 3)

    own_kind = (mod_index * local_experts) // kind_experts
    valid = (flags == own_kind.astype(jnp.float32))[..., None]
    if n_mod == 2:
        value = value.reshape(n_tok, local_experts, capacity, n_mod, columns)
        kept = lax.dynamic_index_in_dim(value, mod_index, 3, False)
        sent = lax.dynamic_index_in_dim(value, 1 - mod_index, 3, False)
        got = lax.ppermute(sent, "mod", [(0, 1), (1, 0)])
        merged = jnp.where(valid, kept, got).reshape(n_tok, slots, columns)
    else:
        value = jnp.where(valid, value, jnp.zeros((), jnp.bfloat16))
        wide = jnp.zeros((n_tok, kind_experts, capacity, n_mod * columns), jnp.bfloat16)
        wide = lax.dynamic_update_slice_in_dim(wide, value, kind_first, 1)
        wide = wide.reshape(n_tok, slots, n_mod * columns)
        merged = lax.psum_scatter(wide, "mod", scatter_dimension=2, tiled=True)
    summed = reduce_tok(merged, n_tok)
    return jnp.dot(
        pick.astype(jnp.float32).T, summed, precision=lax.Precision.HIGHEST
    ).astype(jnp.bfloat16)


SWAP = [(0, 1), (1, 0)]
STRIP = 688
TILE = 16
SCALARS = pl.BlockSpec(memory_space=pltpu.SMEM)
ON_CHIP = pl.BlockSpec(memory_space=pltpu.VMEM)
IN_HBM = pl.BlockSpec(memory_space=pltpu.HBM)
ANYWHERE = pl.BlockSpec(memory_space=pl.ANY)


def crossed(bits, flip):
    return [(i, i ^ flip) for i in range(1 << bits)]


def call(kernel, name, outs, specs, args, scratch=(), flops=0, moved=0, limit=8 << 20):
    return pl.pallas_call(
        kernel,
        out_shape=outs,
        in_specs=specs,
        out_specs=jax.tree.map(lambda _: ON_CHIP, outs),
        scratch_shapes=list(scratch),
        compiler_params=pltpu.CompilerParams(vmem_limit_bytes=limit),
        cost_estimate=pl.CostEstimate(flops=flops, transcendentals=0, bytes_accessed=moved),
        name=name,
    )(*args)


def array(*shape, dtype=jnp.bfloat16):
    return jax.ShapeDtypeStruct(shape, dtype)


def keep_kernel(spans, after_ref, *refs):
    count = len(spans)
    weights, held, semaphores = refs[:count], refs[count : 2 * count], refs[-1]
    copies = [
        pltpu.make_async_copy(weight.at[lax.axis_index("groups"), a:b, c:d], to, semaphores.at[n])
        for n, (weight, to, (a, b, c, d)) in enumerate(zip(weights, held, spans))
    ]
    for copy in copies:
        copy.start()
    for copy in copies:
        copy.wait()


def in_hbm(value):
    return pltpu.with_memory_space_constraint(value, pltpu.HBM)


def keep_on_chip(after, weights, spans, name):
    return call(
        functools.partial(keep_kernel, spans),
        name,
        [pltpu.VMEM((b - a, d - c), jnp.bfloat16) for a, b, c, d in spans],
        [ANYWHERE] + [IN_HBM] * len(spans),
        [after] + [in_hbm(weight) for weight in weights],
        scratch=[pltpu.SemaphoreType.DMA((len(spans),))],
        moved=sum(2 * (b - a) * (d - c) for a, b, c, d in spans),
        limit=1 << 20,
    )


def select_kernel(
    kind_ref, rows_hbm, context_hbm, picked_ref, pick_ref, kind_out, rows_ref, context_ref, semaphores
):
    rows_copy = pltpu.make_async_copy(rows_hbm, rows_ref, semaphores.at[0])
    context_copy = pltpu.make_async_copy(context_hbm, context_ref, semaphores.at[1])
    rows_copy.start()
    context_copy.start()
    rows_copy.wait()
    kind_out[...] = jnp.full(kind_out.shape, kind_ref[0], jnp.int32).astype(jnp.float32)
    capacity = rows_ref.shape[1]
    slots, tokens = pick_ref.shape
    row = lax.broadcasted_iota(jnp.int32, (slots, tokens), 0)
    token = lax.broadcasted_iota(jnp.int32, (slots, tokens), 1)
    wanted = jnp.full((slots, tokens), -1, jnp.int32)
    for e in range(2):
        expert = 2 * kind_ref[0] + (lax.axis_index("groups") ^ e)
        for s in range(capacity):
            wanted = jnp.where(row == e * capacity + s, rows_ref[expert, s], wanted)
    pick = jnp.where(wanted == token, 1.0, 0.0).astype(jnp.bfloat16)
    pick_ref[...] = pick
    context_copy.wait()
    picked_ref[...] = jnp.dot(pick, context_ref[...], preferred_element_type=jnp.float32).astype(jnp.bfloat16)


def keep_gate_kernel(
    pick_ref, residual_hbm, gate_ref, proj_ref, gate_held, proj_held, rest_ref, residual_ref, semaphores
):
    copies = [
        pltpu.make_async_copy(residual_hbm, residual_ref, semaphores.at[0]),
        pltpu.make_async_copy(proj_ref, proj_held, semaphores.at[1]),
        pltpu.make_async_copy(gate_ref.at[lax.axis_index("groups"), : gate_held.shape[0]], gate_held, semaphores.at[2]),
    ]
    for copy in copies:
        copy.start()
    copies[0].wait()
    rest_ref[...] = jnp.dot(pick_ref[...], residual_ref[...], preferred_element_type=jnp.float32)
    for copy in copies[1:]:
        copy.wait()


def join_kernel(near_ref, across_ref, _, out_ref):
    slots = near_ref.shape[0]
    out_ref[:slots, :] = near_ref[...]
    out_ref[slots:, :] = across_ref[...]


def project_kernel(joined_ref, other_ref, weight_ref, out_ref, rows_ref):
    pair = joined_ref.shape[0]
    slots = pair // 2
    rows_ref[:pair, :] = joined_ref[...]
    rows_ref[pair:, :] = other_ref[...]
    product = jnp.dot(rows_ref[...], weight_ref[...], preferred_element_type=jnp.float32)
    product = product.astype(jnp.bfloat16)
    corner = 2 * lax.axis_index("mod") + lax.axis_index("fsdp")
    flip = lax.axis_index("tok") ^ corner
    for n, u in enumerate((0, 2, 1, 3)):
        out_ref[flip ^ u] = product[n * slots : (n + 1) * slots, :]


def split_high_low(value):
    high = value.astype(jnp.bfloat16).astype(jnp.float32)
    return high, value - high


def norm_kernel(kind_ref, rest_ref, partial_ref, one_ref, two_ref, three_ref, gain_ref, router_ref, _, out_ref):
    slots, columns = rest_ref.shape
    hidden = rest_ref[...] + partial_ref[0].astype(jnp.float32)
    for got_ref in (three_ref, two_ref, one_ref):
        hidden = hidden + got_ref[...].astype(jnp.float32)
    kind = kind_ref[0:1, 0:1]
    gains = gain_ref[...].astype(jnp.float32)
    gained = hidden * jnp.where(kind == 0.0, gains[0:1], gains[1:2])
    out_ref[:, :columns] = gained.astype(jnp.bfloat16)
    table = router_ref[...].astype(jnp.float32)
    pieces = []
    for e in range(2):
        second = (lax.axis_index("groups") ^ e) == 1
        text = jnp.where(second, table[1:2], table[0:1])
        image = jnp.where(second, table[3:4], table[2:3])
        weights = jnp.where(kind == 0.0, text, image)
        half = slots // 2
        pieces.append(jnp.sum(gained[e * half : (e + 1) * half] * weights, axis=1, keepdims=True))
    logits = jnp.concatenate(pieces, axis=0)
    squares = jnp.sum(hidden * hidden, axis=1, keepdims=True)
    lane = lax.broadcasted_iota(jnp.int32, (slots, STAT_COLS), 1)
    extra = jnp.where(lane == 4, kind, 0.0)
    for at, stat in enumerate(split_high_low(squares) + split_high_low(logits)):
        extra = jnp.where(lane == at, stat, extra)
    out_ref[:, columns:] = extra.astype(jnp.bfloat16)


def places(packed_refs, columns):
    side = lax.axis_index("mod")
    matches, found, before = [], [], 0
    for v, ref in enumerate(packed_refs):
        flag = ref[:TILE, columns:].astype(jnp.float32)[0, 4]
        kind = jnp.where(flag > 0.5, 1, 0)
        match = kind == side
        place = jnp.minimum(jnp.where(match, before, v - before), len(packed_refs) - 2)
        matches.append(match)
        found.append(place)
        before = before + jnp.where(match, 1, 0)
    return matches, found


def arrange_kernel(zero_ref, one_ref, two_ref, three_ref, _, *out_refs):
    packed_refs = (zero_ref, one_ref, two_ref, three_ref)
    capacity = zero_ref.shape[0] // 2
    for out_ref in out_refs:
        out_ref[...] = jnp.zeros(out_ref.shape, out_ref.dtype)
    matches, found = places(packed_refs, zero_ref.shape[1] - STAT_COLS)
    for ref, match, place in zip(packed_refs, matches, found):
        span = pl.ds(pl.multiple_of(place * capacity, capacity), capacity)
        for wanted, (own_ref, given_ref) in ((True, out_refs[:2]), (False, out_refs[2:])):

            @pl.when(match == wanted)
            def _():
                own_ref[span, :] = ref[:capacity, :]
                given_ref[span, :] = ref[capacity:, :]


def weights_times_rows(weight_refs, rows, out_ref):
    at = 0
    for weight_ref in weight_refs:
        for start in range(0, weight_ref.shape[0], STRIP):
            stop = min(start + STRIP, weight_ref.shape[0])
            out_ref[at : at + stop - start, :] = lax.dot_general(
                weight_ref[start:stop, :], rows, (((1,), (1,)), ((), ())), preferred_element_type=jnp.float32
            ).astype(jnp.bfloat16)
            at += stop - start


def gate_kernel(own_ref, far_ref, side_own_ref, side_far_ref, *refs):
    weight_refs, out_ref, rows_ref = refs[:2], refs[-2], refs[-1]
    half = own_ref.shape[0]
    rows = rows_ref.shape[0]
    units = out_ref.shape[0] - TILE
    columns = rows_ref.shape[1] // 2
    rows_ref[2 * half :, :] = jnp.zeros((rows - 2 * half, 2 * columns), rows_ref.dtype)
    for side in range(2):

        @pl.when(lax.axis_index("mod") == side)
        def _():
            here, there = side * columns, (1 - side) * columns
            rows_ref[:half, here : here + columns] = own_ref[:, :columns]
            rows_ref[half : 2 * half, here : here + columns] = far_ref[:, :columns]
            rows_ref[:half, there : there + columns] = side_own_ref[:, :columns]
            rows_ref[half : 2 * half, there : there + columns] = side_far_ref[:, :columns]

    weights_times_rows(weight_refs, rows_ref[...], out_ref)
    tails = [ref[:, columns:].astype(jnp.float32) for ref in (own_ref, side_own_ref, far_ref, side_far_ref)]
    unused = jnp.zeros((rows - 2 * half, STAT_COLS), jnp.float32)
    stat = jnp.concatenate([tails[0] + tails[1], tails[2] + tails[3], unused], axis=0).T
    squares = stat[0:1] + stat[1:2]
    logits = stat[2:3] + stat[3:4]
    at_row = lax.broadcasted_iota(jnp.int32, (TILE, rows), 0)
    extra = jnp.zeros((TILE, rows), jnp.float32)
    for at, piece in enumerate(split_high_low(squares) + split_high_low(logits)):
        extra = jnp.where(at_row == at, piece, extra)
    out_ref[units:, :] = extra.astype(jnp.bfloat16)


def up_kernel(rows_ref, *refs):
    weight_refs, out_ref = refs[:-1], refs[-1]
    weights_times_rows(weight_refs, rows_ref[...], out_ref)


def silu_kernel(gate_ref, gate_other_ref, out_ref, stat_ref):
    units = out_ref.shape[0]
    stat = gate_ref[units:, :].astype(jnp.float32) + gate_other_ref[units:, :].astype(jnp.float32)
    inverse = lax.rsqrt((stat[0:1] + stat[1:2]) / D + 1e-05)
    logits = (stat[2:3] + stat[3:4]) * inverse
    score = 1.0 / (1.0 + jnp.exp(-logits))
    at_row = lax.broadcasted_iota(jnp.int32, stat_ref.shape, 0)
    stat_ref[...] = jnp.where(at_row == 0, inverse, score)
    for start in range(0, units, STRIP):
        stop = min(start + STRIP, units)
        gate = gate_ref[start:stop, :].astype(jnp.float32) + gate_other_ref[start:stop, :].astype(jnp.float32)
        gate = gate * inverse
        out_ref[start:stop, :] = gate / (1.0 + jnp.exp(-gate)) * inverse


def down_kernel(
    silu_ref, stat_ref, up_ref, up_other_ref, first_ref, second_ref,
    kept_ref, far_ref, side_ref, side_far_ref, act_ref,
):
    units, rows = act_ref.shape
    for start in range(0, units, STRIP):
        stop = min(start + STRIP, units)
        up = up_ref[start:stop, :].astype(jnp.float32) + up_other_ref[start:stop, :].astype(jnp.float32)
        act_ref[start:stop, :] = (silu_ref[start:stop, :] * up).astype(jnp.bfloat16)
    half, columns = kept_ref.shape
    score = jnp.broadcast_to(stat_ref[1:2, :], (rows, rows)).T[:, 0:1]
    first_units = first_ref.shape[0]
    for quarter in range(2):
        span = slice(quarter * columns, (quarter + 1) * columns)
        value = sum(
            lax.dot_general(
                act_ref[a:b, :], weight_ref[:, span], (((0,), (0,)), ((), ())), preferred_element_type=jnp.float32
            )
            for a, b, weight_ref in ((0, first_units, first_ref), (first_units, units, second_ref))
        )
        value = (value * score).astype(jnp.bfloat16)
        for across, (own_out, far_out) in enumerate(((kept_ref, far_ref), (side_ref, side_far_ref))):

            @pl.when((lax.axis_index("mod") ^ quarter) == across)
            def _():
                own_out[...] = value[:half]
                far_out[...] = value[half : 2 * half]


def merge_kernel(zero_ref, one_ref, two_ref, three_ref, kept_ref, side_ref, far_ref, side_far_ref, *out_refs):
    columns = kept_ref.shape[1]
    capacity = zero_ref.shape[0] // 2
    matches, found = places((zero_ref, one_ref, two_ref, three_ref), columns)
    for out_ref, match, place in zip(out_refs, matches, found):
        span = pl.ds(pl.multiple_of(place * capacity, capacity), capacity)
        for wanted, (first_ref, second_ref) in ((True, (kept_ref, far_ref)), (False, (side_ref, side_far_ref))):

            @pl.when(match == wanted)
            def _():
                out_ref[:capacity, :] = first_ref[span, :]
                out_ref[capacity:, :] = second_ref[span, :]


def scatter_kernel(pick_ref, zero_ref, one_ref, two_ref, three_ref, out_ref):
    total = zero_ref[...].astype(jnp.float32)
    for got_ref in (three_ref, two_ref, one_ref):
        total = total + got_ref[...].astype(jnp.float32)
    high, rest = split_high_low(total)
    middle, low = split_high_low(rest)
    result = 0.0
    for piece in (low, middle, high):
        result = result + lax.dot_general(
            pick_ref[...], piece.astype(jnp.bfloat16), (((0,), (0,)), ((), ())),
            preferred_element_type=jnp.float32,
        )
    out_ref[...] = result.astype(jnp.bfloat16)


def paired_local(
    residual,
    context,
    out_proj,
    norm_gain,
    router_weight,
    block_modality,
    expert_rows,
    gate_weight,
    up_weight,
    down_weight,
):
    tokens, columns = residual.shape
    experts, capacity = expert_rows.shape
    slots = 2 * capacity
    half = 4 * capacity
    rows = 2 * half
    units, width = down_weight.shape[1:]
    assert block_modality.shape == (1,) and experts == 4 and gate_weight.shape[0] == 2
    picked, pick, kind = call(
        select_kernel,
        "select",
        [array(slots, columns), array(slots, tokens), array(8, STAT_COLS, dtype=jnp.float32)],
        [SCALARS, IN_HBM, IN_HBM],
        [block_modality, in_hbm(expert_rows), in_hbm(context)],
        scratch=[
            pltpu.SMEM((experts, capacity), jnp.int32),
            pltpu.VMEM((tokens, columns), jnp.bfloat16),
            pltpu.SemaphoreType.DMA((2,)),
        ],
    )
    plane = ("tok", "mod", "fsdp")
    to_first = [(t * 4 + q, q * 4 + t) for t in range(4) for q in range(4)]
    to_second = [(t * 4 + q, q * 4 + (t ^ 2)) for t in range(4) for q in range(4)]
    near = lax.ppermute(picked, plane, to_first)
    across = lax.ppermute(picked, plane, to_second)
    units_first = units // 2
    gate_first, proj_held, rest = call(
        keep_gate_kernel,
        "keep_gate",
        [
            pltpu.VMEM((units_first, width), jnp.bfloat16),
            pltpu.VMEM(out_proj.shape, jnp.bfloat16),
            array(slots, columns, dtype=jnp.float32),
        ],
        [ON_CHIP, IN_HBM, IN_HBM, IN_HBM],
        [pick, in_hbm(residual), in_hbm(gate_weight.swapaxes(1, 2)), in_hbm(out_proj)],
        scratch=[pltpu.VMEM((tokens, columns), jnp.bfloat16), pltpu.SemaphoreType.DMA((3,))],
        moved=units * width,
        limit=2 << 20,
    )
    joined = call(join_kernel, "join", array(half, columns), [ON_CHIP] * 3, [near, across, gate_first])
    other = lax.ppermute(joined, "fsdp", SWAP)
    partial = call(
        project_kernel,
        "project",
        array(4, slots, columns),
        [ON_CHIP] * 3,
        [joined, other, proj_held],
        scratch=[pltpu.VMEM((rows, columns), jnp.bfloat16)],
    )
    sums = [lax.ppermute(partial[v], "tok", crossed(2, v)) for v in (1, 2, 3)]
    gate_second, up_first = keep_on_chip(
        partial,
        [gate_weight.swapaxes(1, 2), up_weight.swapaxes(1, 2)],
        [(units_first, units, 0, width), (0, units // 4, 0, width)],
        "keep_more",
    )
    packed_columns = columns + STAT_COLS
    packed = call(
        norm_kernel,
        "norm",
        array(slots, packed_columns),
        [ON_CHIP] * 9,
        [kind, rest, partial, *sums, norm_gain, router_weight.T, up_first],
    )
    others = [lax.ppermute(packed, "tok", crossed(2, v)) for v in (1, 2, 3)]
    (up_second,) = keep_on_chip(packed, [up_weight.swapaxes(1, 2)], [(units // 4, units, 0, width)], "keep_up")
    kept_slots = 3 * capacity
    own, to_far_rows, to_side_rows, to_corner_rows = call(
        arrange_kernel,
        "arrange",
        [array(kept_slots, packed_columns)] * 4,
        [ON_CHIP] * 5,
        [packed, *others, up_second],
    )
    both_axes = ("groups", "mod")
    side_far = lax.ppermute(to_corner_rows, both_axes, crossed(2, 3))
    far = lax.ppermute(to_far_rows, "groups", SWAP)
    side_own = lax.ppermute(to_side_rows, "mod", SWAP)

    down_units = units // 4 * 3
    (down_first,) = keep_on_chip(own, [down_weight], [(0, down_units, 0, width)], "keep_down")

    flops = 2 * rows * units * width
    gate, gathered = call(
        gate_kernel,
        "gate",
        [array(units + TILE, rows), array(rows, width)],
        [ON_CHIP] * 7,
        [own, far, side_own, side_far, gate_first, gate_second, down_first],
        flops=flops,
    )
    up = call(
        up_kernel, "up", array(units, rows), [ON_CHIP] * 3, [gathered, up_first, up_second], flops=flops
    )
    gate_other = lax.ppermute(gate, "fsdp", SWAP)
    up_other = lax.ppermute(up, "fsdp", SWAP)
    (down_second,) = keep_on_chip(up, [down_weight], [(down_units, units, 0, width)], "keep_last")
    silu, stat = call(
        silu_kernel,
        "silu",
        [array(units, rows, dtype=jnp.float32), array(8, rows, dtype=jnp.float32)],
        [ON_CHIP] * 2,
        [gate, gate_other],
        moved=8 * units * rows,
    )
    kept, to_far, to_side, to_side_far = call(
        down_kernel,
        "down",
        [array(kept_slots, columns)] * 4,
        [ON_CHIP] * 6,
        [silu, stat, up, up_other, down_first, down_second],
        scratch=[pltpu.VMEM((units, rows), jnp.bfloat16)],
        flops=flops,
    )
    from_side_far = lax.ppermute(to_side_far, both_axes, crossed(2, 3))
    from_far = lax.ppermute(to_far, "groups", SWAP)
    from_side = lax.ppermute(to_side, "mod", SWAP)
    merged = call(
        merge_kernel,
        "merge",
        [array(slots, columns)] * 4,
        [ON_CHIP] * 8,
        [packed, *others, kept, from_side, from_far, from_side_far],
    )
    values = [merged[0]] + [lax.ppermute(merged[v], "tok", crossed(2, v)) for v in (1, 2, 3)]
    return call(
        scatter_kernel, "scatter", array(tokens, columns), [ON_CHIP] * 5, [pick, *values]
    )


def solution(mesh):
    placed = (
        P(("groups", "tok"), ("fsdp", "mod")),
        P(("groups", "tok"), ("mod", "fsdp")),
        P("tok", ("fsdp", "mod")),
        P(None, ("fsdp", "mod")),
        P(("fsdp", "mod"), None),
        P(("groups", "tok")),
        P(None, ("groups", "tok")),
        P("mod", "fsdp", "tok"),
        P("mod", "fsdp", "tok"),
        P("mod", "tok", "fsdp"),
    )
    sizes = dict(n_tok=mesh.shape["tok"], n_mod=mesh.shape["mod"], n_fsdp=mesh.shape["fsdp"])
    paired = (
        mesh.shape["groups"] == 2
        and sizes == dict(n_tok=4, n_mod=2, n_fsdp=2)
    )
    body = paired_local if paired else functools.partial(local, **sizes)
    return jax.shard_map(
        body,
        mesh=mesh,
        in_specs=placed,
        out_specs=P(("groups", "tok"), ("fsdp", "mod")),
        check_vma=False,
    )
```

```python
import functools

import jax
import jax.numpy as jnp
from jax import lax
from jax.experimental import pallas as pl
from jax.experimental.pallas import tpu as pltpu
from jax.sharding import PartitionSpec as P

D = 4096
STAT_COLS = 128
FEW = 4


def ring(size, step):
    return [(i, (i + step) % size) for i in range(size)]


def reduce_tok(blocks, n_tok):
    if n_tok > FEW:
        return lax.psum_scatter(blocks, "tok", scatter_dimension=0, tiled=False).astype(jnp.float32)
    own = lax.axis_index("tok")
    total = lax.dynamic_index_in_dim(blocks, own, 0, False).astype(jnp.float32)
    for step in range(1, n_tok):
        sent = lax.dynamic_index_in_dim(blocks, (own + step) % n_tok, 0, False)
        total = total + lax.ppermute(sent, "tok", ring(n_tok, step)).astype(jnp.float32)
    return total


def gather_tok(rows, n_tok):
    if n_tok > FEW:
        return lax.all_gather(rows, "tok", axis=0, tiled=False)
    own = lax.axis_index("tok")
    result = jnp.zeros((n_tok,) + rows.shape, rows.dtype)
    result = lax.dynamic_update_index_in_dim(result, rows, own, 0)
    for step in range(1, n_tok):
        got = lax.ppermute(rows, "tok", ring(n_tok, step))
        result = lax.dynamic_update_index_in_dim(result, got, (own - step) % n_tok, 0)
    return result


def spread_context(rows, n_tok, n_mod, n_fsdp):
    if n_tok > FEW or n_tok != n_mod * n_fsdp:
        full = lax.all_gather(rows, ("mod", "fsdp"), axis=1, tiled=True)
        split = full.reshape(full.shape[0], n_tok, full.shape[1] // n_tok).transpose(1, 0, 2)
        return lax.all_to_all(split, "tok", 0, 0, tiled=True)
    pairs = [(t * n_tok + q, q * n_tok + t) for t in range(n_tok) for q in range(n_tok)]
    swapped = lax.ppermute(rows, ("tok", "mod", "fsdp"), pairs)
    return lax.all_gather(swapped, ("mod", "fsdp"), axis=0, tiled=False)


def local(
    residual,
    context,
    out_proj,
    norm_gain,
    router_weight,
    block_modality,
    expert_rows,
    gate_weight,
    up_weight,
    down_weight,
    *,
    n_tok,
    n_mod,
    n_fsdp,
):
    token_count = residual.shape[0]
    experts, capacity = expert_rows.shape
    kind_experts = experts // 2
    slots = kind_experts * capacity
    local_experts = gate_weight.shape[0]
    columns = residual.shape[1]
    assert block_modality.shape == (1,) and n_mod * local_experts == experts
    modality = block_modality[0]
    first = modality * kind_experts
    mod_index = lax.axis_index("mod")

    own_rows = lax.dynamic_slice_in_dim(expert_rows, first, kind_experts, 0).reshape(slots)
    pick = own_rows[:, None] == lax.iota(jnp.int32, token_count)[None, :]
    pick_half = pick.astype(jnp.bfloat16)
    picked_context = jnp.dot(pick_half, context, preferred_element_type=jnp.float32).astype(jnp.bfloat16)
    picked_residual = jnp.dot(pick_half, residual, preferred_element_type=jnp.float32)

    spread = spread_context(picked_context, n_tok, n_mod, n_fsdp)
    partial = jnp.einsum("tsk,kc->tsc", spread, out_proj, preferred_element_type=jnp.float32)
    hidden = picked_residual + reduce_tok(partial.astype(jnp.bfloat16), n_tok)

    gain_table = norm_gain.astype(jnp.float32)
    gained = hidden * jnp.where(modality == 0, gain_table[0], gain_table[1])[None, :]
    router = lax.dynamic_slice_in_dim(router_weight.astype(jnp.float32), first, kind_experts, 1)
    slot_router = jnp.repeat(router.T, capacity, axis=0)
    squares = jnp.sum(hidden * hidden, axis=1, keepdims=True)
    logits = jnp.sum(gained * slot_router, axis=1, keepdims=True)
    flag = jnp.broadcast_to(modality.astype(jnp.bfloat16), (slots, 1))
    stat_list = []
    for stat in (squares, logits):
        high = lax.reduce_precision(stat, 8, 7)
        stat_list += [high.astype(jnp.bfloat16), (stat - high).astype(jnp.bfloat16)]
    packed = jnp.concatenate(
        [gained.astype(jnp.bfloat16)] + stat_list
        + [flag, jnp.zeros((slots, STAT_COLS - 5), jnp.bfloat16)],
        axis=1,
    )

    everyone = gather_tok(packed, n_tok)
    both = lax.all_gather(everyone, "mod", axis=0, tiled=False)
    kind_first = (mod_index * local_experts) % kind_experts
    both = both.reshape(n_mod, n_tok, kind_experts, capacity, columns + STAT_COLS)
    mine = lax.dynamic_slice_in_dim(both, kind_first, local_experts, 2)
    piece = mine[..., :columns].transpose(2, 1, 3, 0, 4).reshape(
        local_experts, n_tok * capacity, n_mod * columns
    )
    tail = mine[..., columns : columns + 5].astype(jnp.float32)
    half_stats = jnp.sum(
        jnp.stack([tail[..., 0] + tail[..., 1], tail[..., 2] + tail[..., 3]], axis=-1), axis=0
    )
    stats = lax.psum(half_stats, "fsdp")
    flags = tail[0, :, :, :, 4]
    by_expert = stats.transpose(1, 0, 2, 3).reshape(local_experts, n_tok * capacity, 2)
    inverse = lax.rsqrt(by_expert[..., 0:1] / D + 1e-05)
    score = jax.nn.sigmoid(by_expert[..., 1:2] * inverse)

    gate_part = jnp.einsum("esd,edf->esf", piece, gate_weight, preferred_element_type=jnp.float32)
    up_part = jnp.einsum("esd,edf->esf", piece, up_weight, preferred_element_type=jnp.float32)
    gate_half = gate_part.astype(jnp.bfloat16)
    up_half = up_part.astype(jnp.bfloat16)
    if n_fsdp == 2:
        swap = [(0, 1), (1, 0)]
        gate_sum = gate_half.astype(jnp.float32) + lax.ppermute(gate_half, "fsdp", swap).astype(jnp.float32)
        up_sum = up_half.astype(jnp.float32) + lax.ppermute(up_half, "fsdp", swap).astype(jnp.float32)
    else:
        gate_sum = lax.psum(gate_half, "fsdp").astype(jnp.float32)
        up_sum = lax.psum(up_half, "fsdp").astype(jnp.float32)
    activation = (jax.nn.silu(gate_sum * inverse) * (up_sum * inverse)).astype(jnp.bfloat16)
    value = jnp.einsum("esf,efd->esd", activation, down_weight, preferred_element_type=jnp.float32)
    value = (value * score).astype(jnp.bfloat16)
    value = value.reshape(local_experts, n_tok, capacity, n_mod * columns).transpose(1, 0, 2, 3)

    own_kind = (mod_index * local_experts) // kind_experts
    valid = (flags == own_kind.astype(jnp.float32))[..., None]
    if n_mod == 2:
        value = value.reshape(n_tok, local_experts, capacity, n_mod, columns)
        kept = lax.dynamic_index_in_dim(value, mod_index, 3, False)
        sent = lax.dynamic_index_in_dim(value, 1 - mod_index, 3, False)
        got = lax.ppermute(sent, "mod", [(0, 1), (1, 0)])
        merged = jnp.where(valid, kept, got).reshape(n_tok, slots, columns)
    else:
        value = jnp.where(valid, value, jnp.zeros((), jnp.bfloat16))
        wide = jnp.zeros((n_tok, kind_experts, capacity, n_mod * columns), jnp.bfloat16)
        wide = lax.dynamic_update_slice_in_dim(wide, value, kind_first, 1)
        wide = wide.reshape(n_tok, slots, n_mod * columns)
        merged = lax.psum_scatter(wide, "mod", scatter_dimension=2, tiled=True)
    summed = reduce_tok(merged, n_tok)
    return jnp.dot(
        pick.astype(jnp.float32).T, summed, precision=lax.Precision.HIGHEST
    ).astype(jnp.bfloat16)


SWAP = [(0, 1), (1, 0)]
STRIP = 688
TILE = 16
ON_CHIP = pl.BlockSpec(memory_space=pltpu.VMEM)
IN_HBM = pl.BlockSpec(memory_space=pltpu.HBM)
ANYWHERE = pl.BlockSpec(memory_space=pl.ANY)


def crossed(bits, flip):
    return [(i, i ^ flip) for i in range(1 << bits)]


def call(kernel, name, outs, specs, args, scratch=(), flops=0, moved=0, limit=8 << 20):
    return pl.pallas_call(
        kernel,
        out_shape=outs,
        in_specs=specs,
        out_specs=jax.tree.map(lambda _: ON_CHIP, outs),
        scratch_shapes=list(scratch),
        compiler_params=pltpu.CompilerParams(vmem_limit_bytes=limit),
        cost_estimate=pl.CostEstimate(flops=flops, transcendentals=0, bytes_accessed=moved),
        name=name,
    )(*args)


def array(*shape, dtype=jnp.bfloat16):
    return jax.ShapeDtypeStruct(shape, dtype)


def keep_kernel(spans, after_ref, *refs):
    count = len(spans)
    weights, held, semaphores = refs[:count], refs[count : 2 * count], refs[-1]
    copies = [
        pltpu.make_async_copy(weight.at[lax.axis_index("groups"), a:b], to, semaphores.at[n])
        for n, (weight, to, (a, b)) in enumerate(zip(weights, held, spans))
    ]
    for copy in copies:
        copy.start()
    for copy in copies:
        copy.wait()


def in_hbm(value):
    return pltpu.with_memory_space_constraint(value, pltpu.HBM)


def keep_on_chip(after, weights, spans, name):
    return call(
        functools.partial(keep_kernel, spans),
        name,
        [pltpu.VMEM((b - a, weight.shape[2]), jnp.bfloat16) for weight, (a, b) in zip(weights, spans)],
        [ANYWHERE] + [IN_HBM] * len(spans),
        [after] + [in_hbm(weight) for weight in weights],
        scratch=[pltpu.SemaphoreType.DMA((len(spans),))],
        moved=sum(2 * (b - a) * weight.shape[2] for weight, (a, b) in zip(weights, spans)),
        limit=1 << 20,
    )


def select_kernel(
    rows_hbm, context_hbm, picked_ref, pick_ref, kind_ref, rows_ref, context_ref, semaphores
):
    rows_copy = pltpu.make_async_copy(rows_hbm, rows_ref, semaphores.at[0])
    context_copy = pltpu.make_async_copy(context_hbm, context_ref, semaphores.at[1])
    rows_copy.start()
    context_copy.start()
    rows_copy.wait()
    kind = jnp.where(jnp.maximum(rows_ref[2, 0], rows_ref[3, 0]) >= 0, 1, 0)
    kind_ref[...] = jnp.full(kind_ref.shape, kind, jnp.int32).astype(jnp.float32)
    capacity = rows_ref.shape[1]
    slots, tokens = pick_ref.shape
    row = lax.broadcasted_iota(jnp.int32, (slots, tokens), 0)
    token = lax.broadcasted_iota(jnp.int32, (slots, tokens), 1)
    wanted = jnp.full((slots, tokens), -1, jnp.int32)
    for e in range(2):
        expert = 2 * kind + (lax.axis_index("groups") ^ e)
        for s in range(capacity):
            wanted = jnp.where(row == e * capacity + s, rows_ref[expert, s], wanted)
    pick = jnp.where(wanted == token, 1.0, 0.0).astype(jnp.bfloat16)
    pick_ref[...] = pick
    context_copy.wait()
    picked_ref[...] = jnp.dot(pick, context_ref[...], preferred_element_type=jnp.float32).astype(jnp.bfloat16)


def keep_gate_kernel(
    pick_ref, residual_hbm, gate_ref, proj_ref, gate_held, proj_held, rest_ref, residual_ref, semaphores
):
    copies = [
        pltpu.make_async_copy(residual_hbm, residual_ref, semaphores.at[0]),
        pltpu.make_async_copy(proj_ref, proj_held, semaphores.at[1]),
        pltpu.make_async_copy(gate_ref.at[lax.axis_index("groups"), : gate_held.shape[0]], gate_held, semaphores.at[2]),
    ]
    for copy in copies:
        copy.start()
    copies[0].wait()
    rest_ref[...] = jnp.dot(pick_ref[...], residual_ref[...], preferred_element_type=jnp.float32)
    for copy in copies[1:]:
        copy.wait()


def join_kernel(across_ref, near_ref, _, out_ref):
    slots = near_ref.shape[0]
    out_ref[:slots, :] = near_ref[...]
    out_ref[slots:, :] = across_ref[...]


def project_kernel(joined_ref, other_ref, weight_ref, out_ref, rows_ref):
    pair = joined_ref.shape[0]
    slots = pair // 2
    rows_ref[:pair, :] = joined_ref[...]
    rows_ref[pair:, :] = other_ref[...]
    product = jnp.dot(rows_ref[...], weight_ref[...], preferred_element_type=jnp.float32)
    product = product.astype(jnp.bfloat16)
    corner = 2 * lax.axis_index("mod") + lax.axis_index("fsdp")
    flip = lax.axis_index("tok") ^ corner
    for n, u in enumerate((0, 2, 1, 3)):
        out_ref[flip ^ u] = product[n * slots : (n + 1) * slots, :]


def split_high_low(value):
    high = value.astype(jnp.bfloat16).astype(jnp.float32)
    return high, value - high


def norm_kernel(kind_ref, rest_ref, partial_ref, three_ref, two_ref, one_ref, gain_ref, router_ref, _, out_ref):
    slots, columns = rest_ref.shape
    hidden = rest_ref[...] + partial_ref[0].astype(jnp.float32)
    for got_ref in (three_ref, two_ref, one_ref):
        hidden = hidden + got_ref[...].astype(jnp.float32)
    kind = kind_ref[0:1, 0:1]
    gains = gain_ref[...].astype(jnp.float32)
    gained = hidden * jnp.where(kind == 0.0, gains[0:1], gains[1:2])
    out_ref[:, :columns] = gained.astype(jnp.bfloat16)
    table = router_ref[...].astype(jnp.float32)
    pieces = []
    for e in range(2):
        second = (lax.axis_index("groups") ^ e) == 1
        text = jnp.where(second, table[1:2], table[0:1])
        image = jnp.where(second, table[3:4], table[2:3])
        weights = jnp.where(kind == 0.0, text, image)
        half = slots // 2
        pieces.append(jnp.sum(gained[e * half : (e + 1) * half] * weights, axis=1, keepdims=True))
    logits = jnp.concatenate(pieces, axis=0)
    squares = jnp.sum(hidden * hidden, axis=1, keepdims=True)
    lane = lax.broadcasted_iota(jnp.int32, (slots, STAT_COLS), 1)
    extra = jnp.where(lane == 4, kind, 0.0)
    for at, stat in enumerate(split_high_low(squares) + split_high_low(logits)):
        extra = jnp.where(lane == at, stat, extra)
    out_ref[:, columns:] = extra.astype(jnp.bfloat16)


def places(packed_refs, columns):
    side = lax.axis_index("mod")
    matches, found, before = [], [], 0
    for v, ref in enumerate(packed_refs):
        flag = ref[:TILE, columns:].astype(jnp.float32)[0, 4]
        kind = jnp.where(flag > 0.5, 1, 0)
        match = kind == side
        place = jnp.minimum(jnp.where(match, before, v - before), len(packed_refs) - 2)
        matches.append(match)
        found.append(place)
        before = before + jnp.where(match, 1, 0)
    return matches, found


def arrange_kernel(zero_ref, three_ref, two_ref, one_ref, _, *out_refs):
    packed_refs = (zero_ref, one_ref, two_ref, three_ref)
    capacity = zero_ref.shape[0] // 2
    for out_ref in out_refs:
        out_ref[...] = jnp.zeros(out_ref.shape, out_ref.dtype)
    matches, found = places(packed_refs, zero_ref.shape[1] - STAT_COLS)
    for ref, match, place in zip(packed_refs, matches, found):
        span = pl.ds(pl.multiple_of(place * capacity, capacity), capacity)
        for wanted, (own_ref, given_ref) in ((True, out_refs[:2]), (False, out_refs[2:])):

            @pl.when(match == wanted)
            def _():
                own_ref[span, :] = ref[:capacity, :]
                given_ref[span, :] = ref[capacity:, :]


def weights_times_rows(weight_refs, spans, rows, out_ref):
    at = 0
    for weight_ref, (first, last) in zip(weight_refs, spans):
        for start in range(first, last, STRIP):
            stop = min(start + STRIP, last)
            out_ref[at : at + stop - start, :] = lax.dot_general(
                weight_ref[start:stop, :], rows, (((1,), (1,)), ((), ())), preferred_element_type=jnp.float32
            ).astype(jnp.bfloat16)
            at += stop - start


def gate_kernel(own_ref, far_ref, side_own_ref, side_far_ref, *refs):
    weight_refs, out_ref, rows_ref = refs[:2], refs[-2], refs[-1]
    half = own_ref.shape[0]
    rows = rows_ref.shape[0]
    units = out_ref.shape[0] - TILE
    columns = rows_ref.shape[1] // 2
    rows_ref[2 * half :, :] = jnp.zeros((rows - 2 * half, 2 * columns), rows_ref.dtype)
    for side in range(2):

        @pl.when(lax.axis_index("mod") == side)
        def _():
            here, there = side * columns, (1 - side) * columns
            rows_ref[:half, here : here + columns] = own_ref[:, :columns]
            rows_ref[half : 2 * half, here : here + columns] = far_ref[:, :columns]
            rows_ref[:half, there : there + columns] = side_own_ref[:, :columns]
            rows_ref[half : 2 * half, there : there + columns] = side_far_ref[:, :columns]

    spans = [(0, ref.shape[0]) for ref in weight_refs]
    weights_times_rows(weight_refs, spans, rows_ref[...], out_ref)
    tails = [ref[:, columns:].astype(jnp.float32) for ref in (own_ref, side_own_ref, far_ref, side_far_ref)]
    unused = jnp.zeros((rows - 2 * half, STAT_COLS), jnp.float32)
    stat = jnp.concatenate([tails[0] + tails[1], tails[2] + tails[3], unused], axis=0).T
    squares = stat[0:1] + stat[1:2]
    logits = stat[2:3] + stat[3:4]
    at_row = lax.broadcasted_iota(jnp.int32, (TILE, rows), 0)
    extra = jnp.zeros((TILE, rows), jnp.float32)
    for at, piece in enumerate(split_high_low(squares) + split_high_low(logits)):
        extra = jnp.where(at_row == at, piece, extra)
    out_ref[units:, :] = extra.astype(jnp.bfloat16)


def up_kernel(spans, rows_ref, *refs):
    weights_times_rows(refs[:-1], spans, rows_ref[...], refs[-1])


def silu_kernel(gate_ref, gate_other_ref, out_ref, stat_ref):
    units = out_ref.shape[0]
    stat = gate_ref[units:, :].astype(jnp.float32) + gate_other_ref[units:, :].astype(jnp.float32)
    inverse = lax.rsqrt((stat[0:1] + stat[1:2]) / D + 1e-05)
    logits = (stat[2:3] + stat[3:4]) * inverse
    score = 1.0 / (1.0 + jnp.exp(-logits))
    at_row = lax.broadcasted_iota(jnp.int32, stat_ref.shape, 0)
    stat_ref[...] = jnp.where(at_row == 0, inverse, score)
    for start in range(0, units, STRIP):
        stop = min(start + STRIP, units)
        gate = gate_ref[start:stop, :].astype(jnp.float32) + gate_other_ref[start:stop, :].astype(jnp.float32)
        gate = gate * inverse
        out_ref[start:stop, :] = gate / (1.0 + jnp.exp(-gate)) * inverse


def down_kernel(
    silu_ref, stat_ref, up_ref, up_late_ref, other_ref, other_late_ref, first_ref, second_ref,
    kept_ref, far_ref, side_ref, side_far_ref, act_ref,
):
    units, rows = act_ref.shape
    at = 0
    for mine_ref, got_ref in ((up_ref, other_ref), (up_late_ref, other_late_ref)):
        for start in range(0, mine_ref.shape[0], STRIP):
            stop = min(start + STRIP, mine_ref.shape[0])
            up = mine_ref[start:stop, :].astype(jnp.float32) + got_ref[start:stop, :].astype(jnp.float32)
            span = slice(at, at + stop - start)
            act_ref[span, :] = (silu_ref[span, :] * up).astype(jnp.bfloat16)
            at += stop - start
    half, columns = kept_ref.shape
    score = jnp.broadcast_to(stat_ref[1:2, :], (rows, rows)).T[:, 0:1]
    first_units = first_ref.shape[0]
    for quarter in range(2):
        span = slice(quarter * columns, (quarter + 1) * columns)
        value = sum(
            lax.dot_general(
                act_ref[a:b, :], weight_ref[:, span], (((0,), (0,)), ((), ())), preferred_element_type=jnp.float32
            )
            for a, b, weight_ref in ((0, first_units, first_ref), (first_units, units, second_ref))
        )
        value = (value * score).astype(jnp.bfloat16)
        for across, (own_out, far_out) in enumerate(((kept_ref, far_ref), (side_ref, side_far_ref))):

            @pl.when((lax.axis_index("mod") ^ quarter) == across)
            def _():
                own_out[...] = value[:half]
                far_out[...] = value[half : 2 * half]


def merge_kernel(zero_ref, one_ref, two_ref, three_ref, kept_ref, side_ref, far_ref, side_far_ref, *out_refs):
    columns = kept_ref.shape[1]
    capacity = zero_ref.shape[0] // 2
    matches, found = places((zero_ref, one_ref, two_ref, three_ref), columns)
    for out_ref, match, place in zip(out_refs, matches, found):
        span = pl.ds(pl.multiple_of(place * capacity, capacity), capacity)
        for wanted, (first_ref, second_ref) in ((True, (kept_ref, far_ref)), (False, (side_ref, side_far_ref))):

            @pl.when(match == wanted)
            def _():
                out_ref[:capacity, :] = first_ref[span, :]
                out_ref[capacity:, :] = second_ref[span, :]


def scatter_kernel(pick_ref, zero_ref, one_ref, two_ref, three_ref, out_ref):
    total = zero_ref[...].astype(jnp.float32)
    for got_ref in (three_ref, two_ref, one_ref):
        total = total + got_ref[...].astype(jnp.float32)
    result = 0.0
    for piece in split_high_low(total)[::-1]:
        result = result + lax.dot_general(
            pick_ref[...], piece.astype(jnp.bfloat16), (((0,), (0,)), ((), ())),
            preferred_element_type=jnp.float32,
        )
    out_ref[...] = result.astype(jnp.bfloat16)


def paired_local(
    residual,
    context,
    out_proj,
    norm_gain,
    router_weight,
    block_modality,
    expert_rows,
    gate_weight,
    up_weight,
    down_weight,
):
    tokens, columns = residual.shape
    experts, capacity = expert_rows.shape
    slots = 2 * capacity
    half = 4 * capacity
    rows = 2 * half
    units, width = down_weight.shape[1:]
    assert block_modality.shape == (1,) and experts == 4 and gate_weight.shape[0] == 2
    picked, pick, kind = call(
        select_kernel,
        "select",
        [array(slots, columns), array(slots, tokens), array(8, STAT_COLS, dtype=jnp.float32)],
        [IN_HBM] * 2,
        [in_hbm(expert_rows), in_hbm(context)],
        scratch=[
            pltpu.SMEM((experts, capacity), jnp.int32),
            pltpu.VMEM((tokens, columns), jnp.bfloat16),
            pltpu.SemaphoreType.DMA((2,)),
        ],
    )
    plane = ("tok", "mod", "fsdp")
    to_first = [(t * 4 + q, q * 4 + t) for t in range(4) for q in range(4)]
    to_second = [(t * 4 + q, q * 4 + (t ^ 2)) for t in range(4) for q in range(4)]
    across = lax.ppermute(picked, plane, to_second)
    near = lax.ppermute(picked, plane, to_first)
    gate_units, up_units, down_units = [round(units * part / TILE) * TILE for part in (0.58, 0.41, 0.24)]
    gate_first, proj_held, rest = call(
        keep_gate_kernel,
        "keep_gate",
        [
            pltpu.VMEM((gate_units, width), jnp.bfloat16),
            pltpu.VMEM(out_proj.shape, jnp.bfloat16),
            array(slots, columns, dtype=jnp.float32),
        ],
        [ON_CHIP, IN_HBM, IN_HBM, IN_HBM],
        [pick, in_hbm(residual), in_hbm(gate_weight.swapaxes(1, 2)), in_hbm(out_proj)],
        scratch=[pltpu.VMEM((tokens, columns), jnp.bfloat16), pltpu.SemaphoreType.DMA((3,))],
        moved=units * width,
        limit=2 << 20,
    )
    joined = call(join_kernel, "join", array(half, columns), [ON_CHIP] * 3, [across, near, gate_first])
    other = lax.ppermute(joined, "fsdp", SWAP)
    partial = call(
        project_kernel,
        "project",
        array(4, slots, columns),
        [ON_CHIP] * 3,
        [joined, other, proj_held],
        scratch=[pltpu.VMEM((rows, columns), jnp.bfloat16)],
    )
    sums = [lax.ppermute(partial[v], "tok", crossed(2, v)) for v in (3, 2, 1)][::-1]
    gate_second, up_first = keep_on_chip(
        partial,
        [gate_weight.swapaxes(1, 2), up_weight.swapaxes(1, 2)],
        [(gate_units, units), (0, up_units)],
        "keep_more",
    )
    packed_columns = columns + STAT_COLS
    packed = call(
        norm_kernel,
        "norm",
        array(slots, packed_columns),
        [ON_CHIP] * 9,
        [kind, rest, partial, *sums[::-1], norm_gain, router_weight.T, up_first],
    )
    others = [lax.ppermute(packed, "tok", crossed(2, v)) for v in (3, 2, 1)][::-1]
    up_second, down_first = keep_on_chip(
        packed,
        [up_weight.swapaxes(1, 2), down_weight],
        [(up_units, units), (0, down_units)],
        "keep_up",
    )
    kept_slots = 3 * capacity
    own, to_far_rows, to_side_rows, to_corner_rows = call(
        arrange_kernel,
        "arrange",
        [array(kept_slots, packed_columns)] * 4,
        [ON_CHIP] * 5,
        [packed, *others[::-1], up_second],
    )
    both_axes = ("groups", "mod")
    side_far = lax.ppermute(to_corner_rows, both_axes, crossed(2, 3))
    far = lax.ppermute(to_far_rows, "groups", SWAP)
    side_own = lax.ppermute(to_side_rows, "mod", SWAP)

    (down_second,) = keep_on_chip(own, [down_weight], [(down_units, units)], "keep_down")

    flops = 2 * rows * units * width
    gate, gathered = call(
        gate_kernel,
        "gate",
        [array(units + TILE, rows), array(rows, width)],
        [ON_CHIP] * 7,
        [own, far, side_own, side_far, gate_first, gate_second, down_second],
        flops=flops,
    )
    late = units // 4 // TILE * TILE
    up_rest = units - up_units
    up_parts = [
        call(
            functools.partial(up_kernel, spans),
            "up",
            array(sum(b - a for a, b in spans), rows),
            [ON_CHIP] * (1 + len(spans)),
            [gathered, *weights],
            flops=flops * sum(b - a for a, b in spans) // units,
        )
        for spans, weights in (
            (((0, up_units), (0, up_rest - late)), (up_first, up_second)),
            (((up_rest - late, up_rest),), (up_second,)),
        )
    ]
    gate_other = lax.ppermute(gate, "fsdp", SWAP)
    up_others = [lax.ppermute(part, "fsdp", SWAP) for part in up_parts]
    silu, stat = call(
        silu_kernel,
        "silu",
        [array(units, rows, dtype=jnp.float32), array(8, rows, dtype=jnp.float32)],
        [ON_CHIP] * 2,
        [gate, gate_other],
        moved=8 * units * rows,
    )
    kept, to_far, to_side, to_side_far = call(
        down_kernel,
        "down",
        [array(kept_slots, columns)] * 4,
        [ON_CHIP] * 8,
        [silu, stat, *up_parts, *up_others, down_first, down_second],
        scratch=[pltpu.VMEM((units, rows), jnp.bfloat16)],
        flops=flops,
    )
    from_side_far = lax.ppermute(to_side_far, both_axes, crossed(2, 3))
    from_far = lax.ppermute(to_far, "groups", SWAP)
    from_side = lax.ppermute(to_side, "mod", SWAP)
    merged = call(
        merge_kernel,
        "merge",
        [array(slots, columns)] * 4,
        [ON_CHIP] * 8,
        [packed, *others, kept, from_side, from_far, from_side_far],
    )
    values = [merged[0]] + [lax.ppermute(merged[v], "tok", crossed(2, v)) for v in (1, 2, 3)]
    return call(
        scatter_kernel, "scatter", array(tokens, columns), [ON_CHIP] * 5, [pick, *values]
    )


def solution(mesh):
    placed = (
        P(("groups", "tok"), ("fsdp", "mod")),
        P(("groups", "tok"), ("mod", "fsdp")),
        P("tok", ("fsdp", "mod")),
        P(None, ("fsdp", "mod")),
        P(("fsdp", "mod"), None),
        P(("groups", "tok")),
        P(None, ("groups", "tok")),
        P("mod", "fsdp", "tok"),
        P("mod", "fsdp", "tok"),
        P("mod", "tok", "fsdp"),
    )
    sizes = dict(n_tok=mesh.shape["tok"], n_mod=mesh.shape["mod"], n_fsdp=mesh.shape["fsdp"])
    paired = (
        mesh.shape["groups"] == 2
        and sizes == dict(n_tok=4, n_mod=2, n_fsdp=2)
    )
    body = paired_local if paired else functools.partial(local, **sizes)
    return jax.shard_map(
        body,
        mesh=mesh,
        in_specs=placed,
        out_specs=P(("groups", "tok"), ("fsdp", "mod")),
        check_vma=False,
    )
```

```python
import functools

import jax
import jax.numpy as jnp
from jax import lax
from jax.experimental import pallas as pl
from jax.experimental.pallas import tpu as pltpu
from jax.sharding import PartitionSpec as P

D = 4096
STAT_COLS = 128
FEW = 4


def ring(size, step):
    return [(i, (i + step) % size) for i in range(size)]


def reduce_tok(blocks, n_tok):
    if n_tok > FEW:
        return lax.psum_scatter(blocks, "tok", scatter_dimension=0, tiled=False).astype(jnp.float32)
    own = lax.axis_index("tok")
    total = lax.dynamic_index_in_dim(blocks, own, 0, False).astype(jnp.float32)
    for step in range(1, n_tok):
        sent = lax.dynamic_index_in_dim(blocks, (own + step) % n_tok, 0, False)
        total = total + lax.ppermute(sent, "tok", ring(n_tok, step)).astype(jnp.float32)
    return total


def gather_tok(rows, n_tok):
    if n_tok > FEW:
        return lax.all_gather(rows, "tok", axis=0, tiled=False)
    own = lax.axis_index("tok")
    result = jnp.zeros((n_tok,) + rows.shape, rows.dtype)
    result = lax.dynamic_update_index_in_dim(result, rows, own, 0)
    for step in range(1, n_tok):
        got = lax.ppermute(rows, "tok", ring(n_tok, step))
        result = lax.dynamic_update_index_in_dim(result, got, (own - step) % n_tok, 0)
    return result


def spread_context(rows, n_tok, n_mod, n_fsdp):
    if n_tok > FEW or n_tok != n_mod * n_fsdp:
        full = lax.all_gather(rows, ("mod", "fsdp"), axis=1, tiled=True)
        split = full.reshape(full.shape[0], n_tok, full.shape[1] // n_tok).transpose(1, 0, 2)
        return lax.all_to_all(split, "tok", 0, 0, tiled=True)
    pairs = [(t * n_tok + q, q * n_tok + t) for t in range(n_tok) for q in range(n_tok)]
    swapped = lax.ppermute(rows, ("tok", "mod", "fsdp"), pairs)
    return lax.all_gather(swapped, ("mod", "fsdp"), axis=0, tiled=False)


def local(
    residual,
    context,
    out_proj,
    norm_gain,
    router_weight,
    block_modality,
    expert_rows,
    gate_weight,
    up_weight,
    down_weight,
    *,
    n_tok,
    n_mod,
    n_fsdp,
):
    token_count = residual.shape[0]
    experts, capacity = expert_rows.shape
    kind_experts = experts // 2
    slots = kind_experts * capacity
    local_experts = gate_weight.shape[0]
    columns = residual.shape[1]
    assert block_modality.shape == (1,) and n_mod * local_experts == experts
    modality = block_modality[0]
    first = modality * kind_experts
    mod_index = lax.axis_index("mod")

    own_rows = lax.dynamic_slice_in_dim(expert_rows, first, kind_experts, 0).reshape(slots)
    pick = own_rows[:, None] == lax.iota(jnp.int32, token_count)[None, :]
    pick_half = pick.astype(jnp.bfloat16)
    picked_context = jnp.dot(pick_half, context, preferred_element_type=jnp.float32).astype(jnp.bfloat16)
    picked_residual = jnp.dot(pick_half, residual, preferred_element_type=jnp.float32)

    spread = spread_context(picked_context, n_tok, n_mod, n_fsdp)
    partial = jnp.einsum("tsk,kc->tsc", spread, out_proj, preferred_element_type=jnp.float32)
    hidden = picked_residual + reduce_tok(partial.astype(jnp.bfloat16), n_tok)

    gain_table = norm_gain.astype(jnp.float32)
    gained = hidden * jnp.where(modality == 0, gain_table[0], gain_table[1])[None, :]
    router = lax.dynamic_slice_in_dim(router_weight.astype(jnp.float32), first, kind_experts, 1)
    slot_router = jnp.repeat(router.T, capacity, axis=0)
    squares = jnp.sum(hidden * hidden, axis=1, keepdims=True)
    logits = jnp.sum(gained * slot_router, axis=1, keepdims=True)
    flag = jnp.broadcast_to(modality.astype(jnp.bfloat16), (slots, 1))
    stat_list = []
    for stat in (squares, logits):
        high = lax.reduce_precision(stat, 8, 7)
        stat_list += [high.astype(jnp.bfloat16), (stat - high).astype(jnp.bfloat16)]
    packed = jnp.concatenate(
        [gained.astype(jnp.bfloat16)] + stat_list
        + [flag, jnp.zeros((slots, STAT_COLS - 5), jnp.bfloat16)],
        axis=1,
    )

    everyone = gather_tok(packed, n_tok)
    both = lax.all_gather(everyone, "mod", axis=0, tiled=False)
    kind_first = (mod_index * local_experts) % kind_experts
    both = both.reshape(n_mod, n_tok, kind_experts, capacity, columns + STAT_COLS)
    mine = lax.dynamic_slice_in_dim(both, kind_first, local_experts, 2)
    piece = mine[..., :columns].transpose(2, 1, 3, 0, 4).reshape(
        local_experts, n_tok * capacity, n_mod * columns
    )
    tail = mine[..., columns : columns + 5].astype(jnp.float32)
    half_stats = jnp.sum(
        jnp.stack([tail[..., 0] + tail[..., 1], tail[..., 2] + tail[..., 3]], axis=-1), axis=0
    )
    stats = lax.psum(half_stats, "fsdp")
    flags = tail[0, :, :, :, 4]
    by_expert = stats.transpose(1, 0, 2, 3).reshape(local_experts, n_tok * capacity, 2)
    inverse = lax.rsqrt(by_expert[..., 0:1] / D + 1e-05)
    score = jax.nn.sigmoid(by_expert[..., 1:2] * inverse)

    gate_part = jnp.einsum("esd,edf->esf", piece, gate_weight, preferred_element_type=jnp.float32)
    up_part = jnp.einsum("esd,edf->esf", piece, up_weight, preferred_element_type=jnp.float32)
    gate_half = gate_part.astype(jnp.bfloat16)
    up_half = up_part.astype(jnp.bfloat16)
    if n_fsdp == 2:
        swap = [(0, 1), (1, 0)]
        gate_sum = gate_half.astype(jnp.float32) + lax.ppermute(gate_half, "fsdp", swap).astype(jnp.float32)
        up_sum = up_half.astype(jnp.float32) + lax.ppermute(up_half, "fsdp", swap).astype(jnp.float32)
    else:
        gate_sum = lax.psum(gate_half, "fsdp").astype(jnp.float32)
        up_sum = lax.psum(up_half, "fsdp").astype(jnp.float32)
    activation = (jax.nn.silu(gate_sum * inverse) * (up_sum * inverse)).astype(jnp.bfloat16)
    value = jnp.einsum("esf,efd->esd", activation, down_weight, preferred_element_type=jnp.float32)
    value = (value * score).astype(jnp.bfloat16)
    value = value.reshape(local_experts, n_tok, capacity, n_mod * columns).transpose(1, 0, 2, 3)

    own_kind = (mod_index * local_experts) // kind_experts
    valid = (flags == own_kind.astype(jnp.float32))[..., None]
    if n_mod == 2:
        value = value.reshape(n_tok, local_experts, capacity, n_mod, columns)
        kept = lax.dynamic_index_in_dim(value, mod_index, 3, False)
        sent = lax.dynamic_index_in_dim(value, 1 - mod_index, 3, False)
        got = lax.ppermute(sent, "mod", [(0, 1), (1, 0)])
        merged = jnp.where(valid, kept, got).reshape(n_tok, slots, columns)
    else:
        value = jnp.where(valid, value, jnp.zeros((), jnp.bfloat16))
        wide = jnp.zeros((n_tok, kind_experts, capacity, n_mod * columns), jnp.bfloat16)
        wide = lax.dynamic_update_slice_in_dim(wide, value, kind_first, 1)
        wide = wide.reshape(n_tok, slots, n_mod * columns)
        merged = lax.psum_scatter(wide, "mod", scatter_dimension=2, tiled=True)
    summed = reduce_tok(merged, n_tok)
    return jnp.dot(
        pick.astype(jnp.float32).T, summed, precision=lax.Precision.HIGHEST
    ).astype(jnp.bfloat16)


SWAP = [(0, 1), (1, 0)]
STRIP = 688
TILE = 16
ON_CHIP = pl.BlockSpec(memory_space=pltpu.VMEM)
IN_HBM = pl.BlockSpec(memory_space=pltpu.HBM)
ANYWHERE = pl.BlockSpec(memory_space=pl.ANY)


def crossed(bits, flip):
    return [(i, i ^ flip) for i in range(1 << bits)]


def call(kernel, name, outs, specs, args, scratch=(), flops=0, moved=0, limit=8 << 20):
    return pl.pallas_call(
        kernel,
        out_shape=outs,
        in_specs=specs,
        out_specs=jax.tree.map(lambda _: ON_CHIP, outs),
        scratch_shapes=list(scratch),
        compiler_params=pltpu.CompilerParams(vmem_limit_bytes=limit),
        cost_estimate=pl.CostEstimate(flops=flops, transcendentals=0, bytes_accessed=moved),
        name=name,
    )(*args)


def array(*shape, dtype=jnp.bfloat16):
    return jax.ShapeDtypeStruct(shape, dtype)


def keep_kernel(spans, after_ref, *refs):
    count = len(spans)
    weights, held, semaphores = refs[:count], refs[count : 2 * count], refs[-1]
    copies = [
        pltpu.make_async_copy(weight.at[lax.axis_index("groups"), a:b], to, semaphores.at[n])
        for n, (weight, to, (a, b)) in enumerate(zip(weights, held, spans))
    ]
    for copy in copies:
        copy.start()
    for copy in copies:
        copy.wait()


def in_hbm(value):
    return pltpu.with_memory_space_constraint(value, pltpu.HBM)


def keep_on_chip(after, weights, spans, name):
    return call(
        functools.partial(keep_kernel, spans),
        name,
        [pltpu.VMEM((b - a, weight.shape[2]), jnp.bfloat16) for weight, (a, b) in zip(weights, spans)],
        [ANYWHERE] + [IN_HBM] * len(spans),
        [after] + [in_hbm(weight) for weight in weights],
        scratch=[pltpu.SemaphoreType.DMA((len(spans),))],
        moved=sum(2 * (b - a) * weight.shape[2] for weight, (a, b) in zip(weights, spans)),
        limit=1 << 20,
    )


def select_kernel(
    rows_hbm, context_hbm, picked_ref, pick_ref, kind_ref, rows_ref, context_ref, semaphores
):
    rows_copy = pltpu.make_async_copy(rows_hbm, rows_ref, semaphores.at[0])
    context_copy = pltpu.make_async_copy(context_hbm, context_ref, semaphores.at[1])
    rows_copy.start()
    context_copy.start()
    rows_copy.wait()
    kind = jnp.where(jnp.maximum(rows_ref[2, 0], rows_ref[3, 0]) >= 0, 1, 0)
    kind_ref[...] = jnp.full(kind_ref.shape, kind, jnp.int32).astype(jnp.float32)
    capacity = rows_ref.shape[1]
    slots, tokens = pick_ref.shape
    row = lax.broadcasted_iota(jnp.int32, (slots, tokens), 0)
    token = lax.broadcasted_iota(jnp.int32, (slots, tokens), 1)
    wanted = jnp.full((slots, tokens), -1, jnp.int32)
    for e in range(2):
        expert = 2 * kind + (lax.axis_index("groups") ^ e)
        for s in range(capacity):
            wanted = jnp.where(row == e * capacity + s, rows_ref[expert, s], wanted)
    pick = jnp.where(wanted == token, 1.0, 0.0).astype(jnp.bfloat16)
    pick_ref[...] = pick
    context_copy.wait()
    picked_ref[...] = jnp.dot(pick, context_ref[...], preferred_element_type=jnp.float32).astype(jnp.bfloat16)


def keep_gate_kernel(
    pick_ref, residual_hbm, gate_ref, proj_ref, gate_held, proj_held, rest_ref, residual_ref, semaphores
):
    copies = [
        pltpu.make_async_copy(residual_hbm, residual_ref, semaphores.at[0]),
        pltpu.make_async_copy(proj_ref, proj_held, semaphores.at[1]),
        pltpu.make_async_copy(gate_ref.at[lax.axis_index("groups"), : gate_held.shape[0]], gate_held, semaphores.at[2]),
    ]
    for copy in copies:
        copy.start()
    copies[0].wait()
    rest_ref[...] = jnp.dot(pick_ref[...], residual_ref[...], preferred_element_type=jnp.float32)
    for copy in copies[1:]:
        copy.wait()


def join_kernel(near_ref, across_ref, _, out_ref):
    slots = near_ref.shape[0]
    out_ref[:slots, :] = near_ref[...]
    out_ref[slots:, :] = across_ref[...]


def project_kernel(joined_ref, other_ref, weight_ref, out_ref, rows_ref):
    pair = joined_ref.shape[0]
    slots = pair // 2
    rows_ref[:pair, :] = joined_ref[...]
    rows_ref[pair:, :] = other_ref[...]
    product = jnp.dot(rows_ref[...], weight_ref[...], preferred_element_type=jnp.float32)
    product = product.astype(jnp.bfloat16)
    corner = 2 * lax.axis_index("mod") + lax.axis_index("fsdp")
    flip = lax.axis_index("tok") ^ corner
    for n, u in enumerate((0, 2, 1, 3)):
        out_ref[flip ^ u] = product[n * slots : (n + 1) * slots, :]


def split_high_low(value):
    high = value.astype(jnp.bfloat16).astype(jnp.float32)
    return high, value - high


def norm_kernel(kind_ref, rest_ref, partial_ref, three_ref, two_ref, one_ref, gain_ref, router_ref, _, out_ref):
    slots, columns = rest_ref.shape
    hidden = rest_ref[...] + partial_ref[0].astype(jnp.float32)
    for got_ref in (three_ref, two_ref, one_ref):
        hidden = hidden + got_ref[...].astype(jnp.float32)
    kind = kind_ref[0:1, 0:1]
    gains = gain_ref[...].astype(jnp.float32)
    gained = hidden * jnp.where(kind == 0.0, gains[0:1], gains[1:2])
    out_ref[:, :columns] = gained.astype(jnp.bfloat16)
    table = router_ref[...].astype(jnp.float32)
    pieces = []
    for e in range(2):
        second = (lax.axis_index("groups") ^ e) == 1
        text = jnp.where(second, table[1:2], table[0:1])
        image = jnp.where(second, table[3:4], table[2:3])
        weights = jnp.where(kind == 0.0, text, image)
        half = slots // 2
        pieces.append(jnp.sum(gained[e * half : (e + 1) * half] * weights, axis=1, keepdims=True))
    logits = jnp.concatenate(pieces, axis=0)
    squares = jnp.sum(hidden * hidden, axis=1, keepdims=True)
    lane = lax.broadcasted_iota(jnp.int32, (slots, STAT_COLS), 1)
    extra = jnp.where(lane == 4, kind, 0.0)
    for at, stat in enumerate(split_high_low(squares) + split_high_low(logits)):
        extra = jnp.where(lane == at, stat, extra)
    out_ref[:, columns:] = extra.astype(jnp.bfloat16)


def places(packed_refs, columns):
    side = lax.axis_index("mod")
    matches, found, before = [], [], 0
    for v, ref in enumerate(packed_refs):
        flag = ref[:TILE, columns:].astype(jnp.float32)[0, 4]
        kind = jnp.where(flag > 0.5, 1, 0)
        match = kind == side
        place = jnp.minimum(jnp.where(match, before, v - before), len(packed_refs) - 2)
        matches.append(match)
        found.append(place)
        before = before + jnp.where(match, 1, 0)
    return matches, found


def arrange_kernel(zero_ref, three_ref, two_ref, one_ref, _, *out_refs):
    packed_refs = (zero_ref, one_ref, two_ref, three_ref)
    capacity = zero_ref.shape[0] // 2
    for out_ref in out_refs:
        out_ref[...] = jnp.zeros(out_ref.shape, out_ref.dtype)
    matches, found = places(packed_refs, zero_ref.shape[1] - STAT_COLS)
    for ref, match, place in zip(packed_refs, matches, found):
        span = pl.ds(pl.multiple_of(place * capacity, capacity), capacity)
        for wanted, (own_ref, given_ref) in ((True, out_refs[:2]), (False, out_refs[2:])):

            @pl.when(match == wanted)
            def _():
                own_ref[span, :] = ref[:capacity, :]
                given_ref[span, :] = ref[capacity:, :]


def weights_times_rows(weight_refs, spans, rows, out_ref):
    at = 0
    for weight_ref, (first, last) in zip(weight_refs, spans):
        for start in range(first, last, STRIP):
            stop = min(start + STRIP, last)
            out_ref[at : at + stop - start, :] = lax.dot_general(
                weight_ref[start:stop, :], rows, (((1,), (1,)), ((), ())), preferred_element_type=jnp.float32
            ).astype(jnp.bfloat16)
            at += stop - start


def gate_kernel(side_far_ref, side_own_ref, far_ref, own_ref, *refs):
    weight_refs, out_ref, rows_ref = refs[:2], refs[-2], refs[-1]
    half = own_ref.shape[0]
    rows = rows_ref.shape[0]
    units = out_ref.shape[0] - TILE
    columns = rows_ref.shape[1] // 2
    rows_ref[2 * half :, :] = jnp.zeros((rows - 2 * half, 2 * columns), rows_ref.dtype)
    for side in range(2):

        @pl.when(lax.axis_index("mod") == side)
        def _():
            here, there = side * columns, (1 - side) * columns
            rows_ref[:half, here : here + columns] = own_ref[:, :columns]
            rows_ref[half : 2 * half, here : here + columns] = far_ref[:, :columns]
            rows_ref[:half, there : there + columns] = side_own_ref[:, :columns]
            rows_ref[half : 2 * half, there : there + columns] = side_far_ref[:, :columns]

    spans = [(0, ref.shape[0]) for ref in weight_refs]
    weights_times_rows(weight_refs, spans, rows_ref[...], out_ref)
    tails = [ref[:, columns:].astype(jnp.float32) for ref in (own_ref, side_own_ref, far_ref, side_far_ref)]
    unused = jnp.zeros((rows - 2 * half, STAT_COLS), jnp.float32)
    stat = jnp.concatenate([tails[0] + tails[1], tails[2] + tails[3], unused], axis=0).T
    squares = stat[0:1] + stat[1:2]
    logits = stat[2:3] + stat[3:4]
    at_row = lax.broadcasted_iota(jnp.int32, (TILE, rows), 0)
    extra = jnp.zeros((TILE, rows), jnp.float32)
    for at, piece in enumerate(split_high_low(squares) + split_high_low(logits)):
        extra = jnp.where(at_row == at, piece, extra)
    out_ref[units:, :] = extra.astype(jnp.bfloat16)


def up_kernel(spans, rows_ref, *refs):
    weights_times_rows(refs[:-1], spans, rows_ref[...], refs[-1])


def silu_kernel(gate_ref, gate_other_ref, out_ref, stat_ref):
    units = out_ref.shape[0]
    stat = gate_ref[units:, :].astype(jnp.float32) + gate_other_ref[units:, :].astype(jnp.float32)
    inverse = lax.rsqrt((stat[0:1] + stat[1:2]) / D + 1e-05)
    logits = (stat[2:3] + stat[3:4]) * inverse
    score = 1.0 / (1.0 + jnp.exp(-logits))
    at_row = lax.broadcasted_iota(jnp.int32, stat_ref.shape, 0)
    stat_ref[...] = jnp.where(at_row == 0, inverse, score)
    for start in range(0, units, STRIP):
        stop = min(start + STRIP, units)
        gate = gate_ref[start:stop, :].astype(jnp.float32) + gate_other_ref[start:stop, :].astype(jnp.float32)
        gate = gate * inverse
        out_ref[start:stop, :] = gate / (1.0 + jnp.exp(-gate)) * inverse


def down_kernel(
    silu_ref, stat_ref, up_ref, up_late_ref, other_ref, other_late_ref, first_ref, second_ref,
    kept_ref, far_ref, side_ref, side_far_ref, act_ref,
):
    units, rows = act_ref.shape
    at = 0
    for mine_ref, got_ref in ((up_ref, other_ref), (up_late_ref, other_late_ref)):
        for start in range(0, mine_ref.shape[0], STRIP):
            stop = min(start + STRIP, mine_ref.shape[0])
            up = mine_ref[start:stop, :].astype(jnp.float32) + got_ref[start:stop, :].astype(jnp.float32)
            span = slice(at, at + stop - start)
            act_ref[span, :] = (silu_ref[span, :] * up).astype(jnp.bfloat16)
            at += stop - start
    half, columns = kept_ref.shape
    score = jnp.broadcast_to(stat_ref[1:2, :], (rows, rows)).T[:, 0:1]
    first_units = first_ref.shape[0]
    for quarter in range(2):
        span = slice(quarter * columns, (quarter + 1) * columns)
        value = sum(
            lax.dot_general(
                act_ref[a:b, :], weight_ref[:, span], (((0,), (0,)), ((), ())), preferred_element_type=jnp.float32
            )
            for a, b, weight_ref in ((0, first_units, first_ref), (first_units, units, second_ref))
        )
        value = (value * score).astype(jnp.bfloat16)
        for across, (own_out, far_out) in enumerate(((kept_ref, far_ref), (side_ref, side_far_ref))):

            @pl.when((lax.axis_index("mod") ^ quarter) == across)
            def _():
                own_out[...] = value[:half]
                far_out[...] = value[half : 2 * half]


def merge_kernel(zero_ref, three_ref, two_ref, one_ref, side_far_ref, side_ref, far_ref, kept_ref, *out_refs):
    columns = kept_ref.shape[1]
    capacity = zero_ref.shape[0] // 2
    matches, found = places((zero_ref, one_ref, two_ref, three_ref), columns)
    for out_ref, match, place in zip(out_refs, matches, found):
        span = pl.ds(pl.multiple_of(place * capacity, capacity), capacity)
        for wanted, (first_ref, second_ref) in ((True, (kept_ref, far_ref)), (False, (side_ref, side_far_ref))):

            @pl.when(match == wanted)
            def _():
                out_ref[:capacity, :] = first_ref[span, :]
                out_ref[capacity:, :] = second_ref[span, :]


def scatter_kernel(pick_ref, zero_ref, one_ref, two_ref, three_ref, out_hbm, out_ref, semaphores):
    columns = out_ref.shape[1]
    pieces = semaphores.shape[0]
    width = columns // pieces
    copies = []
    for n in range(pieces):
        span = slice(n * width, (n + 1) * width)
        total = zero_ref[:, span].astype(jnp.float32)
        for got_ref in (three_ref, two_ref, one_ref):
            total = total + got_ref[:, span].astype(jnp.float32)
        result = 0.0
        for piece in split_high_low(total)[::-1]:
            result = result + lax.dot_general(
                pick_ref[...], piece.astype(jnp.bfloat16), (((0,), (0,)), ((), ())),
                preferred_element_type=jnp.float32,
            )
        out_ref[:, span] = result.astype(jnp.bfloat16)
        copies.append(pltpu.make_async_copy(out_ref.at[:, span], out_hbm.at[:, span], semaphores.at[n]))
        copies[-1].start()
    for copy in copies:
        copy.wait()


def paired_local(
    residual,
    context,
    out_proj,
    norm_gain,
    router_weight,
    block_modality,
    expert_rows,
    gate_weight,
    up_weight,
    down_weight,
):
    tokens, columns = residual.shape
    experts, capacity = expert_rows.shape
    slots = 2 * capacity
    half = 4 * capacity
    rows = 2 * half
    units, width = down_weight.shape[1:]
    assert block_modality.shape == (1,) and experts == 4 and gate_weight.shape[0] == 2
    picked, pick, kind = call(
        select_kernel,
        "select",
        [array(slots, columns), array(slots, tokens), array(8, STAT_COLS, dtype=jnp.float32)],
        [IN_HBM] * 2,
        [in_hbm(expert_rows), in_hbm(context)],
        scratch=[
            pltpu.SMEM((experts, capacity), jnp.int32),
            pltpu.VMEM((tokens, columns), jnp.bfloat16),
            pltpu.SemaphoreType.DMA((2,)),
        ],
    )
    plane = ("tok", "mod", "fsdp")
    to_first = [(t * 4 + q, q * 4 + t) for t in range(4) for q in range(4)]
    to_second = [(t * 4 + q, q * 4 + (t ^ 2)) for t in range(4) for q in range(4)]
    across = lax.ppermute(picked, plane, to_second)
    near = lax.ppermute(picked, plane, to_first)
    gate_units, up_units, down_units = [round(units * part / TILE) * TILE for part in (0.58, 0.41, 0.24)]
    gate_first, proj_held, rest = call(
        keep_gate_kernel,
        "keep_gate",
        [
            pltpu.VMEM((gate_units, width), jnp.bfloat16),
            pltpu.VMEM(out_proj.shape, jnp.bfloat16),
            array(slots, columns, dtype=jnp.float32),
        ],
        [ON_CHIP, IN_HBM, IN_HBM, IN_HBM],
        [pick, in_hbm(residual), in_hbm(gate_weight.swapaxes(1, 2)), in_hbm(out_proj)],
        scratch=[pltpu.VMEM((tokens, columns), jnp.bfloat16), pltpu.SemaphoreType.DMA((3,))],
        moved=units * width,
        limit=2 << 20,
    )
    joined = call(join_kernel, "join", array(half, columns), [ON_CHIP] * 3, [near, across, gate_first])
    other = lax.ppermute(joined, "fsdp", SWAP)
    partial = call(
        project_kernel,
        "project",
        array(4, slots, columns),
        [ON_CHIP] * 3,
        [joined, other, proj_held],
        scratch=[pltpu.VMEM((rows, columns), jnp.bfloat16)],
    )
    sums = [lax.ppermute(partial[v], "tok", crossed(2, v)) for v in (3, 2, 1)][::-1]
    gate_second, up_first = keep_on_chip(
        partial,
        [gate_weight.swapaxes(1, 2), up_weight.swapaxes(1, 2)],
        [(gate_units, units), (0, up_units)],
        "keep_more",
    )
    packed_columns = columns + STAT_COLS
    packed = call(
        norm_kernel,
        "norm",
        array(slots, packed_columns),
        [ON_CHIP] * 9,
        [kind, rest, partial, *sums[::-1], norm_gain, router_weight.T, up_first],
    )
    others = [lax.ppermute(packed, "tok", crossed(2, v)) for v in (3, 2, 1)][::-1]
    up_second, down_first = keep_on_chip(
        packed,
        [up_weight.swapaxes(1, 2), down_weight],
        [(up_units, units), (0, down_units)],
        "keep_up",
    )
    kept_slots = 3 * capacity
    own, to_far_rows, to_side_rows, to_corner_rows = call(
        arrange_kernel,
        "arrange",
        [array(kept_slots, packed_columns)] * 4,
        [ON_CHIP] * 5,
        [packed, *others[::-1], up_second],
    )
    both_axes = ("groups", "mod")
    side_far = lax.ppermute(to_corner_rows, both_axes, crossed(2, 3))
    far = lax.ppermute(to_far_rows, "groups", SWAP)
    side_own = lax.ppermute(to_side_rows, "mod", SWAP)

    (down_second,) = keep_on_chip(own, [down_weight], [(down_units, units)], "keep_down")

    flops = 2 * rows * units * width
    gate, gathered = call(
        gate_kernel,
        "gate",
        [array(units + TILE, rows), array(rows, width)],
        [ON_CHIP] * 7,
        [side_far, side_own, far, own, gate_first, gate_second, down_second],
        flops=flops,
    )
    late = units // 4 // TILE * TILE
    up_rest = units - up_units
    up_parts = [
        call(
            functools.partial(up_kernel, spans),
            "up",
            array(sum(b - a for a, b in spans), rows),
            [ON_CHIP] * (1 + len(spans)),
            [gathered, *weights],
            flops=flops * sum(b - a for a, b in spans) // units,
        )
        for spans, weights in (
            (((0, up_units), (0, up_rest - late)), (up_first, up_second)),
            (((up_rest - late, up_rest),), (up_second,)),
        )
    ]
    gate_other = lax.ppermute(gate, "fsdp", SWAP)
    up_others = [lax.ppermute(part, "fsdp", SWAP) for part in up_parts]
    silu, stat = call(
        silu_kernel,
        "silu",
        [array(units, rows, dtype=jnp.float32), array(8, rows, dtype=jnp.float32)],
        [ON_CHIP] * 2,
        [gate, gate_other],
        moved=8 * units * rows,
    )
    kept, to_far, to_side, to_side_far = call(
        down_kernel,
        "down",
        [array(kept_slots, columns)] * 4,
        [ON_CHIP] * 8,
        [silu, stat, *up_parts, *up_others, down_first, down_second],
        scratch=[pltpu.VMEM((units, rows), jnp.bfloat16)],
        flops=flops,
    )
    from_side_far = lax.ppermute(to_side_far, both_axes, crossed(2, 3))
    from_far = lax.ppermute(to_far, "groups", SWAP)
    from_side = lax.ppermute(to_side, "mod", SWAP)
    merged = call(
        merge_kernel,
        "merge",
        [array(slots, columns)] * 4,
        [ON_CHIP] * 8,
        [packed, *others[::-1], from_side_far, from_side, from_far, kept],
    )
    values = [merged[0]] + [lax.ppermute(merged[v], "tok", crossed(2, v)) for v in (1, 2, 3)]
    return pl.pallas_call(
        scatter_kernel,
        out_shape=pltpu.HBM((tokens, columns), jnp.bfloat16),
        in_specs=[ON_CHIP] * 5,
        out_specs=IN_HBM,
        scratch_shapes=[pltpu.VMEM((tokens, columns), jnp.bfloat16), pltpu.SemaphoreType.DMA((4,))],
        compiler_params=pltpu.CompilerParams(vmem_limit_bytes=8 << 20),
        name="scatter",
    )(pick, *values)


def solution(mesh):
    placed = (
        P(("groups", "tok"), ("fsdp", "mod")),
        P(("groups", "tok"), ("mod", "fsdp")),
        P("tok", ("fsdp", "mod")),
        P(None, ("fsdp", "mod")),
        P(("fsdp", "mod"), None),
        P(("groups", "tok")),
        P(None, ("groups", "tok")),
        P("mod", "fsdp", "tok"),
        P("mod", "fsdp", "tok"),
        P("mod", "tok", "fsdp"),
    )
    sizes = dict(n_tok=mesh.shape["tok"], n_mod=mesh.shape["mod"], n_fsdp=mesh.shape["fsdp"])
    paired = (
        mesh.shape["groups"] == 2
        and sizes == dict(n_tok=4, n_mod=2, n_fsdp=2)
    )
    body = paired_local if paired else functools.partial(local, **sizes)
    return jax.shard_map(
        body,
        mesh=mesh,
        in_specs=placed,
        out_specs=P(("groups", "tok"), ("fsdp", "mod")),
        check_vma=False,
    )
```

```python
import functools

import jax
import jax.numpy as jnp
from jax import lax
from jax.experimental import pallas as pl
from jax.experimental.pallas import tpu as pltpu
from jax.sharding import PartitionSpec as P

D = 4096
STAT_COLS = 128
FEW = 4


def ring(size, step):
    return [(i, (i + step) % size) for i in range(size)]


def reduce_tok(blocks, n_tok):
    if n_tok > FEW:
        return lax.psum_scatter(blocks, "tok", scatter_dimension=0, tiled=False).astype(jnp.float32)
    own = lax.axis_index("tok")
    total = lax.dynamic_index_in_dim(blocks, own, 0, False).astype(jnp.float32)
    for step in range(1, n_tok):
        sent = lax.dynamic_index_in_dim(blocks, (own + step) % n_tok, 0, False)
        total = total + lax.ppermute(sent, "tok", ring(n_tok, step)).astype(jnp.float32)
    return total


def gather_tok(rows, n_tok):
    if n_tok > FEW:
        return lax.all_gather(rows, "tok", axis=0, tiled=False)
    own = lax.axis_index("tok")
    result = jnp.zeros((n_tok,) + rows.shape, rows.dtype)
    result = lax.dynamic_update_index_in_dim(result, rows, own, 0)
    for step in range(1, n_tok):
        got = lax.ppermute(rows, "tok", ring(n_tok, step))
        result = lax.dynamic_update_index_in_dim(result, got, (own - step) % n_tok, 0)
    return result


def spread_context(rows, n_tok, n_mod, n_fsdp):
    if n_tok > FEW or n_tok != n_mod * n_fsdp:
        full = lax.all_gather(rows, ("mod", "fsdp"), axis=1, tiled=True)
        split = full.reshape(full.shape[0], n_tok, full.shape[1] // n_tok).transpose(1, 0, 2)
        return lax.all_to_all(split, "tok", 0, 0, tiled=True)
    pairs = [(t * n_tok + q, q * n_tok + t) for t in range(n_tok) for q in range(n_tok)]
    swapped = lax.ppermute(rows, ("tok", "mod", "fsdp"), pairs)
    return lax.all_gather(swapped, ("mod", "fsdp"), axis=0, tiled=False)


def local(
    residual,
    context,
    out_proj,
    norm_gain,
    router_weight,
    block_modality,
    expert_rows,
    gate_weight,
    up_weight,
    down_weight,
    *,
    n_tok,
    n_mod,
    n_fsdp,
):
    token_count = residual.shape[0]
    experts, capacity = expert_rows.shape
    kind_experts = experts // 2
    slots = kind_experts * capacity
    local_experts = gate_weight.shape[0]
    columns = residual.shape[1]
    assert block_modality.shape == (1,) and n_mod * local_experts == experts
    modality = block_modality[0]
    first = modality * kind_experts
    mod_index = lax.axis_index("mod")

    own_rows = lax.dynamic_slice_in_dim(expert_rows, first, kind_experts, 0).reshape(slots)
    pick = own_rows[:, None] == lax.iota(jnp.int32, token_count)[None, :]
    pick_half = pick.astype(jnp.bfloat16)
    picked_context = jnp.dot(pick_half, context, preferred_element_type=jnp.float32).astype(jnp.bfloat16)
    picked_residual = jnp.dot(pick_half, residual, preferred_element_type=jnp.float32)

    spread = spread_context(picked_context, n_tok, n_mod, n_fsdp)
    partial = jnp.einsum("tsk,kc->tsc", spread, out_proj, preferred_element_type=jnp.float32)
    hidden = picked_residual + reduce_tok(partial.astype(jnp.bfloat16), n_tok)

    gain_table = norm_gain.astype(jnp.float32)
    gained = hidden * jnp.where(modality == 0, gain_table[0], gain_table[1])[None, :]
    router = lax.dynamic_slice_in_dim(router_weight.astype(jnp.float32), first, kind_experts, 1)
    slot_router = jnp.repeat(router.T, capacity, axis=0)
    squares = jnp.sum(hidden * hidden, axis=1, keepdims=True)
    logits = jnp.sum(gained * slot_router, axis=1, keepdims=True)
    flag = jnp.broadcast_to(modality.astype(jnp.bfloat16), (slots, 1))
    stat_list = []
    for stat in (squares, logits):
        high = lax.reduce_precision(stat, 8, 7)
        stat_list += [high.astype(jnp.bfloat16), (stat - high).astype(jnp.bfloat16)]
    packed = jnp.concatenate(
        [gained.astype(jnp.bfloat16)] + stat_list
        + [flag, jnp.zeros((slots, STAT_COLS - 5), jnp.bfloat16)],
        axis=1,
    )

    everyone = gather_tok(packed, n_tok)
    both = lax.all_gather(everyone, "mod", axis=0, tiled=False)
    kind_first = (mod_index * local_experts) % kind_experts
    both = both.reshape(n_mod, n_tok, kind_experts, capacity, columns + STAT_COLS)
    mine = lax.dynamic_slice_in_dim(both, kind_first, local_experts, 2)
    piece = mine[..., :columns].transpose(2, 1, 3, 0, 4).reshape(
        local_experts, n_tok * capacity, n_mod * columns
    )
    tail = mine[..., columns : columns + 5].astype(jnp.float32)
    half_stats = jnp.sum(
        jnp.stack([tail[..., 0] + tail[..., 1], tail[..., 2] + tail[..., 3]], axis=-1), axis=0
    )
    stats = lax.psum(half_stats, "fsdp")
    flags = tail[0, :, :, :, 4]
    by_expert = stats.transpose(1, 0, 2, 3).reshape(local_experts, n_tok * capacity, 2)
    inverse = lax.rsqrt(by_expert[..., 0:1] / D + 1e-05)
    score = jax.nn.sigmoid(by_expert[..., 1:2] * inverse)

    gate_part = jnp.einsum("esd,edf->esf", piece, gate_weight, preferred_element_type=jnp.float32)
    up_part = jnp.einsum("esd,edf->esf", piece, up_weight, preferred_element_type=jnp.float32)
    gate_half = gate_part.astype(jnp.bfloat16)
    up_half = up_part.astype(jnp.bfloat16)
    if n_fsdp == 2:
        swap = [(0, 1), (1, 0)]
        gate_sum = gate_half.astype(jnp.float32) + lax.ppermute(gate_half, "fsdp", swap).astype(jnp.float32)
        up_sum = up_half.astype(jnp.float32) + lax.ppermute(up_half, "fsdp", swap).astype(jnp.float32)
    else:
        gate_sum = lax.psum(gate_half, "fsdp").astype(jnp.float32)
        up_sum = lax.psum(up_half, "fsdp").astype(jnp.float32)
    activation = (jax.nn.silu(gate_sum * inverse) * (up_sum * inverse)).astype(jnp.bfloat16)
    value = jnp.einsum("esf,efd->esd", activation, down_weight, preferred_element_type=jnp.float32)
    value = (value * score).astype(jnp.bfloat16)
    value = value.reshape(local_experts, n_tok, capacity, n_mod * columns).transpose(1, 0, 2, 3)

    own_kind = (mod_index * local_experts) // kind_experts
    valid = (flags == own_kind.astype(jnp.float32))[..., None]
    if n_mod == 2:
        value = value.reshape(n_tok, local_experts, capacity, n_mod, columns)
        kept = lax.dynamic_index_in_dim(value, mod_index, 3, False)
        sent = lax.dynamic_index_in_dim(value, 1 - mod_index, 3, False)
        got = lax.ppermute(sent, "mod", [(0, 1), (1, 0)])
        merged = jnp.where(valid, kept, got).reshape(n_tok, slots, columns)
    else:
        value = jnp.where(valid, value, jnp.zeros((), jnp.bfloat16))
        wide = jnp.zeros((n_tok, kind_experts, capacity, n_mod * columns), jnp.bfloat16)
        wide = lax.dynamic_update_slice_in_dim(wide, value, kind_first, 1)
        wide = wide.reshape(n_tok, slots, n_mod * columns)
        merged = lax.psum_scatter(wide, "mod", scatter_dimension=2, tiled=True)
    summed = reduce_tok(merged, n_tok)
    return jnp.dot(
        pick.astype(jnp.float32).T, summed, precision=lax.Precision.HIGHEST
    ).astype(jnp.bfloat16)


SWAP = [(0, 1), (1, 0)]
STRIP = 688
TILE = 16
ON_CHIP = pl.BlockSpec(memory_space=pltpu.VMEM)
IN_HBM = pl.BlockSpec(memory_space=pltpu.HBM)
ANYWHERE = pl.BlockSpec(memory_space=pl.ANY)


def crossed(bits, flip):
    return [(i, i ^ flip) for i in range(1 << bits)]


def call(kernel, name, outs, specs, args, scratch=(), flops=0, moved=0, limit=8 << 20):
    return pl.pallas_call(
        kernel,
        out_shape=outs,
        in_specs=specs,
        out_specs=jax.tree.map(lambda _: ON_CHIP, outs),
        scratch_shapes=list(scratch),
        compiler_params=pltpu.CompilerParams(vmem_limit_bytes=limit),
        cost_estimate=pl.CostEstimate(flops=flops, transcendentals=0, bytes_accessed=moved),
        name=name,
    )(*args)


def array(*shape, dtype=jnp.bfloat16):
    return jax.ShapeDtypeStruct(shape, dtype)


def keep_kernel(spans, after_ref, *refs):
    count = len(spans)
    weights, held, semaphores = refs[:count], refs[count : 2 * count], refs[-1]
    copies = [
        pltpu.make_async_copy(weight.at[lax.axis_index("groups"), a:b], to, semaphores.at[n])
        for n, (weight, to, (a, b)) in enumerate(zip(weights, held, spans))
    ]
    for copy in copies:
        copy.start()
    for copy in copies:
        copy.wait()


def in_hbm(value):
    return pltpu.with_memory_space_constraint(value, pltpu.HBM)


def keep_on_chip(after, weights, spans, name):
    return call(
        functools.partial(keep_kernel, spans),
        name,
        [pltpu.VMEM((b - a, weight.shape[2]), jnp.bfloat16) for weight, (a, b) in zip(weights, spans)],
        [ANYWHERE] + [IN_HBM] * len(spans),
        [after] + [in_hbm(weight) for weight in weights],
        scratch=[pltpu.SemaphoreType.DMA((len(spans),))],
        moved=sum(2 * (b - a) * weight.shape[2] for weight, (a, b) in zip(weights, spans)),
        limit=1 << 20,
    )


def select_kernel(
    rows_hbm, context_hbm, picked_ref, pick_ref, kind_ref, rows_ref, context_ref, semaphores
):
    rows_copy = pltpu.make_async_copy(rows_hbm, rows_ref, semaphores.at[0])
    context_copy = pltpu.make_async_copy(context_hbm, context_ref, semaphores.at[1])
    rows_copy.start()
    context_copy.start()
    rows_copy.wait()
    kind = jnp.where(jnp.maximum(rows_ref[2, 0], rows_ref[3, 0]) >= 0, 1, 0)
    kind_ref[...] = jnp.full(kind_ref.shape, kind, jnp.int32).astype(jnp.float32)
    capacity = rows_ref.shape[1]
    slots, tokens = pick_ref.shape
    row = lax.broadcasted_iota(jnp.int32, (slots, tokens), 0)
    token = lax.broadcasted_iota(jnp.int32, (slots, tokens), 1)
    wanted = jnp.full((slots, tokens), -1, jnp.int32)
    for e in range(2):
        expert = 2 * kind + (lax.axis_index("groups") ^ e)
        for s in range(capacity):
            wanted = jnp.where(row == e * capacity + s, rows_ref[expert, s], wanted)
    pick = jnp.where(wanted == token, 1.0, 0.0).astype(jnp.bfloat16)
    pick_ref[...] = pick
    context_copy.wait()
    picked_ref[...] = jnp.dot(pick, context_ref[...], preferred_element_type=jnp.float32).astype(jnp.bfloat16)


def keep_gate_kernel(
    pick_ref, residual_hbm, gate_ref, proj_ref, gate_held, proj_held, rest_ref, residual_ref, semaphores
):
    copies = [
        pltpu.make_async_copy(residual_hbm, residual_ref, semaphores.at[0]),
        pltpu.make_async_copy(proj_ref, proj_held, semaphores.at[1]),
        pltpu.make_async_copy(gate_ref.at[lax.axis_index("groups"), : gate_held.shape[0]], gate_held, semaphores.at[2]),
    ]
    for copy in copies:
        copy.start()
    copies[0].wait()
    rest_ref[...] = jnp.dot(pick_ref[...], residual_ref[...], preferred_element_type=jnp.float32)
    for copy in copies[1:]:
        copy.wait()


def join_kernel(near_ref, across_ref, _, out_ref):
    slots = near_ref.shape[0]
    out_ref[:slots, :] = near_ref[...]
    out_ref[slots:, :] = across_ref[...]


def project_kernel(joined_ref, other_ref, weight_ref, out_ref, rows_ref):
    pair = joined_ref.shape[0]
    slots = pair // 2
    rows_ref[:pair, :] = joined_ref[...]
    rows_ref[pair:, :] = other_ref[...]
    product = jnp.dot(rows_ref[...], weight_ref[...], preferred_element_type=jnp.float32)
    product = product.astype(jnp.bfloat16)
    corner = 2 * lax.axis_index("mod") + lax.axis_index("fsdp")
    flip = lax.axis_index("tok") ^ corner
    for n, u in enumerate((0, 2, 1, 3)):
        out_ref[flip ^ u] = product[n * slots : (n + 1) * slots, :]


def split_high_low(value):
    high = value.astype(jnp.bfloat16).astype(jnp.float32)
    return high, value - high


def norm_kernel(kind_ref, rest_ref, partial_ref, three_ref, two_ref, one_ref, gain_ref, router_ref, _, out_ref):
    slots, columns = rest_ref.shape
    hidden = rest_ref[...] + partial_ref[0].astype(jnp.float32)
    for got_ref in (three_ref, two_ref, one_ref):
        hidden = hidden + got_ref[...].astype(jnp.float32)
    kind = kind_ref[0:1, 0:1]
    gains = gain_ref[...].astype(jnp.float32)
    gained = hidden * jnp.where(kind == 0.0, gains[0:1], gains[1:2])
    out_ref[:, :columns] = gained.astype(jnp.bfloat16)
    table = router_ref[...].astype(jnp.float32)
    pieces = []
    for e in range(2):
        second = (lax.axis_index("groups") ^ e) == 1
        text = jnp.where(second, table[1:2], table[0:1])
        image = jnp.where(second, table[3:4], table[2:3])
        weights = jnp.where(kind == 0.0, text, image)
        half = slots // 2
        pieces.append(jnp.sum(gained[e * half : (e + 1) * half] * weights, axis=1, keepdims=True))
    logits = jnp.concatenate(pieces, axis=0)
    squares = jnp.sum(hidden * hidden, axis=1, keepdims=True)
    lane = lax.broadcasted_iota(jnp.int32, (slots, STAT_COLS), 1)
    extra = jnp.where(lane == 4, kind, 0.0)
    for at, stat in enumerate(split_high_low(squares) + split_high_low(logits)):
        extra = jnp.where(lane == at, stat, extra)
    out_ref[:, columns:] = extra.astype(jnp.bfloat16)


def places(packed_refs, columns):
    side = lax.axis_index("mod")
    matches, found, before = [], [], 0
    for v, ref in enumerate(packed_refs):
        flag = ref[:TILE, columns:].astype(jnp.float32)[0, 4]
        kind = jnp.where(flag > 0.5, 1, 0)
        match = kind == side
        place = jnp.minimum(jnp.where(match, before, v - before), len(packed_refs) - 2)
        matches.append(match)
        found.append(place)
        before = before + jnp.where(match, 1, 0)
    return matches, found


def arrange_kernel(zero_ref, three_ref, two_ref, one_ref, _, *out_refs):
    packed_refs = (zero_ref, one_ref, two_ref, three_ref)
    capacity = zero_ref.shape[0] // 2
    for out_ref in out_refs:
        out_ref[...] = jnp.zeros(out_ref.shape, out_ref.dtype)
    matches, found = places(packed_refs, zero_ref.shape[1] - STAT_COLS)
    for ref, match, place in zip(packed_refs, matches, found):
        span = pl.ds(pl.multiple_of(place * capacity, capacity), capacity)
        for wanted, (own_ref, given_ref) in ((True, out_refs[:2]), (False, out_refs[2:])):

            @pl.when(match == wanted)
            def _():
                own_ref[span, :] = ref[:capacity, :]
                given_ref[span, :] = ref[capacity:, :]


def weights_times_rows(weight_refs, spans, rows, out_ref):
    at = 0
    for weight_ref, (first, last) in zip(weight_refs, spans):
        for start in range(first, last, STRIP):
            stop = min(start + STRIP, last)
            out_ref[at : at + stop - start, :] = lax.dot_general(
                weight_ref[start:stop, :], rows, (((1,), (1,)), ((), ())), preferred_element_type=jnp.float32
            ).astype(jnp.bfloat16)
            at += stop - start


def gate_kernel(side_far_ref, side_own_ref, far_ref, own_ref, *refs):
    weight_refs, out_ref, rows_ref = refs[:2], refs[-2], refs[-1]
    half = own_ref.shape[0]
    rows = rows_ref.shape[0]
    units = out_ref.shape[0] - TILE
    columns = rows_ref.shape[1] // 2
    rows_ref[2 * half :, :] = jnp.zeros((rows - 2 * half, 2 * columns), rows_ref.dtype)
    for side in range(2):

        @pl.when(lax.axis_index("mod") == side)
        def _():
            here, there = side * columns, (1 - side) * columns
            rows_ref[:half, here : here + columns] = own_ref[:, :columns]
            rows_ref[half : 2 * half, here : here + columns] = far_ref[:, :columns]
            rows_ref[:half, there : there + columns] = side_own_ref[:, :columns]
            rows_ref[half : 2 * half, there : there + columns] = side_far_ref[:, :columns]

    spans = [(0, ref.shape[0]) for ref in weight_refs]
    weights_times_rows(weight_refs, spans, rows_ref[...], out_ref)
    tails = [ref[:, columns:].astype(jnp.float32) for ref in (own_ref, side_own_ref, far_ref, side_far_ref)]
    unused = jnp.zeros((rows - 2 * half, STAT_COLS), jnp.float32)
    stat = jnp.concatenate([tails[0] + tails[1], tails[2] + tails[3], unused], axis=0).T
    squares = stat[0:1] + stat[1:2]
    logits = stat[2:3] + stat[3:4]
    at_row = lax.broadcasted_iota(jnp.int32, (TILE, rows), 0)
    extra = jnp.zeros((TILE, rows), jnp.float32)
    for at, piece in enumerate(split_high_low(squares) + split_high_low(logits)):
        extra = jnp.where(at_row == at, piece, extra)
    out_ref[units:, :] = extra.astype(jnp.bfloat16)


def up_kernel(spans, rows_ref, *refs):
    weights_times_rows(refs[:-1], spans, rows_ref[...], refs[-1])


def silu_kernel(gate_ref, gate_other_ref, out_ref, stat_ref):
    units = out_ref.shape[0]
    stat = gate_ref[units:, :].astype(jnp.float32) + gate_other_ref[units:, :].astype(jnp.float32)
    inverse = lax.rsqrt((stat[0:1] + stat[1:2]) / D + 1e-05)
    logits = (stat[2:3] + stat[3:4]) * inverse
    score = 1.0 / (1.0 + jnp.exp(-logits))
    at_row = lax.broadcasted_iota(jnp.int32, stat_ref.shape, 0)
    stat_ref[...] = jnp.where(at_row == 0, inverse, score)
    for start in range(0, units, STRIP):
        stop = min(start + STRIP, units)
        gate = gate_ref[start:stop, :].astype(jnp.float32) + gate_other_ref[start:stop, :].astype(jnp.float32)
        gate = gate * inverse
        out_ref[start:stop, :] = gate / (1.0 + jnp.exp(-gate)) * inverse


def down_kernel(
    silu_ref, stat_ref, up_ref, up_late_ref, other_ref, other_late_ref, first_ref, second_ref,
    kept_ref, far_ref, side_ref, side_far_ref, act_ref,
):
    units, rows = act_ref.shape
    at = 0
    for mine_ref, got_ref in ((up_ref, other_ref), (up_late_ref, other_late_ref)):
        for start in range(0, mine_ref.shape[0], STRIP):
            stop = min(start + STRIP, mine_ref.shape[0])
            up = mine_ref[start:stop, :].astype(jnp.float32) + got_ref[start:stop, :].astype(jnp.float32)
            span = slice(at, at + stop - start)
            act_ref[span, :] = (silu_ref[span, :] * up).astype(jnp.bfloat16)
            at += stop - start
    half, columns = kept_ref.shape
    score = jnp.broadcast_to(stat_ref[1:2, :], (rows, rows)).T[:, 0:1]
    first_units = first_ref.shape[0]
    for quarter in range(2):
        span = slice(quarter * columns, (quarter + 1) * columns)
        value = sum(
            lax.dot_general(
                act_ref[a:b, :], weight_ref[:, span], (((0,), (0,)), ((), ())), preferred_element_type=jnp.float32
            )
            for a, b, weight_ref in ((0, first_units, first_ref), (first_units, units, second_ref))
        )
        value = (value * score).astype(jnp.bfloat16)
        for across, (own_out, far_out) in enumerate(((kept_ref, far_ref), (side_ref, side_far_ref))):

            @pl.when((lax.axis_index("mod") ^ quarter) == across)
            def _():
                own_out[...] = value[:half]
                far_out[...] = value[half : 2 * half]


def merge_kernel(zero_ref, three_ref, two_ref, one_ref, kept_ref, other_ref, *out_refs):
    columns = kept_ref.shape[1]
    capacity = zero_ref.shape[0] // 2
    matches, found = places((zero_ref, one_ref, two_ref, three_ref), columns)
    for out_ref, match, place in zip(out_refs, matches, found):
        span = pl.ds(pl.multiple_of(place * capacity, capacity), capacity)
        for wanted, source_ref in ((True, kept_ref), (False, other_ref)):

            @pl.when(match == wanted)
            def _():
                out_ref[...] = source_ref[span, :]


def scatter_kernel(pick_ref, *refs):
    halves, (out_hbm, out_ref, semaphores) = (refs[:4], refs[4:8]), refs[8:]
    columns = out_ref.shape[1]
    pieces = semaphores.shape[0]
    width = columns // pieces
    copies = []
    for n in range(pieces):
        span = slice(n * width, (n + 1) * width)
        totals = []
        for half in halves:
            total = half[0][:, span].astype(jnp.float32)
            for got_ref in half[1:]:
                total = total + got_ref[:, span].astype(jnp.float32)
            totals.append(total)
        total = jnp.concatenate(totals, axis=0)
        result = 0.0
        for piece in split_high_low(total)[::-1]:
            result = result + lax.dot_general(
                pick_ref[...], piece.astype(jnp.bfloat16), (((0,), (0,)), ((), ())),
                preferred_element_type=jnp.float32,
            )
        out_ref[:, span] = result.astype(jnp.bfloat16)
        copies.append(pltpu.make_async_copy(out_ref.at[:, span], out_hbm.at[:, span], semaphores.at[n]))
        copies[-1].start()
    for copy in copies:
        copy.wait()


def paired_local(
    residual,
    context,
    out_proj,
    norm_gain,
    router_weight,
    block_modality,
    expert_rows,
    gate_weight,
    up_weight,
    down_weight,
):
    tokens, columns = residual.shape
    experts, capacity = expert_rows.shape
    slots = 2 * capacity
    half = 4 * capacity
    rows = 2 * half
    units, width = down_weight.shape[1:]
    assert block_modality.shape == (1,) and experts == 4 and gate_weight.shape[0] == 2
    picked, pick, kind = call(
        select_kernel,
        "select",
        [array(slots, columns), array(slots, tokens), array(8, STAT_COLS, dtype=jnp.float32)],
        [IN_HBM] * 2,
        [in_hbm(expert_rows), in_hbm(context)],
        scratch=[
            pltpu.SMEM((experts, capacity), jnp.int32),
            pltpu.VMEM((tokens, columns), jnp.bfloat16),
            pltpu.SemaphoreType.DMA((2,)),
        ],
    )
    plane = ("tok", "mod", "fsdp")
    to_first = [(t * 4 + q, q * 4 + t) for t in range(4) for q in range(4)]
    to_second = [(t * 4 + q, q * 4 + (t ^ 2)) for t in range(4) for q in range(4)]
    across = lax.ppermute(picked, plane, to_second)
    near = lax.ppermute(picked, plane, to_first)
    gate_units, up_units, down_units = [round(units * part / TILE) * TILE for part in (0.58, 0.41, 0.24)]
    gate_first, proj_held, rest = call(
        keep_gate_kernel,
        "keep_gate",
        [
            pltpu.VMEM((gate_units, width), jnp.bfloat16),
            pltpu.VMEM(out_proj.shape, jnp.bfloat16),
            array(slots, columns, dtype=jnp.float32),
        ],
        [ON_CHIP, IN_HBM, IN_HBM, IN_HBM],
        [pick, in_hbm(residual), in_hbm(gate_weight.swapaxes(1, 2)), in_hbm(out_proj)],
        scratch=[pltpu.VMEM((tokens, columns), jnp.bfloat16), pltpu.SemaphoreType.DMA((3,))],
        moved=units * width,
        limit=2 << 20,
    )
    joined = call(join_kernel, "join", array(half, columns), [ON_CHIP] * 3, [near, across, gate_first])
    other = lax.ppermute(joined, "fsdp", SWAP)
    partial = call(
        project_kernel,
        "project",
        array(4, slots, columns),
        [ON_CHIP] * 3,
        [joined, other, proj_held],
        scratch=[pltpu.VMEM((rows, columns), jnp.bfloat16)],
    )
    sums = [lax.ppermute(partial[v], "tok", crossed(2, v)) for v in (3, 2, 1)][::-1]
    gate_second, up_first = keep_on_chip(
        partial,
        [gate_weight.swapaxes(1, 2), up_weight.swapaxes(1, 2)],
        [(gate_units, units), (0, up_units)],
        "keep_more",
    )
    packed_columns = columns + STAT_COLS
    packed = call(
        norm_kernel,
        "norm",
        array(slots, packed_columns),
        [ON_CHIP] * 9,
        [kind, rest, partial, *sums[::-1], norm_gain, router_weight.T, up_first],
    )
    others = [lax.ppermute(packed, "tok", crossed(2, v)) for v in (3, 2, 1)][::-1]
    up_second, down_first = keep_on_chip(
        packed,
        [up_weight.swapaxes(1, 2), down_weight],
        [(up_units, units), (0, down_units)],
        "keep_up",
    )
    kept_slots = 3 * capacity
    own, to_far_rows, to_side_rows, to_corner_rows = call(
        arrange_kernel,
        "arrange",
        [array(kept_slots, packed_columns)] * 4,
        [ON_CHIP] * 5,
        [packed, *others[::-1], up_second],
    )
    both_axes = ("groups", "mod")
    side_far = lax.ppermute(to_corner_rows, both_axes, crossed(2, 3))
    far = lax.ppermute(to_far_rows, "groups", SWAP)
    side_own = lax.ppermute(to_side_rows, "mod", SWAP)

    (down_second,) = keep_on_chip(own, [down_weight], [(down_units, units)], "keep_down")

    flops = 2 * rows * units * width
    gate, gathered = call(
        gate_kernel,
        "gate",
        [array(units + TILE, rows), array(rows, width)],
        [ON_CHIP] * 7,
        [side_far, side_own, far, own, gate_first, gate_second, down_second],
        flops=flops,
    )
    late = units // 4 // TILE * TILE
    up_rest = units - up_units
    up_parts = [
        call(
            functools.partial(up_kernel, spans),
            "up",
            array(sum(b - a for a, b in spans), rows),
            [ON_CHIP] * (1 + len(spans)),
            [gathered, *weights],
            flops=flops * sum(b - a for a, b in spans) // units,
        )
        for spans, weights in (
            (((0, up_units), (0, up_rest - late)), (up_first, up_second)),
            (((up_rest - late, up_rest),), (up_second,)),
        )
    ]
    gate_other = lax.ppermute(gate, "fsdp", SWAP)
    up_others = [lax.ppermute(part, "fsdp", SWAP) for part in up_parts]
    silu, stat = call(
        silu_kernel,
        "silu",
        [array(units, rows, dtype=jnp.float32), array(8, rows, dtype=jnp.float32)],
        [ON_CHIP] * 2,
        [gate, gate_other],
        moved=8 * units * rows,
    )
    kept, to_far, to_side, to_side_far = call(
        down_kernel,
        "down",
        [array(kept_slots, columns)] * 4,
        [ON_CHIP] * 8,
        [silu, stat, *up_parts, *up_others, down_first, down_second],
        scratch=[pltpu.VMEM((units, rows), jnp.bfloat16)],
        flops=flops,
    )
    from_side = lax.ppermute(to_side, "mod", SWAP)
    from_side_far = lax.ppermute(to_side_far, both_axes, crossed(2, 3))
    from_far = lax.ppermute(to_far, "groups", SWAP)
    values = []
    for mine, got, name in ((kept, from_side, "merge_first"), (from_far, from_side_far, "merge_second")):
        merged = call(
            merge_kernel,
            name,
            [array(capacity, columns)] * 4,
            [ON_CHIP] * 6,
            [packed, *others[::-1], mine, got],
        )
        values += [merged[0]] + [lax.ppermute(merged[v], "tok", crossed(2, v)) for v in (1, 2, 3)]
    return pl.pallas_call(
        scatter_kernel,
        out_shape=pltpu.HBM((tokens, columns), jnp.bfloat16),
        in_specs=[ON_CHIP] * 9,
        out_specs=IN_HBM,
        scratch_shapes=[pltpu.VMEM((tokens, columns), jnp.bfloat16), pltpu.SemaphoreType.DMA((4,))],
        compiler_params=pltpu.CompilerParams(vmem_limit_bytes=8 << 20),
        name="scatter",
    )(pick, *values)


def solution(mesh):
    placed = (
        P(("groups", "tok"), ("fsdp", "mod")),
        P(("groups", "tok"), ("mod", "fsdp")),
        P("tok", ("fsdp", "mod")),
        P(None, ("fsdp", "mod")),
        P(("fsdp", "mod"), None),
        P(("groups", "tok")),
        P(None, ("groups", "tok")),
        P("mod", "fsdp", "tok"),
        P("mod", "fsdp", "tok"),
        P("mod", "tok", "fsdp"),
    )
    sizes = dict(n_tok=mesh.shape["tok"], n_mod=mesh.shape["mod"], n_fsdp=mesh.shape["fsdp"])
    paired = (
        mesh.shape["groups"] == 2
        and sizes == dict(n_tok=4, n_mod=2, n_fsdp=2)
    )
    body = paired_local if paired else functools.partial(local, **sizes)
    return jax.shard_map(
        body,
        mesh=mesh,
        in_specs=placed,
        out_specs=P(("groups", "tok"), ("fsdp", "mod")),
        check_vma=False,
    )
```

```python
import functools

import jax
import jax.numpy as jnp
from jax import lax
from jax.experimental import pallas as pl
from jax.experimental.pallas import tpu as pltpu
from jax.sharding import PartitionSpec as P

D = 4096
STAT_COLS = 128
FEW = 4


def ring(size, step):
    return [(i, (i + step) % size) for i in range(size)]


def reduce_tok(blocks, n_tok):
    if n_tok > FEW:
        return lax.psum_scatter(blocks, "tok", scatter_dimension=0, tiled=False).astype(jnp.float32)
    own = lax.axis_index("tok")
    total = lax.dynamic_index_in_dim(blocks, own, 0, False).astype(jnp.float32)
    for step in range(1, n_tok):
        sent = lax.dynamic_index_in_dim(blocks, (own + step) % n_tok, 0, False)
        total = total + lax.ppermute(sent, "tok", ring(n_tok, step)).astype(jnp.float32)
    return total


def gather_tok(rows, n_tok):
    if n_tok > FEW:
        return lax.all_gather(rows, "tok", axis=0, tiled=False)
    own = lax.axis_index("tok")
    result = jnp.zeros((n_tok,) + rows.shape, rows.dtype)
    result = lax.dynamic_update_index_in_dim(result, rows, own, 0)
    for step in range(1, n_tok):
        got = lax.ppermute(rows, "tok", ring(n_tok, step))
        result = lax.dynamic_update_index_in_dim(result, got, (own - step) % n_tok, 0)
    return result


def spread_context(rows, n_tok, n_mod, n_fsdp):
    if n_tok > FEW or n_tok != n_mod * n_fsdp:
        full = lax.all_gather(rows, ("mod", "fsdp"), axis=1, tiled=True)
        split = full.reshape(full.shape[0], n_tok, full.shape[1] // n_tok).transpose(1, 0, 2)
        return lax.all_to_all(split, "tok", 0, 0, tiled=True)
    pairs = [(t * n_tok + q, q * n_tok + t) for t in range(n_tok) for q in range(n_tok)]
    swapped = lax.ppermute(rows, ("tok", "mod", "fsdp"), pairs)
    return lax.all_gather(swapped, ("mod", "fsdp"), axis=0, tiled=False)


def local(
    residual,
    context,
    out_proj,
    norm_gain,
    router_weight,
    block_modality,
    expert_rows,
    gate_weight,
    up_weight,
    down_weight,
    *,
    n_tok,
    n_mod,
    n_fsdp,
):
    token_count = residual.shape[0]
    experts, capacity = expert_rows.shape
    kind_experts = experts // 2
    slots = kind_experts * capacity
    local_experts = gate_weight.shape[0]
    columns = residual.shape[1]
    assert block_modality.shape == (1,) and n_mod * local_experts == experts
    modality = block_modality[0]
    first = modality * kind_experts
    mod_index = lax.axis_index("mod")

    own_rows = lax.dynamic_slice_in_dim(expert_rows, first, kind_experts, 0).reshape(slots)
    pick = own_rows[:, None] == lax.iota(jnp.int32, token_count)[None, :]
    pick_half = pick.astype(jnp.bfloat16)
    picked_context = jnp.dot(pick_half, context, preferred_element_type=jnp.float32).astype(jnp.bfloat16)
    picked_residual = jnp.dot(pick_half, residual, preferred_element_type=jnp.float32)

    spread = spread_context(picked_context, n_tok, n_mod, n_fsdp)
    partial = jnp.einsum("tsk,kc->tsc", spread, out_proj, preferred_element_type=jnp.float32)
    hidden = picked_residual + reduce_tok(partial.astype(jnp.bfloat16), n_tok)

    gain_table = norm_gain.astype(jnp.float32)
    gained = hidden * jnp.where(modality == 0, gain_table[0], gain_table[1])[None, :]
    router = lax.dynamic_slice_in_dim(router_weight.astype(jnp.float32), first, kind_experts, 1)
    slot_router = jnp.repeat(router.T, capacity, axis=0)
    squares = jnp.sum(hidden * hidden, axis=1, keepdims=True)
    logits = jnp.sum(gained * slot_router, axis=1, keepdims=True)
    flag = jnp.broadcast_to(modality.astype(jnp.bfloat16), (slots, 1))
    stat_list = []
    for stat in (squares, logits):
        high = lax.reduce_precision(stat, 8, 7)
        stat_list += [high.astype(jnp.bfloat16), (stat - high).astype(jnp.bfloat16)]
    packed = jnp.concatenate(
        [gained.astype(jnp.bfloat16)] + stat_list
        + [flag, jnp.zeros((slots, STAT_COLS - 5), jnp.bfloat16)],
        axis=1,
    )

    everyone = gather_tok(packed, n_tok)
    both = lax.all_gather(everyone, "mod", axis=0, tiled=False)
    kind_first = (mod_index * local_experts) % kind_experts
    both = both.reshape(n_mod, n_tok, kind_experts, capacity, columns + STAT_COLS)
    mine = lax.dynamic_slice_in_dim(both, kind_first, local_experts, 2)
    piece = mine[..., :columns].transpose(2, 1, 3, 0, 4).reshape(
        local_experts, n_tok * capacity, n_mod * columns
    )
    tail = mine[..., columns : columns + 5].astype(jnp.float32)
    half_stats = jnp.sum(
        jnp.stack([tail[..., 0] + tail[..., 1], tail[..., 2] + tail[..., 3]], axis=-1), axis=0
    )
    stats = lax.psum(half_stats, "fsdp")
    flags = tail[0, :, :, :, 4]
    by_expert = stats.transpose(1, 0, 2, 3).reshape(local_experts, n_tok * capacity, 2)
    inverse = lax.rsqrt(by_expert[..., 0:1] / D + 1e-05)
    score = jax.nn.sigmoid(by_expert[..., 1:2] * inverse)

    gate_part = jnp.einsum("esd,edf->esf", piece, gate_weight, preferred_element_type=jnp.float32)
    up_part = jnp.einsum("esd,edf->esf", piece, up_weight, preferred_element_type=jnp.float32)
    gate_half = gate_part.astype(jnp.bfloat16)
    up_half = up_part.astype(jnp.bfloat16)
    if n_fsdp == 2:
        swap = [(0, 1), (1, 0)]
        gate_sum = gate_half.astype(jnp.float32) + lax.ppermute(gate_half, "fsdp", swap).astype(jnp.float32)
        up_sum = up_half.astype(jnp.float32) + lax.ppermute(up_half, "fsdp", swap).astype(jnp.float32)
    else:
        gate_sum = lax.psum(gate_half, "fsdp").astype(jnp.float32)
        up_sum = lax.psum(up_half, "fsdp").astype(jnp.float32)
    activation = (jax.nn.silu(gate_sum * inverse) * (up_sum * inverse)).astype(jnp.bfloat16)
    value = jnp.einsum("esf,efd->esd", activation, down_weight, preferred_element_type=jnp.float32)
    value = (value * score).astype(jnp.bfloat16)
    value = value.reshape(local_experts, n_tok, capacity, n_mod * columns).transpose(1, 0, 2, 3)

    own_kind = (mod_index * local_experts) // kind_experts
    valid = (flags == own_kind.astype(jnp.float32))[..., None]
    if n_mod == 2:
        value = value.reshape(n_tok, local_experts, capacity, n_mod, columns)
        kept = lax.dynamic_index_in_dim(value, mod_index, 3, False)
        sent = lax.dynamic_index_in_dim(value, 1 - mod_index, 3, False)
        got = lax.ppermute(sent, "mod", [(0, 1), (1, 0)])
        merged = jnp.where(valid, kept, got).reshape(n_tok, slots, columns)
    else:
        value = jnp.where(valid, value, jnp.zeros((), jnp.bfloat16))
        wide = jnp.zeros((n_tok, kind_experts, capacity, n_mod * columns), jnp.bfloat16)
        wide = lax.dynamic_update_slice_in_dim(wide, value, kind_first, 1)
        wide = wide.reshape(n_tok, slots, n_mod * columns)
        merged = lax.psum_scatter(wide, "mod", scatter_dimension=2, tiled=True)
    summed = reduce_tok(merged, n_tok)
    return jnp.dot(
        pick.astype(jnp.float32).T, summed, precision=lax.Precision.HIGHEST
    ).astype(jnp.bfloat16)


SWAP = [(0, 1), (1, 0)]
STRIP = 688
TILE = 16
ON_CHIP = pl.BlockSpec(memory_space=pltpu.VMEM)
IN_HBM = pl.BlockSpec(memory_space=pltpu.HBM)
ANYWHERE = pl.BlockSpec(memory_space=pl.ANY)


def crossed(bits, flip):
    return [(i, i ^ flip) for i in range(1 << bits)]


def call(kernel, name, outs, specs, args, scratch=(), flops=0, moved=0, limit=8 << 20):
    return pl.pallas_call(
        kernel,
        out_shape=outs,
        in_specs=specs,
        out_specs=jax.tree.map(lambda _: ON_CHIP, outs),
        scratch_shapes=list(scratch),
        compiler_params=pltpu.CompilerParams(vmem_limit_bytes=limit),
        cost_estimate=pl.CostEstimate(flops=flops, transcendentals=0, bytes_accessed=moved),
        name=name,
    )(*args)


def array(*shape, dtype=jnp.bfloat16):
    return jax.ShapeDtypeStruct(shape, dtype)


def keep_kernel(spans, after_ref, *refs):
    count = len(spans)
    weights, held, semaphores = refs[:count], refs[count : 2 * count], refs[-1]
    copies = [
        pltpu.make_async_copy(weight.at[lax.axis_index("groups"), a:b], to, semaphores.at[n])
        for n, (weight, to, (a, b)) in enumerate(zip(weights, held, spans))
    ]
    for copy in copies:
        copy.start()
    for copy in copies:
        copy.wait()


def in_hbm(value):
    return pltpu.with_memory_space_constraint(value, pltpu.HBM)


def keep_on_chip(after, weights, spans, name):
    return call(
        functools.partial(keep_kernel, spans),
        name,
        [pltpu.VMEM((b - a, weight.shape[2]), jnp.bfloat16) for weight, (a, b) in zip(weights, spans)],
        [ANYWHERE] + [IN_HBM] * len(spans),
        [after] + [in_hbm(weight) for weight in weights],
        scratch=[pltpu.SemaphoreType.DMA((len(spans),))],
        moved=sum(2 * (b - a) * weight.shape[2] for weight, (a, b) in zip(weights, spans)),
        limit=1 << 20,
    )


def select_kernel(
    rows_hbm, context_hbm, picked_ref, pick_ref, kind_ref, rows_ref, context_ref, semaphores
):
    rows_copy = pltpu.make_async_copy(rows_hbm, rows_ref, semaphores.at[0])
    context_copy = pltpu.make_async_copy(context_hbm, context_ref, semaphores.at[1])
    rows_copy.start()
    context_copy.start()
    rows_copy.wait()
    kind = jnp.where(jnp.maximum(rows_ref[2, 0], rows_ref[3, 0]) >= 0, 1, 0)
    kind_ref[...] = jnp.full(kind_ref.shape, kind, jnp.int32).astype(jnp.float32)
    capacity = rows_ref.shape[1]
    slots, tokens = pick_ref.shape
    row = lax.broadcasted_iota(jnp.int32, (slots, tokens), 0)
    token = lax.broadcasted_iota(jnp.int32, (slots, tokens), 1)
    wanted = jnp.full((slots, tokens), -1, jnp.int32)
    for e in range(2):
        expert = 2 * kind + (lax.axis_index("groups") ^ e)
        for s in range(capacity):
            wanted = jnp.where(row == e * capacity + s, rows_ref[expert, s], wanted)
    pick = jnp.where(wanted == token, 1.0, 0.0).astype(jnp.bfloat16)
    pick_ref[...] = pick
    context_copy.wait()
    picked_ref[...] = jnp.dot(pick, context_ref[...], preferred_element_type=jnp.float32).astype(jnp.bfloat16)


def keep_gate_kernel(
    pick_ref, residual_hbm, gate_ref, proj_ref, gate_held, proj_held, rest_ref, residual_ref, semaphores
):
    copies = [
        pltpu.make_async_copy(residual_hbm, residual_ref, semaphores.at[0]),
        pltpu.make_async_copy(proj_ref, proj_held, semaphores.at[1]),
        pltpu.make_async_copy(gate_ref.at[lax.axis_index("groups"), : gate_held.shape[0]], gate_held, semaphores.at[2]),
    ]
    for copy in copies:
        copy.start()
    copies[0].wait()
    rest_ref[...] = jnp.dot(pick_ref[...], residual_ref[...], preferred_element_type=jnp.float32)
    for copy in copies[1:]:
        copy.wait()


def join_kernel(near_ref, across_ref, _, out_ref):
    slots = near_ref.shape[0]
    out_ref[:slots, :] = near_ref[...]
    out_ref[slots:, :] = across_ref[...]


def project_kernel(joined_ref, other_ref, weight_ref, out_ref, rows_ref):
    pair = joined_ref.shape[0]
    slots = pair // 2
    rows_ref[:pair, :] = joined_ref[...]
    rows_ref[pair:, :] = other_ref[...]
    product = jnp.dot(rows_ref[...], weight_ref[...], preferred_element_type=jnp.float32)
    product = product.astype(jnp.bfloat16)
    corner = 2 * lax.axis_index("mod") + lax.axis_index("fsdp")
    flip = lax.axis_index("tok") ^ corner
    for n, u in enumerate((0, 2, 1, 3)):
        out_ref[flip ^ u] = product[n * slots : (n + 1) * slots, :]


def split_high_low(value):
    high = value.astype(jnp.bfloat16).astype(jnp.float32)
    return high, value - high


def norm_kernel(kind_ref, rest_ref, partial_ref, three_ref, two_ref, one_ref, gain_ref, router_ref, _, out_ref):
    slots, columns = rest_ref.shape
    hidden = rest_ref[...] + partial_ref[0].astype(jnp.float32)
    for got_ref in (three_ref, two_ref, one_ref):
        hidden = hidden + got_ref[...].astype(jnp.float32)
    kind = kind_ref[0:1, 0:1]
    gains = gain_ref[...].astype(jnp.float32)
    gained = hidden * jnp.where(kind == 0.0, gains[0:1], gains[1:2])
    out_ref[:, :columns] = gained.astype(jnp.bfloat16)
    table = router_ref[...].astype(jnp.float32)
    pieces = []
    for e in range(2):
        second = (lax.axis_index("groups") ^ e) == 1
        text = jnp.where(second, table[1:2], table[0:1])
        image = jnp.where(second, table[3:4], table[2:3])
        weights = jnp.where(kind == 0.0, text, image)
        half = slots // 2
        pieces.append(jnp.sum(gained[e * half : (e + 1) * half] * weights, axis=1, keepdims=True))
    logits = jnp.concatenate(pieces, axis=0)
    squares = jnp.sum(hidden * hidden, axis=1, keepdims=True)
    lane = lax.broadcasted_iota(jnp.int32, (slots, STAT_COLS), 1)
    extra = jnp.where(lane == 4, kind, 0.0)
    for at, stat in enumerate(split_high_low(squares) + split_high_low(logits)):
        extra = jnp.where(lane == at, stat, extra)
    out_ref[:, columns:] = extra.astype(jnp.bfloat16)


def places(packed_refs, columns):
    side = lax.axis_index("mod")
    matches, found, before = [], [], 0
    for v, ref in enumerate(packed_refs):
        flag = ref[:TILE, columns:].astype(jnp.float32)[0, 4]
        kind = jnp.where(flag > 0.5, 1, 0)
        match = kind == side
        place = jnp.minimum(jnp.where(match, before, v - before), len(packed_refs) - 2)
        matches.append(match)
        found.append(place)
        before = before + jnp.where(match, 1, 0)
    return matches, found


def arrange_kernel(zero_ref, three_ref, two_ref, one_ref, _, *out_refs):
    packed_refs = (zero_ref, one_ref, two_ref, three_ref)
    capacity = zero_ref.shape[0] // 2
    for out_ref in out_refs:
        out_ref[...] = jnp.zeros(out_ref.shape, out_ref.dtype)
    matches, found = places(packed_refs, zero_ref.shape[1] - STAT_COLS)
    for ref, match, place in zip(packed_refs, matches, found):
        span = pl.ds(pl.multiple_of(place * capacity, capacity), capacity)
        for wanted, (own_ref, given_ref) in ((True, out_refs[:2]), (False, out_refs[2:])):

            @pl.when(match == wanted)
            def _():
                own_ref[span, :] = ref[:capacity, :]
                given_ref[span, :] = ref[capacity:, :]


def weights_times_rows(weight_refs, spans, rows, out_ref):
    at = 0
    for weight_ref, (first, last) in zip(weight_refs, spans):
        for start in range(first, last, STRIP):
            stop = min(start + STRIP, last)
            out_ref[at : at + stop - start, :] = lax.dot_general(
                weight_ref[start:stop, :], rows, (((1,), (1,)), ((), ())), preferred_element_type=jnp.float32
            ).astype(jnp.bfloat16)
            at += stop - start


def gate_kernel(side_far_ref, side_own_ref, far_ref, own_ref, *refs):
    weight_refs, out_ref, rows_ref = refs[:2], refs[-2], refs[-1]
    half = own_ref.shape[0]
    rows = rows_ref.shape[0]
    units = out_ref.shape[0] - TILE
    columns = rows_ref.shape[1] // 2
    rows_ref[2 * half :, :] = jnp.zeros((rows - 2 * half, 2 * columns), rows_ref.dtype)
    for side in range(2):

        @pl.when(lax.axis_index("mod") == side)
        def _():
            here, there = side * columns, (1 - side) * columns
            rows_ref[:half, here : here + columns] = own_ref[:, :columns]
            rows_ref[half : 2 * half, here : here + columns] = far_ref[:, :columns]
            rows_ref[:half, there : there + columns] = side_own_ref[:, :columns]
            rows_ref[half : 2 * half, there : there + columns] = side_far_ref[:, :columns]

    spans = [(0, ref.shape[0]) for ref in weight_refs]
    weights_times_rows(weight_refs, spans, rows_ref[...], out_ref)
    tails = [ref[:, columns:].astype(jnp.float32) for ref in (own_ref, side_own_ref, far_ref, side_far_ref)]
    unused = jnp.zeros((rows - 2 * half, STAT_COLS), jnp.float32)
    stat = jnp.concatenate([tails[0] + tails[1], tails[2] + tails[3], unused], axis=0).T
    squares = stat[0:1] + stat[1:2]
    logits = stat[2:3] + stat[3:4]
    at_row = lax.broadcasted_iota(jnp.int32, (TILE, rows), 0)
    extra = jnp.zeros((TILE, rows), jnp.float32)
    for at, piece in enumerate(split_high_low(squares) + split_high_low(logits)):
        extra = jnp.where(at_row == at, piece, extra)
    out_ref[units:, :] = extra.astype(jnp.bfloat16)


def up_kernel(spans, rows_ref, *refs):
    weights_times_rows(refs[:-1], spans, rows_ref[...], refs[-1])


def silu_kernel(gate_ref, gate_other_ref, out_ref, stat_ref):
    units = out_ref.shape[0]
    stat = gate_ref[units:, :].astype(jnp.float32) + gate_other_ref[units:, :].astype(jnp.float32)
    inverse = lax.rsqrt((stat[0:1] + stat[1:2]) / D + 1e-05)
    logits = (stat[2:3] + stat[3:4]) * inverse
    score = 1.0 / (1.0 + jnp.exp(-logits))
    at_row = lax.broadcasted_iota(jnp.int32, stat_ref.shape, 0)
    stat_ref[...] = jnp.where(at_row == 0, inverse, score)
    for start in range(0, units, STRIP):
        stop = min(start + STRIP, units)
        gate = gate_ref[start:stop, :].astype(jnp.float32) + gate_other_ref[start:stop, :].astype(jnp.float32)
        gate = gate * inverse
        out_ref[start:stop, :] = gate / (1.0 + jnp.exp(-gate)) * inverse


def down_kernel(
    silu_ref, stat_ref, up_ref, up_late_ref, other_ref, other_late_ref, first_ref, second_ref,
    kept_ref, far_ref, side_ref, side_far_ref, act_ref,
):
    units, rows = act_ref.shape
    at = 0
    for mine_ref, got_ref in ((up_ref, other_ref), (up_late_ref, other_late_ref)):
        for start in range(0, mine_ref.shape[0], STRIP):
            stop = min(start + STRIP, mine_ref.shape[0])
            up = mine_ref[start:stop, :].astype(jnp.float32) + got_ref[start:stop, :].astype(jnp.float32)
            span = slice(at, at + stop - start)
            act_ref[span, :] = (silu_ref[span, :] * up).astype(jnp.bfloat16)
            at += stop - start
    half, columns = kept_ref.shape
    score = jnp.broadcast_to(stat_ref[1:2, :], (rows, rows)).T[:, 0:1]
    first_units = first_ref.shape[0]
    for quarter in range(2):
        span = slice(quarter * columns, (quarter + 1) * columns)
        value = sum(
            lax.dot_general(
                act_ref[a:b, :], weight_ref[:, span], (((0,), (0,)), ((), ())), preferred_element_type=jnp.float32
            )
            for a, b, weight_ref in ((0, first_units, first_ref), (first_units, units, second_ref))
        )
        value = (value * score).astype(jnp.bfloat16)
        for across, (own_out, far_out) in enumerate(((kept_ref, far_ref), (side_ref, side_far_ref))):

            @pl.when((lax.axis_index("mod") ^ quarter) == across)
            def _():
                own_out[...] = value[:half]
                far_out[...] = value[half : 2 * half]


def merge_kernel(zero_ref, three_ref, two_ref, one_ref, kept_ref, side_ref, far_ref, side_far_ref, *out_refs):
    columns = kept_ref.shape[1]
    capacity = zero_ref.shape[0] // 2
    matches, found = places((zero_ref, one_ref, two_ref, three_ref), columns)
    for out_ref, match, place in zip(out_refs, matches, found):
        span = pl.ds(pl.multiple_of(place * capacity, capacity), capacity)
        for wanted, (first_ref, second_ref) in ((True, (kept_ref, far_ref)), (False, (side_ref, side_far_ref))):

            @pl.when(match == wanted)
            def _():
                out_ref[:capacity, :] = first_ref[span, :]
                out_ref[capacity:, :] = second_ref[span, :]


def scatter_kernel(pick_ref, zero_ref, one_ref, two_ref, three_ref, out_hbm, out_ref, semaphores):
    columns = out_ref.shape[1]
    pieces = semaphores.shape[0]
    width = columns // pieces
    copies = []
    for n in range(pieces):
        span = slice(n * width, (n + 1) * width)
        total = zero_ref[:, span].astype(jnp.float32)
        for got_ref in (three_ref, two_ref, one_ref):
            total = total + got_ref[:, span].astype(jnp.float32)
        result = 0.0
        for piece in split_high_low(total)[::-1]:
            result = result + lax.dot_general(
                pick_ref[...], piece.astype(jnp.bfloat16), (((0,), (0,)), ((), ())),
                preferred_element_type=jnp.float32,
            )
        out_ref[:, span] = result.astype(jnp.bfloat16)
        copies.append(pltpu.make_async_copy(out_ref.at[:, span], out_hbm.at[:, span], semaphores.at[n]))
        copies[-1].start()
    for copy in copies:
        copy.wait()


def paired_local(
    residual,
    context,
    out_proj,
    norm_gain,
    router_weight,
    block_modality,
    expert_rows,
    gate_weight,
    up_weight,
    down_weight,
):
    tokens, columns = residual.shape
    experts, capacity = expert_rows.shape
    slots = 2 * capacity
    half = 4 * capacity
    rows = 2 * half
    units, width = down_weight.shape[1:]
    assert block_modality.shape == (1,) and experts == 4 and gate_weight.shape[0] == 2
    picked, pick, kind = call(
        select_kernel,
        "select",
        [array(slots, columns), array(slots, tokens), array(8, STAT_COLS, dtype=jnp.float32)],
        [IN_HBM] * 2,
        [in_hbm(expert_rows), in_hbm(context)],
        scratch=[
            pltpu.SMEM((experts, capacity), jnp.int32),
            pltpu.VMEM((tokens, columns), jnp.bfloat16),
            pltpu.SemaphoreType.DMA((2,)),
        ],
    )
    plane = ("tok", "mod", "fsdp")
    to_first = [(t * 4 + q, q * 4 + t) for t in range(4) for q in range(4)]
    to_second = [(t * 4 + q, q * 4 + (t ^ 2)) for t in range(4) for q in range(4)]
    across = lax.ppermute(picked, plane, to_second)
    near = lax.ppermute(picked, plane, to_first)
    gate_units, up_units, down_units = [round(units * part / TILE) * TILE for part in (0.49, 0.45, 0.3)]
    gate_first, proj_held, rest = call(
        keep_gate_kernel,
        "keep_gate",
        [
            pltpu.VMEM((gate_units, width), jnp.bfloat16),
            pltpu.VMEM(out_proj.shape, jnp.bfloat16),
            array(slots, columns, dtype=jnp.float32),
        ],
        [ON_CHIP, IN_HBM, IN_HBM, IN_HBM],
        [pick, in_hbm(residual), in_hbm(gate_weight.swapaxes(1, 2)), in_hbm(out_proj)],
        scratch=[pltpu.VMEM((tokens, columns), jnp.bfloat16), pltpu.SemaphoreType.DMA((3,))],
        moved=units * width,
        limit=2 << 20,
    )
    joined = call(join_kernel, "join", array(half, columns), [ON_CHIP] * 3, [near, across, gate_first])
    other = lax.ppermute(joined, "fsdp", SWAP)
    partial = call(
        project_kernel,
        "project",
        array(4, slots, columns),
        [ON_CHIP] * 3,
        [joined, other, proj_held],
        scratch=[pltpu.VMEM((rows, columns), jnp.bfloat16)],
    )
    sums = [lax.ppermute(partial[v], "tok", crossed(2, v)) for v in (3, 2, 1)][::-1]
    gate_second, up_first = keep_on_chip(
        partial,
        [gate_weight.swapaxes(1, 2), up_weight.swapaxes(1, 2)],
        [(gate_units, units), (0, up_units)],
        "keep_more",
    )
    packed_columns = columns + STAT_COLS
    packed = call(
        norm_kernel,
        "norm",
        array(slots, packed_columns),
        [ON_CHIP] * 9,
        [kind, rest, partial, *sums[::-1], norm_gain, router_weight.T, up_first],
    )
    others = [lax.ppermute(packed, "tok", crossed(2, v)) for v in (3, 2, 1)][::-1]
    up_second, down_first = keep_on_chip(
        packed,
        [up_weight.swapaxes(1, 2), down_weight],
        [(up_units, units), (0, down_units)],
        "keep_up",
    )
    kept_slots = 3 * capacity
    own, to_far_rows, to_side_rows, to_corner_rows = call(
        arrange_kernel,
        "arrange",
        [array(kept_slots, packed_columns)] * 4,
        [ON_CHIP] * 5,
        [packed, *others[::-1], up_second],
    )
    both_axes = ("groups", "mod")
    side_far = lax.ppermute(to_corner_rows, both_axes, crossed(2, 3))
    far = lax.ppermute(to_far_rows, "groups", SWAP)
    side_own = lax.ppermute(to_side_rows, "mod", SWAP)

    (down_second,) = keep_on_chip(own, [down_weight], [(down_units, units)], "keep_down")

    flops = 2 * rows * units * width
    gate, gathered = call(
        gate_kernel,
        "gate",
        [array(units + TILE, rows), array(rows, width)],
        [ON_CHIP] * 7,
        [side_far, side_own, far, own, gate_first, gate_second, down_second],
        flops=flops,
    )
    late = units // 4 // TILE * TILE
    up_rest = units - up_units
    up_parts = [
        call(
            functools.partial(up_kernel, spans),
            "up",
            array(sum(b - a for a, b in spans), rows),
            [ON_CHIP] * (1 + len(spans)),
            [gathered, *weights],
            flops=flops * sum(b - a for a, b in spans) // units,
        )
        for spans, weights in (
            (((0, up_units), (0, up_rest - late)), (up_first, up_second)),
            (((up_rest - late, up_rest),), (up_second,)),
        )
    ]
    gate_other = lax.ppermute(gate, "fsdp", SWAP)
    up_others = [lax.ppermute(part, "fsdp", SWAP) for part in up_parts]
    silu, stat = call(
        silu_kernel,
        "silu",
        [array(units, rows, dtype=jnp.float32), array(8, rows, dtype=jnp.float32)],
        [ON_CHIP] * 2,
        [gate, gate_other],
        moved=8 * units * rows,
    )
    kept, to_far, to_side, to_side_far = call(
        down_kernel,
        "down",
        [array(kept_slots, columns)] * 4,
        [ON_CHIP] * 8,
        [silu, stat, *up_parts, *up_others, down_first, down_second],
        scratch=[pltpu.VMEM((units, rows), jnp.bfloat16)],
        flops=flops,
    )
    from_side_far = lax.ppermute(to_side_far, both_axes, crossed(2, 3))
    from_far = lax.ppermute(to_far, "groups", SWAP)
    from_side = lax.ppermute(to_side, "mod", SWAP)
    merged = call(
        merge_kernel,
        "merge",
        [array(slots, columns)] * 4,
        [ON_CHIP] * 8,
        [packed, *others[::-1], kept, from_side, from_far, from_side_far],
    )
    values = [merged[0]] + [lax.ppermute(merged[v], "tok", crossed(2, v)) for v in (1, 2, 3)]
    return pl.pallas_call(
        scatter_kernel,
        out_shape=pltpu.HBM((tokens, columns), jnp.bfloat16),
        in_specs=[ON_CHIP] * 5,
        out_specs=IN_HBM,
        scratch_shapes=[pltpu.VMEM((tokens, columns), jnp.bfloat16), pltpu.SemaphoreType.DMA((4,))],
        compiler_params=pltpu.CompilerParams(vmem_limit_bytes=8 << 20),
        name="scatter",
    )(pick, *values)


def solution(mesh):
    placed = (
        P(("groups", "tok"), ("fsdp", "mod")),
        P(("groups", "tok"), ("mod", "fsdp")),
        P("tok", ("fsdp", "mod")),
        P(None, ("fsdp", "mod")),
        P(("fsdp", "mod"), None),
        P(("groups", "tok")),
        P(None, ("groups", "tok")),
        P("mod", "fsdp", "tok"),
        P("mod", "fsdp", "tok"),
        P("mod", "tok", "fsdp"),
    )
    sizes = dict(n_tok=mesh.shape["tok"], n_mod=mesh.shape["mod"], n_fsdp=mesh.shape["fsdp"])
    paired = (
        mesh.shape["groups"] == 2
        and sizes == dict(n_tok=4, n_mod=2, n_fsdp=2)
    )
    body = paired_local if paired else functools.partial(local, **sizes)
    return jax.shard_map(
        body,
        mesh=mesh,
        in_specs=placed,
        out_specs=P(("groups", "tok"), ("fsdp", "mod")),
        check_vma=False,
    )
```

```python
import functools

import jax
import jax.numpy as jnp
from jax import lax
from jax.experimental import pallas as pl
from jax.experimental.pallas import tpu as pltpu
from jax.sharding import PartitionSpec as P

D = 4096
STAT_COLS = 128
FEW = 4


def ring(size, step):
    return [(i, (i + step) % size) for i in range(size)]


def reduce_tok(blocks, n_tok):
    if n_tok > FEW:
        return lax.psum_scatter(blocks, "tok", scatter_dimension=0, tiled=False).astype(jnp.float32)
    own = lax.axis_index("tok")
    total = lax.dynamic_index_in_dim(blocks, own, 0, False).astype(jnp.float32)
    for step in range(1, n_tok):
        sent = lax.dynamic_index_in_dim(blocks, (own + step) % n_tok, 0, False)
        total = total + lax.ppermute(sent, "tok", ring(n_tok, step)).astype(jnp.float32)
    return total


def gather_tok(rows, n_tok):
    if n_tok > FEW:
        return lax.all_gather(rows, "tok", axis=0, tiled=False)
    own = lax.axis_index("tok")
    result = jnp.zeros((n_tok,) + rows.shape, rows.dtype)
    result = lax.dynamic_update_index_in_dim(result, rows, own, 0)
    for step in range(1, n_tok):
        got = lax.ppermute(rows, "tok", ring(n_tok, step))
        result = lax.dynamic_update_index_in_dim(result, got, (own - step) % n_tok, 0)
    return result


def spread_context(rows, n_tok, n_mod, n_fsdp):
    if n_tok > FEW or n_tok != n_mod * n_fsdp:
        full = lax.all_gather(rows, ("mod", "fsdp"), axis=1, tiled=True)
        split = full.reshape(full.shape[0], n_tok, full.shape[1] // n_tok).transpose(1, 0, 2)
        return lax.all_to_all(split, "tok", 0, 0, tiled=True)
    pairs = [(t * n_tok + q, q * n_tok + t) for t in range(n_tok) for q in range(n_tok)]
    swapped = lax.ppermute(rows, ("tok", "mod", "fsdp"), pairs)
    return lax.all_gather(swapped, ("mod", "fsdp"), axis=0, tiled=False)


def local(
    residual,
    context,
    out_proj,
    norm_gain,
    router_weight,
    block_modality,
    expert_rows,
    gate_weight,
    up_weight,
    down_weight,
    *,
    n_tok,
    n_mod,
    n_fsdp,
):
    token_count = residual.shape[0]
    experts, capacity = expert_rows.shape
    kind_experts = experts // 2
    slots = kind_experts * capacity
    local_experts = gate_weight.shape[0]
    columns = residual.shape[1]
    assert block_modality.shape == (1,) and n_mod * local_experts == experts
    modality = block_modality[0]
    first = modality * kind_experts
    mod_index = lax.axis_index("mod")

    own_rows = lax.dynamic_slice_in_dim(expert_rows, first, kind_experts, 0).reshape(slots)
    pick = own_rows[:, None] == lax.iota(jnp.int32, token_count)[None, :]
    pick_half = pick.astype(jnp.bfloat16)
    picked_context = jnp.dot(pick_half, context, preferred_element_type=jnp.float32).astype(jnp.bfloat16)
    picked_residual = jnp.dot(pick_half, residual, preferred_element_type=jnp.float32)

    spread = spread_context(picked_context, n_tok, n_mod, n_fsdp)
    partial = jnp.einsum("tsk,kc->tsc", spread, out_proj, preferred_element_type=jnp.float32)
    hidden = picked_residual + reduce_tok(partial.astype(jnp.bfloat16), n_tok)

    gain_table = norm_gain.astype(jnp.float32)
    gained = hidden * jnp.where(modality == 0, gain_table[0], gain_table[1])[None, :]
    router = lax.dynamic_slice_in_dim(router_weight.astype(jnp.float32), first, kind_experts, 1)
    slot_router = jnp.repeat(router.T, capacity, axis=0)
    squares = jnp.sum(hidden * hidden, axis=1, keepdims=True)
    logits = jnp.sum(gained * slot_router, axis=1, keepdims=True)
    flag = jnp.broadcast_to(modality.astype(jnp.bfloat16), (slots, 1))
    stat_list = []
    for stat in (squares, logits):
        high = lax.reduce_precision(stat, 8, 7)
        stat_list += [high.astype(jnp.bfloat16), (stat - high).astype(jnp.bfloat16)]
    packed = jnp.concatenate(
        [gained.astype(jnp.bfloat16)] + stat_list
        + [flag, jnp.zeros((slots, STAT_COLS - 5), jnp.bfloat16)],
        axis=1,
    )

    everyone = gather_tok(packed, n_tok)
    both = lax.all_gather(everyone, "mod", axis=0, tiled=False)
    kind_first = (mod_index * local_experts) % kind_experts
    both = both.reshape(n_mod, n_tok, kind_experts, capacity, columns + STAT_COLS)
    mine = lax.dynamic_slice_in_dim(both, kind_first, local_experts, 2)
    piece = mine[..., :columns].transpose(2, 1, 3, 0, 4).reshape(
        local_experts, n_tok * capacity, n_mod * columns
    )
    tail = mine[..., columns : columns + 5].astype(jnp.float32)
    half_stats = jnp.sum(
        jnp.stack([tail[..., 0] + tail[..., 1], tail[..., 2] + tail[..., 3]], axis=-1), axis=0
    )
    stats = lax.psum(half_stats, "fsdp")
    flags = tail[0, :, :, :, 4]
    by_expert = stats.transpose(1, 0, 2, 3).reshape(local_experts, n_tok * capacity, 2)
    inverse = lax.rsqrt(by_expert[..., 0:1] / D + 1e-05)
    score = jax.nn.sigmoid(by_expert[..., 1:2] * inverse)

    gate_part = jnp.einsum("esd,edf->esf", piece, gate_weight, preferred_element_type=jnp.float32)
    up_part = jnp.einsum("esd,edf->esf", piece, up_weight, preferred_element_type=jnp.float32)
    gate_half = gate_part.astype(jnp.bfloat16)
    up_half = up_part.astype(jnp.bfloat16)
    if n_fsdp == 2:
        swap = [(0, 1), (1, 0)]
        gate_sum = gate_half.astype(jnp.float32) + lax.ppermute(gate_half, "fsdp", swap).astype(jnp.float32)
        up_sum = up_half.astype(jnp.float32) + lax.ppermute(up_half, "fsdp", swap).astype(jnp.float32)
    else:
        gate_sum = lax.psum(gate_half, "fsdp").astype(jnp.float32)
        up_sum = lax.psum(up_half, "fsdp").astype(jnp.float32)
    activation = (jax.nn.silu(gate_sum * inverse) * (up_sum * inverse)).astype(jnp.bfloat16)
    value = jnp.einsum("esf,efd->esd", activation, down_weight, preferred_element_type=jnp.float32)
    value = (value * score).astype(jnp.bfloat16)
    value = value.reshape(local_experts, n_tok, capacity, n_mod * columns).transpose(1, 0, 2, 3)

    own_kind = (mod_index * local_experts) // kind_experts
    valid = (flags == own_kind.astype(jnp.float32))[..., None]
    if n_mod == 2:
        value = value.reshape(n_tok, local_experts, capacity, n_mod, columns)
        kept = lax.dynamic_index_in_dim(value, mod_index, 3, False)
        sent = lax.dynamic_index_in_dim(value, 1 - mod_index, 3, False)
        got = lax.ppermute(sent, "mod", [(0, 1), (1, 0)])
        merged = jnp.where(valid, kept, got).reshape(n_tok, slots, columns)
    else:
        value = jnp.where(valid, value, jnp.zeros((), jnp.bfloat16))
        wide = jnp.zeros((n_tok, kind_experts, capacity, n_mod * columns), jnp.bfloat16)
        wide = lax.dynamic_update_slice_in_dim(wide, value, kind_first, 1)
        wide = wide.reshape(n_tok, slots, n_mod * columns)
        merged = lax.psum_scatter(wide, "mod", scatter_dimension=2, tiled=True)
    summed = reduce_tok(merged, n_tok)
    return jnp.dot(
        pick.astype(jnp.float32).T, summed, precision=lax.Precision.HIGHEST
    ).astype(jnp.bfloat16)


SWAP = [(0, 1), (1, 0)]
STRIP = 688
TILE = 16
ON_CHIP = pl.BlockSpec(memory_space=pltpu.VMEM)
IN_HBM = pl.BlockSpec(memory_space=pltpu.HBM)
ANYWHERE = pl.BlockSpec(memory_space=pl.ANY)


def crossed(bits, flip):
    return [(i, i ^ flip) for i in range(1 << bits)]


def call(kernel, name, outs, specs, args, scratch=(), flops=0, moved=0, limit=8 << 20):
    return pl.pallas_call(
        kernel,
        out_shape=outs,
        in_specs=specs,
        out_specs=jax.tree.map(lambda _: ON_CHIP, outs),
        scratch_shapes=list(scratch),
        compiler_params=pltpu.CompilerParams(vmem_limit_bytes=limit),
        cost_estimate=pl.CostEstimate(flops=flops, transcendentals=0, bytes_accessed=moved),
        name=name,
    )(*args)


def array(*shape, dtype=jnp.bfloat16):
    return jax.ShapeDtypeStruct(shape, dtype)


def keep_kernel(spans, after_ref, *refs):
    count = len(spans)
    weights, held, semaphores = refs[:count], refs[count : 2 * count], refs[-1]
    copies = [
        pltpu.make_async_copy(weight.at[lax.axis_index("groups"), a:b], to, semaphores.at[n])
        for n, (weight, to, (a, b)) in enumerate(zip(weights, held, spans))
    ]
    for copy in copies:
        copy.start()
    for copy in copies:
        copy.wait()


def in_hbm(value):
    return pltpu.with_memory_space_constraint(value, pltpu.HBM)


def keep_on_chip(after, weights, spans, name):
    return call(
        functools.partial(keep_kernel, spans),
        name,
        [pltpu.VMEM((b - a, weight.shape[2]), jnp.bfloat16) for weight, (a, b) in zip(weights, spans)],
        [ANYWHERE] + [IN_HBM] * len(spans),
        [after] + [in_hbm(weight) for weight in weights],
        scratch=[pltpu.SemaphoreType.DMA((len(spans),))],
        moved=sum(2 * (b - a) * weight.shape[2] for weight, (a, b) in zip(weights, spans)),
        limit=1 << 20,
    )


def keep_on_core_kernel(core, span, after_ref, weight_ref, *refs):
    held_ref, semaphore = refs[-2:]

    @pl.when(lax.axis_index("fsdp") == core)
    def _():
        a, b = span
        copy = pltpu.make_async_copy(weight_ref.at[lax.axis_index("groups"), a:b], held_ref, semaphore)
        copy.start()
        copy.wait()


def keep_on_core(core, after, weight, span, held, name):
    extra = [] if held is None else [held]
    return pl.pallas_call(
        functools.partial(keep_on_core_kernel, core, span),
        out_shape=pltpu.VMEM((span[1] - span[0], weight.shape[2]), jnp.bfloat16),
        in_specs=[ANYWHERE, IN_HBM] + [ON_CHIP] * len(extra),
        out_specs=ON_CHIP,
        input_output_aliases={2: 0} if extra else {},
        scratch_shapes=[pltpu.SemaphoreType.DMA(())],
        compiler_params=pltpu.CompilerParams(vmem_limit_bytes=1 << 20),
        cost_estimate=pl.CostEstimate(
            flops=0, transcendentals=0, bytes_accessed=2 * (span[1] - span[0]) * weight.shape[2]
        ),
        name=name,
    )(after, in_hbm(weight), *extra)


def select_kernel(
    rows_hbm, context_hbm, picked_ref, pick_ref, kind_ref, rows_ref, context_ref, semaphores
):
    rows_copy = pltpu.make_async_copy(rows_hbm, rows_ref, semaphores.at[0])
    context_copy = pltpu.make_async_copy(context_hbm, context_ref, semaphores.at[1])
    rows_copy.start()
    context_copy.start()
    rows_copy.wait()
    kind = jnp.where(jnp.maximum(rows_ref[2, 0], rows_ref[3, 0]) >= 0, 1, 0)
    kind_ref[...] = jnp.full(kind_ref.shape, kind, jnp.int32).astype(jnp.float32)
    capacity = rows_ref.shape[1]
    slots, tokens = pick_ref.shape
    row = lax.broadcasted_iota(jnp.int32, (slots, tokens), 0)
    token = lax.broadcasted_iota(jnp.int32, (slots, tokens), 1)
    wanted = jnp.full((slots, tokens), -1, jnp.int32)
    for e in range(2):
        expert = 2 * kind + (lax.axis_index("groups") ^ e)
        for s in range(capacity):
            wanted = jnp.where(row == e * capacity + s, rows_ref[expert, s], wanted)
    pick = jnp.where(wanted == token, 1.0, 0.0).astype(jnp.bfloat16)
    pick_ref[...] = pick
    context_copy.wait()
    picked_ref[...] = jnp.dot(pick, context_ref[...], preferred_element_type=jnp.float32).astype(jnp.bfloat16)


def keep_gate_kernel(
    pick_ref, residual_hbm, gate_ref, proj_ref, gate_held, proj_held, rest_ref, residual_ref, semaphores
):
    copies = [
        pltpu.make_async_copy(residual_hbm, residual_ref, semaphores.at[0]),
        pltpu.make_async_copy(proj_ref, proj_held, semaphores.at[1]),
        pltpu.make_async_copy(gate_ref.at[lax.axis_index("groups"), : gate_held.shape[0]], gate_held, semaphores.at[2]),
    ]
    for copy in copies:
        copy.start()
    copies[0].wait()
    rest_ref[...] = jnp.dot(pick_ref[...], residual_ref[...], preferred_element_type=jnp.float32)
    for copy in copies[1:]:
        copy.wait()


def join_kernel(near_ref, across_ref, _, out_ref):
    slots = near_ref.shape[0]
    out_ref[:slots, :] = near_ref[...]
    out_ref[slots:, :] = across_ref[...]


def project_kernel(joined_ref, other_ref, weight_ref, out_ref, rows_ref):
    pair = joined_ref.shape[0]
    slots = pair // 2
    rows_ref[:pair, :] = joined_ref[...]
    rows_ref[pair:, :] = other_ref[...]
    product = jnp.dot(rows_ref[...], weight_ref[...], preferred_element_type=jnp.float32)
    product = product.astype(jnp.bfloat16)
    corner = 2 * lax.axis_index("mod") + lax.axis_index("fsdp")
    flip = lax.axis_index("tok") ^ corner
    for n, u in enumerate((0, 2, 1, 3)):
        out_ref[flip ^ u] = product[n * slots : (n + 1) * slots, :]


def split_high_low(value):
    high = value.astype(jnp.bfloat16).astype(jnp.float32)
    return high, value - high


def norm_kernel(kind_ref, rest_ref, partial_ref, three_ref, two_ref, one_ref, gain_ref, router_ref, _, out_ref):
    slots, columns = rest_ref.shape
    hidden = rest_ref[...] + partial_ref[0].astype(jnp.float32)
    for got_ref in (three_ref, two_ref, one_ref):
        hidden = hidden + got_ref[...].astype(jnp.float32)
    kind = kind_ref[0:1, 0:1]
    gains = gain_ref[...].astype(jnp.float32)
    gained = hidden * jnp.where(kind == 0.0, gains[0:1], gains[1:2])
    out_ref[:, :columns] = gained.astype(jnp.bfloat16)
    table = router_ref[...].astype(jnp.float32)
    pieces = []
    for e in range(2):
        second = (lax.axis_index("groups") ^ e) == 1
        text = jnp.where(second, table[1:2], table[0:1])
        image = jnp.where(second, table[3:4], table[2:3])
        weights = jnp.where(kind == 0.0, text, image)
        half = slots // 2
        pieces.append(jnp.sum(gained[e * half : (e + 1) * half] * weights, axis=1, keepdims=True))
    logits = jnp.concatenate(pieces, axis=0)
    squares = jnp.sum(hidden * hidden, axis=1, keepdims=True)
    lane = lax.broadcasted_iota(jnp.int32, (slots, STAT_COLS), 1)
    extra = jnp.where(lane == 4, kind, 0.0)
    for at, stat in enumerate(split_high_low(squares) + split_high_low(logits)):
        extra = jnp.where(lane == at, stat, extra)
    out_ref[:, columns:] = extra.astype(jnp.bfloat16)


def places(packed_refs, columns):
    side = lax.axis_index("mod")
    matches, found, before = [], [], 0
    for v, ref in enumerate(packed_refs):
        flag = ref[:TILE, columns:].astype(jnp.float32)[0, 4]
        kind = jnp.where(flag > 0.5, 1, 0)
        match = kind == side
        place = jnp.minimum(jnp.where(match, before, v - before), len(packed_refs) - 2)
        matches.append(match)
        found.append(place)
        before = before + jnp.where(match, 1, 0)
    return matches, found


def arrange_kernel(zero_ref, three_ref, two_ref, one_ref, _, __, *out_refs):
    packed_refs = (zero_ref, one_ref, two_ref, three_ref)
    capacity = zero_ref.shape[0] // 2
    for out_ref in out_refs:
        out_ref[...] = jnp.zeros(out_ref.shape, out_ref.dtype)
    matches, found = places(packed_refs, zero_ref.shape[1] - STAT_COLS)
    for ref, match, place in zip(packed_refs, matches, found):
        span = pl.ds(pl.multiple_of(place * capacity, capacity), capacity)
        for wanted, (own_ref, given_ref) in ((True, out_refs[:2]), (False, out_refs[2:])):

            @pl.when(match == wanted)
            def _():
                own_ref[span, :] = ref[:capacity, :]
                given_ref[span, :] = ref[capacity:, :]


def weights_times_rows(weight_refs, spans, rows, out_ref):
    at = 0
    for weight_ref, (first, last) in zip(weight_refs, spans):
        for start in range(first, last, STRIP):
            stop = min(start + STRIP, last)
            out_ref[at : at + stop - start, :] = lax.dot_general(
                weight_ref[start:stop, :], rows, (((1,), (1,)), ((), ())), preferred_element_type=jnp.float32
            ).astype(jnp.bfloat16)
            at += stop - start


def gate_kernel(side_far_ref, side_own_ref, far_ref, own_ref, *refs):
    weight_refs, out_ref, rows_ref = refs[:2], refs[-2], refs[-1]
    half = own_ref.shape[0]
    rows = rows_ref.shape[0]
    units = out_ref.shape[0] - TILE
    columns = rows_ref.shape[1] // 2
    rows_ref[2 * half :, :] = jnp.zeros((rows - 2 * half, 2 * columns), rows_ref.dtype)
    for side in range(2):

        @pl.when(lax.axis_index("mod") == side)
        def _():
            here, there = side * columns, (1 - side) * columns
            rows_ref[:half, here : here + columns] = own_ref[:, :columns]
            rows_ref[half : 2 * half, here : here + columns] = far_ref[:, :columns]
            rows_ref[:half, there : there + columns] = side_own_ref[:, :columns]
            rows_ref[half : 2 * half, there : there + columns] = side_far_ref[:, :columns]

    spans = [(0, ref.shape[0]) for ref in weight_refs]
    weights_times_rows(weight_refs, spans, rows_ref[...], out_ref)
    tails = [ref[:, columns:].astype(jnp.float32) for ref in (own_ref, side_own_ref, far_ref, side_far_ref)]
    unused = jnp.zeros((rows - 2 * half, STAT_COLS), jnp.float32)
    stat = jnp.concatenate([tails[0] + tails[1], tails[2] + tails[3], unused], axis=0).T
    squares = stat[0:1] + stat[1:2]
    logits = stat[2:3] + stat[3:4]
    at_row = lax.broadcasted_iota(jnp.int32, (TILE, rows), 0)
    extra = jnp.zeros((TILE, rows), jnp.float32)
    for at, piece in enumerate(split_high_low(squares) + split_high_low(logits)):
        extra = jnp.where(at_row == at, piece, extra)
    out_ref[units:, :] = extra.astype(jnp.bfloat16)


def up_kernel(spans, rows_ref, *refs):
    weights_times_rows(refs[:-1], spans, rows_ref[...], refs[-1])


def silu_kernel(gate_ref, gate_other_ref, out_ref, stat_ref):
    units = out_ref.shape[0]
    stat = gate_ref[units:, :].astype(jnp.float32) + gate_other_ref[units:, :].astype(jnp.float32)
    inverse = lax.rsqrt((stat[0:1] + stat[1:2]) / D + 1e-05)
    logits = (stat[2:3] + stat[3:4]) * inverse
    score = 1.0 / (1.0 + jnp.exp(-logits))
    at_row = lax.broadcasted_iota(jnp.int32, stat_ref.shape, 0)
    stat_ref[...] = jnp.where(at_row == 0, inverse, score)
    for start in range(0, units, STRIP):
        stop = min(start + STRIP, units)
        gate = gate_ref[start:stop, :].astype(jnp.float32) + gate_other_ref[start:stop, :].astype(jnp.float32)
        gate = gate * inverse
        out_ref[start:stop, :] = gate / (1.0 + jnp.exp(-gate)) * inverse


def down_kernel(
    silu_ref, stat_ref, up_ref, up_late_ref, other_ref, other_late_ref, first_ref, second_ref,
    kept_ref, far_ref, side_ref, side_far_ref, act_ref,
):
    units, rows = act_ref.shape
    at = 0
    for mine_ref, got_ref in ((up_ref, other_ref), (up_late_ref, other_late_ref)):
        for start in range(0, mine_ref.shape[0], STRIP):
            stop = min(start + STRIP, mine_ref.shape[0])
            up = mine_ref[start:stop, :].astype(jnp.float32) + got_ref[start:stop, :].astype(jnp.float32)
            span = slice(at, at + stop - start)
            act_ref[span, :] = (silu_ref[span, :] * up).astype(jnp.bfloat16)
            at += stop - start
    half, columns = kept_ref.shape
    score = jnp.broadcast_to(stat_ref[1:2, :], (rows, rows)).T[:, 0:1]
    first_units = first_ref.shape[0]
    for quarter in range(2):
        span = slice(quarter * columns, (quarter + 1) * columns)
        value = sum(
            lax.dot_general(
                act_ref[a:b, :], weight_ref[:, span], (((0,), (0,)), ((), ())), preferred_element_type=jnp.float32
            )
            for a, b, weight_ref in ((0, first_units, first_ref), (first_units, units, second_ref))
        )
        value = (value * score).astype(jnp.bfloat16)
        for across, (own_out, far_out) in enumerate(((kept_ref, far_ref), (side_ref, side_far_ref))):

            @pl.when((lax.axis_index("mod") ^ quarter) == across)
            def _():
                own_out[...] = value[:half]
                far_out[...] = value[half : 2 * half]


def merge_kernel(zero_ref, three_ref, two_ref, one_ref, side_far_ref, side_ref, far_ref, kept_ref, *out_refs):
    columns = kept_ref.shape[1]
    capacity = zero_ref.shape[0] // 2
    matches, found = places((zero_ref, one_ref, two_ref, three_ref), columns)
    for out_ref, match, place in zip(out_refs, matches, found):
        span = pl.ds(pl.multiple_of(place * capacity, capacity), capacity)
        for wanted, (first_ref, second_ref) in ((True, (kept_ref, far_ref)), (False, (side_ref, side_far_ref))):

            @pl.when(match == wanted)
            def _():
                out_ref[:capacity, :] = first_ref[span, :]
                out_ref[capacity:, :] = second_ref[span, :]


def scatter_kernel(pick_ref, zero_ref, one_ref, two_ref, three_ref, out_hbm, out_ref, semaphores):
    columns = out_ref.shape[1]
    pieces = semaphores.shape[0]
    width = columns // pieces
    copies = []
    for n in range(pieces):
        span = slice(n * width, (n + 1) * width)
        total = zero_ref[:, span].astype(jnp.float32)
        for got_ref in (three_ref, two_ref, one_ref):
            total = total + got_ref[:, span].astype(jnp.float32)
        result = 0.0
        for piece in split_high_low(total)[::-1]:
            result = result + lax.dot_general(
                pick_ref[...], piece.astype(jnp.bfloat16), (((0,), (0,)), ((), ())),
                preferred_element_type=jnp.float32,
            )
        out_ref[:, span] = result.astype(jnp.bfloat16)
        copies.append(pltpu.make_async_copy(out_ref.at[:, span], out_hbm.at[:, span], semaphores.at[n]))
        copies[-1].start()
    for copy in copies:
        copy.wait()


def paired_local(
    residual,
    context,
    out_proj,
    norm_gain,
    router_weight,
    block_modality,
    expert_rows,
    gate_weight,
    up_weight,
    down_weight,
):
    tokens, columns = residual.shape
    experts, capacity = expert_rows.shape
    slots = 2 * capacity
    half = 4 * capacity
    rows = 2 * half
    units, width = down_weight.shape[1:]
    assert block_modality.shape == (1,) and experts == 4 and gate_weight.shape[0] == 2
    picked, pick, kind = call(
        select_kernel,
        "select",
        [array(slots, columns), array(slots, tokens), array(8, STAT_COLS, dtype=jnp.float32)],
        [IN_HBM] * 2,
        [in_hbm(expert_rows), in_hbm(context)],
        scratch=[
            pltpu.SMEM((experts, capacity), jnp.int32),
            pltpu.VMEM((tokens, columns), jnp.bfloat16),
            pltpu.SemaphoreType.DMA((2,)),
        ],
    )
    plane = ("tok", "mod", "fsdp")
    to_first = [(t * 4 + q, q * 4 + t) for t in range(4) for q in range(4)]
    to_second = [(t * 4 + q, q * 4 + (t ^ 2)) for t in range(4) for q in range(4)]
    across = lax.ppermute(picked, plane, to_second)
    near = lax.ppermute(picked, plane, to_first)
    gate_units, up_units, down_units = [round(units * part / TILE) * TILE for part in (0.58, 0.41, 0.24)]
    gate_first, proj_held, rest = call(
        keep_gate_kernel,
        "keep_gate",
        [
            pltpu.VMEM((gate_units, width), jnp.bfloat16),
            pltpu.VMEM(out_proj.shape, jnp.bfloat16),
            array(slots, columns, dtype=jnp.float32),
        ],
        [ON_CHIP, IN_HBM, IN_HBM, IN_HBM],
        [pick, in_hbm(residual), in_hbm(gate_weight.swapaxes(1, 2)), in_hbm(out_proj)],
        scratch=[pltpu.VMEM((tokens, columns), jnp.bfloat16), pltpu.SemaphoreType.DMA((3,))],
        moved=units * width,
        limit=2 << 20,
    )
    joined = call(join_kernel, "join", array(half, columns), [ON_CHIP] * 3, [near, across, gate_first])
    other = lax.ppermute(joined, "fsdp", SWAP)
    partial = call(
        project_kernel,
        "project",
        array(4, slots, columns),
        [ON_CHIP] * 3,
        [joined, other, proj_held],
        scratch=[pltpu.VMEM((rows, columns), jnp.bfloat16)],
    )
    sums = [lax.ppermute(partial[v], "tok", crossed(2, v)) for v in (3, 2, 1)][::-1]
    gate_second, up_first = keep_on_chip(
        partial,
        [gate_weight.swapaxes(1, 2), up_weight.swapaxes(1, 2)],
        [(gate_units, units), (0, up_units)],
        "keep_more",
    )
    packed_columns = columns + STAT_COLS
    packed = call(
        norm_kernel,
        "norm",
        array(slots, packed_columns),
        [ON_CHIP] * 9,
        [kind, rest, partial, *sums[::-1], norm_gain, router_weight.T, up_first],
    )
    others = [lax.ppermute(packed, "tok", crossed(2, v)) for v in (3, 2, 1)][::-1]
    up_second, down_first = keep_on_chip(
        packed,
        [up_weight.swapaxes(1, 2), down_weight],
        [(up_units, units), (0, down_units)],
        "keep_up",
    )
    down_early = keep_on_core(1, up_second, down_weight, (down_units, units), None, "keep_down_early")
    kept_slots = 3 * capacity
    own, to_far_rows, to_side_rows, to_corner_rows = call(
        arrange_kernel,
        "arrange",
        [array(kept_slots, packed_columns)] * 4,
        [ON_CHIP] * 6,
        [packed, *others[::-1], up_second, down_early],
    )
    both_axes = ("groups", "mod")
    side_far = lax.ppermute(to_corner_rows, both_axes, crossed(2, 3))
    far = lax.ppermute(to_far_rows, "groups", SWAP)
    side_own = lax.ppermute(to_side_rows, "mod", SWAP)

    down_second = keep_on_core(0, own, down_weight, (down_units, units), down_early, "keep_down")

    flops = 2 * rows * units * width
    gate, gathered = call(
        gate_kernel,
        "gate",
        [array(units + TILE, rows), array(rows, width)],
        [ON_CHIP] * 7,
        [side_far, side_own, far, own, gate_first, gate_second, down_second],
        flops=flops,
    )
    late = units // 4 // TILE * TILE
    up_rest = units - up_units
    up_parts = [
        call(
            functools.partial(up_kernel, spans),
            "up",
            array(sum(b - a for a, b in spans), rows),
            [ON_CHIP] * (1 + len(spans)),
            [gathered, *weights],
            flops=flops * sum(b - a for a, b in spans) // units,
        )
        for spans, weights in (
            (((0, up_units), (0, up_rest - late)), (up_first, up_second)),
            (((up_rest - late, up_rest),), (up_second,)),
        )
    ]
    gate_other = lax.ppermute(gate, "fsdp", SWAP)
    up_others = [lax.ppermute(part, "fsdp", SWAP) for part in up_parts]
    silu, stat = call(
        silu_kernel,
        "silu",
        [array(units, rows, dtype=jnp.float32), array(8, rows, dtype=jnp.float32)],
        [ON_CHIP] * 2,
        [gate, gate_other],
        moved=8 * units * rows,
    )
    kept, to_far, to_side, to_side_far = call(
        down_kernel,
        "down",
        [array(kept_slots, columns)] * 4,
        [ON_CHIP] * 8,
        [silu, stat, *up_parts, *up_others, down_first, down_second],
        scratch=[pltpu.VMEM((units, rows), jnp.bfloat16)],
        flops=flops,
    )
    from_side_far = lax.ppermute(to_side_far, both_axes, crossed(2, 3))
    from_far = lax.ppermute(to_far, "groups", SWAP)
    from_side = lax.ppermute(to_side, "mod", SWAP)
    merged = call(
        merge_kernel,
        "merge",
        [array(slots, columns)] * 4,
        [ON_CHIP] * 8,
        [packed, *others[::-1], from_side_far, from_side, from_far, kept],
    )
    values = [merged[0]] + [lax.ppermute(merged[v], "tok", crossed(2, v)) for v in (1, 2, 3)]
    return pl.pallas_call(
        scatter_kernel,
        out_shape=pltpu.HBM((tokens, columns), jnp.bfloat16),
        in_specs=[ON_CHIP] * 5,
        out_specs=IN_HBM,
        scratch_shapes=[pltpu.VMEM((tokens, columns), jnp.bfloat16), pltpu.SemaphoreType.DMA((4,))],
        compiler_params=pltpu.CompilerParams(vmem_limit_bytes=8 << 20),
        name="scatter",
    )(pick, *values)


def solution(mesh):
    placed = (
        P(("groups", "tok"), ("fsdp", "mod")),
        P(("groups", "tok"), ("mod", "fsdp")),
        P("tok", ("fsdp", "mod")),
        P(None, ("fsdp", "mod")),
        P(("fsdp", "mod"), None),
        P(("groups", "tok")),
        P(None, ("groups", "tok")),
        P("mod", "fsdp", "tok"),
        P("mod", "fsdp", "tok"),
        P("mod", "tok", "fsdp"),
    )
    sizes = dict(n_tok=mesh.shape["tok"], n_mod=mesh.shape["mod"], n_fsdp=mesh.shape["fsdp"])
    paired = (
        mesh.shape["groups"] == 2
        and sizes == dict(n_tok=4, n_mod=2, n_fsdp=2)
    )
    body = paired_local if paired else functools.partial(local, **sizes)
    return jax.shard_map(
        body,
        mesh=mesh,
        in_specs=placed,
        out_specs=P(("groups", "tok"), ("fsdp", "mod")),
        check_vma=False,
    )
```

```python
import functools

import jax
import jax.numpy as jnp
from jax import lax
from jax.experimental import pallas as pl
from jax.experimental.pallas import tpu as pltpu
from jax.sharding import PartitionSpec as P

D = 4096
STAT_COLS = 128
FEW = 4


def ring(size, step):
    return [(i, (i + step) % size) for i in range(size)]


def reduce_tok(blocks, n_tok):
    if n_tok > FEW:
        return lax.psum_scatter(blocks, "tok", scatter_dimension=0, tiled=False).astype(jnp.float32)
    own = lax.axis_index("tok")
    total = lax.dynamic_index_in_dim(blocks, own, 0, False).astype(jnp.float32)
    for step in range(1, n_tok):
        sent = lax.dynamic_index_in_dim(blocks, (own + step) % n_tok, 0, False)
        total = total + lax.ppermute(sent, "tok", ring(n_tok, step)).astype(jnp.float32)
    return total


def gather_tok(rows, n_tok):
    if n_tok > FEW:
        return lax.all_gather(rows, "tok", axis=0, tiled=False)
    own = lax.axis_index("tok")
    result = jnp.zeros((n_tok,) + rows.shape, rows.dtype)
    result = lax.dynamic_update_index_in_dim(result, rows, own, 0)
    for step in range(1, n_tok):
        got = lax.ppermute(rows, "tok", ring(n_tok, step))
        result = lax.dynamic_update_index_in_dim(result, got, (own - step) % n_tok, 0)
    return result


def spread_context(rows, n_tok, n_mod, n_fsdp):
    if n_tok > FEW or n_tok != n_mod * n_fsdp:
        full = lax.all_gather(rows, ("mod", "fsdp"), axis=1, tiled=True)
        split = full.reshape(full.shape[0], n_tok, full.shape[1] // n_tok).transpose(1, 0, 2)
        return lax.all_to_all(split, "tok", 0, 0, tiled=True)
    pairs = [(t * n_tok + q, q * n_tok + t) for t in range(n_tok) for q in range(n_tok)]
    swapped = lax.ppermute(rows, ("tok", "mod", "fsdp"), pairs)
    return lax.all_gather(swapped, ("mod", "fsdp"), axis=0, tiled=False)


def local(
    residual,
    context,
    out_proj,
    norm_gain,
    router_weight,
    block_modality,
    expert_rows,
    gate_weight,
    up_weight,
    down_weight,
    *,
    n_tok,
    n_mod,
    n_fsdp,
):
    token_count = residual.shape[0]
    experts, capacity = expert_rows.shape
    kind_experts = experts // 2
    slots = kind_experts * capacity
    local_experts = gate_weight.shape[0]
    columns = residual.shape[1]
    assert block_modality.shape == (1,) and n_mod * local_experts == experts
    modality = block_modality[0]
    first = modality * kind_experts
    mod_index = lax.axis_index("mod")

    own_rows = lax.dynamic_slice_in_dim(expert_rows, first, kind_experts, 0).reshape(slots)
    pick = own_rows[:, None] == lax.iota(jnp.int32, token_count)[None, :]
    pick_half = pick.astype(jnp.bfloat16)
    picked_context = jnp.dot(pick_half, context, preferred_element_type=jnp.float32).astype(jnp.bfloat16)
    picked_residual = jnp.dot(pick_half, residual, preferred_element_type=jnp.float32)

    spread = spread_context(picked_context, n_tok, n_mod, n_fsdp)
    partial = jnp.einsum("tsk,kc->tsc", spread, out_proj, preferred_element_type=jnp.float32)
    hidden = picked_residual + reduce_tok(partial.astype(jnp.bfloat16), n_tok)

    gain_table = norm_gain.astype(jnp.float32)
    gained = hidden * jnp.where(modality == 0, gain_table[0], gain_table[1])[None, :]
    router = lax.dynamic_slice_in_dim(router_weight.astype(jnp.float32), first, kind_experts, 1)
    slot_router = jnp.repeat(router.T, capacity, axis=0)
    squares = jnp.sum(hidden * hidden, axis=1, keepdims=True)
    logits = jnp.sum(gained * slot_router, axis=1, keepdims=True)
    flag = jnp.broadcast_to(modality.astype(jnp.bfloat16), (slots, 1))
    stat_list = []
    for stat in (squares, logits):
        high = lax.reduce_precision(stat, 8, 7)
        stat_list += [high.astype(jnp.bfloat16), (stat - high).astype(jnp.bfloat16)]
    packed = jnp.concatenate(
        [gained.astype(jnp.bfloat16)] + stat_list
        + [flag, jnp.zeros((slots, STAT_COLS - 5), jnp.bfloat16)],
        axis=1,
    )

    everyone = gather_tok(packed, n_tok)
    both = lax.all_gather(everyone, "mod", axis=0, tiled=False)
    kind_first = (mod_index * local_experts) % kind_experts
    both = both.reshape(n_mod, n_tok, kind_experts, capacity, columns + STAT_COLS)
    mine = lax.dynamic_slice_in_dim(both, kind_first, local_experts, 2)
    piece = mine[..., :columns].transpose(2, 1, 3, 0, 4).reshape(
        local_experts, n_tok * capacity, n_mod * columns
    )
    tail = mine[..., columns : columns + 5].astype(jnp.float32)
    half_stats = jnp.sum(
        jnp.stack([tail[..., 0] + tail[..., 1], tail[..., 2] + tail[..., 3]], axis=-1), axis=0
    )
    stats = lax.psum(half_stats, "fsdp")
    flags = tail[0, :, :, :, 4]
    by_expert = stats.transpose(1, 0, 2, 3).reshape(local_experts, n_tok * capacity, 2)
    inverse = lax.rsqrt(by_expert[..., 0:1] / D + 1e-05)
    score = jax.nn.sigmoid(by_expert[..., 1:2] * inverse)

    gate_part = jnp.einsum("esd,edf->esf", piece, gate_weight, preferred_element_type=jnp.float32)
    up_part = jnp.einsum("esd,edf->esf", piece, up_weight, preferred_element_type=jnp.float32)
    gate_half = gate_part.astype(jnp.bfloat16)
    up_half = up_part.astype(jnp.bfloat16)
    if n_fsdp == 2:
        swap = [(0, 1), (1, 0)]
        gate_sum = gate_half.astype(jnp.float32) + lax.ppermute(gate_half, "fsdp", swap).astype(jnp.float32)
        up_sum = up_half.astype(jnp.float32) + lax.ppermute(up_half, "fsdp", swap).astype(jnp.float32)
    else:
        gate_sum = lax.psum(gate_half, "fsdp").astype(jnp.float32)
        up_sum = lax.psum(up_half, "fsdp").astype(jnp.float32)
    activation = (jax.nn.silu(gate_sum * inverse) * (up_sum * inverse)).astype(jnp.bfloat16)
    value = jnp.einsum("esf,efd->esd", activation, down_weight, preferred_element_type=jnp.float32)
    value = (value * score).astype(jnp.bfloat16)
    value = value.reshape(local_experts, n_tok, capacity, n_mod * columns).transpose(1, 0, 2, 3)

    own_kind = (mod_index * local_experts) // kind_experts
    valid = (flags == own_kind.astype(jnp.float32))[..., None]
    if n_mod == 2:
        value = value.reshape(n_tok, local_experts, capacity, n_mod, columns)
        kept = lax.dynamic_index_in_dim(value, mod_index, 3, False)
        sent = lax.dynamic_index_in_dim(value, 1 - mod_index, 3, False)
        got = lax.ppermute(sent, "mod", [(0, 1), (1, 0)])
        merged = jnp.where(valid, kept, got).reshape(n_tok, slots, columns)
    else:
        value = jnp.where(valid, value, jnp.zeros((), jnp.bfloat16))
        wide = jnp.zeros((n_tok, kind_experts, capacity, n_mod * columns), jnp.bfloat16)
        wide = lax.dynamic_update_slice_in_dim(wide, value, kind_first, 1)
        wide = wide.reshape(n_tok, slots, n_mod * columns)
        merged = lax.psum_scatter(wide, "mod", scatter_dimension=2, tiled=True)
    summed = reduce_tok(merged, n_tok)
    return jnp.dot(
        pick.astype(jnp.float32).T, summed, precision=lax.Precision.HIGHEST
    ).astype(jnp.bfloat16)


SWAP = [(0, 1), (1, 0)]
STRIP = 688
TILE = 16
ON_CHIP = pl.BlockSpec(memory_space=pltpu.VMEM)
IN_HBM = pl.BlockSpec(memory_space=pltpu.HBM)
ANYWHERE = pl.BlockSpec(memory_space=pl.ANY)


def crossed(bits, flip):
    return [(i, i ^ flip) for i in range(1 << bits)]


def call(kernel, name, outs, specs, args, scratch=(), flops=0, moved=0, limit=8 << 20):
    return pl.pallas_call(
        kernel,
        out_shape=outs,
        in_specs=specs,
        out_specs=jax.tree.map(lambda _: ON_CHIP, outs),
        scratch_shapes=list(scratch),
        compiler_params=pltpu.CompilerParams(vmem_limit_bytes=limit),
        cost_estimate=pl.CostEstimate(flops=flops, transcendentals=0, bytes_accessed=moved),
        name=name,
    )(*args)


def array(*shape, dtype=jnp.bfloat16):
    return jax.ShapeDtypeStruct(shape, dtype)


def keep_kernel(spans, after_ref, *refs):
    count = len(spans)
    weights, held, semaphores = refs[:count], refs[count : 2 * count], refs[-1]
    copies = [
        pltpu.make_async_copy(weight.at[lax.axis_index("groups"), a:b], to, semaphores.at[n])
        for n, (weight, to, (a, b)) in enumerate(zip(weights, held, spans))
    ]
    for copy in copies:
        copy.start()
    for copy in copies:
        copy.wait()


def in_hbm(value):
    return pltpu.with_memory_space_constraint(value, pltpu.HBM)


def keep_on_chip(after, weights, spans, name):
    return call(
        functools.partial(keep_kernel, spans),
        name,
        [pltpu.VMEM((b - a, weight.shape[2]), jnp.bfloat16) for weight, (a, b) in zip(weights, spans)],
        [ANYWHERE] + [IN_HBM] * len(spans),
        [after] + [in_hbm(weight) for weight in weights],
        scratch=[pltpu.SemaphoreType.DMA((len(spans),))],
        moved=sum(2 * (b - a) * weight.shape[2] for weight, (a, b) in zip(weights, spans)),
        limit=1 << 20,
    )


def select_kernel(
    rows_hbm, context_hbm, picked_ref, pick_ref, kind_ref, rows_ref, context_ref, semaphores
):
    rows_copy = pltpu.make_async_copy(rows_hbm, rows_ref, semaphores.at[0])
    context_copy = pltpu.make_async_copy(context_hbm, context_ref, semaphores.at[1])
    rows_copy.start()
    context_copy.start()
    rows_copy.wait()
    kind = jnp.where(jnp.maximum(rows_ref[2, 0], rows_ref[3, 0]) >= 0, 1, 0)
    kind_ref[...] = jnp.full(kind_ref.shape, kind, jnp.int32).astype(jnp.float32)
    capacity = rows_ref.shape[1]
    slots, tokens = pick_ref.shape
    row = lax.broadcasted_iota(jnp.int32, (slots, tokens), 0)
    token = lax.broadcasted_iota(jnp.int32, (slots, tokens), 1)
    wanted = jnp.full((slots, tokens), -1, jnp.int32)
    for e in range(2):
        expert = 2 * kind + (lax.axis_index("groups") ^ e)
        for s in range(capacity):
            wanted = jnp.where(row == e * capacity + s, rows_ref[expert, s], wanted)
    pick = jnp.where(wanted == token, 1.0, 0.0).astype(jnp.bfloat16)
    pick_ref[...] = pick
    context_copy.wait()
    picked_ref[...] = jnp.dot(pick, context_ref[...], preferred_element_type=jnp.float32).astype(jnp.bfloat16)


def keep_gate_kernel(
    pick_ref, residual_hbm, gate_ref, proj_ref, gate_held, proj_held, rest_ref, residual_ref, semaphores
):
    copies = [
        pltpu.make_async_copy(residual_hbm, residual_ref, semaphores.at[0]),
        pltpu.make_async_copy(proj_ref, proj_held, semaphores.at[1]),
        pltpu.make_async_copy(gate_ref.at[lax.axis_index("groups"), : gate_held.shape[0]], gate_held, semaphores.at[2]),
    ]
    for copy in copies:
        copy.start()
    copies[0].wait()
    rest_ref[...] = jnp.dot(pick_ref[...], residual_ref[...], preferred_element_type=jnp.float32)
    for copy in copies[1:]:
        copy.wait()


def join_kernel(near_ref, across_ref, _, out_ref):
    slots = near_ref.shape[0]
    out_ref[:slots, :] = near_ref[...]
    out_ref[slots:, :] = across_ref[...]


def project_kernel(joined_ref, other_ref, weight_ref, out_ref, rows_ref):
    pair = joined_ref.shape[0]
    slots = pair // 2
    rows_ref[:pair, :] = joined_ref[...]
    rows_ref[pair:, :] = other_ref[...]
    product = jnp.dot(rows_ref[...], weight_ref[...], preferred_element_type=jnp.float32)
    product = product.astype(jnp.bfloat16)
    corner = 2 * lax.axis_index("mod") + lax.axis_index("fsdp")
    flip = lax.axis_index("tok") ^ corner
    for n, u in enumerate((0, 2, 1, 3)):
        out_ref[flip ^ u] = product[n * slots : (n + 1) * slots, :]


def split_high_low(value):
    high = value.astype(jnp.bfloat16).astype(jnp.float32)
    return high, value - high


def norm_kernel(kind_ref, rest_ref, partial_ref, three_ref, two_ref, one_ref, gain_ref, router_ref, _, out_ref):
    slots, columns = rest_ref.shape
    hidden = rest_ref[...] + partial_ref[0].astype(jnp.float32)
    for got_ref in (three_ref, two_ref, one_ref):
        hidden = hidden + got_ref[...].astype(jnp.float32)
    kind = kind_ref[0:1, 0:1]
    gains = gain_ref[...].astype(jnp.float32)
    gained = hidden * jnp.where(kind == 0.0, gains[0:1], gains[1:2])
    out_ref[:, :columns] = gained.astype(jnp.bfloat16)
    table = router_ref[...].astype(jnp.float32)
    pieces = []
    for e in range(2):
        second = (lax.axis_index("groups") ^ e) == 1
        text = jnp.where(second, table[1:2], table[0:1])
        image = jnp.where(second, table[3:4], table[2:3])
        weights = jnp.where(kind == 0.0, text, image)
        half = slots // 2
        pieces.append(jnp.sum(gained[e * half : (e + 1) * half] * weights, axis=1, keepdims=True))
    logits = jnp.concatenate(pieces, axis=0)
    squares = jnp.sum(hidden * hidden, axis=1, keepdims=True)
    lane = lax.broadcasted_iota(jnp.int32, (slots, STAT_COLS), 1)
    extra = jnp.where(lane == 4, kind, 0.0)
    for at, stat in enumerate(split_high_low(squares) + split_high_low(logits)):
        extra = jnp.where(lane == at, stat, extra)
    out_ref[:, columns:] = extra.astype(jnp.bfloat16)


def places(packed_refs, columns):
    side = lax.axis_index("mod")
    matches, found, before = [], [], 0
    for v, ref in enumerate(packed_refs):
        flag = ref[:TILE, columns:].astype(jnp.float32)[0, 4]
        kind = jnp.where(flag > 0.5, 1, 0)
        match = kind == side
        place = jnp.minimum(jnp.where(match, before, v - before), len(packed_refs) - 2)
        matches.append(match)
        found.append(place)
        before = before + jnp.where(match, 1, 0)
    return matches, found


def arrange_kernel(zero_ref, three_ref, two_ref, one_ref, _, *out_refs):
    packed_refs = (zero_ref, one_ref, two_ref, three_ref)
    capacity = zero_ref.shape[0] // 2
    for out_ref in out_refs:
        out_ref[...] = jnp.zeros(out_ref.shape, out_ref.dtype)
    matches, found = places(packed_refs, zero_ref.shape[1] - STAT_COLS)
    for ref, match, place in zip(packed_refs, matches, found):
        span = pl.ds(pl.multiple_of(place * capacity, capacity), capacity)
        for wanted, (own_ref, given_ref) in ((True, out_refs[:2]), (False, out_refs[2:])):

            @pl.when(match == wanted)
            def _():
                own_ref[span, :] = ref[:capacity, :]
                given_ref[span, :] = ref[capacity:, :]


def weights_times_rows(weight_refs, spans, rows, out_ref):
    at = 0
    for weight_ref, (first, last) in zip(weight_refs, spans):
        for start in range(first, last, STRIP):
            stop = min(start + STRIP, last)
            out_ref[at : at + stop - start, :] = lax.dot_general(
                weight_ref[start:stop, :], rows, (((1,), (1,)), ((), ())), preferred_element_type=jnp.float32
            ).astype(jnp.bfloat16)
            at += stop - start


def gate_kernel(side_far_ref, side_own_ref, far_ref, own_ref, *refs):
    weight_refs, out_ref, rows_ref = refs[:2], refs[-2], refs[-1]
    half = own_ref.shape[0]
    rows = rows_ref.shape[0]
    units = out_ref.shape[0] - TILE
    columns = rows_ref.shape[1] // 2
    rows_ref[2 * half :, :] = jnp.zeros((rows - 2 * half, 2 * columns), rows_ref.dtype)
    for side in range(2):

        @pl.when(lax.axis_index("mod") == side)
        def _():
            here, there = side * columns, (1 - side) * columns
            rows_ref[:half, here : here + columns] = own_ref[:, :columns]
            rows_ref[half : 2 * half, here : here + columns] = far_ref[:, :columns]
            rows_ref[:half, there : there + columns] = side_own_ref[:, :columns]
            rows_ref[half : 2 * half, there : there + columns] = side_far_ref[:, :columns]

    spans = [(0, ref.shape[0]) for ref in weight_refs]
    weights_times_rows(weight_refs, spans, rows_ref[...], out_ref)
    tails = [ref[:, columns:].astype(jnp.float32) for ref in (own_ref, side_own_ref, far_ref, side_far_ref)]
    unused = jnp.zeros((rows - 2 * half, STAT_COLS), jnp.float32)
    stat = jnp.concatenate([tails[0] + tails[1], tails[2] + tails[3], unused], axis=0).T
    squares = stat[0:1] + stat[1:2]
    logits = stat[2:3] + stat[3:4]
    at_row = lax.broadcasted_iota(jnp.int32, (TILE, rows), 0)
    extra = jnp.zeros((TILE, rows), jnp.float32)
    for at, piece in enumerate(split_high_low(squares) + split_high_low(logits)):
        extra = jnp.where(at_row == at, piece, extra)
    out_ref[units:, :] = extra.astype(jnp.bfloat16)


def up_kernel(spans, rows_ref, *refs):
    weights_times_rows(refs[:-1], spans, rows_ref[...], refs[-1])


def activation_kernel(gate_ref, gate_other_ref, up_ref, up_other_ref, act_ref, silu_ref, stat_ref):
    early = act_ref.shape[0]
    units = early + silu_ref.shape[0]
    stat = gate_ref[units:, :].astype(jnp.float32) + gate_other_ref[units:, :].astype(jnp.float32)
    inverse = lax.rsqrt((stat[0:1] + stat[1:2]) / D + 1e-05)
    logits = (stat[2:3] + stat[3:4]) * inverse
    score = 1.0 / (1.0 + jnp.exp(-logits))
    at_row = lax.broadcasted_iota(jnp.int32, stat_ref.shape, 0)
    stat_ref[...] = jnp.where(at_row == 0, inverse, score)
    for start in range(0, units, STRIP):
        stop = min(start + STRIP, units)
        gate = gate_ref[start:stop, :].astype(jnp.float32) + gate_other_ref[start:stop, :].astype(jnp.float32)
        gate = gate * inverse
        silu = gate / (1.0 + jnp.exp(-gate)) * inverse
        inside = max(0, min(stop, early) - start)
        if inside:
            span = slice(start, start + inside)
            up = up_ref[span, :].astype(jnp.float32) + up_other_ref[span, :].astype(jnp.float32)
            act_ref[span, :] = (silu[:inside] * up).astype(jnp.bfloat16)
        if start + inside < stop:
            silu_ref[start + inside - early : stop - early, :] = silu[inside:]


def down_kernel(
    act_early_ref, silu_ref, stat_ref, up_ref, other_ref, first_ref, second_ref,
    kept_ref, far_ref, side_ref, side_far_ref, act_ref,
):
    units, rows = act_ref.shape
    early = act_early_ref.shape[0]
    act_ref[:early, :] = act_early_ref[...]
    up = up_ref[...].astype(jnp.float32) + other_ref[...].astype(jnp.float32)
    act_ref[early:, :] = (silu_ref[...] * up).astype(jnp.bfloat16)
    half, columns = kept_ref.shape
    score = jnp.broadcast_to(stat_ref[1:2, :], (rows, rows)).T[:, 0:1]
    first_units = first_ref.shape[0]
    for quarter in range(2):
        span = slice(quarter * columns, (quarter + 1) * columns)
        value = sum(
            lax.dot_general(
                act_ref[a:b, :], weight_ref[:, span], (((0,), (0,)), ((), ())), preferred_element_type=jnp.float32
            )
            for a, b, weight_ref in ((0, first_units, first_ref), (first_units, units, second_ref))
        )
        value = (value * score).astype(jnp.bfloat16)
        for across, (own_out, far_out) in enumerate(((kept_ref, far_ref), (side_ref, side_far_ref))):

            @pl.when((lax.axis_index("mod") ^ quarter) == across)
            def _():
                own_out[...] = value[:half]
                far_out[...] = value[half : 2 * half]


def merge_kernel(zero_ref, three_ref, two_ref, one_ref, kept_ref, side_ref, far_ref, side_far_ref, *out_refs):
    columns = kept_ref.shape[1]
    capacity = zero_ref.shape[0] // 2
    matches, found = places((zero_ref, one_ref, two_ref, three_ref), columns)
    for out_ref, match, place in zip(out_refs, matches, found):
        span = pl.ds(pl.multiple_of(place * capacity, capacity), capacity)
        for wanted, (first_ref, second_ref) in ((True, (kept_ref, far_ref)), (False, (side_ref, side_far_ref))):

            @pl.when(match == wanted)
            def _():
                out_ref[:capacity, :] = first_ref[span, :]
                out_ref[capacity:, :] = second_ref[span, :]


def scatter_kernel(pick_ref, zero_ref, one_ref, two_ref, three_ref, out_hbm, out_ref, semaphores):
    columns = out_ref.shape[1]
    pieces = semaphores.shape[0]
    width = columns // pieces
    copies = []
    for n in range(pieces):
        span = slice(n * width, (n + 1) * width)
        total = zero_ref[:, span].astype(jnp.float32)
        for got_ref in (three_ref, two_ref, one_ref):
            total = total + got_ref[:, span].astype(jnp.float32)
        result = 0.0
        for piece in split_high_low(total)[::-1]:
            result = result + lax.dot_general(
                pick_ref[...], piece.astype(jnp.bfloat16), (((0,), (0,)), ((), ())),
                preferred_element_type=jnp.float32,
            )
        out_ref[:, span] = result.astype(jnp.bfloat16)
        copies.append(pltpu.make_async_copy(out_ref.at[:, span], out_hbm.at[:, span], semaphores.at[n]))
        copies[-1].start()
    for copy in copies:
        copy.wait()


def paired_local(
    residual,
    context,
    out_proj,
    norm_gain,
    router_weight,
    block_modality,
    expert_rows,
    gate_weight,
    up_weight,
    down_weight,
):
    tokens, columns = residual.shape
    experts, capacity = expert_rows.shape
    slots = 2 * capacity
    half = 4 * capacity
    rows = 2 * half
    units, width = down_weight.shape[1:]
    assert block_modality.shape == (1,) and experts == 4 and gate_weight.shape[0] == 2
    picked, pick, kind = call(
        select_kernel,
        "select",
        [array(slots, columns), array(slots, tokens), array(8, STAT_COLS, dtype=jnp.float32)],
        [IN_HBM] * 2,
        [in_hbm(expert_rows), in_hbm(context)],
        scratch=[
            pltpu.SMEM((experts, capacity), jnp.int32),
            pltpu.VMEM((tokens, columns), jnp.bfloat16),
            pltpu.SemaphoreType.DMA((2,)),
        ],
    )
    plane = ("tok", "mod", "fsdp")
    to_first = [(t * 4 + q, q * 4 + t) for t in range(4) for q in range(4)]
    to_second = [(t * 4 + q, q * 4 + (t ^ 2)) for t in range(4) for q in range(4)]
    across = lax.ppermute(picked, plane, to_second)
    near = lax.ppermute(picked, plane, to_first)
    gate_units, up_units, down_units = [round(units * part / TILE) * TILE for part in (0.54, 0.44, 0.27)]
    gate_first, proj_held, rest = call(
        keep_gate_kernel,
        "keep_gate",
        [
            pltpu.VMEM((gate_units, width), jnp.bfloat16),
            pltpu.VMEM(out_proj.shape, jnp.bfloat16),
            array(slots, columns, dtype=jnp.float32),
        ],
        [ON_CHIP, IN_HBM, IN_HBM, IN_HBM],
        [pick, in_hbm(residual), in_hbm(gate_weight.swapaxes(1, 2)), in_hbm(out_proj)],
        scratch=[pltpu.VMEM((tokens, columns), jnp.bfloat16), pltpu.SemaphoreType.DMA((3,))],
        moved=units * width,
        limit=2 << 20,
    )
    joined = call(join_kernel, "join", array(half, columns), [ON_CHIP] * 3, [near, across, gate_first])
    other = lax.ppermute(joined, "fsdp", SWAP)
    partial = call(
        project_kernel,
        "project",
        array(4, slots, columns),
        [ON_CHIP] * 3,
        [joined, other, proj_held],
        scratch=[pltpu.VMEM((rows, columns), jnp.bfloat16)],
    )
    sums = [lax.ppermute(partial[v], "tok", crossed(2, v)) for v in (3, 2, 1)][::-1]
    gate_second, up_first = keep_on_chip(
        partial,
        [gate_weight.swapaxes(1, 2), up_weight.swapaxes(1, 2)],
        [(gate_units, units), (0, up_units)],
        "keep_more",
    )
    packed_columns = columns + STAT_COLS
    packed = call(
        norm_kernel,
        "norm",
        array(slots, packed_columns),
        [ON_CHIP] * 9,
        [kind, rest, partial, *sums[::-1], norm_gain, router_weight.T, up_first],
    )
    others = [lax.ppermute(packed, "tok", crossed(2, v)) for v in (3, 2, 1)][::-1]
    up_second, down_first = keep_on_chip(
        packed,
        [up_weight.swapaxes(1, 2), down_weight],
        [(up_units, units), (0, down_units)],
        "keep_up",
    )
    kept_slots = 3 * capacity
    own, to_far_rows, to_side_rows, to_corner_rows = call(
        arrange_kernel,
        "arrange",
        [array(kept_slots, packed_columns)] * 4,
        [ON_CHIP] * 5,
        [packed, *others[::-1], up_second],
    )
    both_axes = ("groups", "mod")
    side_far = lax.ppermute(to_corner_rows, both_axes, crossed(2, 3))
    far = lax.ppermute(to_far_rows, "groups", SWAP)
    side_own = lax.ppermute(to_side_rows, "mod", SWAP)

    (down_second,) = keep_on_chip(own, [down_weight], [(down_units, units)], "keep_down")

    flops = 2 * rows * units * width
    gate, gathered = call(
        gate_kernel,
        "gate",
        [array(units + TILE, rows), array(rows, width)],
        [ON_CHIP] * 7,
        [side_far, side_own, far, own, gate_first, gate_second, down_second],
        flops=flops,
    )
    late = units // 4 // TILE * TILE
    up_rest = units - up_units
    up_parts = [
        call(
            functools.partial(up_kernel, spans),
            "up",
            array(sum(b - a for a, b in spans), rows),
            [ON_CHIP] * (1 + len(spans)),
            [gathered, *weights],
            flops=flops * sum(b - a for a, b in spans) // units,
        )
        for spans, weights in (
            (((0, up_units), (0, up_rest - late)), (up_first, up_second)),
            (((up_rest - late, up_rest),), (up_second,)),
        )
    ]
    gate_other = lax.ppermute(gate, "fsdp", SWAP)
    up_others = [lax.ppermute(part, "fsdp", SWAP) for part in up_parts]
    act_early, silu_late, stat = call(
        activation_kernel,
        "activation",
        [
            array(units - late, rows),
            array(late, rows, dtype=jnp.float32),
            array(8, rows, dtype=jnp.float32),
        ],
        [ON_CHIP] * 4,
        [gate, gate_other, up_parts[0], up_others[0]],
        moved=8 * units * rows,
    )
    kept, to_far, to_side, to_side_far = call(
        down_kernel,
        "down",
        [array(kept_slots, columns)] * 4,
        [ON_CHIP] * 7,
        [act_early, silu_late, stat, up_parts[1], up_others[1], down_first, down_second],
        scratch=[pltpu.VMEM((units, rows), jnp.bfloat16)],
        flops=flops,
    )
    from_side_far = lax.ppermute(to_side_far, both_axes, crossed(2, 3))
    from_far = lax.ppermute(to_far, "groups", SWAP)
    from_side = lax.ppermute(to_side, "mod", SWAP)
    merged = call(
        merge_kernel,
        "merge",
        [array(slots, columns)] * 4,
        [ON_CHIP] * 8,
        [packed, *others[::-1], kept, from_side, from_far, from_side_far],
    )
    values = [merged[0]] + [lax.ppermute(merged[v], "tok", crossed(2, v)) for v in (1, 2, 3)]
    return pl.pallas_call(
        scatter_kernel,
        out_shape=pltpu.HBM((tokens, columns), jnp.bfloat16),
        in_specs=[ON_CHIP] * 5,
        out_specs=IN_HBM,
        scratch_shapes=[pltpu.VMEM((tokens, columns), jnp.bfloat16), pltpu.SemaphoreType.DMA((4,))],
        compiler_params=pltpu.CompilerParams(vmem_limit_bytes=8 << 20),
        name="scatter",
    )(pick, *values)


def solution(mesh):
    placed = (
        P(("groups", "tok"), ("fsdp", "mod")),
        P(("groups", "tok"), ("mod", "fsdp")),
        P("tok", ("fsdp", "mod")),
        P(None, ("fsdp", "mod")),
        P(("fsdp", "mod"), None),
        P(("groups", "tok")),
        P(None, ("groups", "tok")),
        P("mod", "fsdp", "tok"),
        P("mod", "fsdp", "tok"),
        P("mod", "tok", "fsdp"),
    )
    sizes = dict(n_tok=mesh.shape["tok"], n_mod=mesh.shape["mod"], n_fsdp=mesh.shape["fsdp"])
    paired = (
        mesh.shape["groups"] == 2
        and sizes == dict(n_tok=4, n_mod=2, n_fsdp=2)
    )
    body = paired_local if paired else functools.partial(local, **sizes)
    return jax.shard_map(
        body,
        mesh=mesh,
        in_specs=placed,
        out_specs=P(("groups", "tok"), ("fsdp", "mod")),
        check_vma=False,
    )
```

```python
import functools

import jax
import jax.numpy as jnp
from jax import lax
from jax.experimental import pallas as pl
from jax.experimental.pallas import tpu as pltpu
from jax.sharding import PartitionSpec as P

D = 4096
STAT_COLS = 128
FEW = 4


def ring(size, step):
    return [(i, (i + step) % size) for i in range(size)]


def reduce_tok(blocks, n_tok):
    if n_tok > FEW:
        return lax.psum_scatter(blocks, "tok", scatter_dimension=0, tiled=False).astype(jnp.float32)
    own = lax.axis_index("tok")
    total = lax.dynamic_index_in_dim(blocks, own, 0, False).astype(jnp.float32)
    for step in range(1, n_tok):
        sent = lax.dynamic_index_in_dim(blocks, (own + step) % n_tok, 0, False)
        total = total + lax.ppermute(sent, "tok", ring(n_tok, step)).astype(jnp.float32)
    return total


def gather_tok(rows, n_tok):
    if n_tok > FEW:
        return lax.all_gather(rows, "tok", axis=0, tiled=False)
    own = lax.axis_index("tok")
    result = jnp.zeros((n_tok,) + rows.shape, rows.dtype)
    result = lax.dynamic_update_index_in_dim(result, rows, own, 0)
    for step in range(1, n_tok):
        got = lax.ppermute(rows, "tok", ring(n_tok, step))
        result = lax.dynamic_update_index_in_dim(result, got, (own - step) % n_tok, 0)
    return result


def spread_context(rows, n_tok, n_mod, n_fsdp):
    if n_tok > FEW or n_tok != n_mod * n_fsdp:
        full = lax.all_gather(rows, ("mod", "fsdp"), axis=1, tiled=True)
        split = full.reshape(full.shape[0], n_tok, full.shape[1] // n_tok).transpose(1, 0, 2)
        return lax.all_to_all(split, "tok", 0, 0, tiled=True)
    pairs = [(t * n_tok + q, q * n_tok + t) for t in range(n_tok) for q in range(n_tok)]
    swapped = lax.ppermute(rows, ("tok", "mod", "fsdp"), pairs)
    return lax.all_gather(swapped, ("mod", "fsdp"), axis=0, tiled=False)


def local(
    residual,
    context,
    out_proj,
    norm_gain,
    router_weight,
    block_modality,
    expert_rows,
    gate_weight,
    up_weight,
    down_weight,
    *,
    n_tok,
    n_mod,
    n_fsdp,
):
    token_count = residual.shape[0]
    experts, capacity = expert_rows.shape
    kind_experts = experts // 2
    slots = kind_experts * capacity
    local_experts = gate_weight.shape[0]
    columns = residual.shape[1]
    assert block_modality.shape == (1,) and n_mod * local_experts == experts
    modality = block_modality[0]
    first = modality * kind_experts
    mod_index = lax.axis_index("mod")

    own_rows = lax.dynamic_slice_in_dim(expert_rows, first, kind_experts, 0).reshape(slots)
    pick = own_rows[:, None] == lax.iota(jnp.int32, token_count)[None, :]
    pick_half = pick.astype(jnp.bfloat16)
    picked_context = jnp.dot(pick_half, context, preferred_element_type=jnp.float32).astype(jnp.bfloat16)
    picked_residual = jnp.dot(pick_half, residual, preferred_element_type=jnp.float32)

    spread = spread_context(picked_context, n_tok, n_mod, n_fsdp)
    partial = jnp.einsum("tsk,kc->tsc", spread, out_proj, preferred_element_type=jnp.float32)
    hidden = picked_residual + reduce_tok(partial.astype(jnp.bfloat16), n_tok)

    gain_table = norm_gain.astype(jnp.float32)
    gained = hidden * jnp.where(modality == 0, gain_table[0], gain_table[1])[None, :]
    router = lax.dynamic_slice_in_dim(router_weight.astype(jnp.float32), first, kind_experts, 1)
    slot_router = jnp.repeat(router.T, capacity, axis=0)
    squares = jnp.sum(hidden * hidden, axis=1, keepdims=True)
    logits = jnp.sum(gained * slot_router, axis=1, keepdims=True)
    flag = jnp.broadcast_to(modality.astype(jnp.bfloat16), (slots, 1))
    stat_list = []
    for stat in (squares, logits):
        high = lax.reduce_precision(stat, 8, 7)
        stat_list += [high.astype(jnp.bfloat16), (stat - high).astype(jnp.bfloat16)]
    packed = jnp.concatenate(
        [gained.astype(jnp.bfloat16)] + stat_list
        + [flag, jnp.zeros((slots, STAT_COLS - 5), jnp.bfloat16)],
        axis=1,
    )

    everyone = gather_tok(packed, n_tok)
    both = lax.all_gather(everyone, "mod", axis=0, tiled=False)
    kind_first = (mod_index * local_experts) % kind_experts
    both = both.reshape(n_mod, n_tok, kind_experts, capacity, columns + STAT_COLS)
    mine = lax.dynamic_slice_in_dim(both, kind_first, local_experts, 2)
    piece = mine[..., :columns].transpose(2, 1, 3, 0, 4).reshape(
        local_experts, n_tok * capacity, n_mod * columns
    )
    tail = mine[..., columns : columns + 5].astype(jnp.float32)
    half_stats = jnp.sum(
        jnp.stack([tail[..., 0] + tail[..., 1], tail[..., 2] + tail[..., 3]], axis=-1), axis=0
    )
    stats = lax.psum(half_stats, "fsdp")
    flags = tail[0, :, :, :, 4]
    by_expert = stats.transpose(1, 0, 2, 3).reshape(local_experts, n_tok * capacity, 2)
    inverse = lax.rsqrt(by_expert[..., 0:1] / D + 1e-05)
    score = jax.nn.sigmoid(by_expert[..., 1:2] * inverse)

    gate_part = jnp.einsum("esd,edf->esf", piece, gate_weight, preferred_element_type=jnp.float32)
    up_part = jnp.einsum("esd,edf->esf", piece, up_weight, preferred_element_type=jnp.float32)
    gate_half = gate_part.astype(jnp.bfloat16)
    up_half = up_part.astype(jnp.bfloat16)
    if n_fsdp == 2:
        swap = [(0, 1), (1, 0)]
        gate_sum = gate_half.astype(jnp.float32) + lax.ppermute(gate_half, "fsdp", swap).astype(jnp.float32)
        up_sum = up_half.astype(jnp.float32) + lax.ppermute(up_half, "fsdp", swap).astype(jnp.float32)
    else:
        gate_sum = lax.psum(gate_half, "fsdp").astype(jnp.float32)
        up_sum = lax.psum(up_half, "fsdp").astype(jnp.float32)
    activation = (jax.nn.silu(gate_sum * inverse) * (up_sum * inverse)).astype(jnp.bfloat16)
    value = jnp.einsum("esf,efd->esd", activation, down_weight, preferred_element_type=jnp.float32)
    value = (value * score).astype(jnp.bfloat16)
    value = value.reshape(local_experts, n_tok, capacity, n_mod * columns).transpose(1, 0, 2, 3)

    own_kind = (mod_index * local_experts) // kind_experts
    valid = (flags == own_kind.astype(jnp.float32))[..., None]
    if n_mod == 2:
        value = value.reshape(n_tok, local_experts, capacity, n_mod, columns)
        kept = lax.dynamic_index_in_dim(value, mod_index, 3, False)
        sent = lax.dynamic_index_in_dim(value, 1 - mod_index, 3, False)
        got = lax.ppermute(sent, "mod", [(0, 1), (1, 0)])
        merged = jnp.where(valid, kept, got).reshape(n_tok, slots, columns)
    else:
        value = jnp.where(valid, value, jnp.zeros((), jnp.bfloat16))
        wide = jnp.zeros((n_tok, kind_experts, capacity, n_mod * columns), jnp.bfloat16)
        wide = lax.dynamic_update_slice_in_dim(wide, value, kind_first, 1)
        wide = wide.reshape(n_tok, slots, n_mod * columns)
        merged = lax.psum_scatter(wide, "mod", scatter_dimension=2, tiled=True)
    summed = reduce_tok(merged, n_tok)
    return jnp.dot(
        pick.astype(jnp.float32).T, summed, precision=lax.Precision.HIGHEST
    ).astype(jnp.bfloat16)


SWAP = [(0, 1), (1, 0)]
STRIP = 688
TILE = 16
ON_CHIP = pl.BlockSpec(memory_space=pltpu.VMEM)
IN_HBM = pl.BlockSpec(memory_space=pltpu.HBM)
ANYWHERE = pl.BlockSpec(memory_space=pl.ANY)


def crossed(bits, flip):
    return [(i, i ^ flip) for i in range(1 << bits)]


def call(kernel, name, outs, specs, args, scratch=(), flops=0, moved=0, limit=8 << 20):
    return pl.pallas_call(
        kernel,
        out_shape=outs,
        in_specs=specs,
        out_specs=jax.tree.map(lambda _: ON_CHIP, outs),
        scratch_shapes=list(scratch),
        compiler_params=pltpu.CompilerParams(vmem_limit_bytes=limit),
        cost_estimate=pl.CostEstimate(flops=flops, transcendentals=0, bytes_accessed=moved),
        name=name,
    )(*args)


def array(*shape, dtype=jnp.bfloat16):
    return jax.ShapeDtypeStruct(shape, dtype)


def keep_kernel(spans, after_ref, *refs):
    count = len(spans)
    weights, held, semaphores = refs[:count], refs[count : 2 * count], refs[-1]
    copies = [
        pltpu.make_async_copy(weight.at[lax.axis_index("groups"), a:b], to, semaphores.at[n])
        for n, (weight, to, (a, b)) in enumerate(zip(weights, held, spans))
    ]
    for copy in copies:
        copy.start()
    for copy in copies:
        copy.wait()


def in_hbm(value):
    return pltpu.with_memory_space_constraint(value, pltpu.HBM)


def keep_on_chip(after, weights, spans, name):
    return call(
        functools.partial(keep_kernel, spans),
        name,
        [pltpu.VMEM((b - a, weight.shape[2]), jnp.bfloat16) for weight, (a, b) in zip(weights, spans)],
        [ANYWHERE] + [IN_HBM] * len(spans),
        [after] + [in_hbm(weight) for weight in weights],
        scratch=[pltpu.SemaphoreType.DMA((len(spans),))],
        moved=sum(2 * (b - a) * weight.shape[2] for weight, (a, b) in zip(weights, spans)),
        limit=1 << 20,
    )


def select_kernel(
    rows_hbm, context_hbm, picked_ref, pick_ref, kind_ref, rows_ref, context_ref, semaphores
):
    rows_copy = pltpu.make_async_copy(rows_hbm, rows_ref, semaphores.at[0])
    context_copy = pltpu.make_async_copy(context_hbm, context_ref, semaphores.at[1])
    rows_copy.start()
    context_copy.start()
    rows_copy.wait()
    kind = jnp.where(jnp.maximum(rows_ref[2, 0], rows_ref[3, 0]) >= 0, 1, 0)
    kind_ref[...] = jnp.full(kind_ref.shape, kind, jnp.int32).astype(jnp.float32)
    capacity = rows_ref.shape[1]
    slots, tokens = pick_ref.shape
    row = lax.broadcasted_iota(jnp.int32, (slots, tokens), 0)
    token = lax.broadcasted_iota(jnp.int32, (slots, tokens), 1)
    wanted = jnp.full((slots, tokens), -1, jnp.int32)
    for e in range(2):
        expert = 2 * kind + (lax.axis_index("groups") ^ e)
        for s in range(capacity):
            wanted = jnp.where(row == e * capacity + s, rows_ref[expert, s], wanted)
    pick = jnp.where(wanted == token, 1.0, 0.0).astype(jnp.bfloat16)
    pick_ref[...] = pick
    context_copy.wait()
    picked_ref[...] = jnp.dot(pick, context_ref[...], preferred_element_type=jnp.float32).astype(jnp.bfloat16)


def keep_gate_kernel(
    pick_ref, residual_hbm, gate_ref, proj_ref, gate_held, proj_held, rest_ref, residual_ref, semaphores
):
    copies = [
        pltpu.make_async_copy(residual_hbm, residual_ref, semaphores.at[0]),
        pltpu.make_async_copy(proj_ref, proj_held, semaphores.at[1]),
        pltpu.make_async_copy(gate_ref.at[lax.axis_index("groups"), : gate_held.shape[0]], gate_held, semaphores.at[2]),
    ]
    for copy in copies:
        copy.start()
    copies[0].wait()
    rest_ref[...] = jnp.dot(pick_ref[...], residual_ref[...], preferred_element_type=jnp.float32)
    for copy in copies[1:]:
        copy.wait()


def pass_kernel(rows_ref, _, out_ref):
    out_ref[...] = rows_ref[...]


def project_kernel(*refs):
    block_refs, (weight_ref, out_ref, rows_ref) = refs[:4], refs[4:]
    slots = block_refs[0].shape[0]
    for u, block_ref in enumerate(block_refs):
        rows_ref[u * slots : (u + 1) * slots, :] = block_ref[...]
    product = jnp.dot(rows_ref[...], weight_ref[...], preferred_element_type=jnp.float32)
    product = product.astype(jnp.bfloat16)
    corner = 2 * lax.axis_index("mod") + lax.axis_index("fsdp")
    flip = lax.axis_index("tok") ^ corner
    for u in range(4):
        out_ref[flip ^ u] = product[u * slots : (u + 1) * slots, :]


def split_high_low(value):
    high = value.astype(jnp.bfloat16).astype(jnp.float32)
    return high, value - high


def norm_kernel(kind_ref, rest_ref, partial_ref, three_ref, two_ref, one_ref, gain_ref, router_ref, _, out_ref):
    slots, columns = rest_ref.shape
    hidden = rest_ref[...] + partial_ref[0].astype(jnp.float32)
    for got_ref in (three_ref, two_ref, one_ref):
        hidden = hidden + got_ref[...].astype(jnp.float32)
    kind = kind_ref[0:1, 0:1]
    gains = gain_ref[...].astype(jnp.float32)
    gained = hidden * jnp.where(kind == 0.0, gains[0:1], gains[1:2])
    out_ref[:, :columns] = gained.astype(jnp.bfloat16)
    table = router_ref[...].astype(jnp.float32)
    pieces = []
    for e in range(2):
        second = (lax.axis_index("groups") ^ e) == 1
        text = jnp.where(second, table[1:2], table[0:1])
        image = jnp.where(second, table[3:4], table[2:3])
        weights = jnp.where(kind == 0.0, text, image)
        half = slots // 2
        pieces.append(jnp.sum(gained[e * half : (e + 1) * half] * weights, axis=1, keepdims=True))
    logits = jnp.concatenate(pieces, axis=0)
    squares = jnp.sum(hidden * hidden, axis=1, keepdims=True)
    lane = lax.broadcasted_iota(jnp.int32, (slots, STAT_COLS), 1)
    extra = jnp.where(lane == 4, kind, 0.0)
    for at, stat in enumerate(split_high_low(squares) + split_high_low(logits)):
        extra = jnp.where(lane == at, stat, extra)
    out_ref[:, columns:] = extra.astype(jnp.bfloat16)


def places(packed_refs, columns):
    side = lax.axis_index("mod")
    matches, found, before = [], [], 0
    for v, ref in enumerate(packed_refs):
        flag = ref[:TILE, columns:].astype(jnp.float32)[0, 4]
        kind = jnp.where(flag > 0.5, 1, 0)
        match = kind == side
        place = jnp.minimum(jnp.where(match, before, v - before), len(packed_refs) - 2)
        matches.append(match)
        found.append(place)
        before = before + jnp.where(match, 1, 0)
    return matches, found


def arrange_kernel(zero_ref, three_ref, two_ref, one_ref, _, *out_refs):
    packed_refs = (zero_ref, one_ref, two_ref, three_ref)
    capacity = zero_ref.shape[0] // 2
    for out_ref in out_refs:
        out_ref[...] = jnp.zeros(out_ref.shape, out_ref.dtype)
    matches, found = places(packed_refs, zero_ref.shape[1] - STAT_COLS)
    for ref, match, place in zip(packed_refs, matches, found):
        span = pl.ds(pl.multiple_of(place * capacity, capacity), capacity)
        for wanted, (own_ref, given_ref) in ((True, out_refs[:2]), (False, out_refs[2:])):

            @pl.when(match == wanted)
            def _():
                own_ref[span, :] = ref[:capacity, :]
                given_ref[span, :] = ref[capacity:, :]


def weights_times_rows(weight_refs, spans, rows, out_ref):
    at = 0
    for weight_ref, (first, last) in zip(weight_refs, spans):
        for start in range(first, last, STRIP):
            stop = min(start + STRIP, last)
            out_ref[at : at + stop - start, :] = lax.dot_general(
                weight_ref[start:stop, :], rows, (((1,), (1,)), ((), ())), preferred_element_type=jnp.float32
            ).astype(jnp.bfloat16)
            at += stop - start


def gate_kernel(side_far_ref, side_own_ref, far_ref, own_ref, *refs):
    weight_refs, out_ref, rows_ref = refs[:2], refs[-2], refs[-1]
    half = own_ref.shape[0]
    rows = rows_ref.shape[0]
    units = out_ref.shape[0] - TILE
    columns = rows_ref.shape[1] // 2
    rows_ref[2 * half :, :] = jnp.zeros((rows - 2 * half, 2 * columns), rows_ref.dtype)
    for side in range(2):

        @pl.when(lax.axis_index("mod") == side)
        def _():
            here, there = side * columns, (1 - side) * columns
            rows_ref[:half, here : here + columns] = own_ref[:, :columns]
            rows_ref[half : 2 * half, here : here + columns] = far_ref[:, :columns]
            rows_ref[:half, there : there + columns] = side_own_ref[:, :columns]
            rows_ref[half : 2 * half, there : there + columns] = side_far_ref[:, :columns]

    spans = [(0, ref.shape[0]) for ref in weight_refs]
    weights_times_rows(weight_refs, spans, rows_ref[...], out_ref)
    tails = [ref[:, columns:].astype(jnp.float32) for ref in (own_ref, side_own_ref, far_ref, side_far_ref)]
    unused = jnp.zeros((rows - 2 * half, STAT_COLS), jnp.float32)
    stat = jnp.concatenate([tails[0] + tails[1], tails[2] + tails[3], unused], axis=0).T
    squares = stat[0:1] + stat[1:2]
    logits = stat[2:3] + stat[3:4]
    at_row = lax.broadcasted_iota(jnp.int32, (TILE, rows), 0)
    extra = jnp.zeros((TILE, rows), jnp.float32)
    for at, piece in enumerate(split_high_low(squares) + split_high_low(logits)):
        extra = jnp.where(at_row == at, piece, extra)
    out_ref[units:, :] = extra.astype(jnp.bfloat16)


def up_kernel(spans, rows_ref, *refs):
    weights_times_rows(refs[:-1], spans, rows_ref[...], refs[-1])


def activation_kernel(gate_ref, gate_other_ref, up_ref, up_other_ref, act_ref, silu_ref, stat_ref):
    early = act_ref.shape[0]
    units = early + silu_ref.shape[0]
    stat = gate_ref[units:, :].astype(jnp.float32) + gate_other_ref[units:, :].astype(jnp.float32)
    inverse = lax.rsqrt((stat[0:1] + stat[1:2]) / D + 1e-05)
    logits = (stat[2:3] + stat[3:4]) * inverse
    score = 1.0 / (1.0 + jnp.exp(-logits))
    at_row = lax.broadcasted_iota(jnp.int32, stat_ref.shape, 0)
    stat_ref[...] = jnp.where(at_row == 0, inverse, score)
    for start in range(0, units, STRIP):
        stop = min(start + STRIP, units)
        gate = gate_ref[start:stop, :].astype(jnp.float32) + gate_other_ref[start:stop, :].astype(jnp.float32)
        gate = gate * inverse
        silu = gate / (1.0 + jnp.exp(-gate)) * inverse
        inside = max(0, min(stop, early) - start)
        if inside:
            span = slice(start, start + inside)
            up = up_ref[span, :].astype(jnp.float32) + up_other_ref[span, :].astype(jnp.float32)
            act_ref[span, :] = (silu[:inside] * up).astype(jnp.bfloat16)
        if start + inside < stop:
            silu_ref[start + inside - early : stop - early, :] = silu[inside:]


def down_kernel(
    act_early_ref, silu_ref, stat_ref, up_ref, other_ref, first_ref, second_ref,
    kept_ref, far_ref, side_ref, side_far_ref, act_ref,
):
    units, rows = act_ref.shape
    early = act_early_ref.shape[0]
    act_ref[:early, :] = act_early_ref[...]
    up = up_ref[...].astype(jnp.float32) + other_ref[...].astype(jnp.float32)
    act_ref[early:, :] = (silu_ref[...] * up).astype(jnp.bfloat16)
    half, columns = kept_ref.shape
    score = jnp.broadcast_to(stat_ref[1:2, :], (rows, rows)).T[:, 0:1]
    first_units = first_ref.shape[0]
    for quarter in range(2):
        span = slice(quarter * columns, (quarter + 1) * columns)
        value = sum(
            lax.dot_general(
                act_ref[a:b, :], weight_ref[:, span], (((0,), (0,)), ((), ())), preferred_element_type=jnp.float32
            )
            for a, b, weight_ref in ((0, first_units, first_ref), (first_units, units, second_ref))
        )
        value = (value * score).astype(jnp.bfloat16)
        for across, (own_out, far_out) in enumerate(((kept_ref, far_ref), (side_ref, side_far_ref))):

            @pl.when((lax.axis_index("mod") ^ quarter) == across)
            def _():
                own_out[...] = value[:half]
                far_out[...] = value[half : 2 * half]


def merge_kernel(zero_ref, three_ref, two_ref, one_ref, kept_ref, side_ref, far_ref, side_far_ref, *out_refs):
    columns = kept_ref.shape[1]
    capacity = zero_ref.shape[0] // 2
    matches, found = places((zero_ref, one_ref, two_ref, three_ref), columns)
    for out_ref, match, place in zip(out_refs, matches, found):
        span = pl.ds(pl.multiple_of(place * capacity, capacity), capacity)
        for wanted, (first_ref, second_ref) in ((True, (kept_ref, far_ref)), (False, (side_ref, side_far_ref))):

            @pl.when(match == wanted)
            def _():
                out_ref[:capacity, :] = first_ref[span, :]
                out_ref[capacity:, :] = second_ref[span, :]


def scatter_kernel(pick_ref, zero_ref, one_ref, two_ref, three_ref, out_hbm, out_ref, semaphores):
    columns = out_ref.shape[1]
    pieces = semaphores.shape[0]
    width = columns // pieces
    copies = []
    for n in range(pieces):
        span = slice(n * width, (n + 1) * width)
        total = zero_ref[:, span].astype(jnp.float32)
        for got_ref in (three_ref, two_ref, one_ref):
            total = total + got_ref[:, span].astype(jnp.float32)
        result = 0.0
        for piece in split_high_low(total)[::-1]:
            result = result + lax.dot_general(
                pick_ref[...], piece.astype(jnp.bfloat16), (((0,), (0,)), ((), ())),
                preferred_element_type=jnp.float32,
            )
        out_ref[:, span] = result.astype(jnp.bfloat16)
        copies.append(pltpu.make_async_copy(out_ref.at[:, span], out_hbm.at[:, span], semaphores.at[n]))
        copies[-1].start()
    for copy in copies:
        copy.wait()


def paired_local(
    residual,
    context,
    out_proj,
    norm_gain,
    router_weight,
    block_modality,
    expert_rows,
    gate_weight,
    up_weight,
    down_weight,
):
    tokens, columns = residual.shape
    experts, capacity = expert_rows.shape
    slots = 2 * capacity
    half = 4 * capacity
    rows = 2 * half
    units, width = down_weight.shape[1:]
    assert block_modality.shape == (1,) and experts == 4 and gate_weight.shape[0] == 2
    picked, pick, kind = call(
        select_kernel,
        "select",
        [array(slots, columns), array(slots, tokens), array(8, STAT_COLS, dtype=jnp.float32)],
        [IN_HBM] * 2,
        [in_hbm(expert_rows), in_hbm(context)],
        scratch=[
            pltpu.SMEM((experts, capacity), jnp.int32),
            pltpu.VMEM((tokens, columns), jnp.bfloat16),
            pltpu.SemaphoreType.DMA((2,)),
        ],
    )
    turned = [(t * 4 + q, q * 4 + t) for t in range(4) for q in range(4)]
    near = lax.ppermute(picked, ("tok", "mod", "fsdp"), turned)
    gate_units, up_units, down_units = [round(units * part / TILE) * TILE for part in (0.54, 0.44, 0.27)]
    gate_first, proj_held, rest = call(
        keep_gate_kernel,
        "keep_gate",
        [
            pltpu.VMEM((gate_units, width), jnp.bfloat16),
            pltpu.VMEM(out_proj.shape, jnp.bfloat16),
            array(slots, columns, dtype=jnp.float32),
        ],
        [ON_CHIP, IN_HBM, IN_HBM, IN_HBM],
        [pick, in_hbm(residual), in_hbm(gate_weight.swapaxes(1, 2)), in_hbm(out_proj)],
        scratch=[pltpu.VMEM((tokens, columns), jnp.bfloat16), pltpu.SemaphoreType.DMA((3,))],
        moved=units * width,
        limit=2 << 20,
    )
    block = call(pass_kernel, "pass", array(slots, columns), [ON_CHIP] * 2, [near, gate_first])
    plane = [lax.ppermute(block, ("mod", "fsdp"), crossed(2, u)) for u in (3, 2, 1)][::-1]
    partial = call(
        project_kernel,
        "project",
        array(4, slots, columns),
        [ON_CHIP] * 5,
        [block, *plane, proj_held],
        scratch=[pltpu.VMEM((rows, columns), jnp.bfloat16)],
    )
    sums = [lax.ppermute(partial[v], "tok", crossed(2, v)) for v in (3, 2, 1)][::-1]
    gate_second, up_first = keep_on_chip(
        partial,
        [gate_weight.swapaxes(1, 2), up_weight.swapaxes(1, 2)],
        [(gate_units, units), (0, up_units)],
        "keep_more",
    )
    packed_columns = columns + STAT_COLS
    packed = call(
        norm_kernel,
        "norm",
        array(slots, packed_columns),
        [ON_CHIP] * 9,
        [kind, rest, partial, *sums[::-1], norm_gain, router_weight.T, up_first],
    )
    others = [lax.ppermute(packed, "tok", crossed(2, v)) for v in (3, 2, 1)][::-1]
    up_second, down_first = keep_on_chip(
        packed,
        [up_weight.swapaxes(1, 2), down_weight],
        [(up_units, units), (0, down_units)],
        "keep_up",
    )
    kept_slots = 3 * capacity
    own, to_far_rows, to_side_rows, to_corner_rows = call(
        arrange_kernel,
        "arrange",
        [array(kept_slots, packed_columns)] * 4,
        [ON_CHIP] * 5,
        [packed, *others[::-1], up_second],
    )
    both_axes = ("groups", "mod")
    side_far = lax.ppermute(to_corner_rows, both_axes, crossed(2, 3))
    far = lax.ppermute(to_far_rows, "groups", SWAP)
    side_own = lax.ppermute(to_side_rows, "mod", SWAP)

    (down_second,) = keep_on_chip(own, [down_weight], [(down_units, units)], "keep_down")

    flops = 2 * rows * units * width
    gate, gathered = call(
        gate_kernel,
        "gate",
        [array(units + TILE, rows), array(rows, width)],
        [ON_CHIP] * 7,
        [side_far, side_own, far, own, gate_first, gate_second, down_second],
        flops=flops,
    )
    late = units // 4 // TILE * TILE
    up_rest = units - up_units
    up_parts = [
        call(
            functools.partial(up_kernel, spans),
            "up",
            array(sum(b - a for a, b in spans), rows),
            [ON_CHIP] * (1 + len(spans)),
            [gathered, *weights],
            flops=flops * sum(b - a for a, b in spans) // units,
        )
        for spans, weights in (
            (((0, up_units), (0, up_rest - late)), (up_first, up_second)),
            (((up_rest - late, up_rest),), (up_second,)),
        )
    ]
    gate_other = lax.ppermute(gate, "fsdp", SWAP)
    up_others = [lax.ppermute(part, "fsdp", SWAP) for part in up_parts]
    act_early, silu_late, stat = call(
        activation_kernel,
        "activation",
        [
            array(units - late, rows),
            array(late, rows, dtype=jnp.float32),
            array(8, rows, dtype=jnp.float32),
        ],
        [ON_CHIP] * 4,
        [gate, gate_other, up_parts[0], up_others[0]],
        moved=8 * units * rows,
    )
    kept, to_far, to_side, to_side_far = call(
        down_kernel,
        "down",
        [array(kept_slots, columns)] * 4,
        [ON_CHIP] * 7,
        [act_early, silu_late, stat, up_parts[1], up_others[1], down_first, down_second],
        scratch=[pltpu.VMEM((units, rows), jnp.bfloat16)],
        flops=flops,
    )
    from_side_far = lax.ppermute(to_side_far, both_axes, crossed(2, 3))
    from_far = lax.ppermute(to_far, "groups", SWAP)
    from_side = lax.ppermute(to_side, "mod", SWAP)
    merged = call(
        merge_kernel,
        "merge",
        [array(slots, columns)] * 4,
        [ON_CHIP] * 8,
        [packed, *others[::-1], kept, from_side, from_far, from_side_far],
    )
    values = [merged[0]] + [lax.ppermute(merged[v], "tok", crossed(2, v)) for v in (1, 2, 3)]
    return pl.pallas_call(
        scatter_kernel,
        out_shape=pltpu.HBM((tokens, columns), jnp.bfloat16),
        in_specs=[ON_CHIP] * 5,
        out_specs=IN_HBM,
        scratch_shapes=[pltpu.VMEM((tokens, columns), jnp.bfloat16), pltpu.SemaphoreType.DMA((4,))],
        compiler_params=pltpu.CompilerParams(vmem_limit_bytes=8 << 20),
        name="scatter",
    )(pick, *values)


def solution(mesh):
    placed = (
        P(("groups", "tok"), ("fsdp", "mod")),
        P(("groups", "tok"), ("mod", "fsdp")),
        P("tok", ("fsdp", "mod")),
        P(None, ("fsdp", "mod")),
        P(("fsdp", "mod"), None),
        P(("groups", "tok")),
        P(None, ("groups", "tok")),
        P("mod", "fsdp", "tok"),
        P("mod", "fsdp", "tok"),
        P("mod", "tok", "fsdp"),
    )
    sizes = dict(n_tok=mesh.shape["tok"], n_mod=mesh.shape["mod"], n_fsdp=mesh.shape["fsdp"])
    paired = (
        mesh.shape["groups"] == 2
        and sizes == dict(n_tok=4, n_mod=2, n_fsdp=2)
    )
    body = paired_local if paired else functools.partial(local, **sizes)
    return jax.shard_map(
        body,
        mesh=mesh,
        in_specs=placed,
        out_specs=P(("groups", "tok"), ("fsdp", "mod")),
        check_vma=False,
    )
```

```python
import functools

import jax
import jax.numpy as jnp
from jax import lax
from jax.experimental import pallas as pl
from jax.experimental.pallas import tpu as pltpu
from jax.sharding import PartitionSpec as P

D = 4096
STAT_COLS = 128
FEW = 4


def ring(size, step):
    return [(i, (i + step) % size) for i in range(size)]


def reduce_tok(blocks, n_tok):
    if n_tok > FEW:
        return lax.psum_scatter(blocks, "tok", scatter_dimension=0, tiled=False).astype(jnp.float32)
    own = lax.axis_index("tok")
    total = lax.dynamic_index_in_dim(blocks, own, 0, False).astype(jnp.float32)
    for step in range(1, n_tok):
        sent = lax.dynamic_index_in_dim(blocks, (own + step) % n_tok, 0, False)
        total = total + lax.ppermute(sent, "tok", ring(n_tok, step)).astype(jnp.float32)
    return total


def gather_tok(rows, n_tok):
    if n_tok > FEW:
        return lax.all_gather(rows, "tok", axis=0, tiled=False)
    own = lax.axis_index("tok")
    result = jnp.zeros((n_tok,) + rows.shape, rows.dtype)
    result = lax.dynamic_update_index_in_dim(result, rows, own, 0)
    for step in range(1, n_tok):
        got = lax.ppermute(rows, "tok", ring(n_tok, step))
        result = lax.dynamic_update_index_in_dim(result, got, (own - step) % n_tok, 0)
    return result


def spread_context(rows, n_tok, n_mod, n_fsdp):
    if n_tok > FEW or n_tok != n_mod * n_fsdp:
        full = lax.all_gather(rows, ("mod", "fsdp"), axis=1, tiled=True)
        split = full.reshape(full.shape[0], n_tok, full.shape[1] // n_tok).transpose(1, 0, 2)
        return lax.all_to_all(split, "tok", 0, 0, tiled=True)
    pairs = [(t * n_tok + q, q * n_tok + t) for t in range(n_tok) for q in range(n_tok)]
    swapped = lax.ppermute(rows, ("tok", "mod", "fsdp"), pairs)
    return lax.all_gather(swapped, ("mod", "fsdp"), axis=0, tiled=False)


def local(
    residual,
    context,
    out_proj,
    norm_gain,
    router_weight,
    block_modality,
    expert_rows,
    gate_weight,
    up_weight,
    down_weight,
    *,
    n_tok,
    n_mod,
    n_fsdp,
):
    token_count = residual.shape[0]
    experts, capacity = expert_rows.shape
    kind_experts = experts // 2
    slots = kind_experts * capacity
    local_experts = gate_weight.shape[0]
    columns = residual.shape[1]
    assert block_modality.shape == (1,) and n_mod * local_experts == experts
    modality = block_modality[0]
    first = modality * kind_experts
    mod_index = lax.axis_index("mod")

    own_rows = lax.dynamic_slice_in_dim(expert_rows, first, kind_experts, 0).reshape(slots)
    pick = own_rows[:, None] == lax.iota(jnp.int32, token_count)[None, :]
    pick_half = pick.astype(jnp.bfloat16)
    picked_context = jnp.dot(pick_half, context, preferred_element_type=jnp.float32).astype(jnp.bfloat16)
    picked_residual = jnp.dot(pick_half, residual, preferred_element_type=jnp.float32)

    spread = spread_context(picked_context, n_tok, n_mod, n_fsdp)
    partial = jnp.einsum("tsk,kc->tsc", spread, out_proj, preferred_element_type=jnp.float32)
    hidden = picked_residual + reduce_tok(partial.astype(jnp.bfloat16), n_tok)

    gain_table = norm_gain.astype(jnp.float32)
    gained = hidden * jnp.where(modality == 0, gain_table[0], gain_table[1])[None, :]
    router = lax.dynamic_slice_in_dim(router_weight.astype(jnp.float32), first, kind_experts, 1)
    slot_router = jnp.repeat(router.T, capacity, axis=0)
    squares = jnp.sum(hidden * hidden, axis=1, keepdims=True)
    logits = jnp.sum(gained * slot_router, axis=1, keepdims=True)
    flag = jnp.broadcast_to(modality.astype(jnp.bfloat16), (slots, 1))
    stat_list = []
    for stat in (squares, logits):
        high = lax.reduce_precision(stat, 8, 7)
        stat_list += [high.astype(jnp.bfloat16), (stat - high).astype(jnp.bfloat16)]
    packed = jnp.concatenate(
        [gained.astype(jnp.bfloat16)] + stat_list
        + [flag, jnp.zeros((slots, STAT_COLS - 5), jnp.bfloat16)],
        axis=1,
    )

    everyone = gather_tok(packed, n_tok)
    both = lax.all_gather(everyone, "mod", axis=0, tiled=False)
    kind_first = (mod_index * local_experts) % kind_experts
    both = both.reshape(n_mod, n_tok, kind_experts, capacity, columns + STAT_COLS)
    mine = lax.dynamic_slice_in_dim(both, kind_first, local_experts, 2)
    piece = mine[..., :columns].transpose(2, 1, 3, 0, 4).reshape(
        local_experts, n_tok * capacity, n_mod * columns
    )
    tail = mine[..., columns : columns + 5].astype(jnp.float32)
    half_stats = jnp.sum(
        jnp.stack([tail[..., 0] + tail[..., 1], tail[..., 2] + tail[..., 3]], axis=-1), axis=0
    )
    stats = lax.psum(half_stats, "fsdp")
    flags = tail[0, :, :, :, 4]
    by_expert = stats.transpose(1, 0, 2, 3).reshape(local_experts, n_tok * capacity, 2)
    inverse = lax.rsqrt(by_expert[..., 0:1] / D + 1e-05)
    score = jax.nn.sigmoid(by_expert[..., 1:2] * inverse)

    gate_part = jnp.einsum("esd,edf->esf", piece, gate_weight, preferred_element_type=jnp.float32)
    up_part = jnp.einsum("esd,edf->esf", piece, up_weight, preferred_element_type=jnp.float32)
    gate_half = gate_part.astype(jnp.bfloat16)
    up_half = up_part.astype(jnp.bfloat16)
    if n_fsdp == 2:
        swap = [(0, 1), (1, 0)]
        gate_sum = gate_half.astype(jnp.float32) + lax.ppermute(gate_half, "fsdp", swap).astype(jnp.float32)
        up_sum = up_half.astype(jnp.float32) + lax.ppermute(up_half, "fsdp", swap).astype(jnp.float32)
    else:
        gate_sum = lax.psum(gate_half, "fsdp").astype(jnp.float32)
        up_sum = lax.psum(up_half, "fsdp").astype(jnp.float32)
    activation = (jax.nn.silu(gate_sum * inverse) * (up_sum * inverse)).astype(jnp.bfloat16)
    value = jnp.einsum("esf,efd->esd", activation, down_weight, preferred_element_type=jnp.float32)
    value = (value * score).astype(jnp.bfloat16)
    value = value.reshape(local_experts, n_tok, capacity, n_mod * columns).transpose(1, 0, 2, 3)

    own_kind = (mod_index * local_experts) // kind_experts
    valid = (flags == own_kind.astype(jnp.float32))[..., None]
    if n_mod == 2:
        value = value.reshape(n_tok, local_experts, capacity, n_mod, columns)
        kept = lax.dynamic_index_in_dim(value, mod_index, 3, False)
        sent = lax.dynamic_index_in_dim(value, 1 - mod_index, 3, False)
        got = lax.ppermute(sent, "mod", [(0, 1), (1, 0)])
        merged = jnp.where(valid, kept, got).reshape(n_tok, slots, columns)
    else:
        value = jnp.where(valid, value, jnp.zeros((), jnp.bfloat16))
        wide = jnp.zeros((n_tok, kind_experts, capacity, n_mod * columns), jnp.bfloat16)
        wide = lax.dynamic_update_slice_in_dim(wide, value, kind_first, 1)
        wide = wide.reshape(n_tok, slots, n_mod * columns)
        merged = lax.psum_scatter(wide, "mod", scatter_dimension=2, tiled=True)
    summed = reduce_tok(merged, n_tok)
    return jnp.dot(
        pick.astype(jnp.float32).T, summed, precision=lax.Precision.HIGHEST
    ).astype(jnp.bfloat16)


SWAP = [(0, 1), (1, 0)]
STRIP = 688
TILE = 16
ON_CHIP = pl.BlockSpec(memory_space=pltpu.VMEM)
IN_HBM = pl.BlockSpec(memory_space=pltpu.HBM)
ANYWHERE = pl.BlockSpec(memory_space=pl.ANY)


def crossed(bits, flip):
    return [(i, i ^ flip) for i in range(1 << bits)]


def call(kernel, name, outs, specs, args, scratch=(), flops=0, moved=0, limit=8 << 20):
    return pl.pallas_call(
        kernel,
        out_shape=outs,
        in_specs=specs,
        out_specs=jax.tree.map(lambda _: ON_CHIP, outs),
        scratch_shapes=list(scratch),
        compiler_params=pltpu.CompilerParams(vmem_limit_bytes=limit),
        cost_estimate=pl.CostEstimate(flops=flops, transcendentals=0, bytes_accessed=moved),
        name=name,
    )(*args)


def array(*shape, dtype=jnp.bfloat16):
    return jax.ShapeDtypeStruct(shape, dtype)


def keep_kernel(spans, after_ref, *refs):
    count = len(spans)
    weights, held, semaphores = refs[:count], refs[count : 2 * count], refs[-1]
    copies = [
        pltpu.make_async_copy(weight.at[lax.axis_index("groups"), a:b], to, semaphores.at[n])
        for n, (weight, to, (a, b)) in enumerate(zip(weights, held, spans))
    ]
    for copy in copies:
        copy.start()
    for copy in copies:
        copy.wait()


def in_hbm(value):
    return pltpu.with_memory_space_constraint(value, pltpu.HBM)


def keep_on_chip(after, weights, spans, name):
    return call(
        functools.partial(keep_kernel, spans),
        name,
        [pltpu.VMEM((b - a, weight.shape[2]), jnp.bfloat16) for weight, (a, b) in zip(weights, spans)],
        [ANYWHERE] + [IN_HBM] * len(spans),
        [after] + [in_hbm(weight) for weight in weights],
        scratch=[pltpu.SemaphoreType.DMA((len(spans),))],
        moved=sum(2 * (b - a) * weight.shape[2] for weight, (a, b) in zip(weights, spans)),
        limit=1 << 20,
    )


def select_kernel(
    rows_hbm, context_hbm, picked_ref, pick_ref, kind_ref, rows_ref, context_ref, semaphores
):
    rows_copy = pltpu.make_async_copy(rows_hbm, rows_ref, semaphores.at[0])
    context_copy = pltpu.make_async_copy(context_hbm, context_ref, semaphores.at[1])
    rows_copy.start()
    context_copy.start()
    rows_copy.wait()
    kind = jnp.where(jnp.maximum(rows_ref[2, 0], rows_ref[3, 0]) >= 0, 1, 0)
    kind_ref[...] = jnp.full(kind_ref.shape, kind, jnp.int32).astype(jnp.float32)
    capacity = rows_ref.shape[1]
    slots, tokens = pick_ref.shape
    row = lax.broadcasted_iota(jnp.int32, (slots, tokens), 0)
    token = lax.broadcasted_iota(jnp.int32, (slots, tokens), 1)
    wanted = jnp.full((slots, tokens), -1, jnp.int32)
    for e in range(2):
        expert = 2 * kind + (lax.axis_index("groups") ^ e)
        for s in range(capacity):
            wanted = jnp.where(row == e * capacity + s, rows_ref[expert, s], wanted)
    pick = jnp.where(wanted == token, 1.0, 0.0).astype(jnp.bfloat16)
    pick_ref[...] = pick
    context_copy.wait()
    picked_ref[...] = jnp.dot(pick, context_ref[...], preferred_element_type=jnp.float32).astype(jnp.bfloat16)


def keep_gate_kernel(
    _, pick_ref, residual_hbm, gate_ref, proj_ref, gate_held, proj_held, rest_ref, residual_ref, semaphores
):
    copies = [
        pltpu.make_async_copy(residual_hbm, residual_ref, semaphores.at[0]),
        pltpu.make_async_copy(proj_ref, proj_held, semaphores.at[1]),
        pltpu.make_async_copy(gate_ref.at[lax.axis_index("groups"), : gate_held.shape[0]], gate_held, semaphores.at[2]),
    ]
    for copy in copies:
        copy.start()
    copies[0].wait()
    rest_ref[...] = jnp.dot(pick_ref[...], residual_ref[...], preferred_element_type=jnp.float32)
    for copy in copies[1:]:
        copy.wait()


def project_kernel(*refs):
    block_refs, weight_ref, (out_ref, rows_ref) = refs[:4], refs[4], refs[-2:]
    slots = block_refs[0].shape[0]
    for u, block_ref in enumerate(block_refs):
        rows_ref[u * slots : (u + 1) * slots, :] = block_ref[...]
    product = jnp.dot(rows_ref[...], weight_ref[...], preferred_element_type=jnp.float32)
    product = product.astype(jnp.bfloat16)
    corner = 2 * lax.axis_index("mod") + lax.axis_index("fsdp")
    flip = lax.axis_index("tok") ^ corner
    for u in range(4):
        out_ref[flip ^ u] = product[u * slots : (u + 1) * slots, :]


def split_high_low(value):
    high = value.astype(jnp.bfloat16).astype(jnp.float32)
    return high, value - high


def norm_kernel(kind_ref, rest_ref, partial_ref, three_ref, two_ref, one_ref, gain_ref, router_ref, _, out_ref):
    slots, columns = rest_ref.shape
    hidden = rest_ref[...] + partial_ref[0].astype(jnp.float32)
    for got_ref in (three_ref, two_ref, one_ref):
        hidden = hidden + got_ref[...].astype(jnp.float32)
    kind = kind_ref[0:1, 0:1]
    gains = gain_ref[...].astype(jnp.float32)
    gained = hidden * jnp.where(kind == 0.0, gains[0:1], gains[1:2])
    out_ref[:, :columns] = gained.astype(jnp.bfloat16)
    table = router_ref[...].astype(jnp.float32)
    pieces = []
    for e in range(2):
        second = (lax.axis_index("groups") ^ e) == 1
        text = jnp.where(second, table[1:2], table[0:1])
        image = jnp.where(second, table[3:4], table[2:3])
        weights = jnp.where(kind == 0.0, text, image)
        half = slots // 2
        pieces.append(jnp.sum(gained[e * half : (e + 1) * half] * weights, axis=1, keepdims=True))
    logits = jnp.concatenate(pieces, axis=0)
    squares = jnp.sum(hidden * hidden, axis=1, keepdims=True)
    lane = lax.broadcasted_iota(jnp.int32, (slots, STAT_COLS), 1)
    extra = jnp.where(lane == 4, kind, 0.0)
    for at, stat in enumerate(split_high_low(squares) + split_high_low(logits)):
        extra = jnp.where(lane == at, stat, extra)
    out_ref[:, columns:] = extra.astype(jnp.bfloat16)


def places(packed_refs, columns):
    side = lax.axis_index("mod")
    matches, found, before = [], [], 0
    for v, ref in enumerate(packed_refs):
        flag = ref[:TILE, columns:].astype(jnp.float32)[0, 4]
        kind = jnp.where(flag > 0.5, 1, 0)
        match = kind == side
        place = jnp.minimum(jnp.where(match, before, v - before), len(packed_refs) - 2)
        matches.append(match)
        found.append(place)
        before = before + jnp.where(match, 1, 0)
    return matches, found


def arrange_kernel(zero_ref, three_ref, two_ref, one_ref, _, *out_refs):
    packed_refs = (zero_ref, one_ref, two_ref, three_ref)
    capacity = zero_ref.shape[0] // 2
    for out_ref in out_refs:
        out_ref[...] = jnp.zeros(out_ref.shape, out_ref.dtype)
    matches, found = places(packed_refs, zero_ref.shape[1] - STAT_COLS)
    for ref, match, place in zip(packed_refs, matches, found):
        span = pl.ds(pl.multiple_of(place * capacity, capacity), capacity)
        for wanted, (own_ref, given_ref) in ((True, out_refs[:2]), (False, out_refs[2:])):

            @pl.when(match == wanted)
            def _():
                own_ref[span, :] = ref[:capacity, :]
                given_ref[span, :] = ref[capacity:, :]


def weights_times_rows(weight_refs, spans, rows, out_ref):
    at = 0
    for weight_ref, (first, last) in zip(weight_refs, spans):
        for start in range(first, last, STRIP):
            stop = min(start + STRIP, last)
            out_ref[at : at + stop - start, :] = lax.dot_general(
                weight_ref[start:stop, :], rows, (((1,), (1,)), ((), ())), preferred_element_type=jnp.float32
            ).astype(jnp.bfloat16)
            at += stop - start


def gate_kernel(side_far_ref, side_own_ref, far_ref, own_ref, *refs):
    weight_refs, out_ref, rows_ref = refs[:2], refs[-2], refs[-1]
    half = own_ref.shape[0]
    rows = rows_ref.shape[0]
    units = out_ref.shape[0] - TILE
    columns = rows_ref.shape[1] // 2
    rows_ref[2 * half :, :] = jnp.zeros((rows - 2 * half, 2 * columns), rows_ref.dtype)
    for side in range(2):

        @pl.when(lax.axis_index("mod") == side)
        def _():
            here, there = side * columns, (1 - side) * columns
            rows_ref[:half, here : here + columns] = own_ref[:, :columns]
            rows_ref[half : 2 * half, here : here + columns] = far_ref[:, :columns]
            rows_ref[:half, there : there + columns] = side_own_ref[:, :columns]
            rows_ref[half : 2 * half, there : there + columns] = side_far_ref[:, :columns]

    spans = [(0, ref.shape[0]) for ref in weight_refs]
    weights_times_rows(weight_refs, spans, rows_ref[...], out_ref)
    tails = [ref[:, columns:].astype(jnp.float32) for ref in (own_ref, side_own_ref, far_ref, side_far_ref)]
    unused = jnp.zeros((rows - 2 * half, STAT_COLS), jnp.float32)
    stat = jnp.concatenate([tails[0] + tails[1], tails[2] + tails[3], unused], axis=0).T
    squares = stat[0:1] + stat[1:2]
    logits = stat[2:3] + stat[3:4]
    at_row = lax.broadcasted_iota(jnp.int32, (TILE, rows), 0)
    extra = jnp.zeros((TILE, rows), jnp.float32)
    for at, piece in enumerate(split_high_low(squares) + split_high_low(logits)):
        extra = jnp.where(at_row == at, piece, extra)
    out_ref[units:, :] = extra.astype(jnp.bfloat16)


def up_kernel(spans, rows_ref, *refs):
    weights_times_rows(refs[:-1], spans, rows_ref[...], refs[-1])


def activation_kernel(gate_ref, gate_other_ref, up_ref, up_other_ref, act_ref, silu_ref, stat_ref):
    early = act_ref.shape[0]
    units = early + silu_ref.shape[0]
    stat = gate_ref[units:, :].astype(jnp.float32) + gate_other_ref[units:, :].astype(jnp.float32)
    inverse = lax.rsqrt((stat[0:1] + stat[1:2]) / D + 1e-05)
    logits = (stat[2:3] + stat[3:4]) * inverse
    score = 1.0 / (1.0 + jnp.exp(-logits))
    at_row = lax.broadcasted_iota(jnp.int32, stat_ref.shape, 0)
    stat_ref[...] = jnp.where(at_row == 0, inverse, score)
    for start in range(0, units, STRIP):
        stop = min(start + STRIP, units)
        gate = gate_ref[start:stop, :].astype(jnp.float32) + gate_other_ref[start:stop, :].astype(jnp.float32)
        gate = gate * inverse
        silu = gate / (1.0 + jnp.exp(-gate)) * inverse
        inside = max(0, min(stop, early) - start)
        if inside:
            span = slice(start, start + inside)
            up = up_ref[span, :].astype(jnp.float32) + up_other_ref[span, :].astype(jnp.float32)
            act_ref[span, :] = (silu[:inside] * up).astype(jnp.bfloat16)
        if start + inside < stop:
            silu_ref[start + inside - early : stop - early, :] = silu[inside:]


def down_kernel(
    act_early_ref, silu_ref, stat_ref, up_ref, other_ref, first_ref, second_ref,
    kept_ref, far_ref, side_ref, side_far_ref, act_ref,
):
    units, rows = act_ref.shape
    early = act_early_ref.shape[0]
    act_ref[:early, :] = act_early_ref[...]
    up = up_ref[...].astype(jnp.float32) + other_ref[...].astype(jnp.float32)
    act_ref[early:, :] = (silu_ref[...] * up).astype(jnp.bfloat16)
    half, columns = kept_ref.shape
    score = jnp.broadcast_to(stat_ref[1:2, :], (rows, rows)).T[:, 0:1]
    first_units = first_ref.shape[0]
    for quarter in range(2):
        span = slice(quarter * columns, (quarter + 1) * columns)
        value = sum(
            lax.dot_general(
                act_ref[a:b, :], weight_ref[:, span], (((0,), (0,)), ((), ())), preferred_element_type=jnp.float32
            )
            for a, b, weight_ref in ((0, first_units, first_ref), (first_units, units, second_ref))
        )
        value = (value * score).astype(jnp.bfloat16)
        for across, (own_out, far_out) in enumerate(((kept_ref, far_ref), (side_ref, side_far_ref))):

            @pl.when((lax.axis_index("mod") ^ quarter) == across)
            def _():
                own_out[...] = value[:half]
                far_out[...] = value[half : 2 * half]


def merge_kernel(zero_ref, three_ref, two_ref, one_ref, kept_ref, side_ref, far_ref, side_far_ref, *out_refs):
    columns = kept_ref.shape[1]
    capacity = zero_ref.shape[0] // 2
    matches, found = places((zero_ref, one_ref, two_ref, three_ref), columns)
    for out_ref, match, place in zip(out_refs, matches, found):
        span = pl.ds(pl.multiple_of(place * capacity, capacity), capacity)
        for wanted, (first_ref, second_ref) in ((True, (kept_ref, far_ref)), (False, (side_ref, side_far_ref))):

            @pl.when(match == wanted)
            def _():
                out_ref[:capacity, :] = first_ref[span, :]
                out_ref[capacity:, :] = second_ref[span, :]


def scatter_kernel(pick_ref, zero_ref, one_ref, two_ref, three_ref, out_hbm, out_ref, semaphores):
    columns = out_ref.shape[1]
    pieces = semaphores.shape[0]
    width = columns // pieces
    copies = []
    for n in range(pieces):
        span = slice(n * width, (n + 1) * width)
        total = zero_ref[:, span].astype(jnp.float32)
        for got_ref in (three_ref, two_ref, one_ref):
            total = total + got_ref[:, span].astype(jnp.float32)
        result = 0.0
        for piece in split_high_low(total)[::-1]:
            result = result + lax.dot_general(
                pick_ref[...], piece.astype(jnp.bfloat16), (((0,), (0,)), ((), ())),
                preferred_element_type=jnp.float32,
            )
        out_ref[:, span] = result.astype(jnp.bfloat16)
        copies.append(pltpu.make_async_copy(out_ref.at[:, span], out_hbm.at[:, span], semaphores.at[n]))
        copies[-1].start()
    for copy in copies:
        copy.wait()


def paired_local(
    residual,
    context,
    out_proj,
    norm_gain,
    router_weight,
    block_modality,
    expert_rows,
    gate_weight,
    up_weight,
    down_weight,
):
    tokens, columns = residual.shape
    experts, capacity = expert_rows.shape
    slots = 2 * capacity
    half = 4 * capacity
    rows = 2 * half
    units, width = down_weight.shape[1:]
    assert block_modality.shape == (1,) and experts == 4 and gate_weight.shape[0] == 2
    picked, pick, kind = call(
        select_kernel,
        "select",
        [array(slots, columns), array(slots, tokens), array(8, STAT_COLS, dtype=jnp.float32)],
        [IN_HBM] * 2,
        [in_hbm(expert_rows), in_hbm(context)],
        scratch=[
            pltpu.SMEM((experts, capacity), jnp.int32),
            pltpu.VMEM((tokens, columns), jnp.bfloat16),
            pltpu.SemaphoreType.DMA((2,)),
        ],
    )
    turned = [(t * 4 + q, q * 4 + t) for t in range(4) for q in range(4)]
    near = lax.ppermute(picked, ("tok", "mod", "fsdp"), turned)
    gate_units, up_units, down_units = [round(units * part / TILE) * TILE for part in (0.54, 0.44, 0.27)]
    gate_first, proj_held, rest = call(
        keep_gate_kernel,
        "keep_gate",
        [
            pltpu.VMEM((gate_units, width), jnp.bfloat16),
            pltpu.VMEM(out_proj.shape, jnp.bfloat16),
            array(slots, columns, dtype=jnp.float32),
        ],
        [ANYWHERE, ON_CHIP, IN_HBM, IN_HBM, IN_HBM],
        [near, pick, in_hbm(residual), in_hbm(gate_weight.swapaxes(1, 2)), in_hbm(out_proj)],
        scratch=[pltpu.VMEM((tokens, columns), jnp.bfloat16), pltpu.SemaphoreType.DMA((3,))],
        moved=units * width,
        limit=2 << 20,
    )
    plane = [lax.ppermute(near, ("mod", "fsdp"), crossed(2, u)) for u in (3, 2, 1)][::-1]
    partial = call(
        project_kernel,
        "project",
        array(4, slots, columns),
        [ON_CHIP] * 6,
        [near, *plane, proj_held, gate_first],
        scratch=[pltpu.VMEM((rows, columns), jnp.bfloat16)],
    )
    sums = [lax.ppermute(partial[v], "tok", crossed(2, v)) for v in (3, 2, 1)][::-1]
    gate_second, up_first = keep_on_chip(
        partial,
        [gate_weight.swapaxes(1, 2), up_weight.swapaxes(1, 2)],
        [(gate_units, units), (0, up_units)],
        "keep_more",
    )
    packed_columns = columns + STAT_COLS
    packed = call(
        norm_kernel,
        "norm",
        array(slots, packed_columns),
        [ON_CHIP] * 9,
        [kind, rest, partial, *sums[::-1], norm_gain, router_weight.T, up_first],
    )
    others = [lax.ppermute(packed, "tok", crossed(2, v)) for v in (3, 2, 1)][::-1]
    up_second, down_first = keep_on_chip(
        packed,
        [up_weight.swapaxes(1, 2), down_weight],
        [(up_units, units), (0, down_units)],
        "keep_up",
    )
    kept_slots = 3 * capacity
    own, to_far_rows, to_side_rows, to_corner_rows = call(
        arrange_kernel,
        "arrange",
        [array(kept_slots, packed_columns)] * 4,
        [ON_CHIP] * 5,
        [packed, *others[::-1], up_second],
    )
    both_axes = ("groups", "mod")
    side_far = lax.ppermute(to_corner_rows, both_axes, crossed(2, 3))
    far = lax.ppermute(to_far_rows, "groups", SWAP)
    side_own = lax.ppermute(to_side_rows, "mod", SWAP)

    (down_second,) = keep_on_chip(own, [down_weight], [(down_units, units)], "keep_down")

    flops = 2 * rows * units * width
    gate, gathered = call(
        gate_kernel,
        "gate",
        [array(units + TILE, rows), array(rows, width)],
        [ON_CHIP] * 7,
        [side_far, side_own, far, own, gate_first, gate_second, down_second],
        flops=flops,
    )
    late = units // 4 // TILE * TILE
    up_rest = units - up_units
    up_parts = [
        call(
            functools.partial(up_kernel, spans),
            "up",
            array(sum(b - a for a, b in spans), rows),
            [ON_CHIP] * (1 + len(spans)),
            [gathered, *weights],
            flops=flops * sum(b - a for a, b in spans) // units,
        )
        for spans, weights in (
            (((0, up_units), (0, up_rest - late)), (up_first, up_second)),
            (((up_rest - late, up_rest),), (up_second,)),
        )
    ]
    gate_other = lax.ppermute(gate, "fsdp", SWAP)
    up_others = [lax.ppermute(part, "fsdp", SWAP) for part in up_parts]
    act_early, silu_late, stat = call(
        activation_kernel,
        "activation",
        [
            array(units - late, rows),
            array(late, rows, dtype=jnp.float32),
            array(8, rows, dtype=jnp.float32),
        ],
        [ON_CHIP] * 4,
        [gate, gate_other, up_parts[0], up_others[0]],
        moved=8 * units * rows,
    )
    kept, to_far, to_side, to_side_far = call(
        down_kernel,
        "down",
        [array(kept_slots, columns)] * 4,
        [ON_CHIP] * 7,
        [act_early, silu_late, stat, up_parts[1], up_others[1], down_first, down_second],
        scratch=[pltpu.VMEM((units, rows), jnp.bfloat16)],
        flops=flops,
    )
    from_side_far = lax.ppermute(to_side_far, both_axes, crossed(2, 3))
    from_far = lax.ppermute(to_far, "groups", SWAP)
    from_side = lax.ppermute(to_side, "mod", SWAP)
    merged = call(
        merge_kernel,
        "merge",
        [array(slots, columns)] * 4,
        [ON_CHIP] * 8,
        [packed, *others[::-1], kept, from_side, from_far, from_side_far],
    )
    values = [merged[0]] + [lax.ppermute(merged[v], "tok", crossed(2, v)) for v in (1, 2, 3)]
    return pl.pallas_call(
        scatter_kernel,
        out_shape=pltpu.HBM((tokens, columns), jnp.bfloat16),
        in_specs=[ON_CHIP] * 5,
        out_specs=IN_HBM,
        scratch_shapes=[pltpu.VMEM((tokens, columns), jnp.bfloat16), pltpu.SemaphoreType.DMA((4,))],
        compiler_params=pltpu.CompilerParams(vmem_limit_bytes=8 << 20),
        name="scatter",
    )(pick, *values)


def solution(mesh):
    placed = (
        P(("groups", "tok"), ("fsdp", "mod")),
        P(("groups", "tok"), ("mod", "fsdp")),
        P("tok", ("fsdp", "mod")),
        P(None, ("fsdp", "mod")),
        P(("fsdp", "mod"), None),
        P(("groups", "tok")),
        P(None, ("groups", "tok")),
        P("mod", "fsdp", "tok"),
        P("mod", "fsdp", "tok"),
        P("mod", "tok", "fsdp"),
    )
    sizes = dict(n_tok=mesh.shape["tok"], n_mod=mesh.shape["mod"], n_fsdp=mesh.shape["fsdp"])
    paired = (
        mesh.shape["groups"] == 2
        and sizes == dict(n_tok=4, n_mod=2, n_fsdp=2)
    )
    body = paired_local if paired else functools.partial(local, **sizes)
    return jax.shard_map(
        body,
        mesh=mesh,
        in_specs=placed,
        out_specs=P(("groups", "tok"), ("fsdp", "mod")),
        check_vma=False,
    )
```

```python
import functools

import jax
import jax.numpy as jnp
from jax import lax
from jax.experimental import pallas as pl
from jax.experimental.pallas import tpu as pltpu
from jax.sharding import PartitionSpec as P

D = 4096
STAT_COLS = 128
FEW = 4


def ring(size, step):
    return [(i, (i + step) % size) for i in range(size)]


def reduce_tok(blocks, n_tok):
    if n_tok > FEW:
        return lax.psum_scatter(blocks, "tok", scatter_dimension=0, tiled=False).astype(jnp.float32)
    own = lax.axis_index("tok")
    total = lax.dynamic_index_in_dim(blocks, own, 0, False).astype(jnp.float32)
    for step in range(1, n_tok):
        sent = lax.dynamic_index_in_dim(blocks, (own + step) % n_tok, 0, False)
        total = total + lax.ppermute(sent, "tok", ring(n_tok, step)).astype(jnp.float32)
    return total


def gather_tok(rows, n_tok):
    if n_tok > FEW:
        return lax.all_gather(rows, "tok", axis=0, tiled=False)
    own = lax.axis_index("tok")
    result = jnp.zeros((n_tok,) + rows.shape, rows.dtype)
    result = lax.dynamic_update_index_in_dim(result, rows, own, 0)
    for step in range(1, n_tok):
        got = lax.ppermute(rows, "tok", ring(n_tok, step))
        result = lax.dynamic_update_index_in_dim(result, got, (own - step) % n_tok, 0)
    return result


def spread_context(rows, n_tok, n_mod, n_fsdp):
    if n_tok > FEW or n_tok != n_mod * n_fsdp:
        full = lax.all_gather(rows, ("mod", "fsdp"), axis=1, tiled=True)
        split = full.reshape(full.shape[0], n_tok, full.shape[1] // n_tok).transpose(1, 0, 2)
        return lax.all_to_all(split, "tok", 0, 0, tiled=True)
    pairs = [(t * n_tok + q, q * n_tok + t) for t in range(n_tok) for q in range(n_tok)]
    swapped = lax.ppermute(rows, ("tok", "mod", "fsdp"), pairs)
    return lax.all_gather(swapped, ("mod", "fsdp"), axis=0, tiled=False)


def local(
    residual,
    context,
    out_proj,
    norm_gain,
    router_weight,
    block_modality,
    expert_rows,
    gate_weight,
    up_weight,
    down_weight,
    *,
    n_tok,
    n_mod,
    n_fsdp,
):
    token_count = residual.shape[0]
    experts, capacity = expert_rows.shape
    kind_experts = experts // 2
    slots = kind_experts * capacity
    local_experts = gate_weight.shape[0]
    columns = residual.shape[1]
    assert block_modality.shape == (1,) and n_mod * local_experts == experts
    modality = block_modality[0]
    first = modality * kind_experts
    mod_index = lax.axis_index("mod")

    own_rows = lax.dynamic_slice_in_dim(expert_rows, first, kind_experts, 0).reshape(slots)
    pick = own_rows[:, None] == lax.iota(jnp.int32, token_count)[None, :]
    pick_half = pick.astype(jnp.bfloat16)
    picked_context = jnp.dot(pick_half, context, preferred_element_type=jnp.float32).astype(jnp.bfloat16)
    picked_residual = jnp.dot(pick_half, residual, preferred_element_type=jnp.float32)

    spread = spread_context(picked_context, n_tok, n_mod, n_fsdp)
    partial = jnp.einsum("tsk,kc->tsc", spread, out_proj, preferred_element_type=jnp.float32)
    hidden = picked_residual + reduce_tok(partial.astype(jnp.bfloat16), n_tok)

    gain_table = norm_gain.astype(jnp.float32)
    gained = hidden * jnp.where(modality == 0, gain_table[0], gain_table[1])[None, :]
    router = lax.dynamic_slice_in_dim(router_weight.astype(jnp.float32), first, kind_experts, 1)
    slot_router = jnp.repeat(router.T, capacity, axis=0)
    squares = jnp.sum(hidden * hidden, axis=1, keepdims=True)
    logits = jnp.sum(gained * slot_router, axis=1, keepdims=True)
    flag = jnp.broadcast_to(modality.astype(jnp.bfloat16), (slots, 1))
    stat_list = []
    for stat in (squares, logits):
        high = lax.reduce_precision(stat, 8, 7)
        stat_list += [high.astype(jnp.bfloat16), (stat - high).astype(jnp.bfloat16)]
    packed = jnp.concatenate(
        [gained.astype(jnp.bfloat16)] + stat_list
        + [flag, jnp.zeros((slots, STAT_COLS - 5), jnp.bfloat16)],
        axis=1,
    )

    everyone = gather_tok(packed, n_tok)
    both = lax.all_gather(everyone, "mod", axis=0, tiled=False)
    kind_first = (mod_index * local_experts) % kind_experts
    both = both.reshape(n_mod, n_tok, kind_experts, capacity, columns + STAT_COLS)
    mine = lax.dynamic_slice_in_dim(both, kind_first, local_experts, 2)
    piece = mine[..., :columns].transpose(2, 1, 3, 0, 4).reshape(
        local_experts, n_tok * capacity, n_mod * columns
    )
    tail = mine[..., columns : columns + 5].astype(jnp.float32)
    half_stats = jnp.sum(
        jnp.stack([tail[..., 0] + tail[..., 1], tail[..., 2] + tail[..., 3]], axis=-1), axis=0
    )
    stats = lax.psum(half_stats, "fsdp")
    flags = tail[0, :, :, :, 4]
    by_expert = stats.transpose(1, 0, 2, 3).reshape(local_experts, n_tok * capacity, 2)
    inverse = lax.rsqrt(by_expert[..., 0:1] / D + 1e-05)
    score = jax.nn.sigmoid(by_expert[..., 1:2] * inverse)

    gate_part = jnp.einsum("esd,edf->esf", piece, gate_weight, preferred_element_type=jnp.float32)
    up_part = jnp.einsum("esd,edf->esf", piece, up_weight, preferred_element_type=jnp.float32)
    gate_half = gate_part.astype(jnp.bfloat16)
    up_half = up_part.astype(jnp.bfloat16)
    if n_fsdp == 2:
        swap = [(0, 1), (1, 0)]
        gate_sum = gate_half.astype(jnp.float32) + lax.ppermute(gate_half, "fsdp", swap).astype(jnp.float32)
        up_sum = up_half.astype(jnp.float32) + lax.ppermute(up_half, "fsdp", swap).astype(jnp.float32)
    else:
        gate_sum = lax.psum(gate_half, "fsdp").astype(jnp.float32)
        up_sum = lax.psum(up_half, "fsdp").astype(jnp.float32)
    activation = (jax.nn.silu(gate_sum * inverse) * (up_sum * inverse)).astype(jnp.bfloat16)
    value = jnp.einsum("esf,efd->esd", activation, down_weight, preferred_element_type=jnp.float32)
    value = (value * score).astype(jnp.bfloat16)
    value = value.reshape(local_experts, n_tok, capacity, n_mod * columns).transpose(1, 0, 2, 3)

    own_kind = (mod_index * local_experts) // kind_experts
    valid = (flags == own_kind.astype(jnp.float32))[..., None]
    if n_mod == 2:
        value = value.reshape(n_tok, local_experts, capacity, n_mod, columns)
        kept = lax.dynamic_index_in_dim(value, mod_index, 3, False)
        sent = lax.dynamic_index_in_dim(value, 1 - mod_index, 3, False)
        got = lax.ppermute(sent, "mod", [(0, 1), (1, 0)])
        merged = jnp.where(valid, kept, got).reshape(n_tok, slots, columns)
    else:
        value = jnp.where(valid, value, jnp.zeros((), jnp.bfloat16))
        wide = jnp.zeros((n_tok, kind_experts, capacity, n_mod * columns), jnp.bfloat16)
        wide = lax.dynamic_update_slice_in_dim(wide, value, kind_first, 1)
        wide = wide.reshape(n_tok, slots, n_mod * columns)
        merged = lax.psum_scatter(wide, "mod", scatter_dimension=2, tiled=True)
    summed = reduce_tok(merged, n_tok)
    return jnp.dot(
        pick.astype(jnp.float32).T, summed, precision=lax.Precision.HIGHEST
    ).astype(jnp.bfloat16)


SWAP = [(0, 1), (1, 0)]
STRIP = 688
TILE = 16
ON_CHIP = pl.BlockSpec(memory_space=pltpu.VMEM)
IN_HBM = pl.BlockSpec(memory_space=pltpu.HBM)
ANYWHERE = pl.BlockSpec(memory_space=pl.ANY)


def crossed(bits, flip):
    return [(i, i ^ flip) for i in range(1 << bits)]


def call(kernel, name, outs, specs, args, scratch=(), flops=0, moved=0, limit=8 << 20):
    return pl.pallas_call(
        kernel,
        out_shape=outs,
        in_specs=specs,
        out_specs=jax.tree.map(lambda _: ON_CHIP, outs),
        scratch_shapes=list(scratch),
        compiler_params=pltpu.CompilerParams(vmem_limit_bytes=limit),
        cost_estimate=pl.CostEstimate(flops=flops, transcendentals=0, bytes_accessed=moved),
        name=name,
    )(*args)


def array(*shape, dtype=jnp.bfloat16):
    return jax.ShapeDtypeStruct(shape, dtype)


def keep_kernel(spans, after_ref, *refs):
    count = len(spans)
    weights, held, semaphores = refs[:count], refs[count : 2 * count], refs[-1]
    copies = [
        pltpu.make_async_copy(weight.at[lax.axis_index("groups"), a:b], to, semaphores.at[n])
        for n, (weight, to, (a, b)) in enumerate(zip(weights, held, spans))
    ]
    for copy in copies:
        copy.start()
    for copy in copies:
        copy.wait()


def in_hbm(value):
    return pltpu.with_memory_space_constraint(value, pltpu.HBM)


def keep_on_chip(after, weights, spans, name):
    return call(
        functools.partial(keep_kernel, spans),
        name,
        [pltpu.VMEM((b - a, weight.shape[2]), jnp.bfloat16) for weight, (a, b) in zip(weights, spans)],
        [ANYWHERE] + [IN_HBM] * len(spans),
        [after] + [in_hbm(weight) for weight in weights],
        scratch=[pltpu.SemaphoreType.DMA((len(spans),))],
        moved=sum(2 * (b - a) * weight.shape[2] for weight, (a, b) in zip(weights, spans)),
        limit=1 << 20,
    )


def select_kernel(
    rows_hbm, context_hbm, picked_ref, pick_ref, kind_ref, rows_ref, context_ref, semaphores
):
    rows_copy = pltpu.make_async_copy(rows_hbm, rows_ref, semaphores.at[0])
    context_copy = pltpu.make_async_copy(context_hbm, context_ref, semaphores.at[1])
    rows_copy.start()
    context_copy.start()
    rows_copy.wait()
    kind = jnp.where(jnp.maximum(rows_ref[2, 0], rows_ref[3, 0]) >= 0, 1, 0)
    kind_ref[...] = jnp.full(kind_ref.shape, kind, jnp.int32).astype(jnp.float32)
    capacity = rows_ref.shape[1]
    slots, tokens = pick_ref.shape
    row = lax.broadcasted_iota(jnp.int32, (slots, tokens), 0)
    token = lax.broadcasted_iota(jnp.int32, (slots, tokens), 1)
    wanted = jnp.full((slots, tokens), -1, jnp.int32)
    for e in range(2):
        expert = 2 * kind + (lax.axis_index("groups") ^ e)
        for s in range(capacity):
            wanted = jnp.where(row == e * capacity + s, rows_ref[expert, s], wanted)
    pick = jnp.where(wanted == token, 1.0, 0.0).astype(jnp.bfloat16)
    pick_ref[...] = pick
    context_copy.wait()
    picked_ref[...] = jnp.dot(pick, context_ref[...], preferred_element_type=jnp.float32).astype(jnp.bfloat16)


def keep_gate_kernel(
    _, pick_ref, residual_hbm, gate_ref, proj_ref, gate_held, proj_held, rest_ref, residual_ref, semaphores
):
    copies = [
        pltpu.make_async_copy(residual_hbm, residual_ref, semaphores.at[0]),
        pltpu.make_async_copy(proj_ref, proj_held, semaphores.at[1]),
        pltpu.make_async_copy(gate_ref.at[lax.axis_index("groups"), : gate_held.shape[0]], gate_held, semaphores.at[2]),
    ]
    for copy in copies:
        copy.start()
    copies[0].wait()
    rest_ref[...] = jnp.dot(pick_ref[...], residual_ref[...], preferred_element_type=jnp.float32)
    for copy in copies[1:]:
        copy.wait()


def project_kernel(*refs):
    block_refs, weight_ref, (out_ref, rows_ref) = refs[:4], refs[4], refs[-2:]
    slots = block_refs[0].shape[0]
    for u, block_ref in enumerate(block_refs):
        rows_ref[u * slots : (u + 1) * slots, :] = block_ref[...]
    product = jnp.dot(rows_ref[...], weight_ref[...], preferred_element_type=jnp.float32)
    product = product.astype(jnp.bfloat16)
    corner = 2 * lax.axis_index("mod") + lax.axis_index("fsdp")
    flip = lax.axis_index("tok") ^ corner
    for u in range(4):
        out_ref[flip ^ u] = product[u * slots : (u + 1) * slots, :]


def split_high_low(value):
    high = value.astype(jnp.bfloat16).astype(jnp.float32)
    return high, value - high


def norm_kernel(kind_ref, rest_ref, partial_ref, three_ref, two_ref, one_ref, gain_ref, router_ref, _, out_ref):
    slots, columns = rest_ref.shape
    hidden = rest_ref[...] + partial_ref[0].astype(jnp.float32)
    for got_ref in (three_ref, two_ref, one_ref):
        hidden = hidden + got_ref[...].astype(jnp.float32)
    kind = kind_ref[0:1, 0:1]
    gains = gain_ref[...].astype(jnp.float32)
    gained = hidden * jnp.where(kind == 0.0, gains[0:1], gains[1:2])
    out_ref[:, :columns] = gained.astype(jnp.bfloat16)
    table = router_ref[...].astype(jnp.float32)
    pieces = []
    for e in range(2):
        second = (lax.axis_index("groups") ^ e) == 1
        text = jnp.where(second, table[1:2], table[0:1])
        image = jnp.where(second, table[3:4], table[2:3])
        weights = jnp.where(kind == 0.0, text, image)
        half = slots // 2
        pieces.append(jnp.sum(gained[e * half : (e + 1) * half] * weights, axis=1, keepdims=True))
    logits = jnp.concatenate(pieces, axis=0)
    squares = jnp.sum(hidden * hidden, axis=1, keepdims=True)
    lane = lax.broadcasted_iota(jnp.int32, (slots, STAT_COLS), 1)
    extra = jnp.where(lane == 4, kind, 0.0)
    for at, stat in enumerate(split_high_low(squares) + split_high_low(logits)):
        extra = jnp.where(lane == at, stat, extra)
    out_ref[:, columns:] = extra.astype(jnp.bfloat16)


def places(packed_refs, columns):
    side = lax.axis_index("mod")
    matches, found, before = [], [], 0
    for v, ref in enumerate(packed_refs):
        flag = ref[:TILE, columns:].astype(jnp.float32)[0, 4]
        kind = jnp.where(flag > 0.5, 1, 0)
        match = kind == side
        place = jnp.minimum(jnp.where(match, before, v - before), len(packed_refs) - 2)
        matches.append(match)
        found.append(place)
        before = before + jnp.where(match, 1, 0)
    return matches, found


def arrange_kernel(zero_ref, three_ref, two_ref, one_ref, _, *out_refs):
    packed_refs = (zero_ref, one_ref, two_ref, three_ref)
    capacity = zero_ref.shape[0] // 2
    for out_ref in out_refs:
        out_ref[...] = jnp.zeros(out_ref.shape, out_ref.dtype)
    matches, found = places(packed_refs, zero_ref.shape[1] - STAT_COLS)
    for ref, match, place in zip(packed_refs, matches, found):
        span = pl.ds(pl.multiple_of(place * capacity, capacity), capacity)
        for wanted, (own_ref, given_ref) in ((True, out_refs[:2]), (False, out_refs[2:])):

            @pl.when(match == wanted)
            def _():
                own_ref[span, :] = ref[:capacity, :]
                given_ref[span, :] = ref[capacity:, :]


def weights_times_rows(weight_refs, spans, rows, out_ref):
    at = 0
    for weight_ref, (first, last) in zip(weight_refs, spans):
        for start in range(first, last, STRIP):
            stop = min(start + STRIP, last)
            out_ref[at : at + stop - start, :] = lax.dot_general(
                weight_ref[start:stop, :], rows, (((1,), (1,)), ((), ())), preferred_element_type=jnp.float32
            ).astype(jnp.bfloat16)
            at += stop - start


def gate_kernel(side_far_ref, side_own_ref, far_ref, own_ref, *refs):
    weight_refs, out_ref, rows_ref = refs[:2], refs[-2], refs[-1]
    half = own_ref.shape[0]
    rows = rows_ref.shape[0]
    units = out_ref.shape[0] - TILE
    columns = rows_ref.shape[1] // 2
    rows_ref[2 * half :, :] = jnp.zeros((rows - 2 * half, 2 * columns), rows_ref.dtype)
    for side in range(2):

        @pl.when(lax.axis_index("mod") == side)
        def _():
            here, there = side * columns, (1 - side) * columns
            rows_ref[:half, here : here + columns] = own_ref[:, :columns]
            rows_ref[half : 2 * half, here : here + columns] = far_ref[:, :columns]
            rows_ref[:half, there : there + columns] = side_own_ref[:, :columns]
            rows_ref[half : 2 * half, there : there + columns] = side_far_ref[:, :columns]

    spans = [(0, ref.shape[0]) for ref in weight_refs]
    weights_times_rows(weight_refs, spans, rows_ref[...], out_ref)
    tails = [ref[:, columns:].astype(jnp.float32) for ref in (own_ref, side_own_ref, far_ref, side_far_ref)]
    unused = jnp.zeros((rows - 2 * half, STAT_COLS), jnp.float32)
    stat = jnp.concatenate([tails[0] + tails[1], tails[2] + tails[3], unused], axis=0).T
    squares = stat[0:1] + stat[1:2]
    logits = stat[2:3] + stat[3:4]
    at_row = lax.broadcasted_iota(jnp.int32, (TILE, rows), 0)
    extra = jnp.zeros((TILE, rows), jnp.float32)
    for at, piece in enumerate(split_high_low(squares) + split_high_low(logits)):
        extra = jnp.where(at_row == at, piece, extra)
    out_ref[units:, :] = extra.astype(jnp.bfloat16)


def up_kernel(spans, rows_ref, *refs):
    weights_times_rows(refs[:-1], spans, rows_ref[...], refs[-1])


def activation_kernel(gate_ref, gate_other_ref, up_ref, up_other_ref, act_ref, silu_ref, stat_ref):
    early = act_ref.shape[0]
    units = early + silu_ref.shape[0]
    stat = gate_ref[units:, :].astype(jnp.float32) + gate_other_ref[units:, :].astype(jnp.float32)
    inverse = lax.rsqrt((stat[0:1] + stat[1:2]) / D + 1e-05)
    logits = (stat[2:3] + stat[3:4]) * inverse
    score = 1.0 / (1.0 + jnp.exp(-logits))
    at_row = lax.broadcasted_iota(jnp.int32, stat_ref.shape, 0)
    stat_ref[...] = jnp.where(at_row == 0, inverse, score)
    for start in range(0, units, STRIP):
        stop = min(start + STRIP, units)
        gate = gate_ref[start:stop, :].astype(jnp.float32) + gate_other_ref[start:stop, :].astype(jnp.float32)
        gate = gate * inverse
        silu = gate / (1.0 + jnp.exp(-gate)) * inverse
        inside = max(0, min(stop, early) - start)
        if inside:
            span = slice(start, start + inside)
            up = up_ref[span, :].astype(jnp.float32) + up_other_ref[span, :].astype(jnp.float32)
            act_ref[span, :] = (silu[:inside] * up).astype(jnp.bfloat16)
        if start + inside < stop:
            silu_ref[start + inside - early : stop - early, :] = silu[inside:]


def down_kernel(
    act_early_ref, silu_ref, stat_ref, up_ref, other_ref, first_ref, second_ref,
    kept_ref, far_ref, side_ref, side_far_ref, act_ref,
):
    units, rows = act_ref.shape
    early = act_early_ref.shape[0]
    act_ref[:early, :] = act_early_ref[...]
    up = up_ref[...].astype(jnp.float32) + other_ref[...].astype(jnp.float32)
    act_ref[early:, :] = (silu_ref[...] * up).astype(jnp.bfloat16)
    half, columns = kept_ref.shape
    score = jnp.broadcast_to(stat_ref[1:2, :], (rows, rows)).T[:, 0:1]
    first_units = first_ref.shape[0]
    for quarter in range(2):
        span = slice(quarter * columns, (quarter + 1) * columns)
        value = sum(
            lax.dot_general(
                act_ref[a:b, :], weight_ref[:, span], (((0,), (0,)), ((), ())), preferred_element_type=jnp.float32
            )
            for a, b, weight_ref in ((0, first_units, first_ref), (first_units, units, second_ref))
        )
        value = (value * score).astype(jnp.bfloat16)
        for across, (own_out, far_out) in enumerate(((kept_ref, far_ref), (side_ref, side_far_ref))):

            @pl.when((lax.axis_index("mod") ^ quarter) == across)
            def _():
                own_out[...] = value[:half]
                far_out[...] = value[half : 2 * half]


def merge_kernel(zero_ref, three_ref, two_ref, one_ref, kept_ref, side_ref, far_ref, side_far_ref, *out_refs):
    columns = kept_ref.shape[1]
    capacity = zero_ref.shape[0] // 2
    matches, found = places((zero_ref, one_ref, two_ref, three_ref), columns)
    for out_ref, match, place in zip(out_refs, matches, found):
        span = pl.ds(pl.multiple_of(place * capacity, capacity), capacity)
        for wanted, (first_ref, second_ref) in ((True, (kept_ref, far_ref)), (False, (side_ref, side_far_ref))):

            @pl.when(match == wanted)
            def _():
                out_ref[:capacity, :] = first_ref[span, :]
                out_ref[capacity:, :] = second_ref[span, :]


def scatter_kernel(pick_ref, zero_ref, one_ref, two_ref, three_ref, out_hbm, out_ref, semaphores):
    columns = out_ref.shape[1]
    pieces = semaphores.shape[0]
    width = columns // pieces
    copies = []
    for n in range(pieces):
        span = slice(n * width, (n + 1) * width)
        total = zero_ref[:, span].astype(jnp.float32)
        for got_ref in (three_ref, two_ref, one_ref):
            total = total + got_ref[:, span].astype(jnp.float32)
        result = 0.0
        for piece in split_high_low(total)[::-1]:
            result = result + lax.dot_general(
                pick_ref[...], piece.astype(jnp.bfloat16), (((0,), (0,)), ((), ())),
                preferred_element_type=jnp.float32,
            )
        out_ref[:, span] = result.astype(jnp.bfloat16)
        copies.append(pltpu.make_async_copy(out_ref.at[:, span], out_hbm.at[:, span], semaphores.at[n]))
        copies[-1].start()
    for copy in copies:
        copy.wait()


def paired_local(
    residual,
    context,
    out_proj,
    norm_gain,
    router_weight,
    block_modality,
    expert_rows,
    gate_weight,
    up_weight,
    down_weight,
):
    tokens, columns = residual.shape
    experts, capacity = expert_rows.shape
    slots = 2 * capacity
    half = 4 * capacity
    rows = 2 * half
    units, width = down_weight.shape[1:]
    assert block_modality.shape == (1,) and experts == 4 and gate_weight.shape[0] == 2
    picked, pick, kind = call(
        select_kernel,
        "select",
        [array(slots, columns), array(slots, tokens), array(8, STAT_COLS, dtype=jnp.float32)],
        [IN_HBM] * 2,
        [in_hbm(expert_rows), in_hbm(context)],
        scratch=[
            pltpu.SMEM((experts, capacity), jnp.int32),
            pltpu.VMEM((tokens, columns), jnp.bfloat16),
            pltpu.SemaphoreType.DMA((2,)),
        ],
    )
    turned = [(t * 4 + q, q * 4 + t) for t in range(4) for q in range(4)]
    near = lax.ppermute(picked, ("tok", "mod", "fsdp"), turned)
    gate_units, up_units, down_units = [round(units * part / TILE) * TILE for part in (0.3, 0.3, 0.25)]
    gate_first, proj_held, rest = call(
        keep_gate_kernel,
        "keep_gate",
        [
            pltpu.VMEM((gate_units, width), jnp.bfloat16),
            pltpu.VMEM(out_proj.shape, jnp.bfloat16),
            array(slots, columns, dtype=jnp.float32),
        ],
        [ANYWHERE, ON_CHIP, IN_HBM, IN_HBM, IN_HBM],
        [near, pick, in_hbm(residual), in_hbm(gate_weight.swapaxes(1, 2)), in_hbm(out_proj)],
        scratch=[pltpu.VMEM((tokens, columns), jnp.bfloat16), pltpu.SemaphoreType.DMA((3,))],
        moved=units * width,
        limit=2 << 20,
    )
    plane = [lax.ppermute(near, ("mod", "fsdp"), crossed(2, u)) for u in (3, 2, 1)][::-1]
    partial = call(
        project_kernel,
        "project",
        array(4, slots, columns),
        [ON_CHIP] * 6,
        [near, *plane, proj_held, gate_first],
        scratch=[pltpu.VMEM((rows, columns), jnp.bfloat16)],
    )
    sums = [lax.ppermute(partial[v], "tok", crossed(2, v)) for v in (3, 2, 1)][::-1]
    gate_second, up_first = keep_on_chip(
        partial,
        [gate_weight.swapaxes(1, 2), up_weight.swapaxes(1, 2)],
        [(gate_units, units), (0, up_units)],
        "keep_more",
    )
    packed_columns = columns + STAT_COLS
    packed = call(
        norm_kernel,
        "norm",
        array(slots, packed_columns),
        [ON_CHIP] * 9,
        [kind, rest, partial, *sums[::-1], norm_gain, router_weight.T, up_first],
    )
    others = [lax.ppermute(packed, "tok", crossed(2, v)) for v in (3, 2, 1)][::-1]
    up_second, down_first = keep_on_chip(
        packed,
        [up_weight.swapaxes(1, 2), down_weight],
        [(up_units, units), (0, down_units)],
        "keep_up",
    )
    kept_slots = 3 * capacity
    own, to_far_rows, to_side_rows, to_corner_rows = call(
        arrange_kernel,
        "arrange",
        [array(kept_slots, packed_columns)] * 4,
        [ON_CHIP] * 5,
        [packed, *others[::-1], up_second],
    )
    both_axes = ("groups", "mod")
    side_far = lax.ppermute(to_corner_rows, both_axes, crossed(2, 3))
    far = lax.ppermute(to_far_rows, "groups", SWAP)
    side_own = lax.ppermute(to_side_rows, "mod", SWAP)

    (down_second,) = keep_on_chip(own, [down_weight], [(down_units, units)], "keep_down")

    flops = 2 * rows * units * width
    gate, gathered = call(
        gate_kernel,
        "gate",
        [array(units + TILE, rows), array(rows, width)],
        [ON_CHIP] * 7,
        [side_far, side_own, far, own, gate_first, gate_second, down_second],
        flops=flops,
    )
    late = units // 4 // TILE * TILE
    up_rest = units - up_units
    up_parts = [
        call(
            functools.partial(up_kernel, spans),
            "up",
            array(sum(b - a for a, b in spans), rows),
            [ON_CHIP] * (1 + len(spans)),
            [gathered, *weights],
            flops=flops * sum(b - a for a, b in spans) // units,
        )
        for spans, weights in (
            (((0, up_units), (0, up_rest - late)), (up_first, up_second)),
            (((up_rest - late, up_rest),), (up_second,)),
        )
    ]
    gate_other = lax.ppermute(gate, "fsdp", SWAP)
    up_others = [lax.ppermute(part, "fsdp", SWAP) for part in up_parts]
    act_early, silu_late, stat = call(
        activation_kernel,
        "activation",
        [
            array(units - late, rows),
            array(late, rows, dtype=jnp.float32),
            array(8, rows, dtype=jnp.float32),
        ],
        [ON_CHIP] * 4,
        [gate, gate_other, up_parts[0], up_others[0]],
        moved=8 * units * rows,
    )
    kept, to_far, to_side, to_side_far = call(
        down_kernel,
        "down",
        [array(kept_slots, columns)] * 4,
        [ON_CHIP] * 7,
        [act_early, silu_late, stat, up_parts[1], up_others[1], down_first, down_second],
        scratch=[pltpu.VMEM((units, rows), jnp.bfloat16)],
        flops=flops,
    )
    from_side_far = lax.ppermute(to_side_far, both_axes, crossed(2, 3))
    from_far = lax.ppermute(to_far, "groups", SWAP)
    from_side = lax.ppermute(to_side, "mod", SWAP)
    merged = call(
        merge_kernel,
        "merge",
        [array(slots, columns)] * 4,
        [ON_CHIP] * 8,
        [packed, *others[::-1], kept, from_side, from_far, from_side_far],
    )
    values = [merged[0]] + [lax.ppermute(merged[v], "tok", crossed(2, v)) for v in (1, 2, 3)]
    return pl.pallas_call(
        scatter_kernel,
        out_shape=pltpu.HBM((tokens, columns), jnp.bfloat16),
        in_specs=[ON_CHIP] * 5,
        out_specs=IN_HBM,
        scratch_shapes=[pltpu.VMEM((tokens, columns), jnp.bfloat16), pltpu.SemaphoreType.DMA((4,))],
        compiler_params=pltpu.CompilerParams(vmem_limit_bytes=8 << 20),
        name="scatter",
    )(pick, *values)


def solution(mesh):
    placed = (
        P(("groups", "tok"), ("fsdp", "mod")),
        P(("groups", "tok"), ("mod", "fsdp")),
        P("tok", ("fsdp", "mod")),
        P(None, ("fsdp", "mod")),
        P(("fsdp", "mod"), None),
        P(("groups", "tok")),
        P(None, ("groups", "tok")),
        P("mod", "fsdp", "tok"),
        P("mod", "fsdp", "tok"),
        P("mod", "tok", "fsdp"),
    )
    sizes = dict(n_tok=mesh.shape["tok"], n_mod=mesh.shape["mod"], n_fsdp=mesh.shape["fsdp"])
    paired = (
        mesh.shape["groups"] == 2
        and sizes == dict(n_tok=4, n_mod=2, n_fsdp=2)
    )
    body = paired_local if paired else functools.partial(local, **sizes)
    return jax.shard_map(
        body,
        mesh=mesh,
        in_specs=placed,
        out_specs=P(("groups", "tok"), ("fsdp", "mod")),
        check_vma=False,
    )
```

```python
import functools

import jax
import jax.numpy as jnp
from jax import lax
from jax.experimental import pallas as pl
from jax.experimental.pallas import tpu as pltpu
from jax.sharding import PartitionSpec as P

D = 4096
STAT_COLS = 128
FEW = 4


def ring(size, step):
    return [(i, (i + step) % size) for i in range(size)]


def reduce_tok(blocks, n_tok):
    if n_tok > FEW:
        return lax.psum_scatter(blocks, "tok", scatter_dimension=0, tiled=False).astype(jnp.float32)
    own = lax.axis_index("tok")
    total = lax.dynamic_index_in_dim(blocks, own, 0, False).astype(jnp.float32)
    for step in range(1, n_tok):
        sent = lax.dynamic_index_in_dim(blocks, (own + step) % n_tok, 0, False)
        total = total + lax.ppermute(sent, "tok", ring(n_tok, step)).astype(jnp.float32)
    return total


def gather_tok(rows, n_tok):
    if n_tok > FEW:
        return lax.all_gather(rows, "tok", axis=0, tiled=False)
    own = lax.axis_index("tok")
    result = jnp.zeros((n_tok,) + rows.shape, rows.dtype)
    result = lax.dynamic_update_index_in_dim(result, rows, own, 0)
    for step in range(1, n_tok):
        got = lax.ppermute(rows, "tok", ring(n_tok, step))
        result = lax.dynamic_update_index_in_dim(result, got, (own - step) % n_tok, 0)
    return result


def spread_context(rows, n_tok, n_mod, n_fsdp):
    if n_tok > FEW or n_tok != n_mod * n_fsdp:
        full = lax.all_gather(rows, ("mod", "fsdp"), axis=1, tiled=True)
        split = full.reshape(full.shape[0], n_tok, full.shape[1] // n_tok).transpose(1, 0, 2)
        return lax.all_to_all(split, "tok", 0, 0, tiled=True)
    pairs = [(t * n_tok + q, q * n_tok + t) for t in range(n_tok) for q in range(n_tok)]
    swapped = lax.ppermute(rows, ("tok", "mod", "fsdp"), pairs)
    return lax.all_gather(swapped, ("mod", "fsdp"), axis=0, tiled=False)


def local(
    residual,
    context,
    out_proj,
    norm_gain,
    router_weight,
    block_modality,
    expert_rows,
    gate_weight,
    up_weight,
    down_weight,
    *,
    n_tok,
    n_mod,
    n_fsdp,
):
    token_count = residual.shape[0]
    experts, capacity = expert_rows.shape
    kind_experts = experts // 2
    slots = kind_experts * capacity
    local_experts = gate_weight.shape[0]
    columns = residual.shape[1]
    assert block_modality.shape == (1,) and n_mod * local_experts == experts
    modality = block_modality[0]
    first = modality * kind_experts
    mod_index = lax.axis_index("mod")

    own_rows = lax.dynamic_slice_in_dim(expert_rows, first, kind_experts, 0).reshape(slots)
    pick = own_rows[:, None] == lax.iota(jnp.int32, token_count)[None, :]
    pick_half = pick.astype(jnp.bfloat16)
    picked_context = jnp.dot(pick_half, context, preferred_element_type=jnp.float32).astype(jnp.bfloat16)
    picked_residual = jnp.dot(pick_half, residual, preferred_element_type=jnp.float32)

    spread = spread_context(picked_context, n_tok, n_mod, n_fsdp)
    partial = jnp.einsum("tsk,kc->tsc", spread, out_proj, preferred_element_type=jnp.float32)
    hidden = picked_residual + reduce_tok(partial.astype(jnp.bfloat16), n_tok)

    gain_table = norm_gain.astype(jnp.float32)
    gained = hidden * jnp.where(modality == 0, gain_table[0], gain_table[1])[None, :]
    router = lax.dynamic_slice_in_dim(router_weight.astype(jnp.float32), first, kind_experts, 1)
    slot_router = jnp.repeat(router.T, capacity, axis=0)
    squares = jnp.sum(hidden * hidden, axis=1, keepdims=True)
    logits = jnp.sum(gained * slot_router, axis=1, keepdims=True)
    flag = jnp.broadcast_to(modality.astype(jnp.bfloat16), (slots, 1))
    stat_list = []
    for stat in (squares, logits):
        high = lax.reduce_precision(stat, 8, 7)
        stat_list += [high.astype(jnp.bfloat16), (stat - high).astype(jnp.bfloat16)]
    packed = jnp.concatenate(
        [gained.astype(jnp.bfloat16)] + stat_list
        + [flag, jnp.zeros((slots, STAT_COLS - 5), jnp.bfloat16)],
        axis=1,
    )

    everyone = gather_tok(packed, n_tok)
    both = lax.all_gather(everyone, "mod", axis=0, tiled=False)
    kind_first = (mod_index * local_experts) % kind_experts
    both = both.reshape(n_mod, n_tok, kind_experts, capacity, columns + STAT_COLS)
    mine = lax.dynamic_slice_in_dim(both, kind_first, local_experts, 2)
    piece = mine[..., :columns].transpose(2, 1, 3, 0, 4).reshape(
        local_experts, n_tok * capacity, n_mod * columns
    )
    tail = mine[..., columns : columns + 5].astype(jnp.float32)
    half_stats = jnp.sum(
        jnp.stack([tail[..., 0] + tail[..., 1], tail[..., 2] + tail[..., 3]], axis=-1), axis=0
    )
    stats = lax.psum(half_stats, "fsdp")
    flags = tail[0, :, :, :, 4]
    by_expert = stats.transpose(1, 0, 2, 3).reshape(local_experts, n_tok * capacity, 2)
    inverse = lax.rsqrt(by_expert[..., 0:1] / D + 1e-05)
    score = jax.nn.sigmoid(by_expert[..., 1:2] * inverse)

    gate_part = jnp.einsum("esd,edf->esf", piece, gate_weight, preferred_element_type=jnp.float32)
    up_part = jnp.einsum("esd,edf->esf", piece, up_weight, preferred_element_type=jnp.float32)
    gate_half = gate_part.astype(jnp.bfloat16)
    up_half = up_part.astype(jnp.bfloat16)
    if n_fsdp == 2:
        swap = [(0, 1), (1, 0)]
        gate_sum = gate_half.astype(jnp.float32) + lax.ppermute(gate_half, "fsdp", swap).astype(jnp.float32)
        up_sum = up_half.astype(jnp.float32) + lax.ppermute(up_half, "fsdp", swap).astype(jnp.float32)
    else:
        gate_sum = lax.psum(gate_half, "fsdp").astype(jnp.float32)
        up_sum = lax.psum(up_half, "fsdp").astype(jnp.float32)
    activation = (jax.nn.silu(gate_sum * inverse) * (up_sum * inverse)).astype(jnp.bfloat16)
    value = jnp.einsum("esf,efd->esd", activation, down_weight, preferred_element_type=jnp.float32)
    value = (value * score).astype(jnp.bfloat16)
    value = value.reshape(local_experts, n_tok, capacity, n_mod * columns).transpose(1, 0, 2, 3)

    own_kind = (mod_index * local_experts) // kind_experts
    valid = (flags == own_kind.astype(jnp.float32))[..., None]
    if n_mod == 2:
        value = value.reshape(n_tok, local_experts, capacity, n_mod, columns)
        kept = lax.dynamic_index_in_dim(value, mod_index, 3, False)
        sent = lax.dynamic_index_in_dim(value, 1 - mod_index, 3, False)
        got = lax.ppermute(sent, "mod", [(0, 1), (1, 0)])
        merged = jnp.where(valid, kept, got).reshape(n_tok, slots, columns)
    else:
        value = jnp.where(valid, value, jnp.zeros((), jnp.bfloat16))
        wide = jnp.zeros((n_tok, kind_experts, capacity, n_mod * columns), jnp.bfloat16)
        wide = lax.dynamic_update_slice_in_dim(wide, value, kind_first, 1)
        wide = wide.reshape(n_tok, slots, n_mod * columns)
        merged = lax.psum_scatter(wide, "mod", scatter_dimension=2, tiled=True)
    summed = reduce_tok(merged, n_tok)
    return jnp.dot(
        pick.astype(jnp.float32).T, summed, precision=lax.Precision.HIGHEST
    ).astype(jnp.bfloat16)


SWAP = [(0, 1), (1, 0)]
STRIP = 688
TILE = 16
ON_CHIP = pl.BlockSpec(memory_space=pltpu.VMEM)
IN_HBM = pl.BlockSpec(memory_space=pltpu.HBM)
ANYWHERE = pl.BlockSpec(memory_space=pl.ANY)


def crossed(bits, flip):
    return [(i, i ^ flip) for i in range(1 << bits)]


def call(kernel, name, outs, specs, args, scratch=(), flops=0, moved=0, limit=8 << 20):
    return pl.pallas_call(
        kernel,
        out_shape=outs,
        in_specs=specs,
        out_specs=jax.tree.map(lambda _: ON_CHIP, outs),
        scratch_shapes=list(scratch),
        compiler_params=pltpu.CompilerParams(vmem_limit_bytes=limit),
        cost_estimate=pl.CostEstimate(flops=flops, transcendentals=0, bytes_accessed=moved),
        name=name,
    )(*args)


def array(*shape, dtype=jnp.bfloat16):
    return jax.ShapeDtypeStruct(shape, dtype)


def keep_kernel(spans, after_ref, *refs):
    count = len(spans)
    weights, held, semaphores = refs[:count], refs[count : 2 * count], refs[-1]
    copies = [
        pltpu.make_async_copy(weight.at[lax.axis_index("groups"), a:b], to, semaphores.at[n])
        for n, (weight, to, (a, b)) in enumerate(zip(weights, held, spans))
    ]
    for copy in copies:
        copy.start()
    for copy in copies:
        copy.wait()


def in_hbm(value):
    return pltpu.with_memory_space_constraint(value, pltpu.HBM)


def keep_on_chip(after, weights, spans, name):
    return call(
        functools.partial(keep_kernel, spans),
        name,
        [pltpu.VMEM((b - a, weight.shape[2]), jnp.bfloat16) for weight, (a, b) in zip(weights, spans)],
        [ANYWHERE] + [IN_HBM] * len(spans),
        [after] + [in_hbm(weight) for weight in weights],
        scratch=[pltpu.SemaphoreType.DMA((len(spans),))],
        moved=sum(2 * (b - a) * weight.shape[2] for weight, (a, b) in zip(weights, spans)),
        limit=1 << 20,
    )


def select_kernel(
    rows_hbm, context_hbm, picked_ref, pick_ref, kind_ref, rows_ref, context_ref, semaphores
):
    rows_copy = pltpu.make_async_copy(rows_hbm, rows_ref, semaphores.at[0])
    context_copy = pltpu.make_async_copy(context_hbm, context_ref, semaphores.at[1])
    rows_copy.start()
    context_copy.start()
    rows_copy.wait()
    kind = jnp.where(jnp.maximum(rows_ref[2, 0], rows_ref[3, 0]) >= 0, 1, 0)
    kind_ref[...] = jnp.full(kind_ref.shape, kind, jnp.int32).astype(jnp.float32)
    capacity = rows_ref.shape[1]
    slots, tokens = pick_ref.shape
    row = lax.broadcasted_iota(jnp.int32, (slots, tokens), 0)
    token = lax.broadcasted_iota(jnp.int32, (slots, tokens), 1)
    wanted = jnp.full((slots, tokens), -1, jnp.int32)
    for e in range(2):
        expert = 2 * kind + (lax.axis_index("groups") ^ e)
        for s in range(capacity):
            wanted = jnp.where(row == e * capacity + s, rows_ref[expert, s], wanted)
    pick = jnp.where(wanted == token, 1.0, 0.0).astype(jnp.bfloat16)
    pick_ref[...] = pick
    context_copy.wait()
    picked_ref[...] = jnp.dot(pick, context_ref[...], preferred_element_type=jnp.float32).astype(jnp.bfloat16)


def keep_gate_kernel(
    pick_ref, residual_hbm, gate_ref, proj_ref, gate_held, proj_held, rest_ref, residual_ref, semaphores
):
    copies = [
        pltpu.make_async_copy(residual_hbm, residual_ref, semaphores.at[0]),
        pltpu.make_async_copy(proj_ref, proj_held, semaphores.at[1]),
        pltpu.make_async_copy(gate_ref.at[lax.axis_index("groups"), : gate_held.shape[0]], gate_held, semaphores.at[2]),
    ]
    for copy in copies:
        copy.start()
    copies[0].wait()
    rest_ref[...] = jnp.dot(pick_ref[...], residual_ref[...], preferred_element_type=jnp.float32)
    for copy in copies[1:]:
        copy.wait()


def join_kernel(near_ref, across_ref, _, out_ref):
    slots = near_ref.shape[0]
    out_ref[:slots, :] = near_ref[...]
    out_ref[slots:, :] = across_ref[...]


def project_kernel(joined_ref, other_ref, weight_ref, out_ref, rows_ref):
    pair = joined_ref.shape[0]
    slots = pair // 2
    rows_ref[:pair, :] = joined_ref[...]
    rows_ref[pair:, :] = other_ref[...]
    product = jnp.dot(rows_ref[...], weight_ref[...], preferred_element_type=jnp.float32)
    product = product.astype(jnp.bfloat16)
    corner = 2 * lax.axis_index("mod") + lax.axis_index("fsdp")
    flip = lax.axis_index("tok") ^ corner
    for n, u in enumerate((0, 2, 1, 3)):
        out_ref[flip ^ u] = product[n * slots : (n + 1) * slots, :]


def split_high_low(value):
    high = value.astype(jnp.bfloat16).astype(jnp.float32)
    return high, value - high


def norm_kernel(kind_ref, rest_ref, partial_ref, three_ref, two_ref, one_ref, gain_ref, router_ref, _, out_ref):
    slots, columns = rest_ref.shape
    hidden = rest_ref[...] + partial_ref[0].astype(jnp.float32)
    for got_ref in (three_ref, two_ref, one_ref):
        hidden = hidden + got_ref[...].astype(jnp.float32)
    kind = kind_ref[0:1, 0:1]
    gains = gain_ref[...].astype(jnp.float32)
    gained = hidden * jnp.where(kind == 0.0, gains[0:1], gains[1:2])
    out_ref[:, :columns] = gained.astype(jnp.bfloat16)
    table = router_ref[...].astype(jnp.float32)
    pieces = []
    for e in range(2):
        second = (lax.axis_index("groups") ^ e) == 1
        text = jnp.where(second, table[1:2], table[0:1])
        image = jnp.where(second, table[3:4], table[2:3])
        weights = jnp.where(kind == 0.0, text, image)
        half = slots // 2
        pieces.append(jnp.sum(gained[e * half : (e + 1) * half] * weights, axis=1, keepdims=True))
    logits = jnp.concatenate(pieces, axis=0)
    squares = jnp.sum(hidden * hidden, axis=1, keepdims=True)
    lane = lax.broadcasted_iota(jnp.int32, (slots, STAT_COLS), 1)
    extra = jnp.where(lane == 4, kind, 0.0)
    for at, stat in enumerate(split_high_low(squares) + split_high_low(logits)):
        extra = jnp.where(lane == at, stat, extra)
    out_ref[:, columns:] = extra.astype(jnp.bfloat16)


def places(packed_refs, columns):
    side = lax.axis_index("mod")
    matches, found, before = [], [], 0
    for v, ref in enumerate(packed_refs):
        flag = ref[:TILE, columns:].astype(jnp.float32)[0, 4]
        kind = jnp.where(flag > 0.5, 1, 0)
        match = kind == side
        place = jnp.minimum(jnp.where(match, before, v - before), len(packed_refs) - 2)
        matches.append(match)
        found.append(place)
        before = before + jnp.where(match, 1, 0)
    return matches, found


def arrange_kernel(zero_ref, three_ref, two_ref, one_ref, _, *out_refs):
    packed_refs = (zero_ref, one_ref, two_ref, three_ref)
    capacity = zero_ref.shape[0] // 2
    for out_ref in out_refs:
        out_ref[...] = jnp.zeros(out_ref.shape, out_ref.dtype)
    matches, found = places(packed_refs, zero_ref.shape[1] - STAT_COLS)
    for ref, match, place in zip(packed_refs, matches, found):
        span = pl.ds(pl.multiple_of(place * capacity, capacity), capacity)
        for wanted, (own_ref, given_ref) in ((True, out_refs[:2]), (False, out_refs[2:])):

            @pl.when(match == wanted)
            def _():
                own_ref[span, :] = ref[:capacity, :]
                given_ref[span, :] = ref[capacity:, :]


def weights_times_rows(weight_refs, spans, rows, out_ref):
    at = 0
    for weight_ref, (first, last) in zip(weight_refs, spans):
        for start in range(first, last, STRIP):
            stop = min(start + STRIP, last)
            out_ref[at : at + stop - start, :] = lax.dot_general(
                weight_ref[start:stop, :], rows, (((1,), (1,)), ((), ())), preferred_element_type=jnp.float32
            ).astype(jnp.bfloat16)
            at += stop - start


def gate_kernel(side_far_ref, side_own_ref, far_ref, own_ref, *refs):
    weight_refs, out_ref, rows_ref = refs[:2], refs[-2], refs[-1]
    half = own_ref.shape[0]
    rows = rows_ref.shape[0]
    units = out_ref.shape[0] - TILE
    columns = rows_ref.shape[1] // 2
    rows_ref[2 * half :, :] = jnp.zeros((rows - 2 * half, 2 * columns), rows_ref.dtype)
    for side in range(2):

        @pl.when(lax.axis_index("mod") == side)
        def _():
            here, there = side * columns, (1 - side) * columns
            rows_ref[:half, here : here + columns] = own_ref[:, :columns]
            rows_ref[half : 2 * half, here : here + columns] = far_ref[:, :columns]
            rows_ref[:half, there : there + columns] = side_own_ref[:, :columns]
            rows_ref[half : 2 * half, there : there + columns] = side_far_ref[:, :columns]

    spans = [(0, ref.shape[0]) for ref in weight_refs]
    weights_times_rows(weight_refs, spans, rows_ref[...], out_ref)
    tails = [ref[:, columns:].astype(jnp.float32) for ref in (own_ref, side_own_ref, far_ref, side_far_ref)]
    unused = jnp.zeros((rows - 2 * half, STAT_COLS), jnp.float32)
    stat = jnp.concatenate([tails[0] + tails[1], tails[2] + tails[3], unused], axis=0).T
    squares = stat[0:1] + stat[1:2]
    logits = stat[2:3] + stat[3:4]
    at_row = lax.broadcasted_iota(jnp.int32, (TILE, rows), 0)
    extra = jnp.zeros((TILE, rows), jnp.float32)
    for at, piece in enumerate(split_high_low(squares) + split_high_low(logits)):
        extra = jnp.where(at_row == at, piece, extra)
    out_ref[units:, :] = extra.astype(jnp.bfloat16)


def up_kernel(spans, rows_ref, *refs):
    weights_times_rows(refs[:-1], spans, rows_ref[...], refs[-1])


def activation_kernel(gate_ref, gate_other_ref, up_ref, up_other_ref, act_ref, silu_ref, stat_ref):
    early = act_ref.shape[0]
    units = early + silu_ref.shape[0]
    stat = gate_ref[units:, :].astype(jnp.float32) + gate_other_ref[units:, :].astype(jnp.float32)
    inverse = lax.rsqrt((stat[0:1] + stat[1:2]) / D + 1e-05)
    logits = (stat[2:3] + stat[3:4]) * inverse
    score = 1.0 / (1.0 + jnp.exp(-logits))
    at_row = lax.broadcasted_iota(jnp.int32, stat_ref.shape, 0)
    stat_ref[...] = jnp.where(at_row == 0, inverse, score)
    for start in range(0, units, STRIP):
        stop = min(start + STRIP, units)
        gate = gate_ref[start:stop, :].astype(jnp.float32) + gate_other_ref[start:stop, :].astype(jnp.float32)
        gate = gate * inverse
        silu = gate / (1.0 + jnp.exp(-gate)) * inverse
        inside = max(0, min(stop, early) - start)
        if inside:
            span = slice(start, start + inside)
            up = up_ref[span, :].astype(jnp.float32) + up_other_ref[span, :].astype(jnp.float32)
            act_ref[span, :] = (silu[:inside] * up).astype(jnp.bfloat16)
        if start + inside < stop:
            silu_ref[start + inside - early : stop - early, :] = silu[inside:]


def down_kernel(
    act_early_ref, silu_ref, stat_ref, up_ref, other_ref, first_ref, second_ref,
    kept_ref, far_ref, side_ref, side_far_ref, act_ref,
):
    units, rows = act_ref.shape
    early = act_early_ref.shape[0]
    act_ref[:early, :] = act_early_ref[...]
    up = up_ref[...].astype(jnp.float32) + other_ref[...].astype(jnp.float32)
    act_ref[early:, :] = (silu_ref[...] * up).astype(jnp.bfloat16)
    half, columns = kept_ref.shape
    score = jnp.broadcast_to(stat_ref[1:2, :], (rows, rows)).T[:, 0:1]
    first_units = first_ref.shape[0]
    for quarter in range(2):
        span = slice(quarter * columns, (quarter + 1) * columns)
        value = sum(
            lax.dot_general(
                act_ref[a:b, :], weight_ref[:, span], (((0,), (0,)), ((), ())), preferred_element_type=jnp.float32
            )
            for a, b, weight_ref in ((0, first_units, first_ref), (first_units, units, second_ref))
        )
        value = (value * score).astype(jnp.bfloat16)
        for across, (own_out, far_out) in enumerate(((kept_ref, far_ref), (side_ref, side_far_ref))):

            @pl.when((lax.axis_index("mod") ^ quarter) == across)
            def _():
                own_out[...] = value[:half]
                far_out[...] = value[half : 2 * half]


def merge_kernel(zero_ref, three_ref, two_ref, one_ref, kept_ref, side_ref, far_ref, side_far_ref, *out_refs):
    columns = kept_ref.shape[1]
    capacity = zero_ref.shape[0] // 2
    matches, found = places((zero_ref, one_ref, two_ref, three_ref), columns)
    for out_ref, match, place in zip(out_refs, matches, found):
        span = pl.ds(pl.multiple_of(place * capacity, capacity), capacity)
        for wanted, (first_ref, second_ref) in ((True, (kept_ref, far_ref)), (False, (side_ref, side_far_ref))):

            @pl.when(match == wanted)
            def _():
                out_ref[:capacity, :] = first_ref[span, :]
                out_ref[capacity:, :] = second_ref[span, :]


def add_kernel(zero_ref, one_ref, two_ref, out_ref):
    out_ref[...] = (
        zero_ref[...].astype(jnp.float32) + one_ref[...].astype(jnp.float32) + two_ref[...].astype(jnp.float32)
    )


def scatter_kernel(pick_ref, sum_ref, three_ref, out_hbm, out_ref, semaphores):
    columns = out_ref.shape[1]
    pieces = semaphores.shape[0]
    width = columns // pieces
    copies = []
    for n in range(pieces):
        span = slice(n * width, (n + 1) * width)
        total = sum_ref[:, span] + three_ref[:, span].astype(jnp.float32)
        result = 0.0
        for piece in split_high_low(total)[::-1]:
            result = result + lax.dot_general(
                pick_ref[...], piece.astype(jnp.bfloat16), (((0,), (0,)), ((), ())),
                preferred_element_type=jnp.float32,
            )
        out_ref[:, span] = result.astype(jnp.bfloat16)
        copies.append(pltpu.make_async_copy(out_ref.at[:, span], out_hbm.at[:, span], semaphores.at[n]))
        copies[-1].start()
    for copy in copies:
        copy.wait()


def paired_local(
    residual,
    context,
    out_proj,
    norm_gain,
    router_weight,
    block_modality,
    expert_rows,
    gate_weight,
    up_weight,
    down_weight,
):
    tokens, columns = residual.shape
    experts, capacity = expert_rows.shape
    slots = 2 * capacity
    half = 4 * capacity
    rows = 2 * half
    units, width = down_weight.shape[1:]
    assert block_modality.shape == (1,) and experts == 4 and gate_weight.shape[0] == 2
    picked, pick, kind = call(
        select_kernel,
        "select",
        [array(slots, columns), array(slots, tokens), array(8, STAT_COLS, dtype=jnp.float32)],
        [IN_HBM] * 2,
        [in_hbm(expert_rows), in_hbm(context)],
        scratch=[
            pltpu.SMEM((experts, capacity), jnp.int32),
            pltpu.VMEM((tokens, columns), jnp.bfloat16),
            pltpu.SemaphoreType.DMA((2,)),
        ],
    )
    plane = ("tok", "mod", "fsdp")
    to_first = [(t * 4 + q, q * 4 + t) for t in range(4) for q in range(4)]
    to_second = [(t * 4 + q, q * 4 + (t ^ 2)) for t in range(4) for q in range(4)]
    across = lax.ppermute(picked, plane, to_second)
    near = lax.ppermute(picked, plane, to_first)
    gate_units, up_units, down_units = [round(units * part / TILE) * TILE for part in (0.4, 0.37, 0.27)]
    gate_first, proj_held, rest = call(
        keep_gate_kernel,
        "keep_gate",
        [
            pltpu.VMEM((gate_units, width), jnp.bfloat16),
            pltpu.VMEM(out_proj.shape, jnp.bfloat16),
            array(slots, columns, dtype=jnp.float32),
        ],
        [ON_CHIP, IN_HBM, IN_HBM, IN_HBM],
        [pick, in_hbm(residual), in_hbm(gate_weight.swapaxes(1, 2)), in_hbm(out_proj)],
        scratch=[pltpu.VMEM((tokens, columns), jnp.bfloat16), pltpu.SemaphoreType.DMA((3,))],
        moved=units * width,
        limit=2 << 20,
    )
    joined = call(join_kernel, "join", array(half, columns), [ON_CHIP] * 3, [near, across, gate_first])
    other = lax.ppermute(joined, "fsdp", SWAP)
    partial = call(
        project_kernel,
        "project",
        array(4, slots, columns),
        [ON_CHIP] * 3,
        [joined, other, proj_held],
        scratch=[pltpu.VMEM((rows, columns), jnp.bfloat16)],
    )
    sums = [lax.ppermute(partial[v], "tok", crossed(2, v)) for v in (3, 2, 1)][::-1]
    gate_second, up_first = keep_on_chip(
        partial,
        [gate_weight.swapaxes(1, 2), up_weight.swapaxes(1, 2)],
        [(gate_units, units), (0, up_units)],
        "keep_more",
    )
    packed_columns = columns + STAT_COLS
    packed = call(
        norm_kernel,
        "norm",
        array(slots, packed_columns),
        [ON_CHIP] * 9,
        [kind, rest, partial, *sums[::-1], norm_gain, router_weight.T, up_first],
    )
    others = [lax.ppermute(packed, "tok", crossed(2, v)) for v in (3, 2, 1)][::-1]
    up_second, down_first = keep_on_chip(
        packed,
        [up_weight.swapaxes(1, 2), down_weight],
        [(up_units, units), (0, down_units)],
        "keep_up",
    )
    kept_slots = 3 * capacity
    own, to_far_rows, to_side_rows, to_corner_rows = call(
        arrange_kernel,
        "arrange",
        [array(kept_slots, packed_columns)] * 4,
        [ON_CHIP] * 5,
        [packed, *others[::-1], up_second],
    )
    both_axes = ("groups", "mod")
    side_far = lax.ppermute(to_corner_rows, both_axes, crossed(2, 3))
    far = lax.ppermute(to_far_rows, "groups", SWAP)
    side_own = lax.ppermute(to_side_rows, "mod", SWAP)

    (down_second,) = keep_on_chip(own, [down_weight], [(down_units, units)], "keep_down")

    flops = 2 * rows * units * width
    gate, gathered = call(
        gate_kernel,
        "gate",
        [array(units + TILE, rows), array(rows, width)],
        [ON_CHIP] * 7,
        [side_far, side_own, far, own, gate_first, gate_second, down_second],
        flops=flops,
    )
    late = units // 4 // TILE * TILE
    up_rest = units - up_units
    up_parts = [
        call(
            functools.partial(up_kernel, spans),
            "up",
            array(sum(b - a for a, b in spans), rows),
            [ON_CHIP] * (1 + len(spans)),
            [gathered, *weights],
            flops=flops * sum(b - a for a, b in spans) // units,
        )
        for spans, weights in (
            (((0, up_units), (0, up_rest - late)), (up_first, up_second)),
            (((up_rest - late, up_rest),), (up_second,)),
        )
    ]
    gate_other = lax.ppermute(gate, "fsdp", SWAP)
    up_others = [lax.ppermute(part, "fsdp", SWAP) for part in up_parts]
    act_early, silu_late, stat = call(
        activation_kernel,
        "activation",
        [
            array(units - late, rows),
            array(late, rows, dtype=jnp.float32),
            array(8, rows, dtype=jnp.float32),
        ],
        [ON_CHIP] * 4,
        [gate, gate_other, up_parts[0], up_others[0]],
        moved=8 * units * rows,
    )
    kept, to_far, to_side, to_side_far = call(
        down_kernel,
        "down",
        [array(kept_slots, columns)] * 4,
        [ON_CHIP] * 7,
        [act_early, silu_late, stat, up_parts[1], up_others[1], down_first, down_second],
        scratch=[pltpu.VMEM((units, rows), jnp.bfloat16)],
        flops=flops,
    )
    from_side_far = lax.ppermute(to_side_far, both_axes, crossed(2, 3))
    from_far = lax.ppermute(to_far, "groups", SWAP)
    from_side = lax.ppermute(to_side, "mod", SWAP)
    merged = call(
        merge_kernel,
        "merge",
        [array(slots, columns)] * 4,
        [ON_CHIP] * 8,
        [packed, *others[::-1], kept, from_side, from_far, from_side_far],
    )
    values = [merged[0]] + [lax.ppermute(merged[v], "tok", crossed(2, v)) for v in (1, 2, 3)]
    begun = call(add_kernel, "add", array(slots, columns, dtype=jnp.float32), [ON_CHIP] * 3, values[:3])
    return pl.pallas_call(
        scatter_kernel,
        out_shape=pltpu.HBM((tokens, columns), jnp.bfloat16),
        in_specs=[ON_CHIP] * 3,
        out_specs=IN_HBM,
        scratch_shapes=[pltpu.VMEM((tokens, columns), jnp.bfloat16), pltpu.SemaphoreType.DMA((4,))],
        compiler_params=pltpu.CompilerParams(vmem_limit_bytes=8 << 20),
        name="scatter",
    )(pick, begun, values[3])


def solution(mesh):
    placed = (
        P(("groups", "tok"), ("fsdp", "mod")),
        P(("groups", "tok"), ("mod", "fsdp")),
        P("tok", ("fsdp", "mod")),
        P(None, ("fsdp", "mod")),
        P(("fsdp", "mod"), None),
        P(("groups", "tok")),
        P(None, ("groups", "tok")),
        P("mod", "fsdp", "tok"),
        P("mod", "fsdp", "tok"),
        P("mod", "tok", "fsdp"),
    )
    sizes = dict(n_tok=mesh.shape["tok"], n_mod=mesh.shape["mod"], n_fsdp=mesh.shape["fsdp"])
    paired = (
        mesh.shape["groups"] == 2
        and sizes == dict(n_tok=4, n_mod=2, n_fsdp=2)
    )
    body = paired_local if paired else functools.partial(local, **sizes)
    return jax.shard_map(
        body,
        mesh=mesh,
        in_specs=placed,
        out_specs=P(("groups", "tok"), ("fsdp", "mod")),
        check_vma=False,
    )
```

```python
import functools

import jax
import jax.numpy as jnp
from jax import lax
from jax.experimental import pallas as pl
from jax.experimental.pallas import tpu as pltpu
from jax.sharding import PartitionSpec as P

D = 4096
STAT_COLS = 128
FEW = 4


def ring(size, step):
    return [(i, (i + step) % size) for i in range(size)]


def reduce_tok(blocks, n_tok):
    if n_tok > FEW:
        return lax.psum_scatter(blocks, "tok", scatter_dimension=0, tiled=False).astype(jnp.float32)
    own = lax.axis_index("tok")
    total = lax.dynamic_index_in_dim(blocks, own, 0, False).astype(jnp.float32)
    for step in range(1, n_tok):
        sent = lax.dynamic_index_in_dim(blocks, (own + step) % n_tok, 0, False)
        total = total + lax.ppermute(sent, "tok", ring(n_tok, step)).astype(jnp.float32)
    return total


def gather_tok(rows, n_tok):
    if n_tok > FEW:
        return lax.all_gather(rows, "tok", axis=0, tiled=False)
    own = lax.axis_index("tok")
    result = jnp.zeros((n_tok,) + rows.shape, rows.dtype)
    result = lax.dynamic_update_index_in_dim(result, rows, own, 0)
    for step in range(1, n_tok):
        got = lax.ppermute(rows, "tok", ring(n_tok, step))
        result = lax.dynamic_update_index_in_dim(result, got, (own - step) % n_tok, 0)
    return result


def spread_context(rows, n_tok, n_mod, n_fsdp):
    if n_tok > FEW or n_tok != n_mod * n_fsdp:
        full = lax.all_gather(rows, ("mod", "fsdp"), axis=1, tiled=True)
        split = full.reshape(full.shape[0], n_tok, full.shape[1] // n_tok).transpose(1, 0, 2)
        return lax.all_to_all(split, "tok", 0, 0, tiled=True)
    pairs = [(t * n_tok + q, q * n_tok + t) for t in range(n_tok) for q in range(n_tok)]
    swapped = lax.ppermute(rows, ("tok", "mod", "fsdp"), pairs)
    return lax.all_gather(swapped, ("mod", "fsdp"), axis=0, tiled=False)


def local(
    residual,
    context,
    out_proj,
    norm_gain,
    router_weight,
    block_modality,
    expert_rows,
    gate_weight,
    up_weight,
    down_weight,
    *,
    n_tok,
    n_mod,
    n_fsdp,
):
    token_count = residual.shape[0]
    experts, capacity = expert_rows.shape
    kind_experts = experts // 2
    slots = kind_experts * capacity
    local_experts = gate_weight.shape[0]
    columns = residual.shape[1]
    assert block_modality.shape == (1,) and n_mod * local_experts == experts
    modality = block_modality[0]
    first = modality * kind_experts
    mod_index = lax.axis_index("mod")

    own_rows = lax.dynamic_slice_in_dim(expert_rows, first, kind_experts, 0).reshape(slots)
    pick = own_rows[:, None] == lax.iota(jnp.int32, token_count)[None, :]
    pick_half = pick.astype(jnp.bfloat16)
    picked_context = jnp.dot(pick_half, context, preferred_element_type=jnp.float32).astype(jnp.bfloat16)
    picked_residual = jnp.dot(pick_half, residual, preferred_element_type=jnp.float32)

    spread = spread_context(picked_context, n_tok, n_mod, n_fsdp)
    partial = jnp.einsum("tsk,kc->tsc", spread, out_proj, preferred_element_type=jnp.float32)
    hidden = picked_residual + reduce_tok(partial.astype(jnp.bfloat16), n_tok)

    gain_table = norm_gain.astype(jnp.float32)
    gained = hidden * jnp.where(modality == 0, gain_table[0], gain_table[1])[None, :]
    router = lax.dynamic_slice_in_dim(router_weight.astype(jnp.float32), first, kind_experts, 1)
    slot_router = jnp.repeat(router.T, capacity, axis=0)
    squares = jnp.sum(hidden * hidden, axis=1, keepdims=True)
    logits = jnp.sum(gained * slot_router, axis=1, keepdims=True)
    flag = jnp.broadcast_to(modality.astype(jnp.bfloat16), (slots, 1))
    stat_list = []
    for stat in (squares, logits):
        high = lax.reduce_precision(stat, 8, 7)
        stat_list += [high.astype(jnp.bfloat16), (stat - high).astype(jnp.bfloat16)]
    packed = jnp.concatenate(
        [gained.astype(jnp.bfloat16)] + stat_list
        + [flag, jnp.zeros((slots, STAT_COLS - 5), jnp.bfloat16)],
        axis=1,
    )

    everyone = gather_tok(packed, n_tok)
    both = lax.all_gather(everyone, "mod", axis=0, tiled=False)
    kind_first = (mod_index * local_experts) % kind_experts
    both = both.reshape(n_mod, n_tok, kind_experts, capacity, columns + STAT_COLS)
    mine = lax.dynamic_slice_in_dim(both, kind_first, local_experts, 2)
    piece = mine[..., :columns].transpose(2, 1, 3, 0, 4).reshape(
        local_experts, n_tok * capacity, n_mod * columns
    )
    tail = mine[..., columns : columns + 5].astype(jnp.float32)
    half_stats = jnp.sum(
        jnp.stack([tail[..., 0] + tail[..., 1], tail[..., 2] + tail[..., 3]], axis=-1), axis=0
    )
    stats = lax.psum(half_stats, "fsdp")
    flags = tail[0, :, :, :, 4]
    by_expert = stats.transpose(1, 0, 2, 3).reshape(local_experts, n_tok * capacity, 2)
    inverse = lax.rsqrt(by_expert[..., 0:1] / D + 1e-05)
    score = jax.nn.sigmoid(by_expert[..., 1:2] * inverse)

    gate_part = jnp.einsum("esd,edf->esf", piece, gate_weight, preferred_element_type=jnp.float32)
    up_part = jnp.einsum("esd,edf->esf", piece, up_weight, preferred_element_type=jnp.float32)
    gate_half = gate_part.astype(jnp.bfloat16)
    up_half = up_part.astype(jnp.bfloat16)
    if n_fsdp == 2:
        swap = [(0, 1), (1, 0)]
        gate_sum = gate_half.astype(jnp.float32) + lax.ppermute(gate_half, "fsdp", swap).astype(jnp.float32)
        up_sum = up_half.astype(jnp.float32) + lax.ppermute(up_half, "fsdp", swap).astype(jnp.float32)
    else:
        gate_sum = lax.psum(gate_half, "fsdp").astype(jnp.float32)
        up_sum = lax.psum(up_half, "fsdp").astype(jnp.float32)
    activation = (jax.nn.silu(gate_sum * inverse) * (up_sum * inverse)).astype(jnp.bfloat16)
    value = jnp.einsum("esf,efd->esd", activation, down_weight, preferred_element_type=jnp.float32)
    value = (value * score).astype(jnp.bfloat16)
    value = value.reshape(local_experts, n_tok, capacity, n_mod * columns).transpose(1, 0, 2, 3)

    own_kind = (mod_index * local_experts) // kind_experts
    valid = (flags == own_kind.astype(jnp.float32))[..., None]
    if n_mod == 2:
        value = value.reshape(n_tok, local_experts, capacity, n_mod, columns)
        kept = lax.dynamic_index_in_dim(value, mod_index, 3, False)
        sent = lax.dynamic_index_in_dim(value, 1 - mod_index, 3, False)
        got = lax.ppermute(sent, "mod", [(0, 1), (1, 0)])
        merged = jnp.where(valid, kept, got).reshape(n_tok, slots, columns)
    else:
        value = jnp.where(valid, value, jnp.zeros((), jnp.bfloat16))
        wide = jnp.zeros((n_tok, kind_experts, capacity, n_mod * columns), jnp.bfloat16)
        wide = lax.dynamic_update_slice_in_dim(wide, value, kind_first, 1)
        wide = wide.reshape(n_tok, slots, n_mod * columns)
        merged = lax.psum_scatter(wide, "mod", scatter_dimension=2, tiled=True)
    summed = reduce_tok(merged, n_tok)
    return jnp.dot(
        pick.astype(jnp.float32).T, summed, precision=lax.Precision.HIGHEST
    ).astype(jnp.bfloat16)


SWAP = [(0, 1), (1, 0)]
STRIP = 688
TILE = 16
ON_CHIP = pl.BlockSpec(memory_space=pltpu.VMEM)
IN_HBM = pl.BlockSpec(memory_space=pltpu.HBM)
ANYWHERE = pl.BlockSpec(memory_space=pl.ANY)


def crossed(bits, flip):
    return [(i, i ^ flip) for i in range(1 << bits)]


def call(kernel, name, outs, specs, args, scratch=(), flops=0, moved=0, limit=8 << 20):
    return pl.pallas_call(
        kernel,
        out_shape=outs,
        in_specs=specs,
        out_specs=jax.tree.map(lambda _: ON_CHIP, outs),
        scratch_shapes=list(scratch),
        compiler_params=pltpu.CompilerParams(vmem_limit_bytes=limit),
        cost_estimate=pl.CostEstimate(flops=flops, transcendentals=0, bytes_accessed=moved),
        name=name,
    )(*args)


def array(*shape, dtype=jnp.bfloat16):
    return jax.ShapeDtypeStruct(shape, dtype)


def keep_kernel(spans, after_ref, *refs):
    count = len(spans)
    weights, held, semaphores = refs[:count], refs[count : 2 * count], refs[-1]
    copies = [
        pltpu.make_async_copy(weight.at[lax.axis_index("groups"), a:b], to, semaphores.at[n])
        for n, (weight, to, (a, b)) in enumerate(zip(weights, held, spans))
    ]
    for copy in copies:
        copy.start()
    for copy in copies:
        copy.wait()


def in_hbm(value):
    return pltpu.with_memory_space_constraint(value, pltpu.HBM)


def keep_on_chip(after, weights, spans, name):
    return call(
        functools.partial(keep_kernel, spans),
        name,
        [pltpu.VMEM((b - a, weight.shape[2]), jnp.bfloat16) for weight, (a, b) in zip(weights, spans)],
        [ANYWHERE] + [IN_HBM] * len(spans),
        [after] + [in_hbm(weight) for weight in weights],
        scratch=[pltpu.SemaphoreType.DMA((len(spans),))],
        moved=sum(2 * (b - a) * weight.shape[2] for weight, (a, b) in zip(weights, spans)),
        limit=1 << 20,
    )


def select_kernel(
    rows_hbm, context_hbm, picked_ref, pick_ref, kind_ref, rows_ref, context_ref, semaphores
):
    rows_copy = pltpu.make_async_copy(rows_hbm, rows_ref, semaphores.at[0])
    context_copy = pltpu.make_async_copy(context_hbm, context_ref, semaphores.at[1])
    rows_copy.start()
    context_copy.start()
    rows_copy.wait()
    kind = jnp.where(jnp.maximum(rows_ref[2, 0], rows_ref[3, 0]) >= 0, 1, 0)
    kind_ref[...] = jnp.full(kind_ref.shape, kind, jnp.int32).astype(jnp.float32)
    capacity = rows_ref.shape[1]
    slots, tokens = pick_ref.shape
    row = lax.broadcasted_iota(jnp.int32, (slots, tokens), 0)
    token = lax.broadcasted_iota(jnp.int32, (slots, tokens), 1)
    wanted = jnp.full((slots, tokens), -1, jnp.int32)
    for e in range(2):
        expert = 2 * kind + (lax.axis_index("groups") ^ e)
        for s in range(capacity):
            wanted = jnp.where(row == e * capacity + s, rows_ref[expert, s], wanted)
    pick = jnp.where(wanted == token, 1.0, 0.0).astype(jnp.bfloat16)
    pick_ref[...] = pick
    context_copy.wait()
    picked_ref[...] = jnp.dot(pick, context_ref[...], preferred_element_type=jnp.float32).astype(jnp.bfloat16)


def keep_gate_kernel(
    pick_ref, residual_hbm, gate_ref, proj_ref, gate_held, proj_held, rest_ref, residual_ref, semaphores
):
    copies = [
        pltpu.make_async_copy(residual_hbm, residual_ref, semaphores.at[0]),
        pltpu.make_async_copy(proj_ref, proj_held, semaphores.at[1]),
        pltpu.make_async_copy(gate_ref.at[lax.axis_index("groups"), : gate_held.shape[0]], gate_held, semaphores.at[2]),
    ]
    for copy in copies:
        copy.start()
    copies[0].wait()
    rest_ref[...] = jnp.dot(pick_ref[...], residual_ref[...], preferred_element_type=jnp.float32)
    for copy in copies[1:]:
        copy.wait()


def join_kernel(near_ref, across_ref, _, out_ref):
    slots = near_ref.shape[0]
    out_ref[:slots, :] = near_ref[...]
    out_ref[slots:, :] = across_ref[...]


def project_kernel(joined_ref, other_ref, weight_ref, out_ref, rows_ref):
    pair = joined_ref.shape[0]
    slots = pair // 2
    rows_ref[:pair, :] = joined_ref[...]
    rows_ref[pair:, :] = other_ref[...]
    product = jnp.dot(rows_ref[...], weight_ref[...], preferred_element_type=jnp.float32)
    product = product.astype(jnp.bfloat16)
    corner = 2 * lax.axis_index("mod") + lax.axis_index("fsdp")
    flip = lax.axis_index("tok") ^ corner
    for n, u in enumerate((0, 2, 1, 3)):
        out_ref[flip ^ u] = product[n * slots : (n + 1) * slots, :]


def split_high_low(value):
    high = value.astype(jnp.bfloat16).astype(jnp.float32)
    return high, value - high


def norm_kernel(kind_ref, rest_ref, partial_ref, three_ref, two_ref, one_ref, gain_ref, router_ref, _, out_ref):
    slots, columns = rest_ref.shape
    hidden = rest_ref[...] + partial_ref[0].astype(jnp.float32)
    for got_ref in (three_ref, two_ref, one_ref):
        hidden = hidden + got_ref[...].astype(jnp.float32)
    kind = kind_ref[0:1, 0:1]
    gains = gain_ref[...].astype(jnp.float32)
    gained = hidden * jnp.where(kind == 0.0, gains[0:1], gains[1:2])
    out_ref[:, :columns] = gained.astype(jnp.bfloat16)
    table = router_ref[...].astype(jnp.float32)
    pieces = []
    for e in range(2):
        second = (lax.axis_index("groups") ^ e) == 1
        text = jnp.where(second, table[1:2], table[0:1])
        image = jnp.where(second, table[3:4], table[2:3])
        weights = jnp.where(kind == 0.0, text, image)
        half = slots // 2
        pieces.append(jnp.sum(gained[e * half : (e + 1) * half] * weights, axis=1, keepdims=True))
    logits = jnp.concatenate(pieces, axis=0)
    squares = jnp.sum(hidden * hidden, axis=1, keepdims=True)
    lane = lax.broadcasted_iota(jnp.int32, (slots, STAT_COLS), 1)
    extra = jnp.where(lane == 4, kind, 0.0)
    for at, stat in enumerate(split_high_low(squares) + split_high_low(logits)):
        extra = jnp.where(lane == at, stat, extra)
    out_ref[:, columns:] = extra.astype(jnp.bfloat16)


def places(packed_refs, columns):
    side = lax.axis_index("mod")
    matches, found, before = [], [], 0
    for v, ref in enumerate(packed_refs):
        flag = ref[:TILE, columns:].astype(jnp.float32)[0, 4]
        kind = jnp.where(flag > 0.5, 1, 0)
        match = kind == side
        place = jnp.minimum(jnp.where(match, before, v - before), len(packed_refs) - 2)
        matches.append(match)
        found.append(place)
        before = before + jnp.where(match, 1, 0)
    return matches, found


def arrange_kernel(zero_ref, three_ref, two_ref, one_ref, _, *out_refs):
    packed_refs = (zero_ref, one_ref, two_ref, three_ref)
    capacity = zero_ref.shape[0] // 2
    for out_ref in out_refs:
        out_ref[...] = jnp.zeros(out_ref.shape, out_ref.dtype)
    matches, found = places(packed_refs, zero_ref.shape[1] - STAT_COLS)
    for ref, match, place in zip(packed_refs, matches, found):
        span = pl.ds(pl.multiple_of(place * capacity, capacity), capacity)
        for wanted, (own_ref, given_ref) in ((True, out_refs[:2]), (False, out_refs[2:])):

            @pl.when(match == wanted)
            def _():
                own_ref[span, :] = ref[:capacity, :]
                given_ref[span, :] = ref[capacity:, :]


def weights_times_rows(weight_refs, spans, rows, out_ref):
    at = 0
    for weight_ref, (first, last) in zip(weight_refs, spans):
        for start in range(first, last, STRIP):
            stop = min(start + STRIP, last)
            out_ref[at : at + stop - start, :] = lax.dot_general(
                weight_ref[start:stop, :], rows, (((1,), (1,)), ((), ())), preferred_element_type=jnp.float32
            ).astype(jnp.bfloat16)
            at += stop - start


def gate_kernel(side_far_ref, side_own_ref, far_ref, own_ref, *refs):
    weight_refs, out_ref, rows_ref = refs[:2], refs[-2], refs[-1]
    half = own_ref.shape[0]
    rows = rows_ref.shape[0]
    units = out_ref.shape[0] - TILE
    columns = rows_ref.shape[1] // 2
    rows_ref[2 * half :, :] = jnp.zeros((rows - 2 * half, 2 * columns), rows_ref.dtype)
    for side in range(2):

        @pl.when(lax.axis_index("mod") == side)
        def _():
            here, there = side * columns, (1 - side) * columns
            rows_ref[:half, here : here + columns] = own_ref[:, :columns]
            rows_ref[half : 2 * half, here : here + columns] = far_ref[:, :columns]
            rows_ref[:half, there : there + columns] = side_own_ref[:, :columns]
            rows_ref[half : 2 * half, there : there + columns] = side_far_ref[:, :columns]

    spans = [(0, ref.shape[0]) for ref in weight_refs]
    weights_times_rows(weight_refs, spans, rows_ref[...], out_ref)
    tails = [ref[:, columns:].astype(jnp.float32) for ref in (own_ref, side_own_ref, far_ref, side_far_ref)]
    unused = jnp.zeros((rows - 2 * half, STAT_COLS), jnp.float32)
    stat = jnp.concatenate([tails[0] + tails[1], tails[2] + tails[3], unused], axis=0).T
    squares = stat[0:1] + stat[1:2]
    logits = stat[2:3] + stat[3:4]
    at_row = lax.broadcasted_iota(jnp.int32, (TILE, rows), 0)
    extra = jnp.zeros((TILE, rows), jnp.float32)
    for at, piece in enumerate(split_high_low(squares) + split_high_low(logits)):
        extra = jnp.where(at_row == at, piece, extra)
    out_ref[units:, :] = extra.astype(jnp.bfloat16)


def up_kernel(spans, rows_ref, *refs):
    weights_times_rows(refs[:-1], spans, rows_ref[...], refs[-1])


def activation_kernel(gate_ref, gate_other_ref, up_ref, up_other_ref, act_ref, silu_ref, stat_ref):
    early = act_ref.shape[0]
    units = early + silu_ref.shape[0]
    stat = gate_ref[units:, :].astype(jnp.float32) + gate_other_ref[units:, :].astype(jnp.float32)
    inverse = lax.rsqrt((stat[0:1] + stat[1:2]) / D + 1e-05)
    logits = (stat[2:3] + stat[3:4]) * inverse
    score = 1.0 / (1.0 + jnp.exp(-logits))
    at_row = lax.broadcasted_iota(jnp.int32, stat_ref.shape, 0)
    stat_ref[...] = jnp.where(at_row == 0, inverse, score)
    for start in range(0, units, STRIP):
        stop = min(start + STRIP, units)
        gate = gate_ref[start:stop, :].astype(jnp.float32) + gate_other_ref[start:stop, :].astype(jnp.float32)
        gate = gate * inverse
        silu = gate / (1.0 + jnp.exp(-gate)) * inverse
        inside = max(0, min(stop, early) - start)
        if inside:
            span = slice(start, start + inside)
            up = up_ref[span, :].astype(jnp.float32) + up_other_ref[span, :].astype(jnp.float32)
            act_ref[span, :] = (silu[:inside] * up).astype(jnp.bfloat16)
        if start + inside < stop:
            silu_ref[start + inside - early : stop - early, :] = silu[inside:]


def down_kernel(
    act_early_ref, silu_ref, stat_ref, up_ref, other_ref, first_ref, second_ref,
    kept_ref, far_ref, side_ref, side_far_ref, act_ref,
):
    units, rows = act_ref.shape
    early = act_early_ref.shape[0]
    act_ref[:early, :] = act_early_ref[...]
    up = up_ref[...].astype(jnp.float32) + other_ref[...].astype(jnp.float32)
    act_ref[early:, :] = (silu_ref[...] * up).astype(jnp.bfloat16)
    half, columns = kept_ref.shape
    score = jnp.broadcast_to(stat_ref[1:2, :], (rows, rows)).T[:, 0:1]
    first_units = first_ref.shape[0]
    for quarter in range(2):
        span = slice(quarter * columns, (quarter + 1) * columns)
        value = sum(
            lax.dot_general(
                act_ref[a:b, :], weight_ref[:, span], (((0,), (0,)), ((), ())), preferred_element_type=jnp.float32
            )
            for a, b, weight_ref in ((0, first_units, first_ref), (first_units, units, second_ref))
        )
        value = (value * score).astype(jnp.bfloat16)
        for across, (own_out, far_out) in enumerate(((kept_ref, far_ref), (side_ref, side_far_ref))):

            @pl.when((lax.axis_index("mod") ^ quarter) == across)
            def _():
                own_out[...] = value[:half]
                far_out[...] = value[half : 2 * half]


def merge_kernel(zero_ref, three_ref, two_ref, one_ref, kept_ref, side_ref, far_ref, side_far_ref, *out_refs):
    columns = kept_ref.shape[1]
    capacity = zero_ref.shape[0] // 2
    matches, found = places((zero_ref, one_ref, two_ref, three_ref), columns)
    for out_ref, match, place in zip(out_refs, matches, found):
        span = pl.ds(pl.multiple_of(place * capacity, capacity), capacity)
        for wanted, (first_ref, second_ref) in ((True, (kept_ref, far_ref)), (False, (side_ref, side_far_ref))):

            @pl.when(match == wanted)
            def _():
                out_ref[:capacity, :] = first_ref[span, :]
                out_ref[capacity:, :] = second_ref[span, :]


def add_kernel(zero_ref, one_ref, two_ref, out_ref):
    out_ref[...] = (
        zero_ref[...].astype(jnp.float32) + one_ref[...].astype(jnp.float32) + two_ref[...].astype(jnp.float32)
    )


def scatter_kernel(pick_ref, sum_ref, three_ref, out_hbm, out_ref, semaphores):
    columns = out_ref.shape[1]
    pieces = semaphores.shape[0]
    width = columns // pieces
    copies = []
    for n in range(pieces):
        span = slice(n * width, (n + 1) * width)
        total = sum_ref[:, span] + three_ref[:, span].astype(jnp.float32)
        result = 0.0
        for piece in split_high_low(total)[::-1]:
            result = result + lax.dot_general(
                pick_ref[...], piece.astype(jnp.bfloat16), (((0,), (0,)), ((), ())),
                preferred_element_type=jnp.float32,
            )
        out_ref[:, span] = result.astype(jnp.bfloat16)
        copies.append(pltpu.make_async_copy(out_ref.at[:, span], out_hbm.at[:, span], semaphores.at[n]))
        copies[-1].start()
    for copy in copies:
        copy.wait()


def paired_local(
    residual,
    context,
    out_proj,
    norm_gain,
    router_weight,
    block_modality,
    expert_rows,
    gate_weight,
    up_weight,
    down_weight,
):
    tokens, columns = residual.shape
    experts, capacity = expert_rows.shape
    slots = 2 * capacity
    half = 4 * capacity
    rows = 2 * half
    units, width = down_weight.shape[1:]
    assert block_modality.shape == (1,) and experts == 4 and gate_weight.shape[0] == 2
    picked, pick, kind = call(
        select_kernel,
        "select",
        [array(slots, columns), array(slots, tokens), array(8, STAT_COLS, dtype=jnp.float32)],
        [IN_HBM] * 2,
        [in_hbm(expert_rows), in_hbm(context)],
        scratch=[
            pltpu.SMEM((experts, capacity), jnp.int32),
            pltpu.VMEM((tokens, columns), jnp.bfloat16),
            pltpu.SemaphoreType.DMA((2,)),
        ],
    )
    plane = ("tok", "mod", "fsdp")
    to_first = [(t * 4 + q, q * 4 + t) for t in range(4) for q in range(4)]
    to_second = [(t * 4 + q, q * 4 + (t ^ 2)) for t in range(4) for q in range(4)]
    across = lax.ppermute(picked, plane, to_second)
    near = lax.ppermute(picked, plane, to_first)
    gate_units, up_units, down_units = [round(units * part / TILE) * TILE for part in (0.3, 0.32, 0.29)]
    gate_first, proj_held, rest = call(
        keep_gate_kernel,
        "keep_gate",
        [
            pltpu.VMEM((gate_units, width), jnp.bfloat16),
            pltpu.VMEM(out_proj.shape, jnp.bfloat16),
            array(slots, columns, dtype=jnp.float32),
        ],
        [ON_CHIP, IN_HBM, IN_HBM, IN_HBM],
        [pick, in_hbm(residual), in_hbm(gate_weight.swapaxes(1, 2)), in_hbm(out_proj)],
        scratch=[pltpu.VMEM((tokens, columns), jnp.bfloat16), pltpu.SemaphoreType.DMA((3,))],
        moved=units * width,
        limit=2 << 20,
    )
    joined = call(join_kernel, "join", array(half, columns), [ON_CHIP] * 3, [near, across, gate_first])
    other = lax.ppermute(joined, "fsdp", SWAP)
    partial = call(
        project_kernel,
        "project",
        array(4, slots, columns),
        [ON_CHIP] * 3,
        [joined, other, proj_held],
        scratch=[pltpu.VMEM((rows, columns), jnp.bfloat16)],
    )
    sums = [lax.ppermute(partial[v], "tok", crossed(2, v)) for v in (3, 2, 1)][::-1]
    gate_second, up_first = keep_on_chip(
        partial,
        [gate_weight.swapaxes(1, 2), up_weight.swapaxes(1, 2)],
        [(gate_units, units), (0, up_units)],
        "keep_more",
    )
    packed_columns = columns + STAT_COLS
    packed = call(
        norm_kernel,
        "norm",
        array(slots, packed_columns),
        [ON_CHIP] * 9,
        [kind, rest, partial, *sums[::-1], norm_gain, router_weight.T, up_first],
    )
    others = [lax.ppermute(packed, "tok", crossed(2, v)) for v in (3, 2, 1)][::-1]
    up_second, down_first = keep_on_chip(
        packed,
        [up_weight.swapaxes(1, 2), down_weight],
        [(up_units, units), (0, down_units)],
        "keep_up",
    )
    kept_slots = 3 * capacity
    own, to_far_rows, to_side_rows, to_corner_rows = call(
        arrange_kernel,
        "arrange",
        [array(kept_slots, packed_columns)] * 4,
        [ON_CHIP] * 5,
        [packed, *others[::-1], up_second],
    )
    both_axes = ("groups", "mod")
    side_far = lax.ppermute(to_corner_rows, both_axes, crossed(2, 3))
    far = lax.ppermute(to_far_rows, "groups", SWAP)
    side_own = lax.ppermute(to_side_rows, "mod", SWAP)

    (down_second,) = keep_on_chip(own, [down_weight], [(down_units, units)], "keep_down")

    flops = 2 * rows * units * width
    gate, gathered = call(
        gate_kernel,
        "gate",
        [array(units + TILE, rows), array(rows, width)],
        [ON_CHIP] * 7,
        [side_far, side_own, far, own, gate_first, gate_second, down_second],
        flops=flops,
    )
    late = units // 4 // TILE * TILE
    up_rest = units - up_units
    up_parts = [
        call(
            functools.partial(up_kernel, spans),
            "up",
            array(sum(b - a for a, b in spans), rows),
            [ON_CHIP] * (1 + len(spans)),
            [gathered, *weights],
            flops=flops * sum(b - a for a, b in spans) // units,
        )
        for spans, weights in (
            (((0, up_units), (0, up_rest - late)), (up_first, up_second)),
            (((up_rest - late, up_rest),), (up_second,)),
        )
    ]
    gate_other = lax.ppermute(gate, "fsdp", SWAP)
    up_others = [lax.ppermute(part, "fsdp", SWAP) for part in up_parts]
    act_early, silu_late, stat = call(
        activation_kernel,
        "activation",
        [
            array(units - late, rows),
            array(late, rows, dtype=jnp.float32),
            array(8, rows, dtype=jnp.float32),
        ],
        [ON_CHIP] * 4,
        [gate, gate_other, up_parts[0], up_others[0]],
        moved=8 * units * rows,
    )
    kept, to_far, to_side, to_side_far = call(
        down_kernel,
        "down",
        [array(kept_slots, columns)] * 4,
        [ON_CHIP] * 7,
        [act_early, silu_late, stat, up_parts[1], up_others[1], down_first, down_second],
        scratch=[pltpu.VMEM((units, rows), jnp.bfloat16)],
        flops=flops,
    )
    from_side_far = lax.ppermute(to_side_far, both_axes, crossed(2, 3))
    from_far = lax.ppermute(to_far, "groups", SWAP)
    from_side = lax.ppermute(to_side, "mod", SWAP)
    merged = call(
        merge_kernel,
        "merge",
        [array(slots, columns)] * 4,
        [ON_CHIP] * 8,
        [packed, *others[::-1], kept, from_side, from_far, from_side_far],
    )
    values = [merged[0]] + [lax.ppermute(merged[v], "tok", crossed(2, v)) for v in (1, 2, 3)]
    begun = call(add_kernel, "add", array(slots, columns, dtype=jnp.float32), [ON_CHIP] * 3, values[:3])
    return pl.pallas_call(
        scatter_kernel,
        out_shape=pltpu.HBM((tokens, columns), jnp.bfloat16),
        in_specs=[ON_CHIP] * 3,
        out_specs=IN_HBM,
        scratch_shapes=[pltpu.VMEM((tokens, columns), jnp.bfloat16), pltpu.SemaphoreType.DMA((4,))],
        compiler_params=pltpu.CompilerParams(vmem_limit_bytes=8 << 20),
        name="scatter",
    )(pick, begun, values[3])


def solution(mesh):
    placed = (
        P(("groups", "tok"), ("fsdp", "mod")),
        P(("groups", "tok"), ("mod", "fsdp")),
        P("tok", ("fsdp", "mod")),
        P(None, ("fsdp", "mod")),
        P(("fsdp", "mod"), None),
        P(("groups", "tok")),
        P(None, ("groups", "tok")),
        P("mod", "fsdp", "tok"),
        P("mod", "fsdp", "tok"),
        P("mod", "tok", "fsdp"),
    )
    sizes = dict(n_tok=mesh.shape["tok"], n_mod=mesh.shape["mod"], n_fsdp=mesh.shape["fsdp"])
    paired = (
        mesh.shape["groups"] == 2
        and sizes == dict(n_tok=4, n_mod=2, n_fsdp=2)
    )
    body = paired_local if paired else functools.partial(local, **sizes)
    return jax.shard_map(
        body,
        mesh=mesh,
        in_specs=placed,
        out_specs=P(("groups", "tok"), ("fsdp", "mod")),
        check_vma=False,
    )
```
